32 devices in a mesh: dp: 8 (over z, x), mp: 4 (over y, core).
Axes of the slice: x: 2, y: 2, z: 4, core: 2. Of those that a mesh axis runs over, the one named last changes fastest.
Arguments:
- token_ids: int32 [16, 1024], P('dp'), may hold values from 0 to 30719
- type_ids: int32 [16, 1024], P('dp'), may hold values from 0 to 1, as said below
- mask_pos: int32 [16, 256], P('dp'), may hold values from 1 to 1023, as said below
- mask_valid: int32 [16, 256], P('dp'), may hold values from 0 to 1, as said below
- mlm_labels: int32 [16, 256], P('dp'), may hold values from 0 to 30719
- nsp_labels: int32 [16], P('dp'), may hold values from 0 to 1
- word_table: float32 [30720, 768], P(('mp', 'dp')), may hold values from -0.4375 to 0.4375
- word_m: float32 [30720, 768], P(('mp', 'dp')), may hold values from -5.722046e-06 to 5.722046e-06
- word_v: float32 [30720, 768], P(('mp', 'dp')), may hold values from 3.8244378e-14 to 6.1191005e-13
- attn_weight: float32 [768, 4, 768], P('dp', None, 'mp')
- attn_m: float32 [768, 4, 768], P('dp', None, 'mp'), may hold values from -5.722046e-06 to 5.722046e-06
- attn_v: float32 [768, 4, 768], P('dp', None, 'mp'), may hold values from 3.8244378e-14 to 6.1191005e-13
- ff_weight: float32 [768, 2, 3072], P('dp', None, 'mp'), may hold values from -0.21875 to 0.21875
- ff_m: float32 [768, 2, 3072], P('dp', None, 'mp'), may hold values from -5.722046e-06 to 5.722046e-06
- ff_v: float32 [768, 2, 3072], P('dp', None, 'mp'), may hold values from 3.8244378e-14 to 6.1191005e-13
- side_weight: float32 [2560, 768], P('dp'), may hold values from -0.21875 to 0.21875
- side_m: float32 [2560, 768], P('dp'), may hold values from -5.722046e-06 to 5.722046e-06
- side_v: float32 [2560, 768], P('dp'), may hold values from 3.8244378e-14 to 6.1191005e-13
- vectors: float32 [16, 768], P(None, 'dp')
- vec_m: float32 [16, 768], P(None, 'dp'), may hold values from -2.2888184e-05 to 2.2888184e-05
- vec_v: float32 [16, 768], P(None, 'dp'), may hold values from 6.1191005e-13 to 9.790561e-12
- split_bias: float32 [6, 768], P(None, 'mp'), may hold values from -1.25 to 1.25
- split_m: float32 [6, 768], P(None, 'mp'), may hold values from -2.2888184e-05 to 2.2888184e-05
- split_v: float32 [6, 768], P(None, 'mp'), may hold values from 6.1191005e-13 to 9.790561e-12
- decoder_bias: float32 [30720], P('mp'), may hold values from -3 to 3
- decoder_m: float32 [30720], P('mp'), may hold values from -2.2888184e-05 to 2.2888184e-05
- decoder_v: float32 [30720], P('mp'), may hold values from 6.1191005e-13 to 9.790561e-12
Outputs:
- total_loss: float32 [], replicated
- grad_norm: float32 [], replicated
- new_word: float32 [30720, 768], P(('mp', 'dp'))
- new_word_m: float32 [30720, 768], P(('mp', 'dp'))
- new_word_v: float32 [30720, 768], P(('mp', 'dp'))
- new_attn: float32 [768, 4, 768], P('dp', None, 'mp')
- new_attn_m: float32 [768, 4, 768], P('dp', None, 'mp')
- new_attn_v: float32 [768, 4, 768], P('dp', None, 'mp')
- new_ff: float32 [768, 2, 3072], P('dp', None, 'mp')
- new_ff_m: float32 [768, 2, 3072], P('dp', None, 'mp')
- new_ff_v: float32 [768, 2, 3072], P('dp', None, 'mp')
- new_side: float32 [2560, 768], P('dp')
- new_side_m: float32 [2560, 768], P('dp')
- new_side_v: float32 [2560, 768], P('dp')
- new_vec: float32 [16, 768], P(None, 'dp')
- new_vec_m: float32 [16, 768], P(None, 'dp')
- new_vec_v: float32 [16, 768], P(None, 'dp')
- new_split: float32 [6, 768], P(None, 'mp')
- new_split_m: float32 [6, 768], P(None, 'mp')
- new_split_v: float32 [6, 768], P(None, 'mp')
- new_decoder: float32 [30720], P('mp')
- new_decoder_m: float32 [30720], P('mp')
- new_decoder_v: float32 [30720], P('mp')
The draws below stay inside these ranges and needn't reach their ends.
Inputs may be any that keep to these rules, and one draw needn't show every extreme that they name: `type_ids`: 0 up to a split point and 1 from it on; the split lies between 256 and 768. `mask_pos`: slots of one sequence hold distinct positions, never 0; slots beyond a sequence's count hold positions too, without effect. `mask_valid`: each sequence's valid slots come first; counts vary from sequence to sequence, between 1 and 256; in every draw one sequence has all 256 slots valid.
All inputs are finite; a program needn't handle non-finite values.
Results may differ from the reference program's by a relative error of at most 0.012.
The reference program's roundings to bfloat16 on the way count: a program that leaves them out, or rounds other values in their place, can miss the bound.
Values may be sent and summed in bfloat16 or wider, within the bound.
A program may use at most 256 MiB of HBM per device.

```python
import math
import jax
import jax.numpy as jnp
import numpy as np
from jax import lax

D = 768
HEADS = 12
HEAD_DIM = 64
FF = 3072
VOCAB = 30720
SEQ = 1024
MASK_MAX = 256
NVEC = 16
SEQS = 16
NPARAM = 32684544


def mask_layout(key):
    jitter_key, order_key = jax.random.split(jax.random.fold_in(key, 7), 2)
    seq_index = lax.iota(jnp.int32, SEQS)
    low_count = MASK_MAX // 8
    ramp = low_count + (MASK_MAX - low_count) * seq_index // max(SEQS - 1, 1)
    jitter = jax.random.randint(jitter_key, (SEQS,), -(MASK_MAX // 16), MASK_MAX // 16 + 1)
    counts = jnp.clip(ramp + jitter, 1, MASK_MAX)
    counts = jnp.where(seq_index == SEQS - 1, MASK_MAX, counts)
    ranking = jax.random.randint(order_key, (SEQS, SEQ - 1), 0, 1 << 20) * SEQ + lax.broadcasted_iota(jnp.int32, (SEQS, SEQ - 1), 1)
    ordering = jnp.argsort(ranking, axis=1)[:, :MASK_MAX].astype(jnp.int32) + 1
    valid_rows = (lax.broadcasted_iota(jnp.int32, (SEQS, MASK_MAX), 1) < counts[:, None]).astype(jnp.int32)
    return (ordering, valid_rows)


def draw_mask_pos(key, part):
    return mask_layout(key)[0]


def draw_mask_valid(key, part):
    return mask_layout(key)[1]


def draw_type_ids(key, part):
    split_at = jax.random.randint(key, (SEQS, 1), SEQ // 4, 3 * SEQ // 4 + 1)
    return (lax.broadcasted_iota(jnp.int32, (SEQS, SEQ), 1) >= split_at).astype(jnp.int32)


def draw_attn_weight(key, part):
    normal_draw = jax.random.normal(key, (D, 4, D), jnp.float32) * D ** (-0.5)
    factor = jnp.where(lax.broadcasted_iota(jnp.int32, (1, 4, 1), 1) == 3, 16.0, 1.0)
    return normal_draw * factor


def draw_vectors(key, part):
    row_index = lax.broadcasted_iota(jnp.int32, (NVEC, D), 0)
    noises = jax.random.normal(key, (NVEC, D), jnp.float32)
    is_gain = (row_index == 0) | (row_index == 3) | (row_index == 6) | (row_index == 9)
    spread = jnp.where(is_gain, 0.1, jnp.where(row_index >= 14, 2.2 * D ** (-0.5), jnp.where(row_index >= 12, 0.07, 0.3)))
    return jnp.where(is_gain, 1.0, 0.0) + noises * spread


def plant(result, key, least, top_value):
    longest = result.shape.index(max(result.shape))
    spots = []
    for shift in (0, 1):
        where = [jax.random.randint(jax.random.fold_in(key, axis), (), 0, length) for axis, length in enumerate(result.shape)]
        where[longest] = (where[longest] + shift) % result.shape[longest]
        spots.append(tuple(where))
    return result.at[spots[0]].set(least).at[spots[1]].set(top_value)


def shard_levels(rng, dims, shards, low, largest):
    def one(axis_at, blocks):
        draws = jax.random.uniform(jax.random.fold_in(jax.random.fold_in(rng, 6), axis_at), (blocks,), jnp.float32, low / len(shards), largest / len(shards))
        return jnp.repeat(jnp.exp(draws), dims[axis_at] // blocks).reshape((-1,) + (1,) * (len(dims) - axis_at - 1))

    factor_of = one(*shards[0])
    for cut in shards[1:]:
        factor_of = factor_of * one(*cut)
    return factor_of


def rank_table(count, lean):
    portions = [(1 << 20) // math.isqrt(grade ** lean) + 1 for grade in range(1, count + 1)]
    scale = 1 + sum(portions) // (1 << 30)
    return np.cumsum(np.array([max(1, weight // scale) for weight in portions]))


def ranked_ids(own_key, extent, number_of, lean):
    listing = rank_table(number_of, lean)
    pick = jax.random.randint(jax.random.fold_in(own_key, 1), extent, 0, int(listing[number_of - 1]))
    standing = jnp.searchsorted(jnp.asarray(listing, jnp.int32), pick, side="right")
    return jax.random.permutation(jax.random.fold_in(own_key, 2), number_of)[standing].astype(jnp.int32)


def normal_values(own_key, shape, width, most, pieces=(), kind=jnp.bfloat16):
    factor_of = shard_levels(own_key, shape, pieces, -0.22, 0.18) if pieces else 1.0
    values = jax.random.normal(own_key, shape, jnp.float32) * width * factor_of
    return jnp.minimum(jnp.maximum(values, -most), most).astype(kind)


def setup_inputs(seed: int = 0) -> dict:
    key_list = jax.random.split(jax.random.key(seed), 28)
    return {
        "token_ids": plant(ranked_ids(key_list[0], (SEQS, SEQ), VOCAB, 2), jax.random.fold_in(key_list[0], 3), 0, VOCAB - 1).astype(jnp.int32),
        "type_ids": draw_type_ids(jax.random.fold_in(key_list[27], 71), 0),
        "mask_pos": draw_mask_pos(jax.random.fold_in(key_list[27], 71), 0),
        "mask_valid": draw_mask_valid(jax.random.fold_in(key_list[27], 71), 0),
        "mlm_labels": plant(ranked_ids(key_list[4], (SEQS, MASK_MAX), VOCAB, 2), jax.random.fold_in(key_list[4], 3), 0, VOCAB - 1).astype(jnp.int32),
        "nsp_labels": plant(jax.random.randint(key_list[5], (SEQS,), 0, 2), jax.random.fold_in(key_list[5], 1), 0, 1).astype(jnp.int32),
        "word_table": normal_values(key_list[6], (VOCAB, D), (D // 4) ** -0.5, 0.4375, ((0, 32),), jnp.float32),
        "word_m": normal_values(key_list[7], (VOCAB, D), (0.0055 * NPARAM ** -0.5), 5.7220458984375e-06, ((0, 32),), jnp.float32),
        "word_v": jnp.clip(jnp.exp(math.log(6.119100452034454e-13) - 2.7725887 * jax.random.uniform(key_list[8], (VOCAB, D), jnp.float32) ** shard_levels(key_list[8], (VOCAB, D), ((0, 32),), -0.2, 0.2)), 3.8244377825215337e-14, 6.119100452034454e-13),
        "attn_weight": draw_attn_weight(jax.random.fold_in(key_list[27], 71), 0),
        "attn_m": normal_values(key_list[10], (D, 4, D), (0.0055 * NPARAM ** -0.5), 5.7220458984375e-06, ((0, 8), (2, 4)), jnp.float32),
        "attn_v": jnp.clip(jnp.exp(math.log(6.119100452034454e-13) - 2.7725887 * jax.random.uniform(key_list[11], (D, 4, D), jnp.float32) ** shard_levels(key_list[11], (D, 4, D), ((0, 8), (2, 4)), -0.2, 0.2)), 3.8244377825215337e-14, 6.119100452034454e-13),
        "ff_weight": normal_values(key_list[12], (D, 2, FF), D ** -0.5, 0.21875, ((0, 8), (2, 4)), jnp.float32),
        "ff_m": normal_values(key_list[13], (D, 2, FF), (0.0055 * NPARAM ** -0.5), 5.7220458984375e-06, ((0, 8), (2, 4)), jnp.float32),
        "ff_v": jnp.clip(jnp.exp(math.log(6.119100452034454e-13) - 2.7725887 * jax.random.uniform(key_list[14], (D, 2, FF), jnp.float32) ** shard_levels(key_list[14], (D, 2, FF), ((0, 8), (2, 4)), -0.2, 0.2)), 3.8244377825215337e-14, 6.119100452034454e-13),
        "side_weight": normal_values(key_list[15], (2 * D + SEQ, D), D ** -0.5, 0.21875, ((0, 8),), jnp.float32),
        "side_m": normal_values(key_list[16], (2 * D + SEQ, D), (0.0055 * NPARAM ** -0.5), 5.7220458984375e-06, ((0, 8),), jnp.float32),
        "side_v": jnp.clip(jnp.exp(math.log(6.119100452034454e-13) - 2.7725887 * jax.random.uniform(key_list[17], (2 * D + SEQ, D), jnp.float32) ** shard_levels(key_list[17], (2 * D + SEQ, D), ((0, 8),), -0.2, 0.2)), 3.8244377825215337e-14, 6.119100452034454e-13),
        "vectors": draw_vectors(jax.random.fold_in(key_list[27], 71), 0),
        "vec_m": normal_values(key_list[19], (NVEC, D), (0.022 * NPARAM ** -0.5), 2.288818359375e-05, ((1, 8),), jnp.float32),
        "vec_v": jnp.clip(jnp.exp(math.log(9.790560723255126e-12) - 2.7725887 * jax.random.uniform(key_list[20], (NVEC, D), jnp.float32) ** shard_levels(key_list[20], (NVEC, D), ((1, 8),), -0.2, 0.2)), 6.119100452034454e-13, 9.790560723255126e-12),
        "split_bias": normal_values(key_list[21], (6, D), 0.2, 1.25, ((1, 4),), jnp.float32),
        "split_m": normal_values(key_list[22], (6, D), (0.022 * NPARAM ** -0.5), 2.288818359375e-05, ((1, 4),), jnp.float32),
        "split_v": jnp.clip(jnp.exp(math.log(9.790560723255126e-12) - 2.7725887 * jax.random.uniform(key_list[23], (6, D), jnp.float32) ** shard_levels(key_list[23], (6, D), ((1, 4),), -0.2, 0.2)), 6.119100452034454e-13, 9.790560723255126e-12),
        "decoder_bias": normal_values(key_list[24], (VOCAB,), 0.5, 3.0, ((0, 4),), jnp.float32),
        "decoder_m": normal_values(key_list[25], (VOCAB,), (0.022 * NPARAM ** -0.5), 2.288818359375e-05, ((0, 4),), jnp.float32),
        "decoder_v": jnp.clip(jnp.exp(math.log(9.790560723255126e-12) - 2.7725887 * jax.random.uniform(key_list[26], (VOCAB,), jnp.float32) ** shard_levels(key_list[26], (VOCAB,), ((0, 4),), -0.2, 0.2)), 6.119100452034454e-13, 9.790560723255126e-12),
    }


beta_one = 0.9
beta_two = 0.999
adam_eps = 1e-06
learn_rate = 0.2
decay_rate = 0.01
step_count = 10
max_norm = 0.05
norm_eps = 1e-12
highest = lax.Precision.HIGHEST

@jax.custom_vjp
def low(v):
    return lax.optimization_barrier(v.astype(jnp.bfloat16)).astype(jnp.float32)

@jax.custom_vjp
def low_back(v):
    return v

def low_keep(v):
    return (low(v), None)

def low_pass(kept, grad):
    return (grad,)

def back_keep(v):
    return (v, None)

def back_low(kept, grad):
    return (low(grad),)
low.defvjp(low_keep, low_pass)
low_back.defvjp(back_keep, back_low)

def layer_norm(inputs, norm_gain, norm_shift):
    center = inputs - lax.optimization_barrier(jnp.mean(inputs, axis=-1, keepdims=True))
    spread = lax.optimization_barrier(jnp.mean(center * center, axis=-1, keepdims=True))
    return center * lax.rsqrt(spread + norm_eps) * norm_gain + norm_shift

def gelu_exact(inputs):
    return jax.nn.gelu(inputs, approximate=False)

def adam_step(weight, moment, square, gradient, clip_scale, decays):
    gradient = gradient * clip_scale
    moment = beta_one * moment + (1 - beta_one) * gradient
    square = beta_two * square + (1 - beta_two) * gradient * gradient
    mean_hat = moment / (1 - beta_one ** step_count)
    var_hat = square / (1 - beta_two ** step_count)
    change = mean_hat / (jnp.sqrt(var_hat) + adam_eps)
    if decays:
        change = change + decay_rate * weight
    return (weight - learn_rate * change, moment, square)

def sequence_loss(params, tokens, type_row, positions, valid_row, labels, nsp_label, total_count, total_seqs):
    word, attn, ffw, side, vecs, split, decoder = params
    word_lo = low(word)
    attn_lo = low(attn)
    ffw_lo = low(ffw)
    side_lo = low(side)
    vecs_lo = low(vecs)
    score_scale = 1.0 / math.sqrt(HEAD_DIM)
    embedded = word_lo[tokens] + side_lo[2 * D:] + jnp.where(type_row[:, None] == 0, vecs_lo[12], vecs_lo[13])
    hidden0 = layer_norm(embedded, vecs_lo[0], vecs_lo[1])
    packed = jnp.einsum('sd,dch->sch', low(hidden0), attn_lo[:, :3, :], precision=highest)
    queries = low(low_back(packed[:, 0] + split[0])).reshape(SEQ, HEADS, HEAD_DIM)
    key_rows = low(low_back(packed[:, 1])).reshape(SEQ, HEADS, HEAD_DIM)
    value_rows = low(low_back(packed[:, 2] + split[1])).reshape(SEQ, HEADS, HEAD_DIM)
    scores = low_back(jnp.einsum('qhe,khe->hqk', queries, key_rows, precision=highest) * score_scale)
    attn_probs = jax.nn.softmax(scores, axis=-1)
    mixed_heads = jnp.einsum('hqk,khe->qhe', low(attn_probs), value_rows, precision=highest).reshape(SEQ, D)
    mixed_heads = low(low_back(mixed_heads))
    attn_out = low_back(jnp.einsum('sh,dh->sd', mixed_heads, attn_lo[:, 3, :], precision=highest) + vecs_lo[2])
    hidden1 = layer_norm(hidden0 + attn_out, vecs_lo[3], vecs_lo[4])
    ff_bias = split[2:6].T.reshape(FF)
    upward = low_back(jnp.einsum('sd,df->sf', low(hidden1), ffw_lo[:, 0, :], precision=highest) + ff_bias)
    active = low(gelu_exact(upward))
    ffn_out = low_back(jnp.einsum('sf,df->sd', active, ffw_lo[:, 1, :], precision=highest) + vecs_lo[5])
    hidden2 = layer_norm(hidden1 + ffn_out, vecs_lo[6], vecs_lo[7])
    picked = hidden2[positions]
    dense_out = low_back(jnp.dot(low(picked), side_lo[D:2 * D], precision=highest) + vecs_lo[8])
    head_rows = layer_norm(gelu_exact(dense_out), vecs_lo[9], vecs_lo[10])
    logits = low_back(jnp.einsum('rd,vd->rv', low(head_rows), word_lo, precision=highest) + decoder)
    logprob = jax.nn.log_softmax(logits, axis=-1)
    target = jnp.take_along_axis(logprob, labels[:, None], axis=1)[:, 0]
    mlm_sum = -jnp.sum(valid_row * target)
    pooled = jnp.tanh(jnp.dot(low(hidden2[0]), side_lo[:D], precision=highest) + vecs_lo[11])
    nsp_logp = jax.nn.log_softmax(jnp.dot(vecs_lo[14:16], pooled, precision=highest))
    nsp_term = -jnp.sum(jnp.where(jnp.arange(2) == nsp_label, nsp_logp, 0.0))
    return mlm_sum / total_count + nsp_term / total_seqs

def reference(token_ids, type_ids, mask_pos, mask_valid, mlm_labels, nsp_labels, word_table, word_m, word_v, attn_weight, attn_m, attn_v, ff_weight, ff_m, ff_v, side_weight, side_m, side_v, vectors, vec_m, vec_v, split_bias, split_m, split_v, decoder_bias, decoder_m, decoder_v):
    params = (word_table, attn_weight, ff_weight, side_weight, vectors, split_bias, decoder_bias)
    validity = mask_valid.astype(jnp.float32)
    total_count = jnp.sum(validity)
    total_seqs = jnp.float32(token_ids.shape[0])

    def one_step(running, seq_items):
        grad_sums, loss_sum = running
        tokens, type_row, positions, valid_row, labels, nsp_label = seq_items

        def loss_of(*members):
            return sequence_loss(members, tokens, type_row, positions, valid_row, labels, nsp_label, total_count, total_seqs)
        seq_loss, pullback = jax.vjp(loss_of, *params)
        gradients = pullback(jnp.ones_like(seq_loss))
        summed = tuple((left_part + right_part for left_part, right_part in zip(grad_sums, gradients)))
        return ((summed, loss_sum + seq_loss), None)
    start = (tuple((jnp.zeros_like(member) for member in params)), jnp.zeros((), jnp.float32))
    (gradients, total_loss), _ = lax.scan(one_step, start, (token_ids, type_ids, mask_pos, validity, mlm_labels, nsp_labels))
    grad_norm = jnp.sqrt(sum((jnp.sum(member * member) for member in gradients)))
    clip_scale = max_norm / jnp.maximum(grad_norm, max_norm)
    word_new = adam_step(word_table, word_m, word_v, gradients[0], clip_scale, True)
    attn_new = adam_step(attn_weight, attn_m, attn_v, gradients[1], clip_scale, True)
    ff_new = adam_step(ff_weight, ff_m, ff_v, gradients[2], clip_scale, True)
    side_new = adam_step(side_weight, side_m, side_v, gradients[3], clip_scale, True)
    vec_new = adam_step(vectors, vec_m, vec_v, gradients[4], clip_scale, False)
    split_new = adam_step(split_bias, split_m, split_v, gradients[5], clip_scale, False)
    decoder_new = adam_step(decoder_bias, decoder_m, decoder_v, gradients[6], clip_scale, False)
    return (total_loss, grad_norm, word_new[0], word_new[1], word_new[2], attn_new[0], attn_new[1], attn_new[2], ff_new[0], ff_new[1], ff_new[2], side_new[0], side_new[1], side_new[2], vec_new[0], vec_new[1], vec_new[2], split_new[0], split_new[1], split_new[2], decoder_new[0], decoder_new[1], decoder_new[2])
```

```python
import functools
import math

import jax
import jax.numpy as jnp
from jax import lax
from jax.sharding import Mesh, PartitionSpec as P

D = 768
HEAD_DIM = 64


beta_one = 0.9
beta_two = 0.999
adam_eps = 1e-06
learn_rate = 0.2
decay_rate = 0.01
step_count = 10
max_norm = 0.05
norm_eps = 1e-12
highest = lax.Precision.HIGHEST


def layer_norm(inputs, norm_gain, norm_shift):
    center = inputs - jnp.mean(inputs, axis=-1, keepdims=True)
    spread = jnp.mean(center * center, axis=-1, keepdims=True)
    return center * lax.rsqrt(spread + norm_eps) * norm_gain + norm_shift


def gelu_exact(inputs):
    return jax.nn.gelu(inputs, approximate=False)


def norm_backward(inputs, norm_gain, norm_shift, upstream):
    _, pullback = jax.vjp(layer_norm, inputs, norm_gain, norm_shift)
    return pullback(upstream)


def gelu_backward(inputs, upstream):
    _, pullback = jax.vjp(gelu_exact, inputs)
    return pullback(upstream)[0]


def adam_step(weight, moment, square, gradient, clip_scale, decays):
    gradient = gradient * clip_scale
    moment = beta_one * moment + (1 - beta_one) * gradient
    square = beta_two * square + (1 - beta_two) * gradient * gradient
    mean_hat = moment / (1 - beta_one**step_count)
    var_hat = square / (1 - beta_two**step_count)
    change = mean_hat / (jnp.sqrt(var_hat) + adam_eps)
    if decays:
        change = change + decay_rate * weight
    return (weight - learn_rate * change, moment, square)


def comm_all_gather(value, axes):
    return lax.all_gather(value, axes, axis=0, tiled=True)


def comm_scatter_sum(value, axes):
    return lax.psum_scatter(value, axes, scatter_dimension=0, tiled=True)


def attention_forward(queries, key_rows, value_rows):
    score_scale = 1.0 / math.sqrt(HEAD_DIM)
    length, width = queries.shape
    heads = width // HEAD_DIM
    q3 = queries.reshape(length, heads, HEAD_DIM)
    k3 = key_rows.reshape(-1, heads, HEAD_DIM)
    v3 = value_rows.reshape(-1, heads, HEAD_DIM)
    scores = jnp.einsum("qhe,khe->hqk", q3, k3, preferred_element_type=jnp.float32) * score_scale
    row_top = jnp.max(scores, axis=-1, keepdims=True)
    exp_scores = jnp.exp(scores - row_top)
    row_total = jnp.sum(exp_scores, axis=-1, keepdims=True)
    attn_probs = exp_scores / row_total
    log_norm = row_top + jnp.log(row_total)
    mixed = jnp.einsum(
        "hqk,khe->qhe", attn_probs.astype(jnp.bfloat16), v3, preferred_element_type=jnp.float32
    )
    return mixed.reshape(length, width).astype(jnp.bfloat16), log_norm


def attention_backward(queries, key_rows, value_rows, log_norm, grad_mixed):
    score_scale = 1.0 / math.sqrt(HEAD_DIM)
    length, width = queries.shape
    heads = width // HEAD_DIM
    q3 = queries.reshape(length, heads, HEAD_DIM)
    k3 = key_rows.reshape(-1, heads, HEAD_DIM)
    v3 = value_rows.reshape(-1, heads, HEAD_DIM)
    g3 = grad_mixed.reshape(length, heads, HEAD_DIM)
    scores = jnp.einsum("qhe,khe->hqk", q3, k3, preferred_element_type=jnp.float32) * score_scale
    attn_probs = jnp.exp(scores - log_norm)
    grad_probs = jnp.einsum("qhe,khe->hqk", g3, v3, preferred_element_type=jnp.float32)
    grad_values = jnp.einsum(
        "hqk,qhe->khe", attn_probs.astype(jnp.bfloat16), g3, preferred_element_type=jnp.float32
    )
    row_dot = jnp.sum(grad_probs * attn_probs, axis=-1, keepdims=True)
    grad_scores = (attn_probs * (grad_probs - row_dot)).astype(jnp.bfloat16)
    grad_queries = (
        jnp.einsum("hqk,khe->qhe", grad_scores, k3, preferred_element_type=jnp.float32)
        * score_scale
    )
    grad_keys = (
        jnp.einsum("hqk,qhe->khe", grad_scores, q3, preferred_element_type=jnp.float32)
        * score_scale
    )
    return (
        grad_queries.reshape(length, width),
        grad_keys.reshape(-1, width),
        grad_values.reshape(-1, width),
    )


def step(sizes, *args):
    (
        token_ids, type_ids, mask_pos, mask_valid, mlm_labels, nsp_labels,
        word_table, word_m, word_v, attn_weight, attn_m, attn_v,
        ff_weight, ff_m, ff_v, side_weight, side_m, side_v,
        vectors, vec_m, vec_v, split_bias, split_m, split_v,
        decoder_bias, decoder_m, decoder_v,
    ) = args
    z_size, x_size, y_size, c_size = sizes
    dp_size, mp_size = z_size * x_size, y_size * c_size
    z_at, x_at, y_at, c_at = (lax.axis_index(a) for a in ("z", "x", "y", "c"))
    dp_rank, mp_rank = z_at * x_size + x_at, y_at * c_size + c_at
    every = ("z", "x", "y", "c")
    mp_first = ("y", "c", "z", "x")
    plane = ("x", "y", "c")
    batch_size, length = token_ids.shape
    slots = mask_pos.shape[1]
    own_len, own_slots = length // c_size, slots // c_size
    vocab_own = word_table.shape[0]
    attn_cols, ff_cols = attn_weight.shape[2], ff_weight.shape[2]
    rows_own = attn_weight.shape[0]
    low = jnp.bfloat16

    def mine(rows, size):
        row = lax.dynamic_index_in_dim(rows, y_at, 0, False)
        return lax.dynamic_slice_in_dim(row, c_at * size, size, 0)

    own_ids = mine(token_ids, own_len)
    own_types = mine(type_ids, own_len)
    seq_pos = lax.dynamic_index_in_dim(mask_pos, y_at, 0, False)
    own_pos = mine(mask_pos, own_slots)
    own_valid = mine(mask_valid, own_slots)
    own_labels = mine(mlm_labels, own_slots)
    first_core = (c_at == 0).astype(jnp.float32)

    word_plane = comm_all_gather(word_table.astype(low), plane)
    ints = comm_all_gather(jnp.concatenate([own_ids, own_labels, own_valid])[None], "z")
    z_ids, z_labels, z_valid = (
        ints[:, :own_len],
        ints[:, own_len : own_len + own_slots],
        ints[:, own_len + own_slots :],
    )
    total_count = lax.psum(jnp.sum(mask_valid.astype(jnp.float32)), ("z", "x"))
    total_seqs = jnp.float32(batch_size * dp_size)
    attn_blocks = comm_all_gather(
        attn_weight.astype(low).reshape(rows_own, 4 * attn_cols), mp_first
    ).reshape(mp_size, D, 4 * attn_cols)
    ff_blocks = comm_all_gather(
        ff_weight.astype(low).reshape(rows_own, 2 * ff_cols), mp_first
    ).reshape(mp_size, D, 2 * ff_cols)
    side_rows = side_weight.shape[0] // mp_size
    side_full = comm_all_gather(
        lax.dynamic_slice_in_dim(side_weight.astype(low), mp_rank * side_rows, side_rows, 0), every
    )
    vec_rows = (
        comm_all_gather(vectors.astype(low)[None], ("z", "x"))
        .transpose(1, 0, 2)
        .reshape(vectors.shape[0], D)
        .astype(jnp.float32)
    )
    stripe = vocab_own * x_size
    bias_mine = lax.dynamic_slice_in_dim(decoder_bias, z_at * stripe, stripe, 0)
    mp_small = comm_all_gather(
        jnp.concatenate([bias_mine, split_bias.reshape(-1)])[None], ("y", "c")
    )
    bias_plane = (
        mp_small[:, :stripe].reshape(mp_size, x_size, vocab_own).transpose(1, 0, 2).reshape(-1)
    )
    split_full = mp_small[:, stripe:].reshape(mp_size, 6, attn_cols)

    def plane_index(ids):
        block = ids // stripe
        offset = ids % stripe
        inside = block % z_size == z_at
        at = ((offset // vocab_own) * mp_size + block // z_size) * vocab_own + offset % vocab_own
        return inside, at

    flat_ids = z_ids.reshape(-1)
    inside, at = plane_index(flat_ids)
    looked = jnp.where(inside[:, None], word_plane[jnp.where(inside, at, 0)], jnp.zeros((), low))
    embedded = comm_scatter_sum(looked, "z").astype(jnp.float32)
    position_rows = lax.dynamic_slice_in_dim(side_full, 2 * D + c_at * own_len, own_len, 0)
    embedded = (
        embedded
        + position_rows.astype(jnp.float32)
        + jnp.where(own_types[:, None] == 0, vec_rows[12], vec_rows[13])
    )
    hidden0 = layer_norm(embedded, vec_rows[0], vec_rows[1])
    hidden0_b = hidden0.astype(low)

    qkv_blocks = attn_blocks[:, :, : 3 * attn_cols]
    out_blocks = attn_blocks[:, :, 3 * attn_cols :]
    packed = jnp.einsum("td,mde->tme", hidden0_b, qkv_blocks, preferred_element_type=jnp.float32)
    packed = packed.reshape(own_len, mp_size, 3, attn_cols)
    queries = (packed[:, :, 0] + split_full[:, 0]).astype(low).reshape(own_len, D)
    own_keys = packed[:, :, 1].astype(low).reshape(own_len, D)
    own_values = (packed[:, :, 2] + split_full[:, 1]).astype(low).reshape(own_len, D)
    both = comm_all_gather(jnp.stack([own_keys, own_values])[None], "c")
    key_rows = both[:, 0].reshape(-1, D)
    value_rows = both[:, 1].reshape(-1, D)
    mixed, log_norm = attention_forward(queries, key_rows, value_rows)
    attn_out = jnp.einsum(
        "tme,mde->td",
        mixed.reshape(own_len, mp_size, attn_cols),
        out_blocks,
        preferred_element_type=jnp.float32,
    )
    resid1 = hidden0 + (attn_out + vec_rows[2])
    hidden1 = layer_norm(resid1, vec_rows[3], vec_rows[4])
    hidden1_b = hidden1.astype(low)
    ff_bias = split_full[:, 2:6].transpose(0, 2, 1).reshape(mp_size, ff_cols)
    ff_in, ff_out = ff_blocks[:, :, :ff_cols], ff_blocks[:, :, ff_cols:]
    upward = jnp.einsum("td,mdf->mtf", hidden1_b, ff_in, preferred_element_type=jnp.float32)
    upward = upward + ff_bias[:, None]
    active = gelu_exact(upward).astype(low)
    ffn_out = jnp.einsum("mtf,mdf->td", active, ff_out, preferred_element_type=jnp.float32)
    resid2 = hidden1 + (ffn_out + vec_rows[5])
    hidden2 = layer_norm(resid2, vec_rows[6], vec_rows[7])

    hidden2_seq = comm_all_gather(hidden2.astype(low), "c")
    picked_b = hidden2_seq[own_pos]
    dense_w = side_full[D : 2 * D]
    dense_out = jnp.dot(picked_b, dense_w, preferred_element_type=jnp.float32) + vec_rows[8]
    act_dense = gelu_exact(dense_out)
    head_rows = layer_norm(act_dense, vec_rows[9], vec_rows[10])
    head_b = comm_all_gather(head_rows.astype(low), "z")
    row_count = head_b.shape[0]
    logits = (
        jnp.einsum("rd,vd->rv", head_b, word_plane, preferred_element_type=jnp.float32)
        + bias_plane
    )
    label_in, label_at = plane_index(z_labels.reshape(-1))
    label_at = jnp.where(label_in, label_at, -1)
    hit_rows = label_at[:, None] == lax.broadcasted_iota(jnp.int32, logits.shape, 1)
    row_top = jnp.max(logits, axis=1)
    row_total = jnp.sum(jnp.exp(logits - row_top[:, None]), axis=1)
    row_target = jnp.sum(jnp.where(hit_rows, logits, 0.0), axis=1)
    stats = comm_all_gather(jnp.stack([row_top, row_total, row_target])[None], "z")
    top_all = jnp.max(stats[:, 0], axis=0)
    total_all = jnp.sum(stats[:, 1] * jnp.exp(stats[:, 0] - top_all), axis=0)
    target_all = jnp.sum(stats[:, 2], axis=0)
    log_total = top_all + jnp.log(total_all)
    valid_rows = z_valid.reshape(-1).astype(jnp.float32)
    mlm_sum = -jnp.sum(valid_rows * (target_all - log_total))
    weight_rows = valid_rows / total_count
    grad_logits = (
        (jnp.exp(logits - log_total[:, None]) - hit_rows.astype(jnp.float32)) * weight_rows[:, None]
    ).astype(low)
    decoder_part = jnp.sum(grad_logits.astype(jnp.float32), axis=0)
    head_part = jnp.dot(grad_logits, word_plane, preferred_element_type=jnp.float32)
    grad_head = comm_scatter_sum(head_part, "z")
    grad_act, grad_g9, grad_s9 = norm_backward(act_dense, vec_rows[9], vec_rows[10], grad_head)
    grad_dense = gelu_backward(dense_out, grad_act).astype(low)
    dense_bias_grad = jnp.sum(grad_dense.astype(jnp.float32), axis=0)
    dense_grad = jnp.einsum("rd,re->de", picked_b, grad_dense, preferred_element_type=jnp.float32)
    grad_picked = jnp.einsum("re,de->rd", grad_dense, dense_w, preferred_element_type=jnp.float32)
    seq_picked = comm_all_gather(grad_picked, "c")
    place = (
        seq_pos[None, :]
        == c_at * own_len + lax.broadcasted_iota(jnp.int32, (own_len, slots), 0)
    ).astype(jnp.float32)
    grad_top = jnp.dot(place, seq_picked, precision=highest)

    cls_row = hidden2_seq[0:1]
    pooler_w = side_full[:D]
    pooled = jnp.tanh(jnp.dot(cls_row, pooler_w, preferred_element_type=jnp.float32) + vec_rows[11])
    classes = vec_rows[14:16]
    nsp_logp = jax.nn.log_softmax(jnp.dot(pooled, classes.T, precision=highest), axis=-1)
    own_nsp = lax.dynamic_slice_in_dim(nsp_labels, y_at, 1, 0)
    pick_nsp = own_nsp[:, None] == lax.broadcasted_iota(jnp.int32, (1, 2), 1)
    nsp_sum = -jnp.sum(jnp.where(pick_nsp, nsp_logp, 0.0)) * first_core
    grad_nsp = (jnp.exp(nsp_logp) - pick_nsp.astype(jnp.float32)) / total_seqs * first_core
    class_grad = grad_nsp[0][:, None] * pooled
    grad_pre = jnp.dot(grad_nsp, classes, precision=highest) * (1.0 - pooled * pooled)
    pooler_bias_grad = grad_pre[0]
    pooler_grad = cls_row.astype(jnp.float32).T * grad_pre
    grad_cls = jnp.dot(grad_pre, pooler_w.astype(jnp.float32).T, precision=highest)
    first_row = lax.broadcasted_iota(jnp.int32, (own_len, 1), 0) == 0
    grad_top = grad_top + jnp.where(first_row, grad_cls, 0.0)

    grad_r2, grad_g2, grad_s2 = norm_backward(resid2, vec_rows[6], vec_rows[7], grad_top)
    ffn_grad_b = grad_r2.astype(low)
    out_bias_two = jnp.sum(ffn_grad_b.astype(jnp.float32), axis=0)
    ff_out_grad = jnp.einsum("td,mtf->mdf", ffn_grad_b, active, preferred_element_type=jnp.float32)
    grad_active = jnp.einsum("td,mdf->mtf", ffn_grad_b, ff_out, preferred_element_type=jnp.float32)
    grad_up = gelu_backward(upward, grad_active).astype(low)
    ff_bias_grad = jnp.sum(grad_up.astype(jnp.float32), axis=1)
    ff_in_grad = jnp.einsum("td,mtf->mdf", hidden1_b, grad_up, preferred_element_type=jnp.float32)
    hidden1_part = jnp.einsum("mtf,mdf->td", grad_up, ff_in, preferred_element_type=jnp.float32)
    ff_grad = jnp.concatenate([ff_in_grad, ff_out_grad], axis=2).astype(low)
    ff_red = comm_scatter_sum(ff_grad.reshape(mp_size * D, 2 * ff_cols), mp_first)
    grad_h1 = grad_r2 + hidden1_part
    grad_r1, grad_g1, grad_s1 = norm_backward(resid1, vec_rows[3], vec_rows[4], grad_h1)
    attn_grad_b = grad_r1.astype(low)
    out_bias_one = jnp.sum(attn_grad_b.astype(jnp.float32), axis=0)
    mixed_blocks = mixed.reshape(own_len, mp_size, attn_cols)
    attn_grad_out = jnp.einsum(
        "td,tme->mde", attn_grad_b, mixed_blocks, preferred_element_type=jnp.float32
    )
    grad_mixed = jnp.einsum(
        "td,mde->tme", attn_grad_b, out_blocks, preferred_element_type=jnp.float32
    )
    grad_mixed = grad_mixed.astype(low).reshape(own_len, D)
    grad_q, part_k, part_v = attention_backward(
        queries, key_rows, value_rows, log_norm, grad_mixed
    )
    part_kv = jnp.concatenate([part_k, part_v], axis=1)
    grad_kv = comm_scatter_sum(part_kv, "c").astype(low)
    grad_packed = jnp.stack(
        [
            grad_q.astype(low).reshape(own_len, mp_size, attn_cols),
            grad_kv[:, :D].reshape(own_len, mp_size, attn_cols),
            grad_kv[:, D:].reshape(own_len, mp_size, attn_cols),
        ],
        axis=2,
    ).reshape(own_len, mp_size, 3 * attn_cols)
    attn_grad_in = jnp.einsum(
        "td,tme->mde", hidden0_b, grad_packed, preferred_element_type=jnp.float32
    )
    packed_sums = jnp.sum(grad_packed.astype(jnp.float32), axis=0).reshape(mp_size, 3, attn_cols)
    hidden0_part = jnp.einsum(
        "tme,mde->td", grad_packed, qkv_blocks, preferred_element_type=jnp.float32
    )
    attn_grad = jnp.concatenate([attn_grad_in, attn_grad_out], axis=2).astype(low)
    attn_red = comm_scatter_sum(attn_grad.reshape(mp_size * D, 4 * attn_cols), mp_first)
    grad_h0 = grad_r1 + hidden0_part
    grad_x0, grad_g0, grad_s0 = norm_backward(embedded, vec_rows[0], vec_rows[1], grad_h0)

    all_x0 = comm_all_gather(grad_x0.astype(low), "z")
    onehot = (
        jnp.where(inside, at, -1)[None, :]
        == lax.broadcasted_iota(jnp.int32, (word_plane.shape[0], flat_ids.shape[0]), 0)
    ).astype(low)
    word_grad = jnp.einsum("rv,rd->vd", grad_logits, head_b, preferred_element_type=jnp.float32)
    word_grad = word_grad + jnp.dot(onehot, all_x0, preferred_element_type=jnp.float32)
    word_red = comm_scatter_sum(word_grad.astype(low), plane).astype(jnp.float32)

    position_grad = lax.dynamic_update_slice_in_dim(
        jnp.zeros((length, D), low), grad_x0.astype(low), c_at * own_len, 0
    )
    side_grad = jnp.concatenate([pooler_grad.astype(low), dense_grad.astype(low), position_grad], axis=0)
    side_quarter = comm_scatter_sum(side_grad, every)
    side_red = comm_all_gather(side_quarter, ("y", "c")).astype(jnp.float32)
    type_zero = jnp.sum(jnp.where(own_types[:, None] == 0, grad_x0, 0.0), axis=0)
    type_one = jnp.sum(jnp.where(own_types[:, None] == 1, grad_x0, 0.0), axis=0)
    vec_grad = jnp.stack(
        [
            grad_g0, grad_s0, out_bias_one, grad_g1, grad_s1, out_bias_two, grad_g2, grad_s2,
            dense_bias_grad, grad_g9, grad_s9, pooler_bias_grad, type_zero, type_one,
            class_grad[0], class_grad[1],
        ],
        axis=0,
    )
    split_grad = jnp.concatenate(
        [
            packed_sums[:, 0:1],
            packed_sums[:, 2:3],
            ff_bias_grad.reshape(mp_size, attn_cols, 4).transpose(0, 2, 1),
        ],
        axis=1,
    )
    small = lax.psum(jnp.concatenate([vec_grad.reshape(-1), split_grad.reshape(-1)]), every)
    vec_all = small[: vec_grad.size].reshape(vec_grad.shape)
    split_all = small[vec_grad.size :].reshape(split_grad.shape)
    vec_cols = vectors.shape[1]
    vec_red = lax.dynamic_slice_in_dim(vec_all, dp_rank * vec_cols, vec_cols, 1)
    split_red = lax.dynamic_index_in_dim(split_all, mp_rank, 0, False)
    decoder_own = comm_scatter_sum(decoder_part, plane)
    decoder_red = comm_all_gather(decoder_own, ("z", "x"))
    word_f, attn_f, ff_f = (
        word_red,
        attn_red.astype(jnp.float32).reshape(attn_weight.shape),
        ff_red.astype(jnp.float32).reshape(ff_weight.shape),
    )
    own_square = (
        jnp.sum(word_f * word_f)
        + jnp.sum(attn_f * attn_f)
        + jnp.sum(ff_f * ff_f)
        + jnp.sum(side_red * side_red) / mp_size
        + jnp.sum(vec_red * vec_red) / mp_size
        + (jnp.sum(split_red * split_red) + jnp.sum(decoder_red * decoder_red)) / dp_size
    )
    loss_part = mlm_sum / total_count / z_size + nsp_sum / total_seqs
    grad_square, total_loss = lax.psum((own_square, loss_part), every)
    grad_norm = jnp.sqrt(grad_square)
    clip_scale = max_norm / jnp.maximum(grad_norm, max_norm)
    return (
        total_loss,
        grad_norm,
        *adam_step(word_table, word_m, word_v, word_f, clip_scale, True),
        *adam_step(attn_weight, attn_m, attn_v, attn_f, clip_scale, True),
        *adam_step(ff_weight, ff_m, ff_v, ff_f, clip_scale, True),
        *adam_step(side_weight, side_m, side_v, side_red, clip_scale, True),
        *adam_step(vectors, vec_m, vec_v, vec_red, clip_scale, False),
        *adam_step(split_bias, split_m, split_v, split_red, clip_scale, False),
        *adam_step(decoder_bias, decoder_m, decoder_v, decoder_red, clip_scale, False),
    )


def solution(mesh):
    dp_size, mp_size = mesh.shape["dp"], mesh.shape["mp"]
    x_size = 2 if dp_size % 2 == 0 else 1
    c_size = 2 if mp_size % 2 == 0 else 1
    sizes = (dp_size // x_size, x_size, mp_size // c_size, c_size)
    fine = Mesh(mesh.devices.reshape(sizes), ("z", "x", "y", "c"))
    dp, mp = ("z", "x"), ("y", "c")
    word = P(("y", "c", "z", "x"), None)
    cube = P(dp, None, mp)
    kinds = (
        [P(dp, None)] * 5
        + [P(dp)]
        + [word] * 3
        + [cube] * 6
        + [P(dp, None)] * 3
        + [P(None, dp)] * 3
        + [P(None, mp)] * 3
        + [P(mp)] * 3
    )
    return jax.shard_map(
        functools.partial(step, sizes),
        mesh=fine,
        in_specs=tuple(kinds),
        out_specs=(P(), P(), *kinds[6:]),
        check_vma=False,
    )
```

```python
import functools
import math

import jax
import jax.numpy as jnp
from jax import lax
from jax.experimental import pallas as pl
from jax.experimental.pallas import tpu as pltpu
from jax.sharding import Mesh, PartitionSpec as P

D = 768
HEAD_DIM = 64


beta_one = 0.9
beta_two = 0.999
adam_eps = 1e-06
learn_rate = 0.2
decay_rate = 0.01
step_count = 10
max_norm = 0.05
norm_eps = 1e-12
highest = lax.Precision.HIGHEST


def layer_norm(inputs, norm_gain, norm_shift):
    center = inputs - jnp.mean(inputs, axis=-1, keepdims=True)
    spread = jnp.mean(center * center, axis=-1, keepdims=True)
    return center * lax.rsqrt(spread + norm_eps) * norm_gain + norm_shift


def gelu_exact(inputs):
    return jax.nn.gelu(inputs, approximate=False)


def norm_backward(inputs, norm_gain, norm_shift, upstream):
    _, pullback = jax.vjp(layer_norm, inputs, norm_gain, norm_shift)
    return pullback(upstream)


def gelu_backward(inputs, upstream):
    _, pullback = jax.vjp(gelu_exact, inputs)
    return pullback(upstream)[0]


def adam_step(weight, moment, square, gradient, clip_scale, decays):
    gradient = gradient * clip_scale
    moment = beta_one * moment + (1 - beta_one) * gradient
    square = beta_two * square + (1 - beta_two) * gradient * gradient
    mean_hat = moment / (1 - beta_one**step_count)
    var_hat = square / (1 - beta_two**step_count)
    change = mean_hat / (jnp.sqrt(var_hat) + adam_eps)
    if decays:
        change = change + decay_rate * weight
    return (weight - learn_rate * change, moment, square)


def comm_all_gather(value, axes):
    return lax.all_gather(value, axes, axis=0, tiled=True)


def comm_scatter_sum(value, axes):
    return lax.psum_scatter(value, axes, scatter_dimension=0, tiled=True)


MESH = pl.DeviceIdType.MESH
BIG, FAST = pl.ANY, pltpu.VMEM


class Links:
    def __init__(self, sizes):
        self.sizes = dict(zip(("z", "x", "y", "c"), sizes))
        self.used = 0

    def next_id(self):
        self.used += 1
        return self.used - 1

    def count(self, axes):
        return math.prod(self.sizes[a] for a in axes)

    def place(self, axes):
        at = 0
        for a in axes:
            at = at * self.sizes[a] + lax.axis_index(a)
        return at

    def target(self, axes, flat):
        where = {}
        for a in reversed(axes):
            where[a] = lax.rem(flat, self.sizes[a])
            flat = lax.div(flat, self.sizes[a])
        return where

    def greet(self, groups):
        barrier = pltpu.get_barrier_semaphore()
        total = 0
        for axes in groups:
            size, me = self.count(axes), self.place(axes)
            for r in range(1, size):
                pl.semaphore_signal(
                    barrier,
                    inc=1,
                    device_id=self.target(axes, lax.rem(me + r, size)),
                    device_id_type=MESH,
                )
            total += size - 1
        pl.semaphore_wait(barrier, total)

    def call(self, kernel, outs, spaces, out_spaces, scratch, values, wire, name):
        result = pl.pallas_call(
            kernel,
            out_shape=outs,
            in_specs=[pl.BlockSpec(memory_space=m) for m in spaces],
            out_specs=[pl.BlockSpec(memory_space=m) for m in out_spaces],
            scratch_shapes=scratch,
            compiler_params=pltpu.CompilerParams(
                collective_id=self.next_id(),
                has_side_effects=True,
                vmem_limit_bytes=40 * 2**20,
            ),
            cost_estimate=pl.CostEstimate(flops=0, bytes_accessed=wire, transcendentals=0),
            name=name,
        )(*values)
        return result

    def exchange(self, name, *moves):
        outs, transfers = [], 0
        for kind, axes, dim, _, value in moves:
            size = self.count(axes)
            shape = value.shape
            if kind == "gather":
                shape = (size, *shape)
            elif kind == "swap":
                shape = shape[:dim] + shape[dim + 1 :]
            elif kind == "spread":
                shape = (size - 1, *shape[1:])
            outs.append(jax.ShapeDtypeStruct(shape, value.dtype))
            transfers += size - 1
        spaces = [m[3] for m in moves]
        groups = list(dict.fromkeys(m[1] for m in moves))

        def kernel(*refs):
            ins, dests = refs[: len(moves)], refs[len(moves) : 2 * len(moves)]
            sends, lands, own_sems = refs[2 * len(moves) :]
            self.greet(groups)
            started, slot = [], 0
            for (kind, axes, dim, _, _), source, dest in zip(moves, ins, dests):
                size, me = self.count(axes), self.place(axes)
                for r in range(1, size):
                    peer = lax.rem(me + r, size)
                    if kind == "gather":
                        src, dst = source, dest.at[me]
                    elif kind == "swap":
                        src, dst = source.at[(slice(None),) * dim + (peer,)], dest
                    elif kind == "spread":
                        src, dst = source.at[peer], dest.at[r - 1]
                    else:
                        src, dst = source, dest
                    copy = pltpu.make_async_remote_copy(
                        src_ref=src,
                        dst_ref=dst,
                        send_sem=sends.at[slot],
                        recv_sem=lands.at[slot],
                        device_id=self.target(axes, peer),
                        device_id_type=MESH,
                    )
                    copy.start()
                    started.append(copy)
                    slot += 1
            for number, ((kind, axes, _, _, _), source, dest) in enumerate(zip(moves, ins, dests)):
                if kind == "gather":
                    copy = pltpu.make_async_copy(
                        source, dest.at[self.place(axes)], own_sems.at[number]
                    )
                    copy.start()
                    started.append(copy)
            for copy in started:
                copy.wait()

        return self.call(
            kernel,
            outs,
            spaces,
            spaces,
            [
                pltpu.SemaphoreType.DMA((transfers,)),
                pltpu.SemaphoreType.DMA((transfers,)),
                pltpu.SemaphoreType.DMA((len(moves),)),
            ],
            [m[4] for m in moves],
            sum(2 * math.prod(o.shape) * o.dtype.itemsize for o in outs),
            name,
        )

    def combine(self, name, value):
        pairs = [a for a in ("c", "x", "y") if self.sizes[a] > 1]
        depth = self.sizes["z"]
        steps = len(pairs)

        def kernel(x_ref, out_ref, sums, land, sends, lands):
            self.greet([(a,) for a in pairs] + [("z",)])
            me = lax.axis_index("z")
            for i, a in enumerate(pairs):
                source = x_ref if i == 0 else sums.at[i - 1]
                copy = pltpu.make_async_remote_copy(
                    src_ref=source,
                    dst_ref=land.at[i],
                    send_sem=sends.at[i],
                    recv_sem=lands.at[i],
                    device_id={a: 1 - lax.axis_index(a)},
                    device_id_type=MESH,
                )
                copy.start()
                copy.wait()
                sums[i] = source[...] + land[i]
            out_ref[me] = sums[steps - 1]
            started = []
            for r in range(1, depth):
                copy = pltpu.make_async_remote_copy(
                    src_ref=sums.at[steps - 1],
                    dst_ref=out_ref.at[me],
                    send_sem=sends.at[steps + r - 1],
                    recv_sem=lands.at[steps + r - 1],
                    device_id={"z": lax.rem(me + r, depth)},
                    device_id_type=MESH,
                )
                copy.start()
                started.append(copy)
            for copy in started:
                copy.wait()

        return self.call(
            kernel,
            [jax.ShapeDtypeStruct((depth, *value.shape), value.dtype)],
            [FAST],
            [FAST],
            [
                pltpu.VMEM((steps, *value.shape), value.dtype),
                pltpu.VMEM((steps, *value.shape), value.dtype),
                pltpu.SemaphoreType.DMA((steps + depth - 1,)),
                pltpu.SemaphoreType.DMA((steps + depth - 1,)),
            ],
            [value],
            16 * value.size * 4,
            name,
        )[0]

    def gather_plane(self, name, value):
        rows, width = value.shape
        parts = 4 if rows % 64 == 0 else 1
        head = (parts + 1) // 2
        value = value.reshape(parts, rows // parts, width)
        shape = (*(self.sizes[a] for a in ("x", "y", "c")), *value.shape)

        def kernel(own, out, sends, lands, own_sem):
            self.greet([("x",), ("y",), ("c",)])
            x, y, c = (lax.axis_index(a) for a in ("x", "y", "c"))
            by_x, by_y, by_c = {"x": 1 - x}, {"y": 1 - y}, {"c": 1 - c}
            started = []

            def send(src, place, part, slot, peer):
                copy = pltpu.make_async_remote_copy(
                    src_ref=src,
                    dst_ref=out.at[(*place, part)],
                    send_sem=sends.at[len(started)],
                    recv_sem=lands.at[slot, part],
                    device_id=peer,
                    device_id_type=MESH,
                )
                copy.start()
                started.append(copy)

            def arrived(place, part, slot):
                landed = out.at[(*place, part)]
                pltpu.make_async_remote_copy(
                    src_ref=landed,
                    dst_ref=landed,
                    send_sem=sends.at[0],
                    recv_sem=lands.at[slot, part],
                    device_id=by_c,
                    device_id_type=MESH,
                ).wait_recv()
                return landed

            me, at_x, at_y, at_xy = (x, y, c), (1 - x, y, c), (x, 1 - y, c), (1 - x, 1 - y, c)
            for part in range(parts):
                send(own.at[part], me, part, 0, by_x)
                send(own.at[part], me, part, 1, by_y)
            for part in range(parts):
                send(own.at[part], me, part, 3, by_c)
            local = pltpu.make_async_copy(own, out.at[me], own_sem.at[0])
            local.start()
            for part in range(parts):
                landed = arrived(at_x, part, 0)
                if part < head:
                    send(landed, at_x, part, 2, by_y)
                send(landed, at_x, part, 4, by_c)
                landed = arrived(at_y, part, 1)
                if part >= head:
                    send(landed, at_y, part, 2, by_x)
                send(landed, at_y, part, 5, by_c)
            for part in range(parts):
                landed = arrived(at_xy, part, 2)
                send(landed, at_xy, part, 6, by_c)
            for slot, place in ((3, me), (4, at_x), (5, at_y), (6, at_xy)):
                for part in range(parts):
                    arrived((place[0], place[1], 1 - c), part, slot)
            for copy in started:
                copy.wait_send()
            local.wait()

        return self.call(
            kernel,
            [jax.ShapeDtypeStruct(shape, value.dtype)],
            [BIG],
            [BIG],
            [
                pltpu.SemaphoreType.DMA((7 * parts,)),
                pltpu.SemaphoreType.DMA((7, parts)),
                pltpu.SemaphoreType.DMA((1,)),
            ],
            [value],
            4 * math.prod(shape),
            name,
        )[0].reshape(-1, width)


def lanes(flat):
    padded = jnp.pad(flat, (0, -flat.size % 1024))
    return padded.reshape(-1, 128)


def attention_forward(queries, key_rows, value_rows):
    score_scale = 1.0 / math.sqrt(HEAD_DIM)
    length, width = queries.shape
    heads = width // HEAD_DIM
    q3 = queries.reshape(length, heads, HEAD_DIM)
    k3 = key_rows.reshape(-1, heads, HEAD_DIM)
    v3 = value_rows.reshape(-1, heads, HEAD_DIM)
    scores = jnp.einsum("qhe,khe->hqk", q3, k3, preferred_element_type=jnp.float32) * score_scale
    row_top = jnp.max(scores, axis=-1, keepdims=True)
    exp_scores = jnp.exp(scores - row_top)
    row_total = jnp.sum(exp_scores, axis=-1, keepdims=True)
    attn_probs = exp_scores / row_total
    log_norm = row_top + jnp.log(row_total)
    mixed = jnp.einsum(
        "hqk,khe->qhe", attn_probs.astype(jnp.bfloat16), v3, preferred_element_type=jnp.float32
    )
    return mixed.reshape(length, width).astype(jnp.bfloat16), log_norm


def attention_backward(queries, key_rows, value_rows, log_norm, grad_mixed):
    score_scale = 1.0 / math.sqrt(HEAD_DIM)
    length, width = queries.shape
    heads = width // HEAD_DIM
    q3 = queries.reshape(length, heads, HEAD_DIM)
    k3 = key_rows.reshape(-1, heads, HEAD_DIM)
    v3 = value_rows.reshape(-1, heads, HEAD_DIM)
    g3 = grad_mixed.reshape(length, heads, HEAD_DIM)
    scores = jnp.einsum("qhe,khe->hqk", q3, k3, preferred_element_type=jnp.float32) * score_scale
    attn_probs = jnp.exp(scores - log_norm)
    grad_probs = jnp.einsum("qhe,khe->hqk", g3, v3, preferred_element_type=jnp.float32)
    grad_values = jnp.einsum(
        "hqk,qhe->khe", attn_probs.astype(jnp.bfloat16), g3, preferred_element_type=jnp.float32
    )
    row_dot = jnp.sum(grad_probs * attn_probs, axis=-1, keepdims=True)
    grad_scores = (attn_probs * (grad_probs - row_dot)).astype(jnp.bfloat16)
    grad_queries = (
        jnp.einsum("hqk,khe->qhe", grad_scores, k3, preferred_element_type=jnp.float32)
        * score_scale
    )
    grad_keys = (
        jnp.einsum("hqk,qhe->khe", grad_scores, q3, preferred_element_type=jnp.float32)
        * score_scale
    )
    return (
        grad_queries.reshape(length, width),
        grad_keys.reshape(-1, width),
        grad_values.reshape(-1, width),
    )


def step(sizes, *args):
    (
        token_ids, type_ids, mask_pos, mask_valid, mlm_labels, nsp_labels,
        word_table, word_m, word_v, attn_weight, attn_m, attn_v,
        ff_weight, ff_m, ff_v, side_weight, side_m, side_v,
        vectors, vec_m, vec_v, split_bias, split_m, split_v,
        decoder_bias, decoder_m, decoder_v,
    ) = args
    z_size, x_size, y_size, c_size = sizes
    dp_size, mp_size = z_size * x_size, y_size * c_size
    z_at, x_at, y_at, c_at = (lax.axis_index(a) for a in ("z", "x", "y", "c"))
    dp_rank, mp_rank = z_at * x_size + x_at, y_at * c_size + c_at
    every = ("z", "x", "y", "c")
    mp_first = ("y", "c", "z", "x")
    plane = ("x", "y", "c")
    batch_size, length = token_ids.shape
    slots = mask_pos.shape[1]
    own_len, own_slots = length // c_size, slots // c_size
    vocab_own = word_table.shape[0]
    attn_cols, ff_cols = attn_weight.shape[2], ff_weight.shape[2]
    rows_own = attn_weight.shape[0]
    low = jnp.bfloat16
    links = Links(sizes)

    def mine(rows, size):
        row = lax.dynamic_index_in_dim(rows, y_at, 0, False)
        return lax.dynamic_slice_in_dim(row, c_at * size, size, 0)

    own_ids = mine(token_ids, own_len)
    own_types = mine(type_ids, own_len)
    seq_pos = lax.dynamic_index_in_dim(mask_pos, y_at, 0, False)
    own_pos = mine(mask_pos, own_slots)
    own_valid = mine(mask_valid, own_slots)
    own_labels = mine(mlm_labels, own_slots)
    first_core = (c_at == 0).astype(jnp.float32)

    side_rows = side_weight.shape[0] // mp_size
    side_full = comm_all_gather(
        lax.dynamic_slice_in_dim(side_weight.astype(low), mp_rank * side_rows, side_rows, 0), every
    )
    attn_blocks = comm_all_gather(
        attn_weight.astype(low).reshape(rows_own, 4 * attn_cols), mp_first
    ).reshape(mp_size, D, 4 * attn_cols)
    ff_blocks = comm_all_gather(
        ff_weight.astype(low).reshape(rows_own, 2 * ff_cols), mp_first
    ).reshape(mp_size, D, 2 * ff_cols)
    vec_cols = vectors.shape[1]
    stripe = vocab_own * x_size
    bias_mine = lax.dynamic_slice_in_dim(decoder_bias, z_at * stripe, stripe, 0)
    int_count = own_len + 2 * own_slots
    ints, vec_parts, counts, mp_small = links.exchange(
        "small_gather",
        ("gather", ("z",), 0, FAST, lanes(jnp.concatenate([own_ids, own_labels, own_valid]))),
        ("gather", ("z", "x"), 0, FAST, jnp.pad(vectors.astype(low), ((0, 0), (0, 128 - vec_cols)))),
        (
            "gather",
            ("z", "x"),
            0,
            FAST,
            jnp.full((8, 128), jnp.sum(mask_valid.astype(jnp.float32))),
        ),
        ("gather", ("y", "c"), 0, FAST, lanes(jnp.concatenate([bias_mine, split_bias.reshape(-1)]))),
    )
    ints = ints.reshape(z_size, -1)[:, :int_count]
    z_ids, z_labels, z_valid = (
        ints[:, :own_len],
        ints[:, own_len : own_len + own_slots],
        ints[:, own_len + own_slots :],
    )
    total_count = jnp.sum(counts[:, 0, 0])
    total_seqs = jnp.float32(batch_size * dp_size)
    vec_rows = (
        vec_parts[:, :, :vec_cols]
        .transpose(1, 0, 2)
        .reshape(vectors.shape[0], D)
        .astype(jnp.float32)
    )
    mp_small = mp_small.reshape(mp_size, -1)
    word_plane = links.gather_plane("word_gather", word_table.astype(low))
    bias_plane = (
        mp_small[:, :stripe].reshape(mp_size, x_size, vocab_own).transpose(1, 0, 2).reshape(-1)
    )
    split_full = mp_small[:, stripe : stripe + 6 * attn_cols].reshape(mp_size, 6, attn_cols)

    def plane_index(ids):
        block = ids // stripe
        offset = ids % stripe
        inside = block % z_size == z_at
        at = ((offset // vocab_own) * mp_size + block // z_size) * vocab_own + offset % vocab_own
        return inside, at

    flat_ids = z_ids.reshape(-1)
    inside, at = plane_index(flat_ids)
    looked = jnp.where(inside[:, None], word_plane[jnp.where(inside, at, 0)], jnp.zeros((), low))
    looked = looked.reshape(z_size, own_len, D)
    (found,) = links.exchange("token_spread", ("spread", ("z",), 0, BIG, looked))
    embedded = lax.dynamic_index_in_dim(looked, z_at, 0, False).astype(jnp.float32)
    embedded = embedded + jnp.sum(found.astype(jnp.float32), axis=0)
    position_rows = lax.dynamic_slice_in_dim(side_full, 2 * D + c_at * own_len, own_len, 0)
    embedded = (
        embedded
        + position_rows.astype(jnp.float32)
        + jnp.where(own_types[:, None] == 0, vec_rows[12], vec_rows[13])
    )
    hidden0 = layer_norm(embedded, vec_rows[0], vec_rows[1])
    hidden0_b = hidden0.astype(low)

    qkv_blocks = attn_blocks[:, :, : 3 * attn_cols]
    out_blocks = attn_blocks[:, :, 3 * attn_cols :]
    packed = jnp.einsum("td,mde->tme", hidden0_b, qkv_blocks, preferred_element_type=jnp.float32)
    packed = packed.reshape(own_len, mp_size, 3, attn_cols)
    queries = (packed[:, :, 0] + split_full[:, 0]).astype(low).reshape(own_len, D)
    own_keys = packed[:, :, 1].astype(low).reshape(own_len, D)
    own_values = (packed[:, :, 2] + split_full[:, 1]).astype(low).reshape(own_len, D)
    other_keys, other_values = links.exchange(
        "key_trade", ("trade", ("c",), 0, FAST, own_keys), ("trade", ("c",), 0, FAST, own_values)
    )
    key_rows = jnp.concatenate([own_keys, other_keys])
    value_rows = jnp.concatenate([own_values, other_values])
    mixed, log_norm = attention_forward(queries, key_rows, value_rows)
    attn_out = jnp.einsum(
        "tme,mde->td",
        mixed.reshape(own_len, mp_size, attn_cols),
        out_blocks,
        preferred_element_type=jnp.float32,
    )
    resid1 = hidden0 + (attn_out + vec_rows[2])
    hidden1 = layer_norm(resid1, vec_rows[3], vec_rows[4])
    hidden1_b = hidden1.astype(low)
    ff_bias = split_full[:, 2:6].transpose(0, 2, 1).reshape(mp_size, ff_cols)
    ff_in, ff_out = ff_blocks[:, :, :ff_cols], ff_blocks[:, :, ff_cols:]
    upward = jnp.einsum("td,mdf->mtf", hidden1_b, ff_in, preferred_element_type=jnp.float32)
    upward = upward + ff_bias[:, None]
    active = gelu_exact(upward).astype(low)
    ffn_out = jnp.einsum("mtf,mdf->td", active, ff_out, preferred_element_type=jnp.float32)
    resid2 = hidden1 + (ffn_out + vec_rows[5])
    hidden2 = layer_norm(resid2, vec_rows[6], vec_rows[7])

    hidden2_b = hidden2.astype(low)
    (other_h2,) = links.exchange("hidden_trade", ("trade", ("c",), 0, FAST, hidden2_b))
    picked_b = jnp.concatenate([hidden2_b, other_h2])[
        own_pos % own_len + jnp.where(own_pos // own_len == c_at, 0, own_len)
    ]
    dense_w = side_full[D : 2 * D]
    dense_out = jnp.dot(picked_b, dense_w, preferred_element_type=jnp.float32) + vec_rows[8]
    act_dense = gelu_exact(dense_out)
    head_rows = layer_norm(act_dense, vec_rows[9], vec_rows[10])
    (head_b,) = links.exchange("head_gather", ("gather", ("z",), 0, FAST, head_rows.astype(low)))
    head_b = head_b.reshape(-1, D)
    row_count = head_b.shape[0]
    logits = (
        jnp.einsum("rd,vd->rv", head_b, word_plane, preferred_element_type=jnp.float32)
        + bias_plane
    )
    label_in, label_at = plane_index(z_labels.reshape(-1))
    label_at = jnp.where(label_in, label_at, -1)
    hit_rows = label_at[:, None] == lax.broadcasted_iota(jnp.int32, logits.shape, 1)
    row_top = jnp.max(logits, axis=1)
    row_total = jnp.sum(jnp.exp(logits - row_top[:, None]), axis=1)
    row_target = jnp.sum(jnp.where(hit_rows, logits, 0.0), axis=1)
    stats = jnp.pad(jnp.stack([row_top, row_total, row_target]), ((0, 5), (0, 0)))
    (stats,) = links.exchange("stat_gather", ("gather", ("z",), 0, FAST, stats))
    top_all = jnp.max(stats[:, 0], axis=0)
    total_all = jnp.sum(stats[:, 1] * jnp.exp(stats[:, 0] - top_all), axis=0)
    target_all = jnp.sum(stats[:, 2], axis=0)
    log_total = top_all + jnp.log(total_all)
    valid_rows = z_valid.reshape(-1).astype(jnp.float32)
    mlm_sum = -jnp.sum(valid_rows * (target_all - log_total))
    weight_rows = valid_rows / total_count
    grad_logits = (
        (jnp.exp(logits - log_total[:, None]) - hit_rows.astype(jnp.float32)) * weight_rows[:, None]
    ).astype(low)
    decoder_part = jnp.sum(grad_logits.astype(jnp.float32), axis=0)
    head_part = jnp.dot(grad_logits, word_plane, preferred_element_type=jnp.float32)
    head_part = head_part.reshape(z_size, own_slots, D)
    (head_others,) = links.exchange("head_spread", ("spread", ("z",), 0, FAST, head_part.astype(low)))
    grad_head = lax.dynamic_index_in_dim(head_part, z_at, 0, False) + jnp.sum(
        head_others.astype(jnp.float32), axis=0
    )
    grad_act, grad_g9, grad_s9 = norm_backward(act_dense, vec_rows[9], vec_rows[10], grad_head)
    grad_dense = gelu_backward(dense_out, grad_act).astype(low)
    dense_bias_grad = jnp.sum(grad_dense.astype(jnp.float32), axis=0)
    dense_grad = jnp.einsum("rd,re->de", picked_b, grad_dense, preferred_element_type=jnp.float32)
    grad_picked = jnp.einsum("re,de->rd", grad_dense, dense_w, preferred_element_type=jnp.float32)
    (other_picked,) = links.exchange("picked_trade", ("trade", ("c",), 0, FAST, grad_picked))
    seq_picked = jnp.concatenate([grad_picked, other_picked])
    other_pos = lax.dynamic_slice_in_dim(seq_pos, (1 - c_at) * own_slots, own_slots, 0)
    place = (
        jnp.concatenate([own_pos, other_pos])[None, :]
        == c_at * own_len + lax.broadcasted_iota(jnp.int32, (own_len, slots), 0)
    ).astype(jnp.float32)
    grad_top = jnp.dot(place, seq_picked, precision=highest)

    cls_row = hidden2_b[0:1]
    pooler_w = side_full[:D]
    pooled = jnp.tanh(jnp.dot(cls_row, pooler_w, preferred_element_type=jnp.float32) + vec_rows[11])
    classes = vec_rows[14:16]
    nsp_logp = jax.nn.log_softmax(jnp.dot(pooled, classes.T, precision=highest), axis=-1)
    own_nsp = lax.dynamic_slice_in_dim(nsp_labels, y_at, 1, 0)
    pick_nsp = own_nsp[:, None] == lax.broadcasted_iota(jnp.int32, (1, 2), 1)
    nsp_sum = -jnp.sum(jnp.where(pick_nsp, nsp_logp, 0.0)) * first_core
    grad_nsp = (jnp.exp(nsp_logp) - pick_nsp.astype(jnp.float32)) / total_seqs * first_core
    class_grad = grad_nsp[0][:, None] * pooled
    grad_pre = jnp.dot(grad_nsp, classes, precision=highest) * (1.0 - pooled * pooled)
    pooler_bias_grad = grad_pre[0]
    pooler_grad = cls_row.astype(jnp.float32).T * grad_pre
    grad_cls = jnp.dot(grad_pre, pooler_w.astype(jnp.float32).T, precision=highest)
    first_row = lax.broadcasted_iota(jnp.int32, (own_len, 1), 0) == 0
    grad_top = grad_top + jnp.where(first_row, grad_cls, 0.0)

    grad_r2, grad_g2, grad_s2 = norm_backward(resid2, vec_rows[6], vec_rows[7], grad_top)
    ffn_grad_b = grad_r2.astype(low)
    out_bias_two = jnp.sum(ffn_grad_b.astype(jnp.float32), axis=0)
    ff_out_grad = jnp.einsum("td,mtf->mdf", ffn_grad_b, active, preferred_element_type=jnp.float32)
    grad_active = jnp.einsum("td,mdf->mtf", ffn_grad_b, ff_out, preferred_element_type=jnp.float32)
    grad_up = gelu_backward(upward, grad_active).astype(low)
    ff_bias_grad = jnp.sum(grad_up.astype(jnp.float32), axis=1)
    ff_in_grad = jnp.einsum("td,mtf->mdf", hidden1_b, grad_up, preferred_element_type=jnp.float32)
    hidden1_part = jnp.einsum("mtf,mdf->td", grad_up, ff_in, preferred_element_type=jnp.float32)
    ff_grad = jnp.concatenate([ff_in_grad, ff_out_grad], axis=2).astype(low)
    ff_red = comm_scatter_sum(ff_grad.reshape(mp_size * D, 2 * ff_cols), mp_first)
    grad_h1 = grad_r2 + hidden1_part
    grad_r1, grad_g1, grad_s1 = norm_backward(resid1, vec_rows[3], vec_rows[4], grad_h1)
    attn_grad_b = grad_r1.astype(low)
    out_bias_one = jnp.sum(attn_grad_b.astype(jnp.float32), axis=0)
    mixed_blocks = mixed.reshape(own_len, mp_size, attn_cols)
    attn_grad_out = jnp.einsum(
        "td,tme->mde", attn_grad_b, mixed_blocks, preferred_element_type=jnp.float32
    )
    grad_mixed = jnp.einsum(
        "td,mde->tme", attn_grad_b, out_blocks, preferred_element_type=jnp.float32
    )
    grad_mixed = grad_mixed.astype(low).reshape(own_len, D)
    grad_q, part_k, part_v = attention_backward(
        queries, key_rows, value_rows, log_norm, grad_mixed
    )
    from_k, from_v = links.exchange(
        "key_grad_trade",
        ("trade", ("c",), 0, FAST, part_k[own_len:]),
        ("trade", ("c",), 0, FAST, part_v[own_len:]),
    )
    grad_k = (part_k[:own_len] + from_k).astype(low)
    grad_v = (part_v[:own_len] + from_v).astype(low)
    grad_packed = jnp.stack(
        [
            grad_q.astype(low).reshape(own_len, mp_size, attn_cols),
            grad_k.reshape(own_len, mp_size, attn_cols),
            grad_v.reshape(own_len, mp_size, attn_cols),
        ],
        axis=2,
    ).reshape(own_len, mp_size, 3 * attn_cols)
    attn_grad_in = jnp.einsum(
        "td,tme->mde", hidden0_b, grad_packed, preferred_element_type=jnp.float32
    )
    packed_sums = jnp.sum(grad_packed.astype(jnp.float32), axis=0).reshape(mp_size, 3, attn_cols)
    hidden0_part = jnp.einsum(
        "tme,mde->td", grad_packed, qkv_blocks, preferred_element_type=jnp.float32
    )
    attn_grad = jnp.concatenate([attn_grad_in, attn_grad_out], axis=2).astype(low)
    attn_grad = attn_grad.reshape(y_size, c_size, z_size, x_size, rows_own, 4 * attn_cols)
    grad_h0 = grad_r1 + hidden0_part
    grad_x0, grad_g0, grad_s0 = norm_backward(embedded, vec_rows[0], vec_rows[1], grad_h0)

    all_x0 = comm_all_gather(grad_x0.astype(low), "z")
    onehot = (
        jnp.where(inside, at, -1)[None, :]
        == lax.broadcasted_iota(jnp.int32, (word_plane.shape[0], flat_ids.shape[0]), 0)
    ).astype(low)
    word_grad = jnp.einsum("rv,rd->vd", grad_logits, head_b, preferred_element_type=jnp.float32)
    word_grad = word_grad + jnp.dot(onehot, all_x0, preferred_element_type=jnp.float32)
    word_red = comm_scatter_sum(word_grad.astype(low), plane).astype(jnp.float32)

    position_grad = lax.dynamic_update_slice_in_dim(
        jnp.zeros((length, D), low), grad_x0.astype(low), c_at * own_len, 0
    )
    side_grad = jnp.concatenate([pooler_grad.astype(low), dense_grad.astype(low), position_grad], axis=0)
    side_grad = side_grad.reshape(z_size, x_size, y_size, c_size, side_rows, D)

    def joined(value, at, dim, received):
        kept = lax.dynamic_index_in_dim(value, at, dim, False)
        return (kept.astype(jnp.float32) + received.astype(jnp.float32)).astype(low)

    from_a, from_s = links.exchange(
        "grad_swap_c", ("swap", ("c",), 1, BIG, attn_grad), ("swap", ("c",), 3, BIG, side_grad)
    )
    attn_grad, side_grad = joined(attn_grad, c_at, 1, from_a), joined(side_grad, c_at, 3, from_s)
    from_a, from_s = links.exchange(
        "grad_swap_xy", ("swap", ("x",), 2, BIG, attn_grad), ("swap", ("y",), 2, BIG, side_grad)
    )
    attn_grad, side_grad = joined(attn_grad, x_at, 2, from_a), joined(side_grad, y_at, 2, from_s)
    from_a, from_s = links.exchange(
        "grad_swap_yx", ("swap", ("y",), 0, BIG, attn_grad), ("swap", ("x",), 1, BIG, side_grad)
    )
    attn_grad, side_grad = joined(attn_grad, y_at, 0, from_a), joined(side_grad, x_at, 1, from_s)
    from_a, from_s = links.exchange(
        "grad_spread_z", ("spread", ("z",), 0, BIG, attn_grad), ("spread", ("z",), 0, BIG, side_grad)
    )

    def total(value, received):
        kept = lax.dynamic_index_in_dim(value, z_at, 0, False).astype(jnp.float32)
        return kept + jnp.sum(received.astype(jnp.float32), axis=0)

    attn_red, side_quarter = total(attn_grad, from_a), total(side_grad, from_s)
    (side_red,) = links.exchange(
        "side_gather", ("gather", ("y", "c"), 0, FAST, side_quarter.astype(low))
    )
    side_red = side_red.reshape(side_weight.shape).astype(jnp.float32)
    type_zero = jnp.sum(jnp.where(own_types[:, None] == 0, grad_x0, 0.0), axis=0)
    type_one = jnp.sum(jnp.where(own_types[:, None] == 1, grad_x0, 0.0), axis=0)
    vec_grad = jnp.stack(
        [
            grad_g0, grad_s0, out_bias_one, grad_g1, grad_s1, out_bias_two, grad_g2, grad_s2,
            dense_bias_grad, grad_g9, grad_s9, pooler_bias_grad, type_zero, type_one,
            class_grad[0], class_grad[1],
        ],
        axis=0,
    )
    split_grad = jnp.concatenate(
        [
            packed_sums[:, 0:1],
            packed_sums[:, 2:3],
            ff_bias_grad.reshape(mp_size, attn_cols, 4).transpose(0, 2, 1),
        ],
        axis=1,
    )
    small = links.combine(
        "small_sum",
        lanes(jnp.concatenate([vec_grad.reshape(-1), split_grad.reshape(-1), decoder_part])),
    ).reshape(z_size, -1)
    narrow = vec_grad.size + split_grad.size
    summed = jnp.sum(small[:, :narrow], axis=0)
    vec_all = summed[: vec_grad.size].reshape(vec_grad.shape)
    split_all = summed[vec_grad.size :].reshape(split_grad.shape)
    vec_red = lax.dynamic_slice_in_dim(vec_all, dp_rank * vec_cols, vec_cols, 1)
    split_red = lax.dynamic_index_in_dim(split_all, mp_rank, 0, False)
    decoder_red = lax.dynamic_index_in_dim(
        small[:, narrow : narrow + decoder_part.size].reshape(z_size, x_size, mp_size, vocab_own),
        mp_rank,
        2,
        False,
    ).reshape(-1)
    word_f, attn_f, ff_f = (
        word_red,
        attn_red.reshape(attn_weight.shape),
        ff_red.astype(jnp.float32).reshape(ff_weight.shape),
    )
    own_square = (
        jnp.sum(word_f * word_f)
        + jnp.sum(attn_f * attn_f)
        + jnp.sum(ff_f * ff_f)
        + jnp.sum(side_red * side_red) / mp_size
        + jnp.sum(vec_red * vec_red) / mp_size
        + (jnp.sum(split_red * split_red) + jnp.sum(decoder_red * decoder_red)) / dp_size
    )
    loss_part = mlm_sum / total_count / z_size + nsp_sum / total_seqs
    ends = jnp.where(
        lax.broadcasted_iota(jnp.int32, (8, 128), 0) == 0, own_square, loss_part
    )
    ends = jnp.sum(links.combine("norm_sum", ends), axis=0)
    grad_square, total_loss = ends[0, 0], ends[1, 0]
    grad_norm = jnp.sqrt(grad_square)
    clip_scale = max_norm / jnp.maximum(grad_norm, max_norm)
    return (
        total_loss,
        grad_norm,
        *adam_step(word_table, word_m, word_v, word_f, clip_scale, True),
        *adam_step(attn_weight, attn_m, attn_v, attn_f, clip_scale, True),
        *adam_step(ff_weight, ff_m, ff_v, ff_f, clip_scale, True),
        *adam_step(side_weight, side_m, side_v, side_red, clip_scale, True),
        *adam_step(vectors, vec_m, vec_v, vec_red, clip_scale, False),
        *adam_step(split_bias, split_m, split_v, split_red, clip_scale, False),
        *adam_step(decoder_bias, decoder_m, decoder_v, decoder_red, clip_scale, False),
    )


def solution(mesh):
    dp_size, mp_size = mesh.shape["dp"], mesh.shape["mp"]
    x_size = 2 if dp_size % 2 == 0 else 1
    c_size = 2 if mp_size % 2 == 0 else 1
    sizes = (dp_size // x_size, x_size, mp_size // c_size, c_size)
    fine = Mesh(mesh.devices.reshape(sizes), ("z", "x", "y", "c"))
    dp, mp = ("z", "x"), ("y", "c")
    word = P(("y", "c", "z", "x"), None)
    cube = P(dp, None, mp)
    kinds = (
        [P(dp, None)] * 5
        + [P(dp)]
        + [word] * 3
        + [cube] * 6
        + [P(dp, None)] * 3
        + [P(None, dp)] * 3
        + [P(None, mp)] * 3
        + [P(mp)] * 3
    )
    return jax.shard_map(
        functools.partial(step, sizes),
        mesh=fine,
        in_specs=tuple(kinds),
        out_specs=(P(), P(), *kinds[6:]),
        check_vma=False,
    )
```

```python
import functools
import math

import jax
import jax.numpy as jnp
from jax import lax
from jax.experimental.layout import Layout, with_layout_constraint
from jax.experimental import pallas as pl
from jax.experimental.pallas import tpu as pltpu
from jax.sharding import Mesh, PartitionSpec as P

D = 768
HEAD_DIM = 64


beta_one = 0.9
beta_two = 0.999
adam_eps = 1e-06
learn_rate = 0.2
decay_rate = 0.01
step_count = 10
max_norm = 0.05
norm_eps = 1e-12
highest = lax.Precision.HIGHEST


def layer_norm(inputs, norm_gain, norm_shift):
    center = inputs - jnp.mean(inputs, axis=-1, keepdims=True)
    spread = jnp.mean(center * center, axis=-1, keepdims=True)
    return center * lax.rsqrt(spread + norm_eps) * norm_gain + norm_shift


def normal_cdf(inputs):
    return 0.5 + 0.5 * lax.erf(inputs * math.sqrt(0.5))


def gelu_exact(inputs):
    return inputs * normal_cdf(inputs)


def gelu_slope(inputs):
    density = jnp.exp(-0.5 * inputs * inputs) * (1.0 / math.sqrt(2.0 * math.pi))
    return normal_cdf(inputs) + inputs * density


def norm_backward(inputs, norm_gain, norm_shift, upstream):
    _, pullback = jax.vjp(layer_norm, inputs, norm_gain, norm_shift)
    return pullback(upstream)


def adam_step(weight, moment, square, gradient, clip_scale, decays):
    gradient = gradient * clip_scale
    moment = beta_one * moment + (1 - beta_one) * gradient
    square = beta_two * square + (1 - beta_two) * gradient * gradient
    mean_hat = moment / (1 - beta_one**step_count)
    var_hat = square / (1 - beta_two**step_count)
    change = mean_hat / (jnp.sqrt(var_hat) + adam_eps)
    if decays:
        change = change + decay_rate * weight
    return (weight - learn_rate * change, moment, square)


def comm_all_gather(value, axes):
    return lax.all_gather(value, axes, axis=0, tiled=True)


def comm_scatter_sum(value, axes):
    return lax.psum_scatter(value, axes, scatter_dimension=0, tiled=True)


MESH = pl.DeviceIdType.MESH
BIG, FAST = pl.ANY, pltpu.VMEM


class Links:
    def __init__(self, sizes):
        self.sizes = dict(zip(("z", "x", "y", "c"), sizes))
        self.used = 0

    def next_id(self):
        self.used += 1
        return self.used - 1

    def count(self, axes):
        return math.prod(self.sizes[a] for a in axes)

    def place(self, axes):
        at = 0
        for a in axes:
            at = at * self.sizes[a] + lax.axis_index(a)
        return at

    def target(self, axes, flat):
        where = {}
        for a in reversed(axes):
            where[a] = lax.rem(flat, self.sizes[a])
            flat = lax.div(flat, self.sizes[a])
        return where

    def greet(self, groups):
        barrier = pltpu.get_barrier_semaphore()
        total = 0
        for axes in groups:
            size, me = self.count(axes), self.place(axes)
            for r in range(1, size):
                pl.semaphore_signal(
                    barrier,
                    inc=1,
                    device_id=self.target(axes, lax.rem(me + r, size)),
                    device_id_type=MESH,
                )
            total += size - 1
        pl.semaphore_wait(barrier, total)

    def call(self, kernel, outs, spaces, out_spaces, scratch, values, wire, name):
        result = pl.pallas_call(
            kernel,
            out_shape=outs,
            in_specs=[pl.BlockSpec(memory_space=m) for m in spaces],
            out_specs=[pl.BlockSpec(memory_space=m) for m in out_spaces],
            scratch_shapes=scratch,
            compiler_params=pltpu.CompilerParams(
                collective_id=self.next_id(),
                has_side_effects=True,
                vmem_limit_bytes=40 * 2**20,
            ),
            cost_estimate=pl.CostEstimate(flops=0, bytes_accessed=wire, transcendentals=0),
            name=name,
        )(*values)
        return result

    def exchange(self, name, *moves):
        outs, transfers = [], 0
        for kind, axes, dim, _, value in moves:
            size = self.count(axes)
            shape = value.shape
            if kind == "gather":
                shape = (size, *shape)
            elif kind == "swap":
                shape = shape[:dim] + shape[dim + 1 :]
            elif kind == "spread":
                shape = (size - 1, *shape[1:])
            outs.append(jax.ShapeDtypeStruct(shape, value.dtype))
            transfers += size - 1
        spaces = [m[3] for m in moves]
        groups = list(dict.fromkeys(m[1] for m in moves))

        def kernel(*refs):
            ins, dests = refs[: len(moves)], refs[len(moves) : 2 * len(moves)]
            sends, lands, own_sems = refs[2 * len(moves) :]
            self.greet(groups)
            started, slot = [], 0
            for (kind, axes, dim, _, _), source, dest in zip(moves, ins, dests):
                size, me = self.count(axes), self.place(axes)
                for r in range(1, size):
                    peer = lax.rem(me + r, size)
                    if kind == "gather":
                        src, dst = source, dest.at[me]
                    elif kind == "swap":
                        src, dst = source.at[(slice(None),) * dim + (peer,)], dest
                    elif kind == "spread":
                        src, dst = source.at[peer], dest.at[r - 1]
                    else:
                        src, dst = source, dest
                    copy = pltpu.make_async_remote_copy(
                        src_ref=src,
                        dst_ref=dst,
                        send_sem=sends.at[slot],
                        recv_sem=lands.at[slot],
                        device_id=self.target(axes, peer),
                        device_id_type=MESH,
                    )
                    copy.start()
                    started.append(copy)
                    slot += 1
            for number, ((kind, axes, _, _, _), source, dest) in enumerate(zip(moves, ins, dests)):
                if kind == "gather":
                    copy = pltpu.make_async_copy(
                        source, dest.at[self.place(axes)], own_sems.at[number]
                    )
                    copy.start()
                    started.append(copy)
            for copy in started:
                copy.wait()

        return self.call(
            kernel,
            outs,
            spaces,
            spaces,
            [
                pltpu.SemaphoreType.DMA((transfers,)),
                pltpu.SemaphoreType.DMA((transfers,)),
                pltpu.SemaphoreType.DMA((len(moves),)),
            ],
            [m[4] for m in moves],
            sum(2 * math.prod(o.shape) * o.dtype.itemsize for o in outs),
            name,
        )

    def combine(self, name, value):
        pairs = [a for a in ("c", "x", "y") if self.sizes[a] > 1]
        depth = self.sizes["z"]
        steps = len(pairs)

        def kernel(x_ref, out_ref, sums, land, sends, lands):
            self.greet([(a,) for a in pairs] + [("z",)])
            me = lax.axis_index("z")
            for i, a in enumerate(pairs):
                source = x_ref if i == 0 else sums.at[i - 1]
                copy = pltpu.make_async_remote_copy(
                    src_ref=source,
                    dst_ref=land.at[i],
                    send_sem=sends.at[i],
                    recv_sem=lands.at[i],
                    device_id={a: 1 - lax.axis_index(a)},
                    device_id_type=MESH,
                )
                copy.start()
                copy.wait()
                sums[i] = source[...] + land[i]
            out_ref[me] = sums[steps - 1]
            started = []
            for r in range(1, depth):
                copy = pltpu.make_async_remote_copy(
                    src_ref=sums.at[steps - 1],
                    dst_ref=out_ref.at[me],
                    send_sem=sends.at[steps + r - 1],
                    recv_sem=lands.at[steps + r - 1],
                    device_id={"z": lax.rem(me + r, depth)},
                    device_id_type=MESH,
                )
                copy.start()
                started.append(copy)
            for copy in started:
                copy.wait()

        return self.call(
            kernel,
            [jax.ShapeDtypeStruct((depth, *value.shape), value.dtype)],
            [FAST],
            [FAST],
            [
                pltpu.VMEM((steps, *value.shape), value.dtype),
                pltpu.VMEM((steps, *value.shape), value.dtype),
                pltpu.SemaphoreType.DMA((steps + depth - 1,)),
                pltpu.SemaphoreType.DMA((steps + depth - 1,)),
            ],
            [value],
            16 * value.size * 4,
            name,
        )[0]

    def gather_plane(self, name, value):
        rows, width = value.shape
        parts = 4 if rows % 64 == 0 else 1
        head = (parts + 1) // 2
        value = value.reshape(parts, rows // parts, width)
        shape = (*(self.sizes[a] for a in ("x", "y", "c")), *value.shape)

        def kernel(own, out, sends, lands, own_sem):
            self.greet([("x",), ("y",), ("c",)])
            x, y, c = (lax.axis_index(a) for a in ("x", "y", "c"))
            by_x, by_y, by_c = {"x": 1 - x}, {"y": 1 - y}, {"c": 1 - c}
            started = []

            def send(src, place, part, slot, peer):
                copy = pltpu.make_async_remote_copy(
                    src_ref=src,
                    dst_ref=out.at[(*place, part)],
                    send_sem=sends.at[len(started)],
                    recv_sem=lands.at[slot, part],
                    device_id=peer,
                    device_id_type=MESH,
                )
                copy.start()
                started.append(copy)

            def arrived(place, part, slot):
                landed = out.at[(*place, part)]
                pltpu.make_async_remote_copy(
                    src_ref=landed,
                    dst_ref=landed,
                    send_sem=sends.at[0],
                    recv_sem=lands.at[slot, part],
                    device_id=by_c,
                    device_id_type=MESH,
                ).wait_recv()
                return landed

            me, at_x, at_y, at_xy = (x, y, c), (1 - x, y, c), (x, 1 - y, c), (1 - x, 1 - y, c)
            for part in range(parts):
                send(own.at[part], me, part, 0, by_x)
                send(own.at[part], me, part, 1, by_y)
            for part in range(parts):
                send(own.at[part], me, part, 3, by_c)
            local = pltpu.make_async_copy(own, out.at[me], own_sem.at[0])
            local.start()
            for part in range(parts):
                landed = arrived(at_x, part, 0)
                if part < head:
                    send(landed, at_x, part, 2, by_y)
                send(landed, at_x, part, 4, by_c)
                landed = arrived(at_y, part, 1)
                if part >= head:
                    send(landed, at_y, part, 2, by_x)
                send(landed, at_y, part, 5, by_c)
            for part in range(parts):
                landed = arrived(at_xy, part, 2)
                send(landed, at_xy, part, 6, by_c)
            for slot, place in ((3, me), (4, at_x), (5, at_y), (6, at_xy)):
                for part in range(parts):
                    arrived((place[0], place[1], 1 - c), part, slot)
            for copy in started:
                copy.wait_send()
            local.wait()

        return self.call(
            kernel,
            [jax.ShapeDtypeStruct(shape, value.dtype)],
            [BIG],
            [BIG],
            [
                pltpu.SemaphoreType.DMA((7 * parts,)),
                pltpu.SemaphoreType.DMA((7, parts)),
                pltpu.SemaphoreType.DMA((1,)),
            ],
            [value],
            4 * math.prod(shape),
            name,
        )[0].reshape(-1, width)


def row_major(value):
    return with_layout_constraint(value, Layout(major_to_minor=tuple(range(value.ndim))))


def lanes(flat):
    padded = jnp.pad(flat, (0, -flat.size % 1024))
    return padded.reshape(-1, 128)


HEAD_SCALE = math.log2(math.e) / math.sqrt(HEAD_DIM)
PAIR = 2 * HEAD_DIM
ROWS = 256


def dots(left, right, left_dim, right_dim):
    return lax.dot_general(
        left, right, (((left_dim,), (right_dim,)), ((), ())), preferred_element_type=jnp.float32
    )


def half_lanes(value, half):
    lane = lax.broadcasted_iota(jnp.int32, value.shape, 1)
    return jnp.where((lane >= HEAD_DIM) == (half == 1), value, jnp.zeros((), value.dtype))


def forward_kernel(q_ref, k0_ref, k1_ref, v0_ref, v1_ref, out_ref, norm_ref):
    keys = jnp.concatenate([k0_ref[...], k1_ref[...]], axis=0)
    values = jnp.concatenate([v0_ref[...], v1_ref[...]], axis=0)
    for start in range(0, q_ref.shape[0], ROWS):
        rows = pl.ds(start, ROWS)
        queries = q_ref[rows, :]
        halves = []
        for half in range(2):
            scores = dots(keys, half_lanes(queries, half), 1, 1)
            top = jnp.max(scores, axis=0, keepdims=True)
            powers = jnp.exp2((scores - top) * HEAD_SCALE)
            total = jnp.sum(powers, axis=0, keepdims=True)
            probs = (powers * (1.0 / total)).astype(jnp.bfloat16)
            norm_ref[0, half : half + 1, rows] = top * HEAD_SCALE + jnp.log2(total)
            mixed = dots(values, probs, 0, 0)
            halves.append(mixed[half * HEAD_DIM : (half + 1) * HEAD_DIM])
        out_ref[rows, :] = jnp.concatenate(halves, axis=0).T.astype(out_ref.dtype)


def attention_forward(queries, keys, values):
    length, width = queries.shape
    pairs = width // PAIR
    block = pl.BlockSpec((length, PAIR), lambda i: (0, i))
    flops = 8 * length * length * width
    return pl.pallas_call(
        forward_kernel,
        grid=(pairs,),
        out_shape=[
            jax.ShapeDtypeStruct((length, width), queries.dtype),
            jax.ShapeDtypeStruct((pairs, 2, length), jnp.float32),
        ],
        in_specs=[block] * 5,
        out_specs=[block, pl.BlockSpec((1, 2, length), lambda i: (i, 0, 0))],
        cost_estimate=pl.CostEstimate(
            flops=2 * flops, bytes_accessed=16 * length * width, transcendentals=flops // 256
        ),
        name="attention_forward",
    )(queries, *keys, *values)


def backward_kernel(
    q_ref, k0_ref, k1_ref, v0_ref, v1_ref, norm_ref, g_ref, dq_ref, dk0_ref, dk1_ref, dv0_ref, dv1_ref
):
    own = k0_ref.shape[0]
    keys = jnp.concatenate([k0_ref[...], k1_ref[...]], axis=0)
    values = jnp.concatenate([v0_ref[...], v1_ref[...]], axis=0)
    grad_keys = grad_values = 0.0
    for start in range(0, q_ref.shape[0], ROWS):
        rows = pl.ds(start, ROWS)
        halves = []
        for half in range(2):
            queries = half_lanes(q_ref[rows, :], half)
            upstream = half_lanes(g_ref[rows, :], half)
            scores = dots(keys, queries, 1, 1)
            probs = jnp.exp2(scores * HEAD_SCALE - norm_ref[0, half : half + 1, rows])
            grad_probs = dots(values, upstream, 1, 1)
            row_dot = jnp.sum(grad_probs * probs, axis=0, keepdims=True)
            grad_scores = (probs * (grad_probs - row_dot)).astype(jnp.bfloat16)
            grad_values = grad_values + dots(probs.astype(jnp.bfloat16), upstream, 1, 0)
            grad_keys = grad_keys + dots(grad_scores, queries, 1, 0)
            grad_queries = dots(keys, grad_scores, 0, 0)
            halves.append(grad_queries[half * HEAD_DIM : (half + 1) * HEAD_DIM])
        grad_queries = jnp.concatenate(halves, axis=0) * (1.0 / math.sqrt(HEAD_DIM))
        dq_ref[rows, :] = grad_queries.T.astype(dq_ref.dtype)
    grad_keys = grad_keys * (1.0 / math.sqrt(HEAD_DIM))
    dk0_ref[...] = grad_keys[:own]
    dk1_ref[...] = grad_keys[own:]
    dv0_ref[...] = grad_values[:own]
    dv1_ref[...] = grad_values[own:]


def attention_backward(queries, keys, values, log_norm, grad_mixed):
    length, width = queries.shape
    pairs = width // PAIR
    block = pl.BlockSpec((length, PAIR), lambda i: (0, i))
    flops = 20 * length * length * width
    wide = jax.ShapeDtypeStruct((length, width), jnp.float32)
    return pl.pallas_call(
        backward_kernel,
        grid=(pairs,),
        out_shape=[jax.ShapeDtypeStruct((length, width), queries.dtype)] + [wide] * 4,
        in_specs=[block] * 5 + [pl.BlockSpec((1, 2, length), lambda i: (i, 0, 0)), block],
        out_specs=[block] * 5,
        cost_estimate=pl.CostEstimate(
            flops=2 * flops, bytes_accessed=32 * length * width, transcendentals=flops // 640
        ),
        name="attention_backward",
    )(queries, *keys, *values, log_norm, grad_mixed)


def step(sizes, *args):
    (
        token_ids, type_ids, mask_pos, mask_valid, mlm_labels, nsp_labels,
        word_table, word_m, word_v, attn_weight, attn_m, attn_v,
        ff_weight, ff_m, ff_v, side_weight, side_m, side_v,
        vectors, vec_m, vec_v, split_bias, split_m, split_v,
        decoder_bias, decoder_m, decoder_v,
    ) = args
    z_size, x_size, y_size, c_size = sizes
    dp_size, mp_size = z_size * x_size, y_size * c_size
    z_at, x_at, y_at, c_at = (lax.axis_index(a) for a in ("z", "x", "y", "c"))
    dp_rank, mp_rank = z_at * x_size + x_at, y_at * c_size + c_at
    every = ("z", "x", "y", "c")
    mp_first = ("y", "c", "z", "x")
    plane = ("x", "y", "c")
    batch_size, length = token_ids.shape
    slots = mask_pos.shape[1]
    own_len, own_slots = length // c_size, slots // c_size
    vocab_own = word_table.shape[0]
    attn_cols, ff_cols = attn_weight.shape[2], ff_weight.shape[2]
    rows_own = attn_weight.shape[0]
    low = jnp.bfloat16
    links = Links(sizes)

    def mine(rows, size):
        row = lax.dynamic_index_in_dim(rows, y_at, 0, False)
        return lax.dynamic_slice_in_dim(row, c_at * size, size, 0)

    own_ids = mine(token_ids, own_len)
    own_types = mine(type_ids, own_len)
    seq_pos = lax.dynamic_index_in_dim(mask_pos, y_at, 0, False)
    own_pos = mine(mask_pos, own_slots)
    own_valid = mine(mask_valid, own_slots)
    own_labels = mine(mlm_labels, own_slots)
    first_core = (c_at == 0).astype(jnp.float32)

    side_rows = side_weight.shape[0] // mp_size
    side_full = comm_all_gather(
        lax.dynamic_slice_in_dim(side_weight.astype(low), mp_rank * side_rows, side_rows, 0), every
    )
    attn_blocks = comm_all_gather(
        attn_weight.astype(low).reshape(rows_own, 4 * attn_cols), mp_first
    ).reshape(mp_size, D, 4 * attn_cols)
    ff_blocks = comm_all_gather(
        ff_weight.astype(low).reshape(rows_own, 2 * ff_cols), mp_first
    ).reshape(mp_size, D, 2 * ff_cols)
    vec_cols = vectors.shape[1]
    stripe = vocab_own * x_size
    bias_mine = lax.dynamic_slice_in_dim(decoder_bias, z_at * stripe, stripe, 0)
    int_count = own_len + 2 * own_slots
    ints, vec_parts, counts, mp_small = links.exchange(
        "small_gather",
        ("gather", ("z",), 0, FAST, lanes(jnp.concatenate([own_ids, own_labels, own_valid]))),
        ("gather", ("z", "x"), 0, FAST, jnp.pad(vectors.astype(low), ((0, 0), (0, 128 - vec_cols)))),
        (
            "gather",
            ("z", "x"),
            0,
            FAST,
            jnp.full((8, 128), jnp.sum(mask_valid.astype(jnp.float32))),
        ),
        ("gather", ("y", "c"), 0, FAST, lanes(jnp.concatenate([bias_mine, split_bias.reshape(-1)]))),
    )
    ints = ints.reshape(z_size, -1)[:, :int_count]
    z_ids, z_labels, z_valid = (
        ints[:, :own_len],
        ints[:, own_len : own_len + own_slots],
        ints[:, own_len + own_slots :],
    )
    total_count = jnp.sum(counts[:, 0, 0])
    total_seqs = jnp.float32(batch_size * dp_size)
    vec_rows = (
        vec_parts[:, :, :vec_cols]
        .transpose(1, 0, 2)
        .reshape(vectors.shape[0], D)
        .astype(jnp.float32)
    )
    mp_small = mp_small.reshape(mp_size, -1)
    word_plane = links.gather_plane("word_gather", word_table.astype(low))
    bias_plane = (
        mp_small[:, :stripe].reshape(mp_size, x_size, vocab_own).transpose(1, 0, 2).reshape(-1)
    )
    split_full = mp_small[:, stripe : stripe + 6 * attn_cols].reshape(mp_size, 6, attn_cols)

    def plane_index(ids):
        block = ids // stripe
        offset = ids % stripe
        inside = block % z_size == z_at
        at = ((offset // vocab_own) * mp_size + block // z_size) * vocab_own + offset % vocab_own
        return inside, at

    flat_ids = z_ids.reshape(-1)
    inside, at = plane_index(flat_ids)
    looked = jnp.where(inside[:, None], word_plane[jnp.where(inside, at, 0)], jnp.zeros((), low))
    looked = looked.reshape(z_size, own_len, D)
    (found,) = links.exchange("token_spread", ("spread", ("z",), 0, BIG, looked))
    embedded = lax.dynamic_index_in_dim(looked, z_at, 0, False).astype(jnp.float32)
    embedded = embedded + jnp.sum(found.astype(jnp.float32), axis=0)
    position_rows = lax.dynamic_slice_in_dim(side_full, 2 * D + c_at * own_len, own_len, 0)
    embedded = (
        embedded
        + position_rows.astype(jnp.float32)
        + jnp.where(own_types[:, None] == 0, vec_rows[12], vec_rows[13])
    )
    hidden0 = layer_norm(embedded, vec_rows[0], vec_rows[1])
    hidden0_b = hidden0.astype(low)

    qkv_blocks = attn_blocks[:, :, : 3 * attn_cols]
    out_blocks = attn_blocks[:, :, 3 * attn_cols :]
    packed = jnp.einsum("td,mde->tme", hidden0_b, qkv_blocks, preferred_element_type=jnp.float32)
    packed = packed.reshape(own_len, mp_size, 3, attn_cols)
    queries = (packed[:, :, 0] + split_full[:, 0]).astype(low).reshape(own_len, D)
    own_keys = packed[:, :, 1].astype(low).reshape(own_len, D)
    own_values = (packed[:, :, 2] + split_full[:, 1]).astype(low).reshape(own_len, D)
    other_keys, other_values = links.exchange(
        "key_trade", ("trade", ("c",), 0, FAST, own_keys), ("trade", ("c",), 0, FAST, own_values)
    )
    keys, values = (own_keys, other_keys), (own_values, other_values)
    mixed, log_norm = attention_forward(queries, keys, values)
    attn_out = jnp.einsum(
        "tme,mde->td",
        mixed.reshape(own_len, mp_size, attn_cols),
        out_blocks,
        preferred_element_type=jnp.float32,
    )
    resid1 = hidden0 + (attn_out + vec_rows[2])
    hidden1 = layer_norm(resid1, vec_rows[3], vec_rows[4])
    hidden1_b = hidden1.astype(low)
    ff_bias = split_full[:, 2:6].transpose(0, 2, 1).reshape(mp_size, ff_cols)
    ff_in, ff_out = ff_blocks[:, :, :ff_cols], ff_blocks[:, :, ff_cols:]
    upward = jnp.einsum("td,mdf->mtf", hidden1_b, ff_in, preferred_element_type=jnp.float32)
    upward = upward + ff_bias[:, None]
    active = gelu_exact(upward).astype(low)
    ffn_out = jnp.einsum("mtf,mdf->td", active, ff_out, preferred_element_type=jnp.float32)
    resid2 = hidden1 + (ffn_out + vec_rows[5])
    hidden2 = layer_norm(resid2, vec_rows[6], vec_rows[7])

    hidden2_b = hidden2.astype(low)
    (other_h2,) = links.exchange("hidden_trade", ("trade", ("c",), 0, FAST, hidden2_b))
    picked_b = jnp.concatenate([hidden2_b, other_h2])[
        own_pos % own_len + jnp.where(own_pos // own_len == c_at, 0, own_len)
    ]
    dense_w = side_full[D : 2 * D]
    dense_out = jnp.dot(picked_b, dense_w, preferred_element_type=jnp.float32) + vec_rows[8]
    act_dense = gelu_exact(dense_out)
    head_rows = layer_norm(act_dense, vec_rows[9], vec_rows[10])
    (head_b,) = links.exchange("head_gather", ("gather", ("z",), 0, FAST, head_rows.astype(low)))
    head_b = head_b.reshape(-1, D)
    row_count = head_b.shape[0]
    logits = (
        jnp.einsum("rd,vd->rv", head_b, word_plane, preferred_element_type=jnp.float32)
        + bias_plane
    )
    label_in, label_at = plane_index(z_labels.reshape(-1))
    label_at = jnp.where(label_in, label_at, -1)
    hit_rows = label_at[:, None] == lax.broadcasted_iota(jnp.int32, logits.shape, 1)
    row_top = jnp.max(logits, axis=1)
    row_total = jnp.sum(jnp.exp(logits - row_top[:, None]), axis=1)
    row_target = jnp.sum(jnp.where(hit_rows, logits, 0.0), axis=1)
    stats = jnp.pad(jnp.stack([row_top, row_total, row_target]), ((0, 5), (0, 0)))
    (stats,) = links.exchange("stat_gather", ("gather", ("z",), 0, FAST, stats))
    top_all = jnp.max(stats[:, 0], axis=0)
    total_all = jnp.sum(stats[:, 1] * jnp.exp(stats[:, 0] - top_all), axis=0)
    target_all = jnp.sum(stats[:, 2], axis=0)
    log_total = top_all + jnp.log(total_all)
    valid_rows = z_valid.reshape(-1).astype(jnp.float32)
    mlm_sum = -jnp.sum(valid_rows * (target_all - log_total))
    weight_rows = valid_rows / total_count
    grad_logits = (
        (jnp.exp(logits - log_total[:, None]) - hit_rows.astype(jnp.float32)) * weight_rows[:, None]
    ).astype(low)
    decoder_part = jnp.sum(grad_logits.astype(jnp.float32), axis=0)
    head_part = jnp.dot(grad_logits, word_plane, preferred_element_type=jnp.float32)
    head_part = head_part.reshape(z_size, own_slots, D)
    (head_others,) = links.exchange("head_spread", ("spread", ("z",), 0, FAST, head_part.astype(low)))
    grad_head = lax.dynamic_index_in_dim(head_part, z_at, 0, False) + jnp.sum(
        head_others.astype(jnp.float32), axis=0
    )
    grad_act, grad_g9, grad_s9 = norm_backward(act_dense, vec_rows[9], vec_rows[10], grad_head)
    grad_dense = (grad_act * gelu_slope(dense_out)).astype(low)
    dense_bias_grad = jnp.sum(grad_dense.astype(jnp.float32), axis=0)
    dense_grad = jnp.einsum("rd,re->de", picked_b, grad_dense, preferred_element_type=jnp.float32)
    grad_picked = jnp.einsum("re,de->rd", grad_dense, dense_w, preferred_element_type=jnp.float32)
    (other_picked,) = links.exchange("picked_trade", ("trade", ("c",), 0, FAST, grad_picked))
    seq_picked = jnp.concatenate([grad_picked, other_picked])
    other_pos = lax.dynamic_slice_in_dim(seq_pos, (1 - c_at) * own_slots, own_slots, 0)
    place = (
        jnp.concatenate([own_pos, other_pos])[None, :]
        == c_at * own_len + lax.broadcasted_iota(jnp.int32, (own_len, slots), 0)
    ).astype(jnp.float32)
    grad_top = jnp.dot(place, seq_picked, precision=highest)

    cls_row = hidden2_b[0:1]
    pooler_w = side_full[:D]
    pooled = jnp.tanh(jnp.dot(cls_row, pooler_w, preferred_element_type=jnp.float32) + vec_rows[11])
    classes = vec_rows[14:16]
    nsp_logp = jax.nn.log_softmax(jnp.dot(pooled, classes.T, precision=highest), axis=-1)
    own_nsp = lax.dynamic_slice_in_dim(nsp_labels, y_at, 1, 0)
    pick_nsp = own_nsp[:, None] == lax.broadcasted_iota(jnp.int32, (1, 2), 1)
    nsp_sum = -jnp.sum(jnp.where(pick_nsp, nsp_logp, 0.0)) * first_core
    grad_nsp = (jnp.exp(nsp_logp) - pick_nsp.astype(jnp.float32)) / total_seqs * first_core
    class_grad = grad_nsp[0][:, None] * pooled
    grad_pre = jnp.dot(grad_nsp, classes, precision=highest) * (1.0 - pooled * pooled)
    pooler_bias_grad = grad_pre[0]
    pooler_grad = cls_row.astype(jnp.float32).T * grad_pre
    grad_cls = jnp.dot(grad_pre, pooler_w.astype(jnp.float32).T, precision=highest)
    first_row = lax.broadcasted_iota(jnp.int32, (own_len, 1), 0) == 0
    grad_top = grad_top + jnp.where(first_row, grad_cls, 0.0)

    grad_r2, grad_g2, grad_s2 = norm_backward(resid2, vec_rows[6], vec_rows[7], grad_top)
    ffn_grad_b = grad_r2.astype(low)
    out_bias_two = jnp.sum(ffn_grad_b.astype(jnp.float32), axis=0)
    ff_out_grad = jnp.einsum("td,mtf->mdf", ffn_grad_b, active, preferred_element_type=jnp.float32)
    grad_active = jnp.einsum("td,mdf->mtf", ffn_grad_b, ff_out, preferred_element_type=jnp.float32)
    grad_up = (grad_active * gelu_slope(upward)).astype(low)
    ff_bias_grad = jnp.sum(grad_up.astype(jnp.float32), axis=1)
    ff_in_grad = jnp.einsum("td,mtf->mdf", hidden1_b, grad_up, preferred_element_type=jnp.float32)
    hidden1_part = jnp.einsum("mtf,mdf->td", grad_up, ff_in, preferred_element_type=jnp.float32)
    ff_grad = jnp.stack(
        [
            row_major(g.astype(low)).reshape(mp_size * dp_size, rows_own, ff_cols)
            for g in (ff_in_grad, ff_out_grad)
        ],
        axis=1,
    )
    ff_grad, hidden1_part = lax.optimization_barrier((ff_grad, hidden1_part))
    ff_red = comm_scatter_sum(ff_grad.reshape(-1, ff_cols), mp_first)
    grad_h1 = grad_r2 + hidden1_part
    grad_r1, grad_g1, grad_s1 = norm_backward(resid1, vec_rows[3], vec_rows[4], grad_h1)
    attn_grad_b = grad_r1.astype(low)
    out_bias_one = jnp.sum(attn_grad_b.astype(jnp.float32), axis=0)
    mixed_blocks = mixed.reshape(own_len, mp_size, attn_cols)
    attn_grad_out = jnp.einsum(
        "td,tme->mde", attn_grad_b, mixed_blocks, preferred_element_type=jnp.float32
    )
    grad_mixed = jnp.einsum(
        "td,mde->tme", attn_grad_b, out_blocks, preferred_element_type=jnp.float32
    )
    grad_mixed = grad_mixed.astype(low).reshape(own_len, D)
    grad_q, own_k, part_k, own_v, part_v = attention_backward(
        queries, keys, values, log_norm, grad_mixed
    )
    from_k, from_v = links.exchange(
        "key_grad_trade",
        ("trade", ("c",), 0, FAST, part_k),
        ("trade", ("c",), 0, FAST, part_v),
    )
    grad_k = (own_k + from_k).astype(low)
    grad_v = (own_v + from_v).astype(low)
    grad_packed = jnp.stack(
        [
            grad_q.reshape(own_len, mp_size, attn_cols),
            grad_k.reshape(own_len, mp_size, attn_cols),
            grad_v.reshape(own_len, mp_size, attn_cols),
        ],
        axis=2,
    ).reshape(own_len, mp_size, 3 * attn_cols)
    attn_grad_in = jnp.einsum(
        "td,tme->mde", hidden0_b, grad_packed, preferred_element_type=jnp.float32
    )
    packed_sums = jnp.sum(grad_packed.astype(jnp.float32), axis=0).reshape(mp_size, 3, attn_cols)
    hidden0_part = jnp.einsum(
        "tme,mde->td", grad_packed, qkv_blocks, preferred_element_type=jnp.float32
    )
    attn_grad = jnp.concatenate([attn_grad_in, attn_grad_out], axis=2).astype(low)
    attn_grad = attn_grad.reshape(y_size, c_size, z_size, x_size, rows_own, 4 * attn_cols)
    grad_h0 = grad_r1 + hidden0_part
    grad_x0, grad_g0, grad_s0 = norm_backward(embedded, vec_rows[0], vec_rows[1], grad_h0)

    position_grad = lax.dynamic_update_slice_in_dim(
        jnp.zeros((length, D), low), grad_x0.astype(low), c_at * own_len, 0
    )
    side_grad = jnp.concatenate([pooler_grad.astype(low), dense_grad.astype(low), position_grad], axis=0)
    side_grad = side_grad.reshape(z_size, x_size, y_size, c_size, side_rows, D)

    def joined(value, at, dim, received):
        kept = lax.dynamic_index_in_dim(value, at, dim, False)
        return (kept.astype(jnp.float32) + received.astype(jnp.float32)).astype(low)

    x0_b = grad_x0.astype(low)
    cut_one, cut_two = own_len // 8, 5 * own_len // 8
    from_a, from_s, x0_one = links.exchange(
        "grad_swap_c",
        ("swap", ("c",), 1, BIG, attn_grad),
        ("swap", ("c",), 3, BIG, side_grad),
        ("gather", ("z",), 0, BIG, x0_b[:cut_one]),
    )
    attn_grad, side_grad = joined(attn_grad, c_at, 1, from_a), joined(side_grad, c_at, 3, from_s)
    from_a, from_s, x0_two = links.exchange(
        "grad_swap_xy",
        ("swap", ("x",), 2, BIG, attn_grad),
        ("swap", ("y",), 2, BIG, side_grad),
        ("gather", ("z",), 0, BIG, x0_b[cut_one:cut_two]),
    )
    attn_grad, side_grad = joined(attn_grad, x_at, 2, from_a), joined(side_grad, y_at, 2, from_s)
    from_a, from_s, x0_three = links.exchange(
        "grad_swap_yx",
        ("swap", ("y",), 0, BIG, attn_grad),
        ("swap", ("x",), 1, BIG, side_grad),
        ("gather", ("z",), 0, BIG, x0_b[cut_two:]),
    )
    attn_grad, side_grad = joined(attn_grad, y_at, 0, from_a), joined(side_grad, x_at, 1, from_s)

    ff_red, x0_three = lax.optimization_barrier((ff_red, x0_three))
    all_x0 = jnp.concatenate([x0_one, x0_two, x0_three], axis=1).reshape(-1, D)
    onehot = (
        jnp.where(inside, at, -1)[None, :]
        == lax.broadcasted_iota(jnp.int32, (word_plane.shape[0], flat_ids.shape[0]), 0)
    ).astype(low)
    word_grad = jnp.einsum("rv,rd->vd", grad_logits, head_b, preferred_element_type=jnp.float32)
    word_grad = word_grad + jnp.dot(onehot, all_x0, preferred_element_type=jnp.float32)
    word_grad, attn_grad, side_grad = lax.optimization_barrier(
        (word_grad.astype(low), attn_grad, side_grad)
    )
    word_red = comm_scatter_sum(word_grad, plane).astype(jnp.float32)
    from_a, from_s = links.exchange(
        "grad_spread_z", ("spread", ("z",), 0, BIG, attn_grad), ("spread", ("z",), 0, BIG, side_grad)
    )

    def total(value, received):
        kept = lax.dynamic_index_in_dim(value, z_at, 0, False).astype(jnp.float32)
        return kept + jnp.sum(received.astype(jnp.float32), axis=0)

    attn_red, side_quarter = total(attn_grad, from_a), total(side_grad, from_s)
    type_zero = jnp.sum(jnp.where(own_types[:, None] == 0, grad_x0, 0.0), axis=0)
    type_one = jnp.sum(jnp.where(own_types[:, None] == 1, grad_x0, 0.0), axis=0)
    vec_grad = jnp.stack(
        [
            grad_g0, grad_s0, out_bias_one, grad_g1, grad_s1, out_bias_two, grad_g2, grad_s2,
            dense_bias_grad, grad_g9, grad_s9, pooler_bias_grad, type_zero, type_one,
            class_grad[0], class_grad[1],
        ],
        axis=0,
    )
    split_grad = jnp.concatenate(
        [
            packed_sums[:, 0:1],
            packed_sums[:, 2:3],
            ff_bias_grad.reshape(mp_size, attn_cols, 4).transpose(0, 2, 1),
        ],
        axis=1,
    )
    late = lanes(jnp.concatenate([vec_grad.reshape(-1), split_grad.reshape(-1), decoder_part]))
    late, side_quarter = lax.optimization_barrier((late, side_quarter))
    small = links.combine(
        "small_sum",
        late,
    ).reshape(z_size, -1)
    (side_red,) = links.exchange(
        "side_gather", ("gather", ("y", "c"), 0, FAST, side_quarter.astype(low))
    )
    side_red = side_red.reshape(side_weight.shape).astype(jnp.float32)
    narrow = vec_grad.size + split_grad.size
    summed = jnp.sum(small[:, :narrow], axis=0)
    vec_all = summed[: vec_grad.size].reshape(vec_grad.shape)
    split_all = summed[vec_grad.size :].reshape(split_grad.shape)
    vec_red = lax.dynamic_slice_in_dim(vec_all, dp_rank * vec_cols, vec_cols, 1)
    split_red = lax.dynamic_index_in_dim(split_all, mp_rank, 0, False)
    decoder_red = lax.dynamic_index_in_dim(
        small[:, narrow : narrow + decoder_part.size].reshape(z_size, x_size, mp_size, vocab_own),
        mp_rank,
        2,
        False,
    ).reshape(-1)
    word_f, attn_f, ff_f = (
        word_red,
        attn_red.reshape(attn_weight.shape),
        lax.optimization_barrier(
            ff_red.astype(jnp.float32).reshape(2, rows_own, ff_cols).transpose(1, 0, 2)
        ),
    )
    own_square = (
        jnp.sum(word_f * word_f)
        + jnp.sum(attn_f * attn_f)
        + jnp.sum(ff_f * ff_f)
        + jnp.sum(side_red * side_red) / mp_size
        + jnp.sum(vec_red * vec_red) / mp_size
        + (jnp.sum(split_red * split_red) + jnp.sum(decoder_red * decoder_red)) / dp_size
    )
    loss_part = mlm_sum / total_count / z_size + nsp_sum / total_seqs
    ends = jnp.where(
        lax.broadcasted_iota(jnp.int32, (8, 128), 0) == 0, own_square, loss_part
    )
    ends = jnp.sum(links.combine("norm_sum", ends), axis=0)
    grad_square, total_loss = ends[0, 0], ends[1, 0]
    grad_norm = jnp.sqrt(grad_square)
    clip_scale = max_norm / jnp.maximum(grad_norm, max_norm)
    return (
        total_loss,
        grad_norm,
        *adam_step(word_table, word_m, word_v, word_f, clip_scale, True),
        *adam_step(attn_weight, attn_m, attn_v, attn_f, clip_scale, True),
        *adam_step(ff_weight, ff_m, ff_v, ff_f, clip_scale, True),
        *adam_step(side_weight, side_m, side_v, side_red, clip_scale, True),
        *adam_step(vectors, vec_m, vec_v, vec_red, clip_scale, False),
        *adam_step(split_bias, split_m, split_v, split_red, clip_scale, False),
        *adam_step(decoder_bias, decoder_m, decoder_v, decoder_red, clip_scale, False),
    )


def solution(mesh):
    dp_size, mp_size = mesh.shape["dp"], mesh.shape["mp"]
    x_size = 2 if dp_size % 2 == 0 else 1
    c_size = 2 if mp_size % 2 == 0 else 1
    sizes = (dp_size // x_size, x_size, mp_size // c_size, c_size)
    fine = Mesh(mesh.devices.reshape(sizes), ("z", "x", "y", "c"))
    dp, mp = ("z", "x"), ("y", "c")
    word = P(("y", "c", "z", "x"), None)
    cube = P(dp, None, mp)
    kinds = (
        [P(dp, None)] * 5
        + [P(dp)]
        + [word] * 3
        + [cube] * 6
        + [P(dp, None)] * 3
        + [P(None, dp)] * 3
        + [P(None, mp)] * 3
        + [P(mp)] * 3
    )
    return jax.shard_map(
        functools.partial(step, sizes),
        mesh=fine,
        in_specs=tuple(kinds),
        out_specs=(P(), P(), *kinds[6:]),
        check_vma=False,
    )
```

```python
import functools
import math

import jax
import jax.numpy as jnp
from jax import lax
from jax.experimental.layout import Layout, with_layout_constraint
from jax.experimental import pallas as pl
from jax.experimental.pallas import tpu as pltpu
from jax.sharding import Mesh, PartitionSpec as P

D = 768
HEAD_DIM = 64


beta_one = 0.9
beta_two = 0.999
adam_eps = 1e-06
learn_rate = 0.2
decay_rate = 0.01
step_count = 10
max_norm = 0.05
norm_eps = 1e-12
highest = lax.Precision.HIGHEST


def layer_norm(inputs, norm_gain, norm_shift):
    center = inputs - jnp.mean(inputs, axis=-1, keepdims=True)
    spread = jnp.mean(center * center, axis=-1, keepdims=True)
    return center * lax.rsqrt(spread + norm_eps) * norm_gain + norm_shift


def normal_cdf(inputs):
    return 0.5 + 0.5 * lax.erf(inputs * math.sqrt(0.5))


def gelu_exact(inputs):
    return inputs * normal_cdf(inputs)


def gelu_slope(inputs):
    density = jnp.exp(-0.5 * inputs * inputs) * (1.0 / math.sqrt(2.0 * math.pi))
    return normal_cdf(inputs) + inputs * density


def norm_backward(inputs, norm_gain, norm_shift, upstream):
    _, pullback = jax.vjp(layer_norm, inputs, norm_gain, norm_shift)
    return pullback(upstream)


def adam_step(weight, moment, square, gradient, clip_scale, decays):
    gradient = gradient * clip_scale
    moment = beta_one * moment + (1 - beta_one) * gradient
    square = beta_two * square + (1 - beta_two) * gradient * gradient
    mean_hat = moment / (1 - beta_one**step_count)
    var_hat = square / (1 - beta_two**step_count)
    change = mean_hat / (jnp.sqrt(var_hat) + adam_eps)
    if decays:
        change = change + decay_rate * weight
    return (weight - learn_rate * change, moment, square)


def comm_all_gather(value, axes):
    return lax.all_gather(value, axes, axis=0, tiled=True)


def comm_scatter_sum(value, axes):
    return lax.psum_scatter(value, axes, scatter_dimension=0, tiled=True)


MESH = pl.DeviceIdType.MESH
BIG, FAST = pl.ANY, pltpu.VMEM


class Links:
    def __init__(self, sizes):
        self.sizes = dict(zip(("z", "x", "y", "c"), sizes))
        self.used = 0

    def next_id(self):
        self.used += 1
        return self.used - 1

    def count(self, axes):
        return math.prod(self.sizes[a] for a in axes)

    def place(self, axes):
        at = 0
        for a in axes:
            at = at * self.sizes[a] + lax.axis_index(a)
        return at

    def target(self, axes, flat):
        where = {}
        for a in reversed(axes):
            where[a] = lax.rem(flat, self.sizes[a])
            flat = lax.div(flat, self.sizes[a])
        return where

    def greet(self, groups):
        barrier = pltpu.get_barrier_semaphore()
        total = 0
        for axes in groups:
            size, me = self.count(axes), self.place(axes)
            for r in range(1, size):
                pl.semaphore_signal(
                    barrier,
                    inc=1,
                    device_id=self.target(axes, lax.rem(me + r, size)),
                    device_id_type=MESH,
                )
            total += size - 1
        pl.semaphore_wait(barrier, total)

    def call(self, kernel, outs, spaces, out_spaces, scratch, values, wire, name):
        result = pl.pallas_call(
            kernel,
            out_shape=outs,
            in_specs=[pl.BlockSpec(memory_space=m) for m in spaces],
            out_specs=[pl.BlockSpec(memory_space=m) for m in out_spaces],
            scratch_shapes=scratch,
            compiler_params=pltpu.CompilerParams(
                collective_id=self.next_id(),
                has_side_effects=True,
                vmem_limit_bytes=40 * 2**20,
            ),
            cost_estimate=pl.CostEstimate(flops=0, bytes_accessed=wire, transcendentals=0),
            name=name,
        )(*values)
        return result

    def exchange(self, name, *moves):
        outs, scratch = [], []
        for kind, axes, dim, _, value in moves:
            size = self.count(axes)
            shape, sends, lands = value.shape, (size - 1,), (size - 1,)
            if kind == "gather":
                shape = (size, *shape)
            elif kind == "swap":
                shape = shape[:dim] + shape[dim + 1 :]
            elif kind == "spread":
                shape = (size - 1, *shape[1:])
            elif kind == "relay":
                shape, sends = (size, *shape), (2, size - 1, shape[0])
                lands = sends
            elif kind == "plane":
                shape, sends, lands = (2, 2, 2, *shape), (7 * shape[0],), (7, shape[0])
            outs.append(jax.ShapeDtypeStruct(shape, value.dtype))
            scratch += [
                pltpu.SemaphoreType.DMA(sends),
                pltpu.SemaphoreType.DMA(lands),
                pltpu.SemaphoreType.DMA((1,)),
            ]
        spaces = [m[3] for m in moves]
        groups = []
        for kind, axes, *_ in moves:
            groups += [(a,) for a in axes] if kind == "plane" else [axes]
        groups = list(dict.fromkeys(groups))

        def kernel(*refs):
            ins, dests = refs[: len(moves)], refs[len(moves) : 2 * len(moves)]
            sems = refs[2 * len(moves) :]
            self.greet(groups)
            started, later = [], []
            for i, ((kind, axes, dim, _, _), source, dest) in enumerate(zip(moves, ins, dests)):
                sends, lands, own_sem = sems[3 * i : 3 * i + 3]
                size, me = self.count(axes), self.place(axes)
                if kind in ("relay", "plane"):
                    act = self.relay if kind == "relay" else self.plane
                    later.append(functools.partial(act, axes, source, dest, sends, lands))
                for r in range(1, size):
                    peer = lax.rem(me + r, size)
                    if kind == "gather":
                        src, dst = source, dest.at[me]
                    elif kind == "swap":
                        src, dst = source.at[(slice(None),) * dim + (peer,)], dest
                    elif kind == "spread":
                        src, dst = source.at[peer], dest.at[r - 1]
                    elif kind == "trade":
                        src, dst = source, dest
                    else:
                        continue
                    copy = pltpu.make_async_remote_copy(
                        src_ref=src,
                        dst_ref=dst,
                        send_sem=sends.at[r - 1],
                        recv_sem=lands.at[r - 1],
                        device_id=self.target(axes, peer),
                        device_id_type=MESH,
                    )
                    copy.start()
                    started.append(copy)
            runs = [act() for act in later]
            for run in runs:
                next(run)
            for i, ((kind, axes, *_), source, dest) in enumerate(zip(moves, ins, dests)):
                if kind in ("gather", "relay", "plane"):
                    at = self.place(axes)
                    if kind == "plane":
                        at = tuple(lax.axis_index(a) for a in axes)
                    copy = pltpu.make_async_copy(source, dest.at[at], sems[3 * i + 2].at[0])
                    copy.start()
                    started.append(copy)
            for run in runs:
                next(run, None)
            for copy in started:
                copy.wait()

        return self.call(
            kernel,
            outs,
            spaces,
            spaces,
            scratch,
            [m[4] for m in moves],
            sum(2 * math.prod(o.shape) * o.dtype.itemsize for o in outs),
            name,
        )

    def relay(self, axes, source, dest, sends, lands):
        (axis,) = axes
        size, parts = self.sizes[axis], source.shape[0]
        me = lax.axis_index(axis)

        def copy_of(way, hop, part):
            step = 1 if way == 0 else -1
            place = (me - step * hop, part)
            return pltpu.make_async_remote_copy(
                src_ref=source.at[part] if hop == 0 else dest.at[place],
                dst_ref=dest.at[place],
                send_sem=sends.at[way, hop, part],
                recv_sem=lands.at[way, hop, part],
                device_id={axis: me + step},
                device_id_type=MESH,
            )

        def landing(way, hop, part):
            step = 1 if way == 0 else -1
            landed = dest.at[me - step * hop, part]
            return pltpu.make_async_remote_copy(
                src_ref=landed,
                dst_ref=landed,
                send_sem=sends.at[way, hop - 1, part],
                recv_sem=lands.at[way, hop - 1, part],
                device_id={axis: me - step},
                device_id_type=MESH,
            )

        def held(way, hop):
            return me - hop >= 0 if way == 0 else me + hop <= size - 1

        def sending(way, hop):
            return held(way, hop) & (me < size - 1 if way == 0 else me > 0)

        for hop in range(size):
            for part in range(parts):
                for way in range(2):
                    if hop > 0:

                        @pl.when(held(way, hop))
                        def _():
                            landing(way, hop, part).wait_recv()

                    if hop < size - 1:

                        @pl.when(sending(way, hop))
                        def _():
                            copy_of(way, hop, part).start()

            if hop == 0:
                yield
        for hop in range(size - 1):
            for part in range(parts):
                for way in range(2):

                    @pl.when(sending(way, hop))
                    def _():
                        copy_of(way, hop, part).wait_send()

    def plane(self, axes, own, out, sends, lands):
        parts = own.shape[0]
        head = (parts + 1) // 2
        x, y, c = (lax.axis_index(a) for a in axes)
        by_x, by_y, by_c = {"x": 1 - x}, {"y": 1 - y}, {"c": 1 - c}
        started = []

        def send(src, place, part, slot, peer):
            copy = pltpu.make_async_remote_copy(
                src_ref=src,
                dst_ref=out.at[(*place, part)],
                send_sem=sends.at[len(started)],
                recv_sem=lands.at[slot, part],
                device_id=peer,
                device_id_type=MESH,
            )
            copy.start()
            started.append(copy)

        def arrived(place, part, slot):
            landed = out.at[(*place, part)]
            pltpu.make_async_remote_copy(
                src_ref=landed,
                dst_ref=landed,
                send_sem=sends.at[0],
                recv_sem=lands.at[slot, part],
                device_id=by_c,
                device_id_type=MESH,
            ).wait_recv()
            return landed

        me, at_x, at_y, at_xy = (x, y, c), (1 - x, y, c), (x, 1 - y, c), (1 - x, 1 - y, c)
        for part in range(parts):
            send(own.at[part], me, part, 0, by_x)
            send(own.at[part], me, part, 1, by_y)
        for part in range(parts):
            send(own.at[part], me, part, 3, by_c)
        yield
        for part in range(parts):
            landed = arrived(at_x, part, 0)
            if part < head:
                send(landed, at_x, part, 2, by_y)
            send(landed, at_x, part, 4, by_c)
            landed = arrived(at_y, part, 1)
            if part >= head:
                send(landed, at_y, part, 2, by_x)
            send(landed, at_y, part, 5, by_c)
        for part in range(parts):
            landed = arrived(at_xy, part, 2)
            send(landed, at_xy, part, 6, by_c)
        for slot, place in ((3, me), (4, at_x), (5, at_y), (6, at_xy)):
            for part in range(parts):
                arrived((place[0], place[1], 1 - c), part, slot)
        for copy in started:
            copy.wait_send()

    def line_move(self, value, part_rows, memory):
        parts = value.shape[0] // part_rows if value.shape[0] % part_rows == 0 else 1
        kind = "relay" if self.sizes["z"] <= 8 else "gather"
        return (kind, ("z",), 0, memory, value.reshape(parts, -1, value.shape[1]))

    def combine(self, name, value):
        pairs = [a for a in ("c", "x", "y") if self.sizes[a] > 1]
        depth = self.sizes["z"]
        steps = len(pairs)

        def kernel(x_ref, out_ref, sums, land, sends, lands):
            self.greet([(a,) for a in pairs] + [("z",)])
            me = lax.axis_index("z")
            for i, a in enumerate(pairs):
                source = x_ref if i == 0 else sums.at[i - 1]
                copy = pltpu.make_async_remote_copy(
                    src_ref=source,
                    dst_ref=land.at[i],
                    send_sem=sends.at[i],
                    recv_sem=lands.at[i],
                    device_id={a: 1 - lax.axis_index(a)},
                    device_id_type=MESH,
                )
                copy.start()
                copy.wait()
                sums[i] = source[...] + land[i]
            out_ref[me] = sums[steps - 1]
            started = []
            for r in range(1, depth):
                copy = pltpu.make_async_remote_copy(
                    src_ref=sums.at[steps - 1],
                    dst_ref=out_ref.at[me],
                    send_sem=sends.at[steps + r - 1],
                    recv_sem=lands.at[steps + r - 1],
                    device_id={"z": lax.rem(me + r, depth)},
                    device_id_type=MESH,
                )
                copy.start()
                started.append(copy)
            for copy in started:
                copy.wait()

        return self.call(
            kernel,
            [jax.ShapeDtypeStruct((depth, *value.shape), value.dtype)],
            [FAST],
            [FAST],
            [
                pltpu.VMEM((steps, *value.shape), value.dtype),
                pltpu.VMEM((steps, *value.shape), value.dtype),
                pltpu.SemaphoreType.DMA((steps + depth - 1,)),
                pltpu.SemaphoreType.DMA((steps + depth - 1,)),
            ],
            [value],
            16 * value.size * 4,
            name,
        )[0]


def row_major(value):
    return with_layout_constraint(value, Layout(major_to_minor=tuple(range(value.ndim))))


def lanes(flat):
    padded = jnp.pad(flat, (0, -flat.size % 1024))
    return padded.reshape(-1, 128)


HEAD_SCALE = math.log2(math.e) / math.sqrt(HEAD_DIM)
PAIR = 2 * HEAD_DIM
ROWS = 256


def dots(left, right, left_dim, right_dim):
    return lax.dot_general(
        left, right, (((left_dim,), (right_dim,)), ((), ())), preferred_element_type=jnp.float32
    )


def half_lanes(value, half):
    lane = lax.broadcasted_iota(jnp.int32, value.shape, 1)
    return jnp.where((lane >= HEAD_DIM) == (half == 1), value, jnp.zeros((), value.dtype))


def forward_kernel(q_ref, k0_ref, k1_ref, v0_ref, v1_ref, out_ref, norm_ref):
    keys = jnp.concatenate([k0_ref[...], k1_ref[...]], axis=0)
    values = jnp.concatenate([v0_ref[...], v1_ref[...]], axis=0)
    for start in range(0, q_ref.shape[0], ROWS):
        rows = pl.ds(start, ROWS)
        queries = q_ref[rows, :]
        halves = []
        for half in range(2):
            scores = dots(keys, half_lanes(queries, half), 1, 1)
            top = jnp.max(scores, axis=0, keepdims=True)
            powers = jnp.exp2((scores - top) * HEAD_SCALE)
            total = jnp.sum(powers, axis=0, keepdims=True)
            probs = (powers * (1.0 / total)).astype(jnp.bfloat16)
            norm_ref[0, half : half + 1, rows] = top * HEAD_SCALE + jnp.log2(total)
            mixed = dots(values, probs, 0, 0)
            halves.append(mixed[half * HEAD_DIM : (half + 1) * HEAD_DIM])
        out_ref[rows, :] = jnp.concatenate(halves, axis=0).T.astype(out_ref.dtype)


def attention_forward(queries, keys, values):
    length, width = queries.shape
    pairs = width // PAIR
    block = pl.BlockSpec((length, PAIR), lambda i: (0, i))
    flops = 8 * length * length * width
    return pl.pallas_call(
        forward_kernel,
        grid=(pairs,),
        out_shape=[
            jax.ShapeDtypeStruct((length, width), queries.dtype),
            jax.ShapeDtypeStruct((pairs, 2, length), jnp.float32),
        ],
        in_specs=[block] * 5,
        out_specs=[block, pl.BlockSpec((1, 2, length), lambda i: (i, 0, 0))],
        cost_estimate=pl.CostEstimate(
            flops=2 * flops, bytes_accessed=16 * length * width, transcendentals=flops // 256
        ),
        name="attention_forward",
    )(queries, *keys, *values)


def backward_kernel(
    q_ref, k0_ref, k1_ref, v0_ref, v1_ref, norm_ref, g_ref, dq_ref, dk0_ref, dk1_ref, dv0_ref, dv1_ref
):
    own = k0_ref.shape[0]
    keys = jnp.concatenate([k0_ref[...], k1_ref[...]], axis=0)
    values = jnp.concatenate([v0_ref[...], v1_ref[...]], axis=0)
    grad_keys = grad_values = 0.0
    for start in range(0, q_ref.shape[0], ROWS):
        rows = pl.ds(start, ROWS)
        halves = []
        for half in range(2):
            queries = half_lanes(q_ref[rows, :], half)
            upstream = half_lanes(g_ref[rows, :], half)
            scores = dots(keys, queries, 1, 1)
            probs = jnp.exp2(scores * HEAD_SCALE - norm_ref[0, half : half + 1, rows])
            grad_probs = dots(values, upstream, 1, 1)
            row_dot = jnp.sum(grad_probs * probs, axis=0, keepdims=True)
            grad_scores = (probs * (grad_probs - row_dot)).astype(jnp.bfloat16)
            grad_values = grad_values + dots(probs.astype(jnp.bfloat16), upstream, 1, 0)
            grad_keys = grad_keys + dots(grad_scores, queries, 1, 0)
            grad_queries = dots(keys, grad_scores, 0, 0)
            halves.append(grad_queries[half * HEAD_DIM : (half + 1) * HEAD_DIM])
        grad_queries = jnp.concatenate(halves, axis=0) * (1.0 / math.sqrt(HEAD_DIM))
        dq_ref[rows, :] = grad_queries.T.astype(dq_ref.dtype)
    grad_keys = grad_keys * (1.0 / math.sqrt(HEAD_DIM))
    dk0_ref[...] = grad_keys[:own]
    dk1_ref[...] = grad_keys[own:]
    dv0_ref[...] = grad_values[:own]
    dv1_ref[...] = grad_values[own:]


def attention_backward(queries, keys, values, log_norm, grad_mixed):
    length, width = queries.shape
    pairs = width // PAIR
    block = pl.BlockSpec((length, PAIR), lambda i: (0, i))
    flops = 20 * length * length * width
    wide = jax.ShapeDtypeStruct((length, width), jnp.float32)
    return pl.pallas_call(
        backward_kernel,
        grid=(pairs,),
        out_shape=[jax.ShapeDtypeStruct((length, width), queries.dtype)] + [wide] * 4,
        in_specs=[block] * 5 + [pl.BlockSpec((1, 2, length), lambda i: (i, 0, 0)), block],
        out_specs=[block] * 5,
        cost_estimate=pl.CostEstimate(
            flops=2 * flops, bytes_accessed=32 * length * width, transcendentals=flops // 640
        ),
        name="attention_backward",
    )(queries, *keys, *values, log_norm, grad_mixed)


def step(sizes, *args):
    (
        token_ids, type_ids, mask_pos, mask_valid, mlm_labels, nsp_labels,
        word_table, word_m, word_v, attn_weight, attn_m, attn_v,
        ff_weight, ff_m, ff_v, side_weight, side_m, side_v,
        vectors, vec_m, vec_v, split_bias, split_m, split_v,
        decoder_bias, decoder_m, decoder_v,
    ) = args
    z_size, x_size, y_size, c_size = sizes
    dp_size, mp_size = z_size * x_size, y_size * c_size
    z_at, x_at, y_at, c_at = (lax.axis_index(a) for a in ("z", "x", "y", "c"))
    dp_rank, mp_rank = z_at * x_size + x_at, y_at * c_size + c_at
    every = ("z", "x", "y", "c")
    mp_first = ("y", "c", "z", "x")
    plane = ("x", "y", "c")
    batch_size, length = token_ids.shape
    slots = mask_pos.shape[1]
    own_len, own_slots = length // c_size, slots // c_size
    vocab_own = word_table.shape[0]
    attn_cols, ff_cols = attn_weight.shape[2], ff_weight.shape[2]
    rows_own = attn_weight.shape[0]
    low = jnp.bfloat16
    links = Links(sizes)

    def mine(rows, size):
        row = lax.dynamic_index_in_dim(rows, y_at, 0, False)
        return lax.dynamic_slice_in_dim(row, c_at * size, size, 0)

    own_ids = mine(token_ids, own_len)
    own_types = mine(type_ids, own_len)
    seq_pos = lax.dynamic_index_in_dim(mask_pos, y_at, 0, False)
    own_pos = mine(mask_pos, own_slots)
    own_valid = mine(mask_valid, own_slots)
    own_labels = mine(mlm_labels, own_slots)
    first_core = (c_at == 0).astype(jnp.float32)

    side_rows = side_weight.shape[0] // mp_size
    side_own = lax.dynamic_slice_in_dim(side_weight, mp_rank * side_rows, side_rows, 0)
    both = jnp.concatenate([attn_weight.reshape(rows_own, 4 * attn_cols), side_own]).astype(low)
    both = comm_all_gather(both, mp_first).reshape(mp_size, dp_size, -1, D)
    attn_blocks = both[:, :, :rows_own].reshape(mp_size, D, 4 * attn_cols)
    side_full = both[:, :, rows_own:].transpose(1, 0, 2, 3).reshape(-1, D)
    ff_blocks = comm_all_gather(
        ff_weight.astype(low).reshape(rows_own, 2 * ff_cols), mp_first
    ).reshape(mp_size, D, 2 * ff_cols)
    vec_cols = vectors.shape[1]
    stripe = vocab_own * x_size
    bias_mine = lax.dynamic_slice_in_dim(decoder_bias, z_at * stripe, stripe, 0)
    int_count = own_len + 2 * own_slots
    word_parts = 4 if vocab_own % 64 == 0 else 1
    word_plane, ints, vec_parts, counts, mp_small = links.exchange(
        "word_gather",
        ("plane", plane, 0, BIG, word_table.astype(low).reshape(word_parts, -1, D)),
        ("gather", ("z",), 0, FAST, lanes(jnp.concatenate([own_ids, own_labels, own_valid]))),
        ("gather", ("z", "x"), 0, FAST, jnp.pad(vectors.astype(low), ((0, 0), (0, 128 - vec_cols)))),
        (
            "gather",
            ("z", "x"),
            0,
            FAST,
            jnp.full((8, 128), jnp.sum(mask_valid.astype(jnp.float32))),
        ),
        ("gather", ("y", "c"), 0, FAST, lanes(jnp.concatenate([bias_mine, split_bias.reshape(-1)]))),
    )
    ints = ints.reshape(z_size, -1)[:, :int_count]
    z_ids, z_labels, z_valid = (
        ints[:, :own_len],
        ints[:, own_len : own_len + own_slots],
        ints[:, own_len + own_slots :],
    )
    total_count = jnp.sum(counts[:, 0, 0])
    total_seqs = jnp.float32(batch_size * dp_size)
    vec_rows = (
        vec_parts[:, :, :vec_cols]
        .transpose(1, 0, 2)
        .reshape(vectors.shape[0], D)
        .astype(jnp.float32)
    )
    mp_small = mp_small.reshape(mp_size, -1)
    word_plane = word_plane.reshape(-1, D)
    bias_plane = (
        mp_small[:, :stripe].reshape(mp_size, x_size, vocab_own).transpose(1, 0, 2).reshape(-1)
    )
    split_full = mp_small[:, stripe : stripe + 6 * attn_cols].reshape(mp_size, 6, attn_cols)

    def plane_index(ids):
        block = ids // stripe
        offset = ids % stripe
        inside = block % z_size == z_at
        at = ((offset // vocab_own) * mp_size + block // z_size) * vocab_own + offset % vocab_own
        return inside, at

    flat_ids = z_ids.reshape(-1)
    inside, at = plane_index(flat_ids)
    looked = jnp.where(inside[:, None], word_plane[jnp.where(inside, at, 0)], jnp.zeros((), low))
    looked = looked.reshape(z_size, own_len, D)
    (found,) = links.exchange("token_spread", ("spread", ("z",), 0, BIG, looked))
    embedded = lax.dynamic_index_in_dim(looked, z_at, 0, False).astype(jnp.float32)
    embedded = embedded + jnp.sum(found.astype(jnp.float32), axis=0)
    position_rows = lax.dynamic_slice_in_dim(side_full, 2 * D + c_at * own_len, own_len, 0)
    embedded = (
        embedded
        + position_rows.astype(jnp.float32)
        + jnp.where(own_types[:, None] == 0, vec_rows[12], vec_rows[13])
    )
    hidden0 = layer_norm(embedded, vec_rows[0], vec_rows[1])
    hidden0_b = hidden0.astype(low)

    qkv_blocks = attn_blocks[:, :, : 3 * attn_cols]
    out_blocks = attn_blocks[:, :, 3 * attn_cols :]
    packed = jnp.einsum("td,mde->tme", hidden0_b, qkv_blocks, preferred_element_type=jnp.float32)
    packed = packed.reshape(own_len, mp_size, 3, attn_cols)
    queries = (packed[:, :, 0] + split_full[:, 0]).astype(low).reshape(own_len, D)
    own_keys = packed[:, :, 1].astype(low).reshape(own_len, D)
    own_values = (packed[:, :, 2] + split_full[:, 1]).astype(low).reshape(own_len, D)
    other_keys, other_values = links.exchange(
        "key_trade", ("trade", ("c",), 0, FAST, own_keys), ("trade", ("c",), 0, FAST, own_values)
    )
    keys, values = (own_keys, other_keys), (own_values, other_values)
    mixed, log_norm = attention_forward(queries, keys, values)
    attn_out = jnp.einsum(
        "tme,mde->td",
        mixed.reshape(own_len, mp_size, attn_cols),
        out_blocks,
        preferred_element_type=jnp.float32,
    )
    resid1 = hidden0 + (attn_out + vec_rows[2])
    hidden1 = layer_norm(resid1, vec_rows[3], vec_rows[4])
    hidden1_b = hidden1.astype(low)
    ff_bias = split_full[:, 2:6].transpose(0, 2, 1).reshape(mp_size, ff_cols)
    ff_in, ff_out = ff_blocks[:, :, :ff_cols], ff_blocks[:, :, ff_cols:]
    upward = jnp.einsum("td,mdf->mtf", hidden1_b, ff_in, preferred_element_type=jnp.float32)
    upward = upward + ff_bias[:, None]
    active = gelu_exact(upward).astype(low)
    ffn_out = jnp.einsum("mtf,mdf->td", active, ff_out, preferred_element_type=jnp.float32)
    resid2 = hidden1 + (ffn_out + vec_rows[5])
    hidden2 = layer_norm(resid2, vec_rows[6], vec_rows[7])

    hidden2_b = hidden2.astype(low)
    (other_h2,) = links.exchange("hidden_trade", ("trade", ("c",), 0, FAST, hidden2_b))
    picked_b = jnp.concatenate([hidden2_b, other_h2])[
        own_pos % own_len + jnp.where(own_pos // own_len == c_at, 0, own_len)
    ]
    dense_w = side_full[D : 2 * D]
    dense_out = jnp.dot(picked_b, dense_w, preferred_element_type=jnp.float32) + vec_rows[8]
    act_dense = gelu_exact(dense_out)
    head_rows = layer_norm(act_dense, vec_rows[9], vec_rows[10])
    (head_b,) = links.exchange("head_gather", links.line_move(head_rows.astype(low), 32, FAST))
    head_b = head_b.reshape(-1, D)
    row_count = head_b.shape[0]
    logits = (
        jnp.einsum("rd,vd->rv", head_b, word_plane, preferred_element_type=jnp.float32)
        + bias_plane
    )
    label_in, label_at = plane_index(z_labels.reshape(-1))
    label_at = jnp.where(label_in, label_at, -1)
    hit_rows = label_at[:, None] == lax.broadcasted_iota(jnp.int32, logits.shape, 1)
    row_top = jnp.max(logits, axis=1)
    row_total = jnp.sum(jnp.exp(logits - row_top[:, None]), axis=1)
    row_target = jnp.sum(jnp.where(hit_rows, logits, 0.0), axis=1)
    stats = jnp.pad(jnp.stack([row_top, row_total, row_target]), ((0, 5), (0, 0)))
    (stats,) = links.exchange("stat_gather", ("gather", ("z",), 0, FAST, stats))
    top_all = jnp.max(stats[:, 0], axis=0)
    total_all = jnp.sum(stats[:, 1] * jnp.exp(stats[:, 0] - top_all), axis=0)
    target_all = jnp.sum(stats[:, 2], axis=0)
    log_total = top_all + jnp.log(total_all)
    valid_rows = z_valid.reshape(-1).astype(jnp.float32)
    mlm_sum = -jnp.sum(valid_rows * (target_all - log_total))
    weight_rows = valid_rows / total_count
    grad_logits = (
        (jnp.exp(logits - log_total[:, None]) - hit_rows.astype(jnp.float32)) * weight_rows[:, None]
    ).astype(low)
    decoder_part = jnp.sum(grad_logits.astype(jnp.float32), axis=0)
    head_part = jnp.dot(grad_logits, word_plane, preferred_element_type=jnp.float32)
    head_part = head_part.reshape(z_size, own_slots, D)
    (head_others,) = links.exchange("head_spread", ("spread", ("z",), 0, FAST, head_part.astype(low)))
    grad_head = lax.dynamic_index_in_dim(head_part, z_at, 0, False) + jnp.sum(
        head_others.astype(jnp.float32), axis=0
    )
    grad_act, grad_g9, grad_s9 = norm_backward(act_dense, vec_rows[9], vec_rows[10], grad_head)
    grad_dense = (grad_act * gelu_slope(dense_out)).astype(low)
    dense_bias_grad = jnp.sum(grad_dense.astype(jnp.float32), axis=0)
    dense_grad = jnp.einsum("rd,re->de", picked_b, grad_dense, preferred_element_type=jnp.float32)
    grad_picked = jnp.einsum("re,de->rd", grad_dense, dense_w, preferred_element_type=jnp.float32)
    (other_picked,) = links.exchange("picked_trade", ("trade", ("c",), 0, FAST, grad_picked))
    seq_picked = jnp.concatenate([grad_picked, other_picked])
    other_pos = lax.dynamic_slice_in_dim(seq_pos, (1 - c_at) * own_slots, own_slots, 0)
    place = (
        jnp.concatenate([own_pos, other_pos])[None, :]
        == c_at * own_len + lax.broadcasted_iota(jnp.int32, (own_len, slots), 0)
    ).astype(jnp.float32)
    grad_top = jnp.dot(place, seq_picked, precision=highest)

    cls_row = hidden2_b[0:1]
    pooler_w = side_full[:D]
    pooled = jnp.tanh(jnp.dot(cls_row, pooler_w, preferred_element_type=jnp.float32) + vec_rows[11])
    classes = vec_rows[14:16]
    nsp_logp = jax.nn.log_softmax(jnp.dot(pooled, classes.T, precision=highest), axis=-1)
    own_nsp = lax.dynamic_slice_in_dim(nsp_labels, y_at, 1, 0)
    pick_nsp = own_nsp[:, None] == lax.broadcasted_iota(jnp.int32, (1, 2), 1)
    nsp_sum = -jnp.sum(jnp.where(pick_nsp, nsp_logp, 0.0)) * first_core
    grad_nsp = (jnp.exp(nsp_logp) - pick_nsp.astype(jnp.float32)) / total_seqs * first_core
    class_grad = grad_nsp[0][:, None] * pooled
    grad_pre = jnp.dot(grad_nsp, classes, precision=highest) * (1.0 - pooled * pooled)
    pooler_bias_grad = grad_pre[0]
    pooler_grad = cls_row.astype(jnp.float32).T * grad_pre
    grad_cls = jnp.dot(grad_pre, pooler_w.astype(jnp.float32).T, precision=highest)
    first_row = lax.broadcasted_iota(jnp.int32, (own_len, 1), 0) == 0
    grad_top = grad_top + jnp.where(first_row, grad_cls, 0.0)

    grad_r2, grad_g2, grad_s2 = norm_backward(resid2, vec_rows[6], vec_rows[7], grad_top)
    ffn_grad_b = grad_r2.astype(low)
    out_bias_two = jnp.sum(ffn_grad_b.astype(jnp.float32), axis=0)
    ff_out_grad = jnp.einsum("td,mtf->mdf", ffn_grad_b, active, preferred_element_type=jnp.float32)
    grad_active = jnp.einsum("td,mdf->mtf", ffn_grad_b, ff_out, preferred_element_type=jnp.float32)
    grad_up = (grad_active * gelu_slope(upward)).astype(low)
    ff_bias_grad = jnp.sum(grad_up.astype(jnp.float32), axis=1)
    ff_in_grad = jnp.einsum("td,mtf->mdf", hidden1_b, grad_up, preferred_element_type=jnp.float32)
    hidden1_part = jnp.einsum("mtf,mdf->td", grad_up, ff_in, preferred_element_type=jnp.float32)
    ff_grad = jnp.stack(
        [
            row_major(g.astype(low)).reshape(mp_size * dp_size, rows_own, ff_cols)
            for g in (ff_in_grad, ff_out_grad)
        ],
        axis=1,
    )
    ff_grad, hidden1_part = lax.optimization_barrier((ff_grad, hidden1_part))
    ff_red = comm_scatter_sum(ff_grad.reshape(-1, ff_cols), mp_first)
    grad_h1 = grad_r2 + hidden1_part
    grad_r1, grad_g1, grad_s1 = norm_backward(resid1, vec_rows[3], vec_rows[4], grad_h1)
    attn_grad_b = grad_r1.astype(low)
    out_bias_one = jnp.sum(attn_grad_b.astype(jnp.float32), axis=0)
    mixed_blocks = mixed.reshape(own_len, mp_size, attn_cols)
    attn_grad_out = jnp.einsum(
        "td,tme->mde", attn_grad_b, mixed_blocks, preferred_element_type=jnp.float32
    )
    grad_mixed = jnp.einsum(
        "td,mde->tme", attn_grad_b, out_blocks, preferred_element_type=jnp.float32
    )
    grad_mixed = grad_mixed.astype(low).reshape(own_len, D)
    grad_q, own_k, part_k, own_v, part_v = attention_backward(
        queries, keys, values, log_norm, grad_mixed
    )
    from_k, from_v = links.exchange(
        "key_grad_trade",
        ("trade", ("c",), 0, FAST, part_k),
        ("trade", ("c",), 0, FAST, part_v),
    )
    grad_k = (own_k + from_k).astype(low)
    grad_v = (own_v + from_v).astype(low)
    grad_packed = jnp.stack(
        [
            grad_q.reshape(own_len, mp_size, attn_cols),
            grad_k.reshape(own_len, mp_size, attn_cols),
            grad_v.reshape(own_len, mp_size, attn_cols),
        ],
        axis=2,
    ).reshape(own_len, mp_size, 3 * attn_cols)
    attn_grad_in = jnp.einsum(
        "td,tme->mde", hidden0_b, grad_packed, preferred_element_type=jnp.float32
    )
    packed_sums = jnp.sum(grad_packed.astype(jnp.float32), axis=0).reshape(mp_size, 3, attn_cols)
    hidden0_part = jnp.einsum(
        "tme,mde->td", grad_packed, qkv_blocks, preferred_element_type=jnp.float32
    )
    attn_grad = jnp.concatenate([attn_grad_in, attn_grad_out], axis=2).astype(low)
    attn_grad = attn_grad.reshape(y_size, c_size, z_size, x_size, rows_own, 4 * attn_cols)
    grad_h0 = grad_r1 + hidden0_part
    grad_x0, grad_g0, grad_s0 = norm_backward(embedded, vec_rows[0], vec_rows[1], grad_h0)

    position_grad = lax.dynamic_update_slice_in_dim(
        jnp.zeros((length, D), low), grad_x0.astype(low), c_at * own_len, 0
    )
    side_grad = jnp.concatenate([pooler_grad.astype(low), dense_grad.astype(low), position_grad], axis=0)
    side_grad = side_grad.reshape(z_size, x_size, y_size, c_size, side_rows, D)

    def joined(value, at, dim, received):
        kept = lax.dynamic_index_in_dim(value, at, dim, False)
        return (kept.astype(jnp.float32) + received.astype(jnp.float32)).astype(low)

    x0_b = grad_x0.astype(low)
    cut_one, cut_two = own_len // 8, 5 * own_len // 8
    from_a, from_s, x0_one = links.exchange(
        "grad_swap_c",
        ("swap", ("c",), 1, BIG, attn_grad),
        ("swap", ("c",), 3, BIG, side_grad),
        links.line_move(x0_b[:cut_one], 64, BIG),
    )
    attn_grad, side_grad = joined(attn_grad, c_at, 1, from_a), joined(side_grad, c_at, 3, from_s)
    from_a, from_s, x0_two = links.exchange(
        "grad_swap_xy",
        ("swap", ("x",), 2, BIG, attn_grad),
        ("swap", ("y",), 2, BIG, side_grad),
        links.line_move(x0_b[cut_one:cut_two], 64, BIG),
    )
    attn_grad, side_grad = joined(attn_grad, x_at, 2, from_a), joined(side_grad, y_at, 2, from_s)
    from_a, from_s, x0_three = links.exchange(
        "grad_swap_yx",
        ("swap", ("y",), 0, BIG, attn_grad),
        ("swap", ("x",), 1, BIG, side_grad),
        links.line_move(x0_b[cut_two:], 64, BIG),
    )
    attn_grad, side_grad = joined(attn_grad, y_at, 0, from_a), joined(side_grad, x_at, 1, from_s)

    ff_red, x0_three = lax.optimization_barrier((ff_red, x0_three))
    all_x0 = [x.reshape(z_size, -1, D) for x in (x0_one, x0_two, x0_three)]
    all_x0 = jnp.concatenate(all_x0, axis=1).reshape(-1, D)
    onehot = (
        jnp.where(inside, at, -1)[None, :]
        == lax.broadcasted_iota(jnp.int32, (word_plane.shape[0], flat_ids.shape[0]), 0)
    ).astype(low)
    word_grad = jnp.einsum("rv,rd->vd", grad_logits, head_b, preferred_element_type=jnp.float32)
    word_grad = word_grad + jnp.dot(onehot, all_x0, preferred_element_type=jnp.float32)
    word_grad, attn_grad, side_grad = lax.optimization_barrier(
        (word_grad.astype(low), attn_grad, side_grad)
    )
    word_red = comm_scatter_sum(word_grad, plane).astype(jnp.float32)
    from_a, from_s = links.exchange(
        "grad_spread_z", ("spread", ("z",), 0, BIG, attn_grad), ("spread", ("z",), 0, BIG, side_grad)
    )

    def total(value, received):
        kept = lax.dynamic_index_in_dim(value, z_at, 0, False).astype(jnp.float32)
        return kept + jnp.sum(received.astype(jnp.float32), axis=0)

    attn_red, side_quarter = total(attn_grad, from_a), total(side_grad, from_s)
    type_zero = jnp.sum(jnp.where(own_types[:, None] == 0, grad_x0, 0.0), axis=0)
    type_one = jnp.sum(jnp.where(own_types[:, None] == 1, grad_x0, 0.0), axis=0)
    vec_grad = jnp.stack(
        [
            grad_g0, grad_s0, out_bias_one, grad_g1, grad_s1, out_bias_two, grad_g2, grad_s2,
            dense_bias_grad, grad_g9, grad_s9, pooler_bias_grad, type_zero, type_one,
            class_grad[0], class_grad[1],
        ],
        axis=0,
    )
    split_grad = jnp.concatenate(
        [
            packed_sums[:, 0:1],
            packed_sums[:, 2:3],
            ff_bias_grad.reshape(mp_size, attn_cols, 4).transpose(0, 2, 1),
        ],
        axis=1,
    )
    late = lanes(jnp.concatenate([vec_grad.reshape(-1), split_grad.reshape(-1), decoder_part]))
    late, side_quarter = lax.optimization_barrier((late, side_quarter))
    small = links.combine(
        "small_sum",
        late,
    ).reshape(z_size, -1)
    (side_red,) = links.exchange(
        "side_gather", ("gather", ("y", "c"), 0, FAST, side_quarter.astype(low))
    )
    side_red = side_red.reshape(side_weight.shape).astype(jnp.float32)
    narrow = vec_grad.size + split_grad.size
    summed = jnp.sum(small[:, :narrow], axis=0)
    vec_all = summed[: vec_grad.size].reshape(vec_grad.shape)
    split_all = summed[vec_grad.size :].reshape(split_grad.shape)
    vec_red = lax.dynamic_slice_in_dim(vec_all, dp_rank * vec_cols, vec_cols, 1)
    split_red = lax.dynamic_index_in_dim(split_all, mp_rank, 0, False)
    decoder_red = lax.dynamic_index_in_dim(
        small[:, narrow : narrow + decoder_part.size].reshape(z_size, x_size, mp_size, vocab_own),
        mp_rank,
        2,
        False,
    ).reshape(-1)
    word_f, attn_f, ff_f = (
        word_red,
        attn_red.reshape(attn_weight.shape),
        row_major(
            ff_red.astype(jnp.float32).reshape(2, rows_own, ff_cols).transpose(1, 0, 2)
        ),
    )
    own_square = (
        jnp.sum(word_f * word_f)
        + jnp.sum(attn_f * attn_f)
        + jnp.sum(ff_f * ff_f)
        + jnp.sum(side_red * side_red) / mp_size
        + jnp.sum(vec_red * vec_red) / mp_size
        + (jnp.sum(split_red * split_red) + jnp.sum(decoder_red * decoder_red)) / dp_size
    )
    loss_part = mlm_sum / total_count / z_size + nsp_sum / total_seqs
    ends = jnp.where(
        lax.broadcasted_iota(jnp.int32, (8, 128), 0) == 0, own_square, loss_part
    )
    ends = jnp.sum(links.combine("norm_sum", ends), axis=0)
    grad_square, total_loss = ends[0, 0], ends[1, 0]
    grad_norm = jnp.sqrt(grad_square)
    clip_scale = max_norm / jnp.maximum(grad_norm, max_norm)
    return (
        total_loss,
        grad_norm,
        *adam_step(word_table, word_m, word_v, word_f, clip_scale, True),
        *adam_step(attn_weight, attn_m, attn_v, attn_f, clip_scale, True),
        *adam_step(ff_weight, ff_m, ff_v, ff_f, clip_scale, True),
        *adam_step(side_weight, side_m, side_v, side_red, clip_scale, True),
        *adam_step(vectors, vec_m, vec_v, vec_red, clip_scale, False),
        *adam_step(split_bias, split_m, split_v, split_red, clip_scale, False),
        *adam_step(decoder_bias, decoder_m, decoder_v, decoder_red, clip_scale, False),
    )


def solution(mesh):
    dp_size, mp_size = mesh.shape["dp"], mesh.shape["mp"]
    x_size = 2 if dp_size % 2 == 0 else 1
    c_size = 2 if mp_size % 2 == 0 else 1
    sizes = (dp_size // x_size, x_size, mp_size // c_size, c_size)
    fine = Mesh(mesh.devices.reshape(sizes), ("z", "x", "y", "c"))
    dp, mp = ("z", "x"), ("y", "c")
    word = P(("y", "c", "z", "x"), None)
    cube = P(dp, None, mp)
    kinds = (
        [P(dp, None)] * 5
        + [P(dp)]
        + [word] * 3
        + [cube] * 6
        + [P(dp, None)] * 3
        + [P(None, dp)] * 3
        + [P(None, mp)] * 3
        + [P(mp)] * 3
    )
    return jax.shard_map(
        functools.partial(step, sizes),
        mesh=fine,
        in_specs=tuple(kinds),
        out_specs=(P(), P(), *kinds[6:]),
        check_vma=False,
    )
```

```python
import functools
import math

import jax
import jax.numpy as jnp
from jax import lax
from jax.experimental.layout import Layout, with_layout_constraint
from jax.experimental import pallas as pl
from jax.experimental.pallas import tpu as pltpu
from jax.sharding import Mesh, PartitionSpec as P

D = 768
HEAD_DIM = 64


beta_one = 0.9
beta_two = 0.999
adam_eps = 1e-06
learn_rate = 0.2
decay_rate = 0.01
step_count = 10
max_norm = 0.05
norm_eps = 1e-12
highest = lax.Precision.HIGHEST


def layer_norm(inputs, norm_gain, norm_shift):
    center = inputs - jnp.mean(inputs, axis=-1, keepdims=True)
    spread = jnp.mean(center * center, axis=-1, keepdims=True)
    return center * lax.rsqrt(spread + norm_eps) * norm_gain + norm_shift


def normal_cdf(inputs):
    return 0.5 + 0.5 * lax.erf(inputs * math.sqrt(0.5))


def gelu_exact(inputs):
    return inputs * normal_cdf(inputs)


def gelu_slope(inputs):
    density = jnp.exp(-0.5 * inputs * inputs) * (1.0 / math.sqrt(2.0 * math.pi))
    return normal_cdf(inputs) + inputs * density


def norm_backward(inputs, norm_gain, norm_shift, upstream):
    _, pullback = jax.vjp(layer_norm, inputs, norm_gain, norm_shift)
    return pullback(upstream)


def adam_step(weight, moment, square, gradient, clip_scale, decays):
    gradient = gradient * clip_scale
    moment = beta_one * moment + (1 - beta_one) * gradient
    square = beta_two * square + (1 - beta_two) * gradient * gradient
    mean_hat = moment / (1 - beta_one**step_count)
    var_hat = square / (1 - beta_two**step_count)
    change = mean_hat / (jnp.sqrt(var_hat) + adam_eps)
    if decays:
        change = change + decay_rate * weight
    return (weight - learn_rate * change, moment, square)


def comm_all_gather(value, axes):
    return lax.all_gather(value, axes, axis=0, tiled=True)


def comm_scatter_sum(value, axes):
    return lax.psum_scatter(value, axes, scatter_dimension=0, tiled=True)


MESH = pl.DeviceIdType.MESH
BIG, FAST = pl.ANY, pltpu.VMEM


class Links:
    def __init__(self, sizes):
        self.sizes = dict(zip(("z", "x", "y", "c"), sizes))
        self.used = 0

    def next_id(self):
        self.used += 1
        return self.used - 1

    def count(self, axes):
        return math.prod(self.sizes[a] for a in axes)

    def place(self, axes):
        at = 0
        for a in axes:
            at = at * self.sizes[a] + lax.axis_index(a)
        return at

    def target(self, axes, flat):
        where = {}
        for a in reversed(axes):
            where[a] = lax.rem(flat, self.sizes[a])
            flat = lax.div(flat, self.sizes[a])
        return where

    def greet(self, groups):
        barrier = pltpu.get_barrier_semaphore()
        total = 0
        for axes in groups:
            size, me = self.count(axes), self.place(axes)
            for r in range(1, size):
                pl.semaphore_signal(
                    barrier,
                    inc=1,
                    device_id=self.target(axes, lax.rem(me + r, size)),
                    device_id_type=MESH,
                )
            total += size - 1
        pl.semaphore_wait(barrier, total)

    def call(self, kernel, outs, spaces, out_spaces, scratch, values, wire, name):
        result = pl.pallas_call(
            kernel,
            out_shape=outs,
            in_specs=[pl.BlockSpec(memory_space=m) for m in spaces],
            out_specs=[pl.BlockSpec(memory_space=m) for m in out_spaces],
            scratch_shapes=scratch,
            compiler_params=pltpu.CompilerParams(
                collective_id=self.next_id(),
                has_side_effects=True,
                vmem_limit_bytes=40 * 2**20,
            ),
            cost_estimate=pl.CostEstimate(flops=0, bytes_accessed=wire, transcendentals=0),
            name=name,
        )(*values)
        return result

    def exchange(self, name, *moves):
        outs, scratch = [], []
        for kind, axes, dim, _, value in moves:
            size = self.count(axes)
            shape, sends, lands = value.shape, (size - 1,), (size - 1,)
            if kind == "gather":
                shape = (size, *shape)
            elif kind == "swap":
                shape = shape[:dim] + shape[dim + 1 :]
            elif kind == "spread":
                shape = (size - 1, *shape[1:])
            elif kind == "relay":
                shape, sends = (size, *shape), (2, size - 1, shape[0])
                lands = sends
            elif kind == "plane":
                shape, sends, lands = (2, 2, 2, *shape), (7 * shape[0],), (7, shape[0])
            outs.append(jax.ShapeDtypeStruct(shape, value.dtype))
            scratch += [
                pltpu.SemaphoreType.DMA(sends),
                pltpu.SemaphoreType.DMA(lands),
                pltpu.SemaphoreType.DMA((1,)),
            ]
        spaces = [m[3] for m in moves]
        groups = []
        for kind, axes, *_ in moves:
            groups += [(a,) for a in axes] if kind == "plane" else [axes]
        groups = list(dict.fromkeys(groups))

        def kernel(*refs):
            ins, dests = refs[: len(moves)], refs[len(moves) : 2 * len(moves)]
            sems = refs[2 * len(moves) :]
            self.greet(groups)
            started, later = [], []
            for i, ((kind, axes, dim, _, _), source, dest) in enumerate(zip(moves, ins, dests)):
                sends, lands, own_sem = sems[3 * i : 3 * i + 3]
                size, me = self.count(axes), self.place(axes)
                if kind in ("relay", "plane"):
                    act = self.relay if kind == "relay" else self.plane
                    later.append(functools.partial(act, axes, source, dest, sends, lands))
                for r in range(1, size):
                    peer = lax.rem(me + r, size)
                    if kind == "gather":
                        src, dst = source, dest.at[me]
                    elif kind == "swap":
                        src, dst = source.at[(slice(None),) * dim + (peer,)], dest
                    elif kind == "spread":
                        src, dst = source.at[peer], dest.at[r - 1]
                    elif kind == "trade":
                        src, dst = source, dest
                    else:
                        continue
                    copy = pltpu.make_async_remote_copy(
                        src_ref=src,
                        dst_ref=dst,
                        send_sem=sends.at[r - 1],
                        recv_sem=lands.at[r - 1],
                        device_id=self.target(axes, peer),
                        device_id_type=MESH,
                    )
                    copy.start()
                    started.append(copy)
            runs = [act() for act in later]
            for run in runs:
                next(run)
            for i, ((kind, axes, *_), source, dest) in enumerate(zip(moves, ins, dests)):
                if kind in ("gather", "relay", "plane"):
                    at = self.place(axes)
                    if kind == "plane":
                        at = tuple(lax.axis_index(a) for a in axes)
                    copy = pltpu.make_async_copy(source, dest.at[at], sems[3 * i + 2].at[0])
                    copy.start()
                    started.append(copy)
            for run in runs:
                next(run, None)
            for copy in started:
                copy.wait()

        return self.call(
            kernel,
            outs,
            spaces,
            spaces,
            scratch,
            [m[4] for m in moves],
            sum(2 * math.prod(o.shape) * o.dtype.itemsize for o in outs),
            name,
        )

    def relay(self, axes, source, dest, sends, lands):
        (axis,) = axes
        size, parts = self.sizes[axis], source.shape[0]
        me = lax.axis_index(axis)

        def copy_of(way, hop, part):
            step = 1 if way == 0 else -1
            place = (me - step * hop, part)
            return pltpu.make_async_remote_copy(
                src_ref=source.at[part] if hop == 0 else dest.at[place],
                dst_ref=dest.at[place],
                send_sem=sends.at[way, hop, part],
                recv_sem=lands.at[way, hop, part],
                device_id={axis: me + step},
                device_id_type=MESH,
            )

        def landing(way, hop, part):
            step = 1 if way == 0 else -1
            landed = dest.at[me - step * hop, part]
            return pltpu.make_async_remote_copy(
                src_ref=landed,
                dst_ref=landed,
                send_sem=sends.at[way, hop - 1, part],
                recv_sem=lands.at[way, hop - 1, part],
                device_id={axis: me - step},
                device_id_type=MESH,
            )

        def held(way, hop):
            return me - hop >= 0 if way == 0 else me + hop <= size - 1

        def sending(way, hop):
            return held(way, hop) & (me < size - 1 if way == 0 else me > 0)

        for hop in range(size):
            for part in range(parts):
                for way in range(2):
                    if hop > 0:

                        @pl.when(held(way, hop))
                        def _():
                            landing(way, hop, part).wait_recv()

                    if hop < size - 1:

                        @pl.when(sending(way, hop))
                        def _():
                            copy_of(way, hop, part).start()

            if hop == 0:
                yield
        for hop in range(size - 1):
            for part in range(parts):
                for way in range(2):

                    @pl.when(sending(way, hop))
                    def _():
                        copy_of(way, hop, part).wait_send()

    def plane(self, axes, own, out, sends, lands):
        parts = own.shape[0]
        head = (parts + 1) // 2
        x, y, c = (lax.axis_index(a) for a in axes)
        by_x, by_y, by_c = {"x": 1 - x}, {"y": 1 - y}, {"c": 1 - c}
        started = []

        def send(src, place, part, slot, peer):
            copy = pltpu.make_async_remote_copy(
                src_ref=src,
                dst_ref=out.at[(*place, part)],
                send_sem=sends.at[len(started)],
                recv_sem=lands.at[slot, part],
                device_id=peer,
                device_id_type=MESH,
            )
            copy.start()
            started.append(copy)

        def arrived(place, part, slot):
            landed = out.at[(*place, part)]
            pltpu.make_async_remote_copy(
                src_ref=landed,
                dst_ref=landed,
                send_sem=sends.at[0],
                recv_sem=lands.at[slot, part],
                device_id=by_c,
                device_id_type=MESH,
            ).wait_recv()
            return landed

        me, at_x, at_y, at_xy = (x, y, c), (1 - x, y, c), (x, 1 - y, c), (1 - x, 1 - y, c)
        for part in range(parts):
            send(own.at[part], me, part, 0, by_x)
            send(own.at[part], me, part, 1, by_y)
        for part in range(parts):
            send(own.at[part], me, part, 3, by_c)
        yield
        for part in range(parts):
            landed = arrived(at_x, part, 0)
            if part < head:
                send(landed, at_x, part, 2, by_y)
            send(landed, at_x, part, 4, by_c)
            landed = arrived(at_y, part, 1)
            if part >= head:
                send(landed, at_y, part, 2, by_x)
            send(landed, at_y, part, 5, by_c)
        for part in range(parts):
            landed = arrived(at_xy, part, 2)
            send(landed, at_xy, part, 6, by_c)
        for slot, place in ((3, me), (4, at_x), (5, at_y), (6, at_xy)):
            for part in range(parts):
                arrived((place[0], place[1], 1 - c), part, slot)
        for copy in started:
            copy.wait_send()

    def fold(self, name, value):
        size, parts = value.shape[:2]
        block = value.shape[1:]

        def kernel(source, out, land, sends, lands):
            self.greet([("z",)])
            me = lax.axis_index("z")

            def beyond(way, hop):
                return me + hop <= size - 1 if way == 0 else me - hop >= 0

            def behind(way):
                return me > 0 if way == 0 else me < size - 1

            def copy_of(way, hop, part, src):
                return pltpu.make_async_remote_copy(
                    src_ref=src,
                    dst_ref=land.at[way, hop - 1, part],
                    send_sem=sends.at[way, hop - 1, part],
                    recv_sem=lands.at[way, hop - 1, part],
                    device_id={"z": me + (1 if way == 0 else -1)},
                    device_id_type=MESH,
                )

            def landing(way, hop, part):
                landed = land.at[way, hop, part]
                return pltpu.make_async_remote_copy(
                    src_ref=landed,
                    dst_ref=landed,
                    send_sem=sends.at[way, hop, part],
                    recv_sem=lands.at[way, hop, part],
                    device_id={"z": me - (1 if way == 0 else -1)},
                    device_id_type=MESH,
                )

            for hop in range(size - 1, 0, -1):
                for part in range(parts):
                    for way in range(2):
                        goal = me + hop if way == 0 else me - hop

                        @pl.when(beyond(way, hop) & jnp.logical_not(behind(way)))
                        def _():
                            copy_of(way, hop, part, source.at[goal, part]).start()

                        if hop < size - 1:

                            @pl.when(beyond(way, hop) & behind(way))
                            def _():
                                landing(way, hop, part).wait_recv()
                                land[way, hop, part] += source[goal, part]
                                copy_of(way, hop, part, land.at[way, hop, part]).start()

            for part in range(parts):
                out[part] = source[me, part]
                for way in range(2):

                    @pl.when(behind(way))
                    def _():
                        landing(way, 0, part).wait_recv()
                        out[part] += land[way, 0, part]

            for hop in range(size - 1, 0, -1):
                for part in range(parts):
                    for way in range(2):

                        @pl.when(beyond(way, hop))
                        def _():
                            copy_of(way, hop, part, source.at[0, part]).wait_send()

        return self.call(
            kernel,
            [jax.ShapeDtypeStruct(block, value.dtype)],
            [FAST],
            [FAST],
            [
                pltpu.VMEM((2, size - 1, *block), value.dtype),
                pltpu.SemaphoreType.DMA((2, size - 1, parts)),
                pltpu.SemaphoreType.DMA((2, size - 1, parts)),
            ],
            [value],
            4 * value.size,
            name,
        )[0]

    def line_move(self, value, part_rows, memory):
        parts = value.shape[0] // part_rows if value.shape[0] % part_rows == 0 else 1
        kind = "relay" if self.sizes["z"] <= 8 else "gather"
        return (kind, ("z",), 0, memory, value.reshape(parts, -1, value.shape[1]))

    def combine(self, name, value):
        pairs = [a for a in ("c", "x", "y") if self.sizes[a] > 1]
        depth = self.sizes["z"]
        steps = len(pairs)

        def kernel(x_ref, out_ref, sums, land, sends, lands):
            self.greet([(a,) for a in pairs] + [("z",)])
            me = lax.axis_index("z")
            for i, a in enumerate(pairs):
                source = x_ref if i == 0 else sums.at[i - 1]
                copy = pltpu.make_async_remote_copy(
                    src_ref=source,
                    dst_ref=land.at[i],
                    send_sem=sends.at[i],
                    recv_sem=lands.at[i],
                    device_id={a: 1 - lax.axis_index(a)},
                    device_id_type=MESH,
                )
                copy.start()
                copy.wait()
                sums[i] = source[...] + land[i]
            out_ref[me] = sums[steps - 1]
            started = []
            for r in range(1, depth):
                copy = pltpu.make_async_remote_copy(
                    src_ref=sums.at[steps - 1],
                    dst_ref=out_ref.at[me],
                    send_sem=sends.at[steps + r - 1],
                    recv_sem=lands.at[steps + r - 1],
                    device_id={"z": lax.rem(me + r, depth)},
                    device_id_type=MESH,
                )
                copy.start()
                started.append(copy)
            for copy in started:
                copy.wait()

        return self.call(
            kernel,
            [jax.ShapeDtypeStruct((depth, *value.shape), value.dtype)],
            [FAST],
            [FAST],
            [
                pltpu.VMEM((steps, *value.shape), value.dtype),
                pltpu.VMEM((steps, *value.shape), value.dtype),
                pltpu.SemaphoreType.DMA((steps + depth - 1,)),
                pltpu.SemaphoreType.DMA((steps + depth - 1,)),
            ],
            [value],
            16 * value.size * 4,
            name,
        )[0]


def row_major(value):
    return with_layout_constraint(value, Layout(major_to_minor=tuple(range(value.ndim))))


def lanes(flat):
    padded = jnp.pad(flat, (0, -flat.size % 1024))
    return padded.reshape(-1, 128)


HEAD_SCALE = math.log2(math.e) / math.sqrt(HEAD_DIM)
PAIR = 2 * HEAD_DIM
ROWS = 256


def dots(left, right, left_dim, right_dim):
    return lax.dot_general(
        left, right, (((left_dim,), (right_dim,)), ((), ())), preferred_element_type=jnp.float32
    )


def half_lanes(value, half):
    lane = lax.broadcasted_iota(jnp.int32, value.shape, 1)
    return jnp.where((lane >= HEAD_DIM) == (half == 1), value, jnp.zeros((), value.dtype))


def forward_kernel(q_ref, k0_ref, k1_ref, v0_ref, v1_ref, out_ref, norm_ref):
    keys = jnp.concatenate([k0_ref[...], k1_ref[...]], axis=0)
    values = jnp.concatenate([v0_ref[...], v1_ref[...]], axis=0)
    for start in range(0, q_ref.shape[0], ROWS):
        rows = pl.ds(start, ROWS)
        queries = q_ref[rows, :]
        halves = []
        for half in range(2):
            scores = dots(keys, half_lanes(queries, half), 1, 1)
            top = jnp.max(scores, axis=0, keepdims=True)
            powers = jnp.exp2((scores - top) * HEAD_SCALE)
            total = jnp.sum(powers, axis=0, keepdims=True)
            probs = (powers * (1.0 / total)).astype(jnp.bfloat16)
            norm_ref[0, half : half + 1, rows] = top * HEAD_SCALE + jnp.log2(total)
            mixed = dots(values, probs, 0, 0)
            halves.append(mixed[half * HEAD_DIM : (half + 1) * HEAD_DIM])
        out_ref[rows, :] = jnp.concatenate(halves, axis=0).T.astype(out_ref.dtype)


def attention_forward(queries, keys, values):
    length, width = queries.shape
    pairs = width // PAIR
    block = pl.BlockSpec((length, PAIR), lambda i: (0, i))
    flops = 8 * length * length * width
    return pl.pallas_call(
        forward_kernel,
        grid=(pairs,),
        out_shape=[
            jax.ShapeDtypeStruct((length, width), queries.dtype),
            jax.ShapeDtypeStruct((pairs, 2, length), jnp.float32),
        ],
        in_specs=[block] * 5,
        out_specs=[block, pl.BlockSpec((1, 2, length), lambda i: (i, 0, 0))],
        cost_estimate=pl.CostEstimate(
            flops=2 * flops, bytes_accessed=16 * length * width, transcendentals=flops // 256
        ),
        name="attention_forward",
    )(queries, *keys, *values)


def backward_kernel(
    q_ref, k0_ref, k1_ref, v0_ref, v1_ref, norm_ref, g_ref, dq_ref, dk0_ref, dk1_ref, dv0_ref, dv1_ref
):
    own = k0_ref.shape[0]
    keys = jnp.concatenate([k0_ref[...], k1_ref[...]], axis=0)
    values = jnp.concatenate([v0_ref[...], v1_ref[...]], axis=0)
    grad_keys = grad_values = 0.0
    for start in range(0, q_ref.shape[0], ROWS):
        rows = pl.ds(start, ROWS)
        halves = []
        for half in range(2):
            queries = half_lanes(q_ref[rows, :], half)
            upstream = half_lanes(g_ref[rows, :], half)
            scores = dots(keys, queries, 1, 1)
            probs = jnp.exp2(scores * HEAD_SCALE - norm_ref[0, half : half + 1, rows])
            grad_probs = dots(values, upstream, 1, 1)
            row_dot = jnp.sum(grad_probs * probs, axis=0, keepdims=True)
            grad_scores = (probs * (grad_probs - row_dot)).astype(jnp.bfloat16)
            grad_values = grad_values + dots(probs.astype(jnp.bfloat16), upstream, 1, 0)
            grad_keys = grad_keys + dots(grad_scores, queries, 1, 0)
            grad_queries = dots(keys, grad_scores, 0, 0)
            halves.append(grad_queries[half * HEAD_DIM : (half + 1) * HEAD_DIM])
        grad_queries = jnp.concatenate(halves, axis=0) * (1.0 / math.sqrt(HEAD_DIM))
        dq_ref[rows, :] = grad_queries.T.astype(dq_ref.dtype)
    grad_keys = grad_keys * (1.0 / math.sqrt(HEAD_DIM))
    dk0_ref[...] = grad_keys[:own]
    dk1_ref[...] = grad_keys[own:]
    dv0_ref[...] = grad_values[:own]
    dv1_ref[...] = grad_values[own:]


def attention_backward(queries, keys, values, log_norm, grad_mixed):
    length, width = queries.shape
    pairs = width // PAIR
    block = pl.BlockSpec((length, PAIR), lambda i: (0, i))
    flops = 20 * length * length * width
    wide = jax.ShapeDtypeStruct((length, width), jnp.float32)
    return pl.pallas_call(
        backward_kernel,
        grid=(pairs,),
        out_shape=[jax.ShapeDtypeStruct((length, width), queries.dtype)] + [wide] * 4,
        in_specs=[block] * 5 + [pl.BlockSpec((1, 2, length), lambda i: (i, 0, 0)), block],
        out_specs=[block] * 5,
        cost_estimate=pl.CostEstimate(
            flops=2 * flops, bytes_accessed=32 * length * width, transcendentals=flops // 640
        ),
        name="attention_backward",
    )(queries, *keys, *values, log_norm, grad_mixed)


def score_kernel(head_ref, word_ref, bias_ref, label_ref, stat_ref, top, total, target):
    at, last = pl.program_id(1), pl.num_programs(1) - 1
    logits = dots(head_ref[...], word_ref[...], 1, 1) + bias_ref[...]
    column = at * logits.shape[1] + lax.broadcasted_iota(jnp.int32, logits.shape, 1)

    @pl.when(at == 0)
    def _():
        top[...] = jnp.full(top.shape, -jnp.inf, jnp.float32)
        total[...] = jnp.zeros(total.shape, jnp.float32)
        target[...] = jnp.zeros(target.shape, jnp.float32)

    old = top[...]
    new = jnp.maximum(old, jnp.max(logits, axis=1, keepdims=True))
    added = jnp.sum(jnp.exp(logits - new), axis=1, keepdims=True)
    total[...] = total[...] * jnp.exp(old - new) + added
    top[...] = new
    hits = jnp.where(column == label_ref[...], logits, 0.0)
    target[...] += jnp.sum(hits, axis=1, keepdims=True)

    @pl.when(at == last)
    def _():
        lane = lax.broadcasted_iota(jnp.int32, stat_ref.shape, 1)
        stat_ref[...] = jnp.where(
            lane == 0, top[...], jnp.where(lane == 1, total[...], target[...])
        )


def slope_kernel(
    head_ref, word_ref, bias_ref, label_ref, norm_ref, weight_ref, slope_ref, sum_ref, grad_ref
):
    at = pl.program_id(1)
    logits = dots(head_ref[...], word_ref[...], 1, 1) + bias_ref[...]
    column = at * logits.shape[1] + lax.broadcasted_iota(jnp.int32, logits.shape, 1)
    hits = jnp.where(column == label_ref[...], 1.0, 0.0)
    slope = ((jnp.exp(logits - norm_ref[...]) - hits) * weight_ref[...]).astype(jnp.bfloat16)
    slope_ref[...] = slope
    sum_ref[0] = jnp.sum(slope.astype(jnp.float32), axis=0, keepdims=True)
    part = dots(slope, word_ref[...], 1, 0)

    @pl.when(at == 0)
    def _():
        grad_ref[...] = part

    @pl.when(at > 0)
    def _():
        grad_ref[...] += part


def head_blocks(head, word, bias):
    rows, vocab = head.shape[0], word.shape[0]
    row_block = 512 if rows % 512 == 0 else rows
    block = 768 if vocab % 768 == 0 else vocab
    grid = (rows // row_block, vocab // block)
    column = pl.BlockSpec((row_block, 1), lambda i, j: (i, 0))
    specs = [
        pl.BlockSpec((row_block, D), lambda i, j: (i, 0)),
        pl.BlockSpec((block, D), lambda i, j: (j, 0)),
        pl.BlockSpec((1, block), lambda i, j: (0, j)),
        column,
    ]
    cost = pl.CostEstimate(
        flops=2 * rows * vocab * D, bytes_accessed=2 * vocab * D, transcendentals=rows * vocab
    )
    return row_block, block, grid, column, specs, cost


def head_scores(head, word, bias, labels):
    row_block, _, grid, _, specs, cost = head_blocks(head, word, bias)
    stats = pl.pallas_call(
        score_kernel,
        grid=grid,
        out_shape=jax.ShapeDtypeStruct((head.shape[0], 128), jnp.float32),
        in_specs=specs,
        out_specs=pl.BlockSpec((row_block, 128), lambda i, j: (i, 0)),
        scratch_shapes=[pltpu.VMEM((row_block, 1), jnp.float32)] * 3,
        cost_estimate=cost,
        name="head_scores",
    )(head, word, bias[None], labels[:, None])
    return stats[:, :3].T


def head_slopes(head, word, bias, labels, norms, weights):
    row_block, block, grid, column, specs, cost = head_blocks(head, word, bias)
    rows, vocab = head.shape[0], word.shape[0]
    slopes, sums, grad = pl.pallas_call(
        slope_kernel,
        grid=grid,
        out_shape=[
            jax.ShapeDtypeStruct((rows, vocab), head.dtype),
            jax.ShapeDtypeStruct((grid[0], 1, vocab), jnp.float32),
            jax.ShapeDtypeStruct((rows, D), jnp.float32),
        ],
        in_specs=specs + [column] * 2,
        out_specs=[
            pl.BlockSpec((row_block, block), lambda i, j: (i, j)),
            pl.BlockSpec((1, 1, block), lambda i, j: (i, 0, j)),
            pl.BlockSpec((row_block, D), lambda i, j: (i, 0)),
        ],
        cost_estimate=cost,
        name="head_slopes",
    )(head, word, bias[None], labels[:, None], norms[:, None], weights[:, None])
    return slopes, jnp.sum(sums[:, 0], axis=0), grad


def step(sizes, *args):
    (
        token_ids, type_ids, mask_pos, mask_valid, mlm_labels, nsp_labels,
        word_table, word_m, word_v, attn_weight, attn_m, attn_v,
        ff_weight, ff_m, ff_v, side_weight, side_m, side_v,
        vectors, vec_m, vec_v, split_bias, split_m, split_v,
        decoder_bias, decoder_m, decoder_v,
    ) = args
    z_size, x_size, y_size, c_size = sizes
    dp_size, mp_size = z_size * x_size, y_size * c_size
    z_at, x_at, y_at, c_at = (lax.axis_index(a) for a in ("z", "x", "y", "c"))
    dp_rank, mp_rank = z_at * x_size + x_at, y_at * c_size + c_at
    every = ("z", "x", "y", "c")
    mp_first = ("y", "c", "z", "x")
    plane = ("x", "y", "c")
    batch_size, length = token_ids.shape
    slots = mask_pos.shape[1]
    own_len, own_slots = length // c_size, slots // c_size
    vocab_own = word_table.shape[0]
    attn_cols, ff_cols = attn_weight.shape[2], ff_weight.shape[2]
    rows_own = attn_weight.shape[0]
    low = jnp.bfloat16
    links = Links(sizes)

    def mine(rows, size):
        row = lax.dynamic_index_in_dim(rows, y_at, 0, False)
        return lax.dynamic_slice_in_dim(row, c_at * size, size, 0)

    own_ids = mine(token_ids, own_len)
    own_types = mine(type_ids, own_len)
    seq_pos = lax.dynamic_index_in_dim(mask_pos, y_at, 0, False)
    own_pos = mine(mask_pos, own_slots)
    own_valid = mine(mask_valid, own_slots)
    own_labels = mine(mlm_labels, own_slots)
    first_core = (c_at == 0).astype(jnp.float32)

    side_rows = side_weight.shape[0] // mp_size
    side_own = lax.dynamic_slice_in_dim(side_weight, mp_rank * side_rows, side_rows, 0)
    both = jnp.concatenate([attn_weight.reshape(rows_own, 4 * attn_cols), side_own]).astype(low)
    both = comm_all_gather(both, mp_first).reshape(mp_size, dp_size, -1, D)
    attn_blocks = both[:, :, :rows_own].reshape(mp_size, D, 4 * attn_cols)
    side_full = both[:, :, rows_own:].transpose(1, 0, 2, 3).reshape(-1, D)
    ff_blocks = comm_all_gather(
        ff_weight.astype(low).reshape(rows_own, 2 * ff_cols), mp_first
    ).reshape(mp_size, D, 2 * ff_cols)
    vec_cols = vectors.shape[1]
    stripe = vocab_own * x_size
    bias_mine = lax.dynamic_slice_in_dim(decoder_bias, z_at * stripe, stripe, 0)
    int_count = own_len + 2 * own_slots
    word_parts = 4 if vocab_own % 64 == 0 else 1
    word_plane, ints, vec_parts, counts, mp_small = links.exchange(
        "word_gather",
        ("plane", plane, 0, BIG, word_table.astype(low).reshape(word_parts, -1, D)),
        ("gather", ("z",), 0, FAST, lanes(jnp.concatenate([own_ids, own_labels, own_valid]))),
        ("gather", ("z", "x"), 0, FAST, jnp.pad(vectors.astype(low), ((0, 0), (0, 128 - vec_cols)))),
        (
            "gather",
            ("z", "x"),
            0,
            FAST,
            jnp.full((8, 128), jnp.sum(mask_valid.astype(jnp.float32))),
        ),
        ("gather", ("y", "c"), 0, FAST, lanes(jnp.concatenate([bias_mine, split_bias.reshape(-1)]))),
    )
    ints = ints.reshape(z_size, -1)[:, :int_count]
    z_ids, z_labels, z_valid = (
        ints[:, :own_len],
        ints[:, own_len : own_len + own_slots],
        ints[:, own_len + own_slots :],
    )
    total_count = jnp.sum(counts[:, 0, 0])
    total_seqs = jnp.float32(batch_size * dp_size)
    vec_rows = (
        vec_parts[:, :, :vec_cols]
        .transpose(1, 0, 2)
        .reshape(vectors.shape[0], D)
        .astype(jnp.float32)
    )
    mp_small = mp_small.reshape(mp_size, -1)
    word_plane = word_plane.reshape(-1, D)
    bias_plane = (
        mp_small[:, :stripe].reshape(mp_size, x_size, vocab_own).transpose(1, 0, 2).reshape(-1)
    )
    split_full = mp_small[:, stripe : stripe + 6 * attn_cols].reshape(mp_size, 6, attn_cols)

    def plane_index(ids):
        block = ids // stripe
        offset = ids % stripe
        inside = block % z_size == z_at
        at = ((offset // vocab_own) * mp_size + block // z_size) * vocab_own + offset % vocab_own
        return inside, at

    flat_ids = z_ids.reshape(-1)
    inside, at = plane_index(flat_ids)
    looked = jnp.where(inside[:, None], word_plane[jnp.where(inside, at, 0)], jnp.zeros((), low))
    if z_size <= 8:
        looked = looked.reshape(z_size, 8, own_len // 8, D)
        embedded = links.fold("token_fold", looked).reshape(own_len, D).astype(jnp.float32)
    else:
        looked = looked.reshape(z_size, own_len, D)
        (found,) = links.exchange("token_spread", ("spread", ("z",), 0, BIG, looked))
        embedded = lax.dynamic_index_in_dim(looked, z_at, 0, False).astype(jnp.float32)
        embedded = embedded + jnp.sum(found.astype(jnp.float32), axis=0)
    position_rows = lax.dynamic_slice_in_dim(side_full, 2 * D + c_at * own_len, own_len, 0)
    embedded = (
        embedded
        + position_rows.astype(jnp.float32)
        + jnp.where(own_types[:, None] == 0, vec_rows[12], vec_rows[13])
    )
    hidden0 = layer_norm(embedded, vec_rows[0], vec_rows[1])
    hidden0_b = hidden0.astype(low)

    qkv_blocks = attn_blocks[:, :, : 3 * attn_cols]
    out_blocks = attn_blocks[:, :, 3 * attn_cols :]
    packed = jnp.einsum("td,mde->tme", hidden0_b, qkv_blocks, preferred_element_type=jnp.float32)
    packed = packed.reshape(own_len, mp_size, 3, attn_cols)
    queries = (packed[:, :, 0] + split_full[:, 0]).astype(low).reshape(own_len, D)
    own_keys = packed[:, :, 1].astype(low).reshape(own_len, D)
    own_values = (packed[:, :, 2] + split_full[:, 1]).astype(low).reshape(own_len, D)
    other_keys, other_values = links.exchange(
        "key_trade", ("trade", ("c",), 0, FAST, own_keys), ("trade", ("c",), 0, FAST, own_values)
    )
    keys, values = (own_keys, other_keys), (own_values, other_values)
    mixed, log_norm = attention_forward(queries, keys, values)
    attn_out = jnp.einsum(
        "tme,mde->td",
        mixed.reshape(own_len, mp_size, attn_cols),
        out_blocks,
        preferred_element_type=jnp.float32,
    )
    resid1 = hidden0 + (attn_out + vec_rows[2])
    hidden1 = layer_norm(resid1, vec_rows[3], vec_rows[4])
    hidden1_b = hidden1.astype(low)
    ff_bias = split_full[:, 2:6].transpose(0, 2, 1).reshape(mp_size, ff_cols)
    ff_in, ff_out = ff_blocks[:, :, :ff_cols], ff_blocks[:, :, ff_cols:]
    upward = jnp.einsum("td,mdf->mtf", hidden1_b, ff_in, preferred_element_type=jnp.float32)
    upward = upward + ff_bias[:, None]
    active = gelu_exact(upward).astype(low)
    ffn_out = jnp.einsum("mtf,mdf->td", active, ff_out, preferred_element_type=jnp.float32)
    resid2 = hidden1 + (ffn_out + vec_rows[5])
    hidden2 = layer_norm(resid2, vec_rows[6], vec_rows[7])

    hidden2_b = hidden2.astype(low)
    (other_h2,) = links.exchange("hidden_trade", ("trade", ("c",), 0, FAST, hidden2_b))
    picked_b = jnp.concatenate([hidden2_b, other_h2])[
        own_pos % own_len + jnp.where(own_pos // own_len == c_at, 0, own_len)
    ]
    dense_w = side_full[D : 2 * D]
    dense_out = jnp.dot(picked_b, dense_w, preferred_element_type=jnp.float32) + vec_rows[8]
    act_dense = gelu_exact(dense_out)
    head_rows = layer_norm(act_dense, vec_rows[9], vec_rows[10])
    (head_b,) = links.exchange("head_gather", links.line_move(head_rows.astype(low), 32, FAST))
    head_b = head_b.reshape(-1, D)
    label_in, label_at = plane_index(z_labels.reshape(-1))
    label_at = jnp.where(label_in, label_at, -1)
    stats = jnp.pad(head_scores(head_b, word_plane, bias_plane, label_at), ((0, 5), (0, 0)))
    (stats,) = links.exchange("stat_gather", ("gather", ("z",), 0, FAST, stats))
    top_all = jnp.max(stats[:, 0], axis=0)
    total_all = jnp.sum(stats[:, 1] * jnp.exp(stats[:, 0] - top_all), axis=0)
    target_all = jnp.sum(stats[:, 2], axis=0)
    log_total = top_all + jnp.log(total_all)
    valid_rows = z_valid.reshape(-1).astype(jnp.float32)
    mlm_sum = -jnp.sum(valid_rows * (target_all - log_total))
    weight_rows = valid_rows / total_count
    grad_logits, decoder_part, head_part = head_slopes(
        head_b, word_plane, bias_plane, label_at, log_total, weight_rows
    )
    head_part = head_part.reshape(z_size, own_slots, D)
    (head_others,) = links.exchange("head_spread", ("spread", ("z",), 0, FAST, head_part.astype(low)))
    grad_head = lax.dynamic_index_in_dim(head_part, z_at, 0, False) + jnp.sum(
        head_others.astype(jnp.float32), axis=0
    )
    grad_act, grad_g9, grad_s9 = norm_backward(act_dense, vec_rows[9], vec_rows[10], grad_head)
    grad_dense = (grad_act * gelu_slope(dense_out)).astype(low)
    dense_bias_grad = jnp.sum(grad_dense.astype(jnp.float32), axis=0)
    dense_grad = jnp.einsum("rd,re->de", picked_b, grad_dense, preferred_element_type=jnp.float32)
    grad_picked = jnp.einsum("re,de->rd", grad_dense, dense_w, preferred_element_type=jnp.float32)
    (other_picked,) = links.exchange("picked_trade", ("trade", ("c",), 0, FAST, grad_picked))
    seq_picked = jnp.concatenate([grad_picked, other_picked])
    other_pos = lax.dynamic_slice_in_dim(seq_pos, (1 - c_at) * own_slots, own_slots, 0)
    place = (
        jnp.concatenate([own_pos, other_pos])[None, :]
        == c_at * own_len + lax.broadcasted_iota(jnp.int32, (own_len, slots), 0)
    ).astype(jnp.float32)
    grad_top = jnp.dot(place, seq_picked, precision=highest)

    cls_row = hidden2_b[0:1]
    pooler_w = side_full[:D]
    pooled = jnp.tanh(jnp.dot(cls_row, pooler_w, preferred_element_type=jnp.float32) + vec_rows[11])
    classes = vec_rows[14:16]
    nsp_logp = jax.nn.log_softmax(jnp.dot(pooled, classes.T, precision=highest), axis=-1)
    own_nsp = lax.dynamic_slice_in_dim(nsp_labels, y_at, 1, 0)
    pick_nsp = own_nsp[:, None] == lax.broadcasted_iota(jnp.int32, (1, 2), 1)
    nsp_sum = -jnp.sum(jnp.where(pick_nsp, nsp_logp, 0.0)) * first_core
    grad_nsp = (jnp.exp(nsp_logp) - pick_nsp.astype(jnp.float32)) / total_seqs * first_core
    class_grad = grad_nsp[0][:, None] * pooled
    grad_pre = jnp.dot(grad_nsp, classes, precision=highest) * (1.0 - pooled * pooled)
    pooler_bias_grad = grad_pre[0]
    pooler_grad = cls_row.astype(jnp.float32).T * grad_pre
    grad_cls = jnp.dot(grad_pre, pooler_w.astype(jnp.float32).T, precision=highest)
    first_row = lax.broadcasted_iota(jnp.int32, (own_len, 1), 0) == 0
    grad_top = grad_top + jnp.where(first_row, grad_cls, 0.0)

    grad_r2, grad_g2, grad_s2 = norm_backward(resid2, vec_rows[6], vec_rows[7], grad_top)
    ffn_grad_b = grad_r2.astype(low)
    out_bias_two = jnp.sum(ffn_grad_b.astype(jnp.float32), axis=0)
    ff_out_grad = jnp.einsum("td,mtf->mdf", ffn_grad_b, active, preferred_element_type=jnp.float32)
    grad_active = jnp.einsum("td,mdf->mtf", ffn_grad_b, ff_out, preferred_element_type=jnp.float32)
    grad_up = (grad_active * gelu_slope(upward)).astype(low)
    ff_bias_grad = jnp.sum(grad_up.astype(jnp.float32), axis=1)
    ff_in_grad = jnp.einsum("td,mtf->mdf", hidden1_b, grad_up, preferred_element_type=jnp.float32)
    hidden1_part = jnp.einsum("mtf,mdf->td", grad_up, ff_in, preferred_element_type=jnp.float32)
    ff_grad = jnp.stack(
        [
            row_major(g.astype(low)).reshape(mp_size * dp_size, rows_own, ff_cols)
            for g in (ff_in_grad, ff_out_grad)
        ],
        axis=1,
    )
    ff_grad, hidden1_part = lax.optimization_barrier((ff_grad, hidden1_part))
    ff_red = comm_scatter_sum(ff_grad.reshape(-1, ff_cols), mp_first)
    grad_h1 = grad_r2 + hidden1_part
    grad_r1, grad_g1, grad_s1 = norm_backward(resid1, vec_rows[3], vec_rows[4], grad_h1)
    attn_grad_b = grad_r1.astype(low)
    out_bias_one = jnp.sum(attn_grad_b.astype(jnp.float32), axis=0)
    mixed_blocks = mixed.reshape(own_len, mp_size, attn_cols)
    attn_grad_out = jnp.einsum(
        "td,tme->mde", attn_grad_b, mixed_blocks, preferred_element_type=jnp.float32
    )
    grad_mixed = jnp.einsum(
        "td,mde->tme", attn_grad_b, out_blocks, preferred_element_type=jnp.float32
    )
    grad_mixed = grad_mixed.astype(low).reshape(own_len, D)
    grad_q, own_k, part_k, own_v, part_v = attention_backward(
        queries, keys, values, log_norm, grad_mixed
    )
    from_k, from_v = links.exchange(
        "key_grad_trade",
        ("trade", ("c",), 0, FAST, part_k),
        ("trade", ("c",), 0, FAST, part_v),
    )
    grad_k = (own_k + from_k).astype(low)
    grad_v = (own_v + from_v).astype(low)
    grad_packed = jnp.stack(
        [
            grad_q.reshape(own_len, mp_size, attn_cols),
            grad_k.reshape(own_len, mp_size, attn_cols),
            grad_v.reshape(own_len, mp_size, attn_cols),
        ],
        axis=2,
    ).reshape(own_len, mp_size, 3 * attn_cols)
    attn_grad_in = jnp.einsum(
        "td,tme->mde", hidden0_b, grad_packed, preferred_element_type=jnp.float32
    )
    packed_sums = jnp.sum(grad_packed.astype(jnp.float32), axis=0).reshape(mp_size, 3, attn_cols)
    hidden0_part = jnp.einsum(
        "tme,mde->td", grad_packed, qkv_blocks, preferred_element_type=jnp.float32
    )
    attn_grad = jnp.concatenate([attn_grad_in, attn_grad_out], axis=2).astype(low)
    attn_grad = attn_grad.reshape(y_size, c_size, z_size, x_size, rows_own, 4 * attn_cols)
    grad_h0 = grad_r1 + hidden0_part
    grad_x0, grad_g0, grad_s0 = norm_backward(embedded, vec_rows[0], vec_rows[1], grad_h0)

    position_grad = lax.dynamic_update_slice_in_dim(
        jnp.zeros((length, D), low), grad_x0.astype(low), c_at * own_len, 0
    )
    side_grad = jnp.concatenate([pooler_grad.astype(low), dense_grad.astype(low), position_grad], axis=0)
    side_grad = side_grad.reshape(z_size, x_size, y_size, c_size, side_rows, D)

    def joined(value, at, dim, received):
        kept = lax.dynamic_index_in_dim(value, at, dim, False)
        return (kept.astype(jnp.float32) + received.astype(jnp.float32)).astype(low)

    x0_b = grad_x0.astype(low)
    cut_one, cut_two = own_len // 8, 5 * own_len // 8
    from_a, from_s, x0_one = links.exchange(
        "grad_swap_c",
        ("swap", ("c",), 1, BIG, attn_grad),
        ("swap", ("c",), 3, BIG, side_grad),
        links.line_move(x0_b[:cut_one], 64, BIG),
    )
    attn_grad, side_grad = joined(attn_grad, c_at, 1, from_a), joined(side_grad, c_at, 3, from_s)
    from_a, from_s, x0_two = links.exchange(
        "grad_swap_xy",
        ("swap", ("x",), 2, BIG, attn_grad),
        ("swap", ("y",), 2, BIG, side_grad),
        links.line_move(x0_b[cut_one:cut_two], 64, BIG),
    )
    attn_grad, side_grad = joined(attn_grad, x_at, 2, from_a), joined(side_grad, y_at, 2, from_s)
    from_a, from_s, x0_three = links.exchange(
        "grad_swap_yx",
        ("swap", ("y",), 0, BIG, attn_grad),
        ("swap", ("x",), 1, BIG, side_grad),
        links.line_move(x0_b[cut_two:], 64, BIG),
    )
    attn_grad, side_grad = joined(attn_grad, y_at, 0, from_a), joined(side_grad, x_at, 1, from_s)

    ff_red, x0_three = lax.optimization_barrier((ff_red, x0_three))
    all_x0 = [x.reshape(z_size, -1, D) for x in (x0_one, x0_two, x0_three)]
    all_x0 = jnp.concatenate(all_x0, axis=1).reshape(-1, D)
    onehot = (
        jnp.where(inside, at, -1)[None, :]
        == lax.broadcasted_iota(jnp.int32, (word_plane.shape[0], flat_ids.shape[0]), 0)
    ).astype(low)
    word_grad = jnp.einsum("rv,rd->vd", grad_logits, head_b, preferred_element_type=jnp.float32)
    word_grad = word_grad + jnp.dot(onehot, all_x0, preferred_element_type=jnp.float32)
    word_grad, attn_grad, side_grad = lax.optimization_barrier(
        (word_grad.astype(low), attn_grad, side_grad)
    )
    word_red = comm_scatter_sum(word_grad, plane).astype(jnp.float32)
    from_a, from_s = links.exchange(
        "grad_spread_z", ("spread", ("z",), 0, BIG, attn_grad), ("spread", ("z",), 0, BIG, side_grad)
    )

    def total(value, received):
        kept = lax.dynamic_index_in_dim(value, z_at, 0, False).astype(jnp.float32)
        return kept + jnp.sum(received.astype(jnp.float32), axis=0)

    attn_red, side_quarter = total(attn_grad, from_a), total(side_grad, from_s)
    type_zero = jnp.sum(jnp.where(own_types[:, None] == 0, grad_x0, 0.0), axis=0)
    type_one = jnp.sum(jnp.where(own_types[:, None] == 1, grad_x0, 0.0), axis=0)
    vec_grad = jnp.stack(
        [
            grad_g0, grad_s0, out_bias_one, grad_g1, grad_s1, out_bias_two, grad_g2, grad_s2,
            dense_bias_grad, grad_g9, grad_s9, pooler_bias_grad, type_zero, type_one,
            class_grad[0], class_grad[1],
        ],
        axis=0,
    )
    split_grad = jnp.concatenate(
        [
            packed_sums[:, 0:1],
            packed_sums[:, 2:3],
            ff_bias_grad.reshape(mp_size, attn_cols, 4).transpose(0, 2, 1),
        ],
        axis=1,
    )
    late = lanes(jnp.concatenate([vec_grad.reshape(-1), split_grad.reshape(-1), decoder_part]))
    late, side_quarter = lax.optimization_barrier((late, side_quarter))
    small = links.combine(
        "small_sum",
        late,
    ).reshape(z_size, -1)
    (side_red,) = links.exchange(
        "side_gather", ("gather", ("y", "c"), 0, FAST, side_quarter.astype(low))
    )
    side_red = side_red.reshape(side_weight.shape).astype(jnp.float32)
    narrow = vec_grad.size + split_grad.size
    summed = jnp.sum(small[:, :narrow], axis=0)
    vec_all = summed[: vec_grad.size].reshape(vec_grad.shape)
    split_all = summed[vec_grad.size :].reshape(split_grad.shape)
    vec_red = lax.dynamic_slice_in_dim(vec_all, dp_rank * vec_cols, vec_cols, 1)
    split_red = lax.dynamic_index_in_dim(split_all, mp_rank, 0, False)
    decoder_red = lax.dynamic_index_in_dim(
        small[:, narrow : narrow + decoder_part.size].reshape(z_size, x_size, mp_size, vocab_own),
        mp_rank,
        2,
        False,
    ).reshape(-1)
    word_f, attn_f, ff_f = (
        word_red,
        attn_red.reshape(attn_weight.shape),
        row_major(
            ff_red.astype(jnp.float32).reshape(2, rows_own, ff_cols).transpose(1, 0, 2)
        ),
    )
    own_square = (
        jnp.sum(word_f * word_f)
        + jnp.sum(attn_f * attn_f)
        + jnp.sum(ff_f * ff_f)
        + jnp.sum(side_red * side_red) / mp_size
        + jnp.sum(vec_red * vec_red) / mp_size
        + (jnp.sum(split_red * split_red) + jnp.sum(decoder_red * decoder_red)) / dp_size
    )
    loss_part = mlm_sum / total_count / z_size + nsp_sum / total_seqs
    ends = jnp.where(
        lax.broadcasted_iota(jnp.int32, (8, 128), 0) == 0, own_square, loss_part
    )
    ends = jnp.sum(links.combine("norm_sum", ends), axis=0)
    grad_square, total_loss = ends[0, 0], ends[1, 0]
    grad_norm = jnp.sqrt(grad_square)
    clip_scale = max_norm / jnp.maximum(grad_norm, max_norm)
    return (
        total_loss,
        grad_norm,
        *adam_step(word_table, word_m, word_v, word_f, clip_scale, True),
        *adam_step(attn_weight, attn_m, attn_v, attn_f, clip_scale, True),
        *adam_step(ff_weight, ff_m, ff_v, ff_f, clip_scale, True),
        *adam_step(side_weight, side_m, side_v, side_red, clip_scale, True),
        *adam_step(vectors, vec_m, vec_v, vec_red, clip_scale, False),
        *adam_step(split_bias, split_m, split_v, split_red, clip_scale, False),
        *adam_step(decoder_bias, decoder_m, decoder_v, decoder_red, clip_scale, False),
    )


def solution(mesh):
    dp_size, mp_size = mesh.shape["dp"], mesh.shape["mp"]
    x_size = 2 if dp_size % 2 == 0 else 1
    c_size = 2 if mp_size % 2 == 0 else 1
    sizes = (dp_size // x_size, x_size, mp_size // c_size, c_size)
    fine = Mesh(mesh.devices.reshape(sizes), ("z", "x", "y", "c"))
    dp, mp = ("z", "x"), ("y", "c")
    word = P(("y", "c", "z", "x"), None)
    cube = P(dp, None, mp)
    kinds = (
        [P(dp, None)] * 5
        + [P(dp)]
        + [word] * 3
        + [cube] * 6
        + [P(dp, None)] * 3
        + [P(None, dp)] * 3
        + [P(None, mp)] * 3
        + [P(mp)] * 3
    )
    return jax.shard_map(
        functools.partial(step, sizes),
        mesh=fine,
        in_specs=tuple(kinds),
        out_specs=(P(), P(), *kinds[6:]),
        check_vma=False,
    )
```

```python
import functools
import math

import jax
import jax.numpy as jnp
from jax import lax
from jax.experimental.layout import Layout, with_layout_constraint
from jax.experimental import pallas as pl
from jax.experimental.pallas import tpu as pltpu
from jax.sharding import Mesh, PartitionSpec as P

D = 768
HEAD_DIM = 64


beta_one = 0.9
beta_two = 0.999
adam_eps = 1e-06
learn_rate = 0.2
decay_rate = 0.01
step_count = 10
max_norm = 0.05
norm_eps = 1e-12
highest = lax.Precision.HIGHEST


def layer_norm(inputs, norm_gain, norm_shift):
    center = inputs - jnp.mean(inputs, axis=-1, keepdims=True)
    spread = jnp.mean(center * center, axis=-1, keepdims=True)
    return center * lax.rsqrt(spread + norm_eps) * norm_gain + norm_shift


def normal_cdf(inputs):
    return 0.5 + 0.5 * lax.erf(inputs * math.sqrt(0.5))


def gelu_exact(inputs):
    return inputs * normal_cdf(inputs)


def gelu_slope(inputs):
    density = jnp.exp(-0.5 * inputs * inputs) * (1.0 / math.sqrt(2.0 * math.pi))
    return normal_cdf(inputs) + inputs * density


def norm_backward(inputs, norm_gain, norm_shift, upstream):
    _, pullback = jax.vjp(layer_norm, inputs, norm_gain, norm_shift)
    return pullback(upstream)


def adam_step(weight, moment, square, gradient, clip_scale, decays):
    gradient = gradient * clip_scale
    moment = beta_one * moment + (1 - beta_one) * gradient
    square = beta_two * square + (1 - beta_two) * gradient * gradient
    mean_hat = moment / (1 - beta_one**step_count)
    var_hat = square / (1 - beta_two**step_count)
    change = mean_hat / (jnp.sqrt(var_hat) + adam_eps)
    if decays:
        change = change + decay_rate * weight
    return (weight - learn_rate * change, moment, square)


def comm_all_gather(value, axes):
    return lax.all_gather(value, axes, axis=0, tiled=True)


def comm_scatter_sum(value, axes):
    return lax.psum_scatter(value, axes, scatter_dimension=0, tiled=True)


MESH = pl.DeviceIdType.MESH
BIG, FAST = pl.ANY, pltpu.VMEM


class Links:
    def __init__(self, sizes):
        self.sizes = dict(zip(("z", "x", "y", "c"), sizes))
        self.used = 0

    def next_id(self):
        self.used += 1
        return self.used - 1

    def count(self, axes):
        return math.prod(self.sizes[a] for a in axes)

    def place(self, axes):
        at = 0
        for a in axes:
            at = at * self.sizes[a] + lax.axis_index(a)
        return at

    def target(self, axes, flat):
        where = {}
        for a in reversed(axes):
            where[a] = lax.rem(flat, self.sizes[a])
            flat = lax.div(flat, self.sizes[a])
        return where

    def greet(self, groups):
        barrier = pltpu.get_barrier_semaphore()
        total = 0
        for axes in groups:
            size, me = self.count(axes), self.place(axes)
            for r in range(1, size):
                pl.semaphore_signal(
                    barrier,
                    inc=1,
                    device_id=self.target(axes, lax.rem(me + r, size)),
                    device_id_type=MESH,
                )
            total += size - 1
        pl.semaphore_wait(barrier, total)

    def call(self, kernel, outs, spaces, out_spaces, scratch, values, wire, name):
        result = pl.pallas_call(
            kernel,
            out_shape=outs,
            in_specs=[pl.BlockSpec(memory_space=m) for m in spaces],
            out_specs=[pl.BlockSpec(memory_space=m) for m in out_spaces],
            scratch_shapes=scratch,
            compiler_params=pltpu.CompilerParams(
                collective_id=self.next_id(),
                has_side_effects=True,
                vmem_limit_bytes=40 * 2**20,
            ),
            cost_estimate=pl.CostEstimate(flops=0, bytes_accessed=wire, transcendentals=0),
            name=name,
        )(*values)
        return result

    def exchange(self, name, *moves):
        outs, scratch = [], []
        for kind, axes, dim, _, value in moves:
            size = self.count(axes)
            shape, sends, lands = value.shape, (size - 1,), (size - 1,)
            if kind == "gather":
                shape = (size, *shape)
            elif kind == "swap":
                shape = shape[:dim] + shape[dim + 1 :]
            elif kind == "spread":
                shape = (size - 1, *shape[1:])
            elif kind == "relay":
                shape, sends = (size, *shape), (2, size - 1, shape[0])
                lands = sends
            elif kind == "plane":
                shape, sends, lands = (2, 2, 2, *shape), (7 * shape[0],), (7, shape[0])
            outs.append(jax.ShapeDtypeStruct(shape, value.dtype))
            scratch += [
                pltpu.SemaphoreType.DMA(sends),
                pltpu.SemaphoreType.DMA(lands),
                pltpu.SemaphoreType.DMA((1,)),
            ]
        spaces = [m[3] for m in moves]
        groups = []
        for kind, axes, *_ in moves:
            groups += [(a,) for a in axes] if kind == "plane" else [axes]
        groups = list(dict.fromkeys(groups))

        def kernel(*refs):
            ins, dests = refs[: len(moves)], refs[len(moves) : 2 * len(moves)]
            sems = refs[2 * len(moves) :]
            self.greet(groups)
            started, later = [], []
            for i, ((kind, axes, dim, _, _), source, dest) in enumerate(zip(moves, ins, dests)):
                sends, lands, own_sem = sems[3 * i : 3 * i + 3]
                size, me = self.count(axes), self.place(axes)
                if kind in ("relay", "plane"):
                    act = self.relay if kind == "relay" else self.plane
                    later.append(functools.partial(act, axes, source, dest, sends, lands))
                for r in range(1, size):
                    peer = lax.rem(me + r, size)
                    if kind == "gather":
                        src, dst = source, dest.at[me]
                    elif kind == "swap":
                        src, dst = source.at[(slice(None),) * dim + (peer,)], dest
                    elif kind == "spread":
                        src, dst = source.at[peer], dest.at[r - 1]
                    elif kind == "trade":
                        src, dst = source, dest
                    else:
                        continue
                    copy = pltpu.make_async_remote_copy(
                        src_ref=src,
                        dst_ref=dst,
                        send_sem=sends.at[r - 1],
                        recv_sem=lands.at[r - 1],
                        device_id=self.target(axes, peer),
                        device_id_type=MESH,
                    )
                    copy.start()
                    started.append(copy)
            runs = [act() for act in later]
            for run in runs:
                next(run)
            for i, ((kind, axes, *_), source, dest) in enumerate(zip(moves, ins, dests)):
                if kind in ("gather", "relay", "plane"):
                    at = self.place(axes)
                    if kind == "plane":
                        at = tuple(lax.axis_index(a) for a in axes)
                    copy = pltpu.make_async_copy(source, dest.at[at], sems[3 * i + 2].at[0])
                    copy.start()
                    started.append(copy)
            for run in runs:
                next(run, None)
            for copy in started:
                copy.wait()

        return self.call(
            kernel,
            outs,
            spaces,
            spaces,
            scratch,
            [m[4] for m in moves],
            sum(2 * math.prod(o.shape) * o.dtype.itemsize for o in outs),
            name,
        )

    def relay(self, axes, source, dest, sends, lands):
        (axis,) = axes
        size, parts = self.sizes[axis], source.shape[0]
        me = lax.axis_index(axis)

        def copy_of(way, hop, part):
            step = 1 if way == 0 else -1
            place = (me - step * hop, part)
            return pltpu.make_async_remote_copy(
                src_ref=source.at[part] if hop == 0 else dest.at[place],
                dst_ref=dest.at[place],
                send_sem=sends.at[way, hop, part],
                recv_sem=lands.at[way, hop, part],
                device_id={axis: me + step},
                device_id_type=MESH,
            )

        def landing(way, hop, part):
            step = 1 if way == 0 else -1
            landed = dest.at[me - step * hop, part]
            return pltpu.make_async_remote_copy(
                src_ref=landed,
                dst_ref=landed,
                send_sem=sends.at[way, hop - 1, part],
                recv_sem=lands.at[way, hop - 1, part],
                device_id={axis: me - step},
                device_id_type=MESH,
            )

        def held(way, hop):
            return me - hop >= 0 if way == 0 else me + hop <= size - 1

        def sending(way, hop):
            return held(way, hop) & (me < size - 1 if way == 0 else me > 0)

        for hop in range(size):
            for part in range(parts):
                for way in range(2):
                    if hop > 0:

                        @pl.when(held(way, hop))
                        def _():
                            landing(way, hop, part).wait_recv()

                    if hop < size - 1:

                        @pl.when(sending(way, hop))
                        def _():
                            copy_of(way, hop, part).start()

            if hop == 0:
                yield
        for hop in range(size - 1):
            for part in range(parts):
                for way in range(2):

                    @pl.when(sending(way, hop))
                    def _():
                        copy_of(way, hop, part).wait_send()

    def plane(self, axes, own, out, sends, lands):
        parts = own.shape[0]
        head = (parts + 1) // 2
        x, y, c = (lax.axis_index(a) for a in axes)
        by_x, by_y, by_c = {"x": 1 - x}, {"y": 1 - y}, {"c": 1 - c}
        started = []

        def send(src, place, part, slot, peer):
            copy = pltpu.make_async_remote_copy(
                src_ref=src,
                dst_ref=out.at[(*place, part)],
                send_sem=sends.at[len(started)],
                recv_sem=lands.at[slot, part],
                device_id=peer,
                device_id_type=MESH,
            )
            copy.start()
            started.append(copy)

        def arrived(place, part, slot):
            landed = out.at[(*place, part)]
            pltpu.make_async_remote_copy(
                src_ref=landed,
                dst_ref=landed,
                send_sem=sends.at[0],
                recv_sem=lands.at[slot, part],
                device_id=by_c,
                device_id_type=MESH,
            ).wait_recv()
            return landed

        me, at_x, at_y, at_xy = (x, y, c), (1 - x, y, c), (x, 1 - y, c), (1 - x, 1 - y, c)
        for part in range(parts):
            send(own.at[part], me, part, 0, by_x)
            send(own.at[part], me, part, 1, by_y)
        for part in range(parts):
            send(own.at[part], me, part, 3, by_c)
        yield
        for part in range(parts):
            landed = arrived(at_x, part, 0)
            if part < head:
                send(landed, at_x, part, 2, by_y)
            send(landed, at_x, part, 4, by_c)
            landed = arrived(at_y, part, 1)
            if part >= head:
                send(landed, at_y, part, 2, by_x)
            send(landed, at_y, part, 5, by_c)
        for part in range(parts):
            landed = arrived(at_xy, part, 2)
            send(landed, at_xy, part, 6, by_c)
        for slot, place in ((3, me), (4, at_x), (5, at_y), (6, at_xy)):
            for part in range(parts):
                arrived((place[0], place[1], 1 - c), part, slot)
        for copy in started:
            copy.wait_send()

    def fold(self, name, value):
        size, parts = value.shape[:2]
        block = value.shape[1:]

        def kernel(source, out, land, sends, lands):
            self.greet([("z",)])
            me = lax.axis_index("z")

            def beyond(way, hop):
                return me + hop <= size - 1 if way == 0 else me - hop >= 0

            def behind(way):
                return me > 0 if way == 0 else me < size - 1

            def copy_of(way, hop, part, src):
                return pltpu.make_async_remote_copy(
                    src_ref=src,
                    dst_ref=land.at[way, hop - 1, part],
                    send_sem=sends.at[way, hop - 1, part],
                    recv_sem=lands.at[way, hop - 1, part],
                    device_id={"z": me + (1 if way == 0 else -1)},
                    device_id_type=MESH,
                )

            def landing(way, hop, part):
                landed = land.at[way, hop, part]
                return pltpu.make_async_remote_copy(
                    src_ref=landed,
                    dst_ref=landed,
                    send_sem=sends.at[way, hop, part],
                    recv_sem=lands.at[way, hop, part],
                    device_id={"z": me - (1 if way == 0 else -1)},
                    device_id_type=MESH,
                )

            for hop in range(size - 1, 0, -1):
                for part in range(parts):
                    for way in range(2):
                        goal = me + hop if way == 0 else me - hop

                        @pl.when(beyond(way, hop) & jnp.logical_not(behind(way)))
                        def _():
                            copy_of(way, hop, part, source.at[goal, part]).start()

                        if hop < size - 1:

                            @pl.when(beyond(way, hop) & behind(way))
                            def _():
                                landing(way, hop, part).wait_recv()
                                land[way, hop, part] += source[goal, part]
                                copy_of(way, hop, part, land.at[way, hop, part]).start()

            for part in range(parts):
                out[part] = source[me, part]
                for way in range(2):

                    @pl.when(behind(way))
                    def _():
                        landing(way, 0, part).wait_recv()
                        out[part] += land[way, 0, part]

            for hop in range(size - 1, 0, -1):
                for part in range(parts):
                    for way in range(2):

                        @pl.when(beyond(way, hop))
                        def _():
                            copy_of(way, hop, part, source.at[0, part]).wait_send()

        return self.call(
            kernel,
            [jax.ShapeDtypeStruct(block, value.dtype)],
            [FAST],
            [FAST],
            [
                pltpu.VMEM((2, size - 1, *block), value.dtype),
                pltpu.SemaphoreType.DMA((2, size - 1, parts)),
                pltpu.SemaphoreType.DMA((2, size - 1, parts)),
            ],
            [value],
            4 * value.size,
            name,
        )[0]

    def line_move(self, value, part_rows, memory):
        parts = value.shape[0] // part_rows if value.shape[0] % part_rows == 0 else 1
        kind = "relay" if self.sizes["z"] <= 8 else "gather"
        return (kind, ("z",), 0, memory, value.reshape(parts, -1, value.shape[1]))

    def combine(self, name, value):
        pairs = [a for a in ("c", "x", "y") if self.sizes[a] > 1]
        depth = self.sizes["z"]
        steps = len(pairs)

        def kernel(x_ref, out_ref, sums, land, sends, lands):
            self.greet([(a,) for a in pairs] + [("z",)])
            me = lax.axis_index("z")
            for i, a in enumerate(pairs):
                source = x_ref if i == 0 else sums.at[i - 1]
                copy = pltpu.make_async_remote_copy(
                    src_ref=source,
                    dst_ref=land.at[i],
                    send_sem=sends.at[i],
                    recv_sem=lands.at[i],
                    device_id={a: 1 - lax.axis_index(a)},
                    device_id_type=MESH,
                )
                copy.start()
                copy.wait()
                sums[i] = source[...] + land[i]
            out_ref[me] = sums[steps - 1]
            started = []
            for r in range(1, depth):
                copy = pltpu.make_async_remote_copy(
                    src_ref=sums.at[steps - 1],
                    dst_ref=out_ref.at[me],
                    send_sem=sends.at[steps + r - 1],
                    recv_sem=lands.at[steps + r - 1],
                    device_id={"z": lax.rem(me + r, depth)},
                    device_id_type=MESH,
                )
                copy.start()
                started.append(copy)
            for copy in started:
                copy.wait()

        return self.call(
            kernel,
            [jax.ShapeDtypeStruct((depth, *value.shape), value.dtype)],
            [FAST],
            [FAST],
            [
                pltpu.VMEM((steps, *value.shape), value.dtype),
                pltpu.VMEM((steps, *value.shape), value.dtype),
                pltpu.SemaphoreType.DMA((steps + depth - 1,)),
                pltpu.SemaphoreType.DMA((steps + depth - 1,)),
            ],
            [value],
            16 * value.size * 4,
            name,
        )[0]


def row_major(value):
    return with_layout_constraint(value, Layout(major_to_minor=tuple(range(value.ndim))))


def lanes(flat):
    padded = jnp.pad(flat, (0, -flat.size % 1024))
    return padded.reshape(-1, 128)


HEAD_SCALE = math.log2(math.e) / math.sqrt(HEAD_DIM)
PAIR = 2 * HEAD_DIM
ROWS = 256


def dots(left, right, left_dim, right_dim):
    return lax.dot_general(
        left, right, (((left_dim,), (right_dim,)), ((), ())), preferred_element_type=jnp.float32
    )


def half_lanes(value, half):
    lane = lax.broadcasted_iota(jnp.int32, value.shape, 1)
    return jnp.where((lane >= HEAD_DIM) == (half == 1), value, jnp.zeros((), value.dtype))


def forward_kernel(q_ref, k0_ref, k1_ref, v0_ref, v1_ref, out_ref, norm_ref):
    keys = jnp.concatenate([k0_ref[...], k1_ref[...]], axis=0)
    values = jnp.concatenate([v0_ref[...], v1_ref[...]], axis=0)
    for start in range(0, q_ref.shape[0], ROWS):
        rows = pl.ds(start, ROWS)
        queries = q_ref[rows, :]
        halves = []
        for half in range(2):
            scores = dots(keys, half_lanes(queries, half), 1, 1)
            top = jnp.max(scores, axis=0, keepdims=True)
            powers = jnp.exp2((scores - top) * HEAD_SCALE)
            total = jnp.sum(powers, axis=0, keepdims=True)
            probs = (powers * (1.0 / total)).astype(jnp.bfloat16)
            norm_ref[0, half : half + 1, rows] = top * HEAD_SCALE + jnp.log2(total)
            mixed = dots(values, probs, 0, 0)
            halves.append(mixed[half * HEAD_DIM : (half + 1) * HEAD_DIM])
        out_ref[rows, :] = jnp.concatenate(halves, axis=0).T.astype(out_ref.dtype)


def attention_forward(queries, keys, values):
    length, width = queries.shape
    pairs = width // PAIR
    block = pl.BlockSpec((length, PAIR), lambda i: (0, i))
    flops = 8 * length * length * width
    return pl.pallas_call(
        forward_kernel,
        grid=(pairs,),
        out_shape=[
            jax.ShapeDtypeStruct((length, width), queries.dtype),
            jax.ShapeDtypeStruct((pairs, 2, length), jnp.float32),
        ],
        in_specs=[block] * 5,
        out_specs=[block, pl.BlockSpec((1, 2, length), lambda i: (i, 0, 0))],
        cost_estimate=pl.CostEstimate(
            flops=2 * flops, bytes_accessed=16 * length * width, transcendentals=flops // 256
        ),
        name="attention_forward",
    )(queries, *keys, *values)


def backward_kernel(
    q_ref, k0_ref, k1_ref, v0_ref, v1_ref, norm_ref, g_ref, dq_ref, dk0_ref, dk1_ref, dv0_ref, dv1_ref
):
    own = k0_ref.shape[0]
    keys = jnp.concatenate([k0_ref[...], k1_ref[...]], axis=0)
    values = jnp.concatenate([v0_ref[...], v1_ref[...]], axis=0)
    grad_keys = grad_values = 0.0
    for start in range(0, q_ref.shape[0], ROWS):
        rows = pl.ds(start, ROWS)
        halves = []
        for half in range(2):
            queries = half_lanes(q_ref[rows, :], half)
            upstream = half_lanes(g_ref[rows, :], half)
            scores = dots(keys, queries, 1, 1)
            probs = jnp.exp2(scores * HEAD_SCALE - norm_ref[0, half : half + 1, rows])
            grad_probs = dots(values, upstream, 1, 1)
            row_dot = jnp.sum(grad_probs * probs, axis=0, keepdims=True)
            grad_scores = (probs * (grad_probs - row_dot)).astype(jnp.bfloat16)
            grad_values = grad_values + dots(probs.astype(jnp.bfloat16), upstream, 1, 0)
            grad_keys = grad_keys + dots(grad_scores, queries, 1, 0)
            grad_queries = dots(keys, grad_scores, 0, 0)
            halves.append(grad_queries[half * HEAD_DIM : (half + 1) * HEAD_DIM])
        grad_queries = jnp.concatenate(halves, axis=0) * (1.0 / math.sqrt(HEAD_DIM))
        dq_ref[rows, :] = grad_queries.T.astype(dq_ref.dtype)
    grad_keys = grad_keys * (1.0 / math.sqrt(HEAD_DIM))
    dk0_ref[...] = grad_keys[:own]
    dk1_ref[...] = grad_keys[own:]
    dv0_ref[...] = grad_values[:own]
    dv1_ref[...] = grad_values[own:]


def attention_backward(queries, keys, values, log_norm, grad_mixed):
    length, width = queries.shape
    pairs = width // PAIR
    block = pl.BlockSpec((length, PAIR), lambda i: (0, i))
    flops = 20 * length * length * width
    wide = jax.ShapeDtypeStruct((length, width), jnp.float32)
    return pl.pallas_call(
        backward_kernel,
        grid=(pairs,),
        out_shape=[jax.ShapeDtypeStruct((length, width), queries.dtype)] + [wide] * 4,
        in_specs=[block] * 5 + [pl.BlockSpec((1, 2, length), lambda i: (i, 0, 0)), block],
        out_specs=[block] * 5,
        cost_estimate=pl.CostEstimate(
            flops=2 * flops, bytes_accessed=32 * length * width, transcendentals=flops // 640
        ),
        name="attention_backward",
    )(queries, *keys, *values, log_norm, grad_mixed)


def project_kernel(hidden_ref, weight_ref, bias_ref, q_ref, k_ref, v_ref):
    blocks, width = weight_ref.shape[0], weight_ref.shape[2] // 4
    packed = [dots(hidden_ref[...], weight_ref[m], 1, 0) for m in range(blocks)]

    def slot(at):
        return jnp.concatenate([p[:, at * width : (at + 1) * width] for p in packed], axis=1)

    q_ref[...] = (slot(0) + bias_ref[0:1]).astype(q_ref.dtype)
    k_ref[...] = slot(1).astype(k_ref.dtype)
    v_ref[...] = (slot(2) + bias_ref[1:2]).astype(v_ref.dtype)


def project(hidden, blocks, biases):
    rows = hidden.shape[0]
    return pl.pallas_call(
        project_kernel,
        out_shape=[jax.ShapeDtypeStruct((rows, D), hidden.dtype)] * 3,
        cost_estimate=pl.CostEstimate(
            flops=8 * rows * D * D, bytes_accessed=8 * D * D, transcendentals=0
        ),
        name="project_heads",
    )(hidden, blocks, biases)


def mixed_grad_kernel(dy_ref, weight_ref, out_ref):
    blocks, width = weight_ref.shape[0], weight_ref.shape[2] // 4
    dy = dy_ref[...]
    packed = [dots(dy, weight_ref[m][:, 3 * width :], 1, 0) for m in range(blocks)]
    out_ref[...] = jnp.concatenate(packed, axis=1).astype(out_ref.dtype)


def hidden_grad_kernel(dq_ref, dk_ref, dv_ref, weight_ref, out_ref):
    blocks, width = weight_ref.shape[0], weight_ref.shape[2] // 4
    grads = [r[...].astype(jnp.float32) for r in (dq_ref, dk_ref, dv_ref)]
    empty = jnp.zeros((grads[0].shape[0], width), jnp.float32)
    total = 0.0
    for m in range(blocks):
        block = [g[:, m * width : (m + 1) * width] for g in grads] + [empty]
        block = jnp.concatenate(block, axis=1).astype(weight_ref.dtype)
        total = total + dots(block, weight_ref[m], 1, 1)
    out_ref[...] = total


def projected(kernel, name, kind, *values):
    rows = values[0].shape[0]
    return pl.pallas_call(
        kernel,
        out_shape=jax.ShapeDtypeStruct((rows, D), kind),
        cost_estimate=pl.CostEstimate(
            flops=8 * rows * D * D, bytes_accessed=8 * D * D, transcendentals=0
        ),
        name=name,
    )(*values)


def attn_grad_kernel(hidden_ref, dq_ref, dk_ref, dv_ref, dy_ref, mixed_ref, out_ref):
    blocks, width = out_ref.shape[0], out_ref.shape[2] // 4
    hidden, dy = hidden_ref[...], dy_ref[...]
    grads = [dots(hidden, r[...], 0, 0) for r in (dq_ref, dk_ref, dv_ref)]
    grads.append(dots(dy, mixed_ref[...], 0, 0))
    for m in range(blocks):
        block = [g[:, m * width : (m + 1) * width] for g in grads]
        out_ref[m] = jnp.concatenate(block, axis=1).astype(out_ref.dtype)


def attn_weight_grad(blocks, *values):
    rows = values[0].shape[0]
    return pl.pallas_call(
        attn_grad_kernel,
        out_shape=jax.ShapeDtypeStruct((blocks, D, 4 * D // blocks), values[0].dtype),
        cost_estimate=pl.CostEstimate(
            flops=8 * rows * D * D, bytes_accessed=8 * D * D, transcendentals=0
        ),
        name="attn_weight_grad",
    )(*values)


def ff_grad_kernel(hidden_ref, dz_ref, up_ref, active_ref, out_ref):
    def put(left, right):
        grad = dots(left[...], right[0], 0, 0).astype(out_ref.dtype)
        out_ref[0, :, 0] = grad.reshape(out_ref.shape[1], *out_ref.shape[3:])

    @pl.when(pl.program_id(1) == 0)
    def _():
        put(hidden_ref, up_ref)

    @pl.when(pl.program_id(1) == 1)
    def _():
        put(dz_ref, active_ref)


def ff_weight_grad(shards, hidden, dz, grad_up, active):
    blocks, rows, width = active.shape
    whole = pl.BlockSpec((rows, D), lambda m, s: (0, 0))
    block = pl.BlockSpec((1, rows, width), lambda m, s: (m, 0, 0))
    return pl.pallas_call(
        ff_grad_kernel,
        grid=(blocks, 2),
        out_shape=jax.ShapeDtypeStruct((blocks, shards, 2, D // shards, width), hidden.dtype),
        in_specs=[whole, whole, block, block],
        out_specs=pl.BlockSpec((1, shards, 1, D // shards, width), lambda m, s: (m, 0, s, 0, 0)),
        cost_estimate=pl.CostEstimate(
            flops=4 * rows * D * blocks * width,
            bytes_accessed=4 * D * blocks * width,
            transcendentals=0,
        ),
        name="ff_weight_grad",
    )(hidden, dz, grad_up, active)


def score_kernel(head_ref, word_ref, bias_ref, label_ref, stat_ref, top, total, target):
    at, last = pl.program_id(1), pl.num_programs(1) - 1
    logits = dots(head_ref[...], word_ref[...], 1, 1) + bias_ref[...]
    column = at * logits.shape[1] + lax.broadcasted_iota(jnp.int32, logits.shape, 1)

    @pl.when(at == 0)
    def _():
        top[...] = jnp.full(top.shape, -jnp.inf, jnp.float32)
        total[...] = jnp.zeros(total.shape, jnp.float32)
        target[...] = jnp.zeros(target.shape, jnp.float32)

    old = top[...]
    new = jnp.maximum(old, jnp.max(logits, axis=1, keepdims=True))
    added = jnp.sum(jnp.exp(logits - new), axis=1, keepdims=True)
    total[...] = total[...] * jnp.exp(old - new) + added
    top[...] = new
    hits = jnp.where(column == label_ref[...], logits, 0.0)
    target[...] += jnp.sum(hits, axis=1, keepdims=True)

    @pl.when(at == last)
    def _():
        lane = lax.broadcasted_iota(jnp.int32, stat_ref.shape, 1)
        stat_ref[...] = jnp.where(
            lane == 0, top[...], jnp.where(lane == 1, total[...], target[...])
        )


def slope_kernel(
    head_ref, word_ref, bias_ref, label_ref, norm_ref, weight_ref, slope_ref, sum_ref, grad_ref
):
    at = pl.program_id(1)
    logits = dots(head_ref[...], word_ref[...], 1, 1) + bias_ref[...]
    column = at * logits.shape[1] + lax.broadcasted_iota(jnp.int32, logits.shape, 1)
    hits = jnp.where(column == label_ref[...], 1.0, 0.0)
    slope = ((jnp.exp(logits - norm_ref[...]) - hits) * weight_ref[...]).astype(jnp.bfloat16)
    slope_ref[...] = slope
    sum_ref[0] = jnp.sum(slope.astype(jnp.float32), axis=0, keepdims=True)
    part = dots(slope, word_ref[...], 1, 0)

    @pl.when(at == 0)
    def _():
        grad_ref[...] = part

    @pl.when(at > 0)
    def _():
        grad_ref[...] += part


def head_blocks(head, word, bias):
    rows, vocab = head.shape[0], word.shape[0]
    row_block = 512 if rows % 512 == 0 else rows
    block = 768 if vocab % 768 == 0 else vocab
    grid = (rows // row_block, vocab // block)
    column = pl.BlockSpec((row_block, 1), lambda i, j: (i, 0))
    specs = [
        pl.BlockSpec((row_block, D), lambda i, j: (i, 0)),
        pl.BlockSpec((block, D), lambda i, j: (j, 0)),
        pl.BlockSpec((1, block), lambda i, j: (0, j)),
        column,
    ]
    cost = pl.CostEstimate(
        flops=2 * rows * vocab * D, bytes_accessed=2 * vocab * D, transcendentals=rows * vocab
    )
    return row_block, block, grid, column, specs, cost


def head_scores(head, word, bias, labels):
    row_block, _, grid, _, specs, cost = head_blocks(head, word, bias)
    stats = pl.pallas_call(
        score_kernel,
        grid=grid,
        out_shape=jax.ShapeDtypeStruct((head.shape[0], 128), jnp.float32),
        in_specs=specs,
        out_specs=pl.BlockSpec((row_block, 128), lambda i, j: (i, 0)),
        scratch_shapes=[pltpu.VMEM((row_block, 1), jnp.float32)] * 3,
        cost_estimate=cost,
        name="head_scores",
    )(head, word, bias[None], labels[:, None])
    return stats[:, :3].T


def head_slopes(head, word, bias, labels, norms, weights):
    row_block, block, grid, column, specs, cost = head_blocks(head, word, bias)
    rows, vocab = head.shape[0], word.shape[0]
    slopes, sums, grad = pl.pallas_call(
        slope_kernel,
        grid=grid,
        out_shape=[
            jax.ShapeDtypeStruct((rows, vocab), head.dtype),
            jax.ShapeDtypeStruct((grid[0], 1, vocab), jnp.float32),
            jax.ShapeDtypeStruct((rows, D), jnp.float32),
        ],
        in_specs=specs + [column] * 2,
        out_specs=[
            pl.BlockSpec((row_block, block), lambda i, j: (i, j)),
            pl.BlockSpec((1, 1, block), lambda i, j: (i, 0, j)),
            pl.BlockSpec((row_block, D), lambda i, j: (i, 0)),
        ],
        cost_estimate=cost,
        name="head_slopes",
    )(head, word, bias[None], labels[:, None], norms[:, None], weights[:, None])
    return slopes, jnp.sum(sums[:, 0], axis=0), grad


def step(sizes, *args):
    (
        token_ids, type_ids, mask_pos, mask_valid, mlm_labels, nsp_labels,
        word_table, word_m, word_v, attn_weight, attn_m, attn_v,
        ff_weight, ff_m, ff_v, side_weight, side_m, side_v,
        vectors, vec_m, vec_v, split_bias, split_m, split_v,
        decoder_bias, decoder_m, decoder_v,
    ) = args
    z_size, x_size, y_size, c_size = sizes
    dp_size, mp_size = z_size * x_size, y_size * c_size
    z_at, x_at, y_at, c_at = (lax.axis_index(a) for a in ("z", "x", "y", "c"))
    dp_rank, mp_rank = z_at * x_size + x_at, y_at * c_size + c_at
    every = ("z", "x", "y", "c")
    mp_first = ("y", "c", "z", "x")
    plane = ("x", "y", "c")
    batch_size, length = token_ids.shape
    slots = mask_pos.shape[1]
    own_len, own_slots = length // c_size, slots // c_size
    vocab_own = word_table.shape[0]
    attn_cols, ff_cols = attn_weight.shape[2], ff_weight.shape[2]
    rows_own = attn_weight.shape[0]
    low = jnp.bfloat16
    links = Links(sizes)

    def mine(rows, size):
        row = lax.dynamic_index_in_dim(rows, y_at, 0, False)
        return lax.dynamic_slice_in_dim(row, c_at * size, size, 0)

    own_ids = mine(token_ids, own_len)
    own_types = mine(type_ids, own_len)
    seq_pos = lax.dynamic_index_in_dim(mask_pos, y_at, 0, False)
    own_pos = mine(mask_pos, own_slots)
    own_valid = mine(mask_valid, own_slots)
    own_labels = mine(mlm_labels, own_slots)
    first_core = (c_at == 0).astype(jnp.float32)

    side_rows = side_weight.shape[0] // mp_size
    vec_cols = vectors.shape[1]
    stripe = vocab_own * x_size
    bias_mine = lax.dynamic_slice_in_dim(decoder_bias, z_at * stripe, stripe, 0)
    int_count = own_len + 2 * own_slots
    word_parts = 4 if vocab_own % 64 == 0 else 1
    word_plane, ints, vec_parts, counts, mp_small = links.exchange(
        "word_gather",
        ("plane", plane, 0, BIG, word_table.astype(low).reshape(word_parts, -1, D)),
        ("gather", ("z",), 0, FAST, lanes(jnp.concatenate([own_ids, own_labels, own_valid]))),
        ("gather", ("z", "x"), 0, FAST, jnp.pad(vectors.astype(low), ((0, 0), (0, 128 - vec_cols)))),
        (
            "gather",
            ("z", "x"),
            0,
            FAST,
            jnp.full((8, 128), jnp.sum(mask_valid.astype(jnp.float32))),
        ),
        ("gather", ("y", "c"), 0, FAST, lanes(jnp.concatenate([bias_mine, split_bias.reshape(-1)]))),
    )
    ints = ints.reshape(z_size, -1)[:, :int_count]
    z_ids, z_labels, z_valid = (
        ints[:, :own_len],
        ints[:, own_len : own_len + own_slots],
        ints[:, own_len + own_slots :],
    )
    total_count = jnp.sum(counts[:, 0, 0])
    total_seqs = jnp.float32(batch_size * dp_size)
    vec_rows = (
        vec_parts[:, :, :vec_cols]
        .transpose(1, 0, 2)
        .reshape(vectors.shape[0], D)
        .astype(jnp.float32)
    )
    mp_small = mp_small.reshape(mp_size, -1)
    word_plane = word_plane.reshape(-1, D)
    side_own = lax.dynamic_slice_in_dim(side_weight, mp_rank * side_rows, side_rows, 0)
    both = jnp.concatenate([attn_weight.reshape(rows_own, 4 * attn_cols), side_own]).astype(low)
    ff_own = ff_weight.astype(low).reshape(rows_own, 2 * ff_cols)
    word_plane, both, ff_own = lax.optimization_barrier((word_plane, both, ff_own))
    both = comm_all_gather(both, mp_first).reshape(mp_size, dp_size, -1, D)
    attn_blocks = both[:, :, :rows_own].reshape(mp_size, D, 4 * attn_cols)
    side_full = both[:, :, rows_own:].transpose(1, 0, 2, 3).reshape(-1, D)
    ff_blocks = comm_all_gather(ff_own, mp_first).reshape(mp_size, D, 2 * ff_cols)
    bias_plane = (
        mp_small[:, :stripe].reshape(mp_size, x_size, vocab_own).transpose(1, 0, 2).reshape(-1)
    )
    split_full = mp_small[:, stripe : stripe + 6 * attn_cols].reshape(mp_size, 6, attn_cols)

    def plane_index(ids):
        block = ids // stripe
        offset = ids % stripe
        inside = block % z_size == z_at
        at = ((offset // vocab_own) * mp_size + block // z_size) * vocab_own + offset % vocab_own
        return inside, at

    flat_ids = z_ids.reshape(-1)
    inside, at = plane_index(flat_ids)
    looked = jnp.where(inside[:, None], word_plane[jnp.where(inside, at, 0)], jnp.zeros((), low))
    if z_size <= 8:
        looked = looked.reshape(z_size, 8, own_len // 8, D)
        embedded = links.fold("token_fold", looked).reshape(own_len, D).astype(jnp.float32)
    else:
        looked = looked.reshape(z_size, own_len, D)
        (found,) = links.exchange("token_spread", ("spread", ("z",), 0, BIG, looked))
        embedded = lax.dynamic_index_in_dim(looked, z_at, 0, False).astype(jnp.float32)
        embedded = embedded + jnp.sum(found.astype(jnp.float32), axis=0)
    position_rows = lax.dynamic_slice_in_dim(side_full, 2 * D + c_at * own_len, own_len, 0)
    embedded = (
        embedded
        + position_rows.astype(jnp.float32)
        + jnp.where(own_types[:, None] == 0, vec_rows[12], vec_rows[13])
    )
    hidden0 = layer_norm(embedded, vec_rows[0], vec_rows[1])
    hidden0_b = hidden0.astype(low)

    out_blocks = attn_blocks[:, :, 3 * attn_cols :]
    head_bias = split_full[:, :2].transpose(1, 0, 2).reshape(2, D)
    queries, own_keys, own_values = project(hidden0_b, attn_blocks, head_bias)
    other_keys, other_values = links.exchange(
        "key_trade", ("trade", ("c",), 0, FAST, own_keys), ("trade", ("c",), 0, FAST, own_values)
    )
    keys, values = (own_keys, other_keys), (own_values, other_values)
    mixed, log_norm = attention_forward(queries, keys, values)
    attn_out = jnp.einsum(
        "tme,mde->td",
        mixed.reshape(own_len, mp_size, attn_cols),
        out_blocks,
        preferred_element_type=jnp.float32,
    )
    resid1 = hidden0 + (attn_out + vec_rows[2])
    hidden1 = layer_norm(resid1, vec_rows[3], vec_rows[4])
    hidden1_b = hidden1.astype(low)
    ff_bias = split_full[:, 2:6].transpose(0, 2, 1).reshape(mp_size, ff_cols)
    ff_in, ff_out = ff_blocks[:, :, :ff_cols], ff_blocks[:, :, ff_cols:]
    upward = jnp.einsum("td,mdf->mtf", hidden1_b, ff_in, preferred_element_type=jnp.float32)
    upward = upward + ff_bias[:, None]
    active = gelu_exact(upward).astype(low)
    ffn_out = jnp.einsum("mtf,mdf->td", active, ff_out, preferred_element_type=jnp.float32)
    resid2 = hidden1 + (ffn_out + vec_rows[5])
    hidden2 = layer_norm(resid2, vec_rows[6], vec_rows[7])

    hidden2_b = hidden2.astype(low)
    (other_h2,) = links.exchange("hidden_trade", ("trade", ("c",), 0, FAST, hidden2_b))
    picked_b = jnp.concatenate([hidden2_b, other_h2])[
        own_pos % own_len + jnp.where(own_pos // own_len == c_at, 0, own_len)
    ]
    dense_w = side_full[D : 2 * D]
    dense_out = jnp.dot(picked_b, dense_w, preferred_element_type=jnp.float32) + vec_rows[8]
    act_dense = gelu_exact(dense_out)
    head_rows = layer_norm(act_dense, vec_rows[9], vec_rows[10])
    (head_b,) = links.exchange("head_gather", links.line_move(head_rows.astype(low), 32, FAST))
    head_b = head_b.reshape(-1, D)
    label_in, label_at = plane_index(z_labels.reshape(-1))
    label_at = jnp.where(label_in, label_at, -1)
    stats = jnp.pad(head_scores(head_b, word_plane, bias_plane, label_at), ((0, 5), (0, 0)))
    (stats,) = links.exchange("stat_gather", ("gather", ("z",), 0, FAST, stats))
    top_all = jnp.max(stats[:, 0], axis=0)
    total_all = jnp.sum(stats[:, 1] * jnp.exp(stats[:, 0] - top_all), axis=0)
    target_all = jnp.sum(stats[:, 2], axis=0)
    log_total = top_all + jnp.log(total_all)
    valid_rows = z_valid.reshape(-1).astype(jnp.float32)
    mlm_sum = -jnp.sum(valid_rows * (target_all - log_total))
    weight_rows = valid_rows / total_count
    grad_logits, decoder_part, head_part = head_slopes(
        head_b, word_plane, bias_plane, label_at, log_total, weight_rows
    )
    head_part = head_part.reshape(z_size, own_slots, D)
    (head_others,) = links.exchange("head_spread", ("spread", ("z",), 0, FAST, head_part.astype(low)))
    grad_head = lax.dynamic_index_in_dim(head_part, z_at, 0, False) + jnp.sum(
        head_others.astype(jnp.float32), axis=0
    )
    grad_act, grad_g9, grad_s9 = norm_backward(act_dense, vec_rows[9], vec_rows[10], grad_head)
    grad_dense = (grad_act * gelu_slope(dense_out)).astype(low)
    dense_bias_grad = jnp.sum(grad_dense.astype(jnp.float32), axis=0)
    dense_grad = jnp.einsum("rd,re->de", picked_b, grad_dense, preferred_element_type=jnp.float32)
    grad_picked = jnp.einsum("re,de->rd", grad_dense, dense_w, preferred_element_type=jnp.float32)
    (other_picked,) = links.exchange("picked_trade", ("trade", ("c",), 0, FAST, grad_picked))
    seq_picked = jnp.concatenate([grad_picked, other_picked])
    other_pos = lax.dynamic_slice_in_dim(seq_pos, (1 - c_at) * own_slots, own_slots, 0)
    place = (
        jnp.concatenate([own_pos, other_pos])[None, :]
        == c_at * own_len + lax.broadcasted_iota(jnp.int32, (own_len, slots), 0)
    ).astype(jnp.float32)
    grad_top = jnp.dot(place, seq_picked, precision=highest)

    cls_row = hidden2_b[0:1]
    pooler_w = side_full[:D]
    pooled = jnp.tanh(jnp.dot(cls_row, pooler_w, preferred_element_type=jnp.float32) + vec_rows[11])
    classes = vec_rows[14:16]
    nsp_logp = jax.nn.log_softmax(jnp.dot(pooled, classes.T, precision=highest), axis=-1)
    own_nsp = lax.dynamic_slice_in_dim(nsp_labels, y_at, 1, 0)
    pick_nsp = own_nsp[:, None] == lax.broadcasted_iota(jnp.int32, (1, 2), 1)
    nsp_sum = -jnp.sum(jnp.where(pick_nsp, nsp_logp, 0.0)) * first_core
    grad_nsp = (jnp.exp(nsp_logp) - pick_nsp.astype(jnp.float32)) / total_seqs * first_core
    class_grad = grad_nsp[0][:, None] * pooled
    grad_pre = jnp.dot(grad_nsp, classes, precision=highest) * (1.0 - pooled * pooled)
    pooler_bias_grad = grad_pre[0]
    pooler_grad = cls_row.astype(jnp.float32).T * grad_pre
    grad_cls = jnp.dot(grad_pre, pooler_w.astype(jnp.float32).T, precision=highest)
    first_row = lax.broadcasted_iota(jnp.int32, (own_len, 1), 0) == 0
    grad_top = grad_top + jnp.where(first_row, grad_cls, 0.0)

    grad_r2, grad_g2, grad_s2 = norm_backward(resid2, vec_rows[6], vec_rows[7], grad_top)
    ffn_grad_b = grad_r2.astype(low)
    out_bias_two = jnp.sum(ffn_grad_b.astype(jnp.float32), axis=0)
    grad_active = jnp.einsum("td,mdf->mtf", ffn_grad_b, ff_out, preferred_element_type=jnp.float32)
    grad_up = (grad_active * gelu_slope(upward)).astype(low)
    ff_bias_grad = jnp.sum(grad_up.astype(jnp.float32), axis=1)
    hidden1_part = jnp.einsum("mtf,mdf->td", grad_up, ff_in, preferred_element_type=jnp.float32)
    if rows_own % 16 == 0:
        ff_grad = ff_weight_grad(dp_size, hidden1_b, ffn_grad_b, grad_up, active)
    else:
        ff_grad = jnp.stack(
            [
                jnp.einsum("td,mtf->mdf", left, right, preferred_element_type=jnp.float32)
                .astype(low)
                .reshape(mp_size * dp_size, rows_own, ff_cols)
                for left, right in ((hidden1_b, grad_up), (ffn_grad_b, active))
            ],
            axis=1,
        )
    ff_grad, hidden1_part = lax.optimization_barrier((ff_grad, hidden1_part))
    ff_red = comm_scatter_sum(ff_grad.reshape(-1, ff_cols), mp_first)
    grad_h1 = grad_r2 + hidden1_part
    grad_r1, grad_g1, grad_s1 = norm_backward(resid1, vec_rows[3], vec_rows[4], grad_h1)
    attn_grad_b = grad_r1.astype(low)
    out_bias_one = jnp.sum(attn_grad_b.astype(jnp.float32), axis=0)
    grad_mixed = projected(mixed_grad_kernel, "mixed_grad", low, attn_grad_b, attn_blocks)
    grad_q, own_k, part_k, own_v, part_v = attention_backward(
        queries, keys, values, log_norm, grad_mixed
    )
    from_k, from_v = links.exchange(
        "key_grad_trade",
        ("trade", ("c",), 0, FAST, part_k),
        ("trade", ("c",), 0, FAST, part_v),
    )
    grad_k = (own_k + from_k).astype(low)
    grad_v = (own_v + from_v).astype(low)
    packed_sums = jnp.stack(
        [
            jnp.sum(g.astype(jnp.float32), axis=0).reshape(mp_size, attn_cols)
            for g in (grad_q, grad_v)
        ],
        axis=1,
    )
    hidden0_part = projected(
        hidden_grad_kernel, "hidden_grad", jnp.float32, grad_q, grad_k, grad_v, attn_blocks
    )
    attn_grad = attn_weight_grad(mp_size, hidden0_b, grad_q, grad_k, grad_v, attn_grad_b, mixed)
    attn_grad = attn_grad.reshape(y_size, c_size, z_size, x_size, rows_own, 4 * attn_cols)
    grad_h0 = grad_r1 + hidden0_part
    grad_x0, grad_g0, grad_s0 = norm_backward(embedded, vec_rows[0], vec_rows[1], grad_h0)

    position_grad = lax.dynamic_update_slice_in_dim(
        jnp.zeros((length, D), low), grad_x0.astype(low), c_at * own_len, 0
    )
    side_grad = jnp.concatenate([pooler_grad.astype(low), dense_grad.astype(low), position_grad], axis=0)
    side_grad = side_grad.reshape(z_size, x_size, y_size, c_size, side_rows, D)

    def joined(value, at, dim, received):
        kept = lax.dynamic_index_in_dim(value, at, dim, False)
        return (kept.astype(jnp.float32) + received.astype(jnp.float32)).astype(low)

    x0_b = grad_x0.astype(low)
    cut_one, cut_two = own_len // 8, 5 * own_len // 8
    from_a, from_s, x0_one = links.exchange(
        "grad_swap_c",
        ("swap", ("c",), 1, BIG, attn_grad),
        ("swap", ("c",), 3, BIG, side_grad),
        links.line_move(x0_b[:cut_one], 64, BIG),
    )
    attn_grad, side_grad = joined(attn_grad, c_at, 1, from_a), joined(side_grad, c_at, 3, from_s)
    from_a, from_s, x0_two = links.exchange(
        "grad_swap_xy",
        ("swap", ("x",), 2, BIG, attn_grad),
        ("swap", ("y",), 2, BIG, side_grad),
        links.line_move(x0_b[cut_one:cut_two], 64, BIG),
    )
    attn_grad, side_grad = joined(attn_grad, x_at, 2, from_a), joined(side_grad, y_at, 2, from_s)
    from_a, from_s, x0_three = links.exchange(
        "grad_swap_yx",
        ("swap", ("y",), 0, BIG, attn_grad),
        ("swap", ("x",), 1, BIG, side_grad),
        links.line_move(x0_b[cut_two:], 64, BIG),
    )
    attn_grad, side_grad = joined(attn_grad, y_at, 0, from_a), joined(side_grad, x_at, 1, from_s)

    ff_red, x0_three = lax.optimization_barrier((ff_red, x0_three))
    all_x0 = [x.reshape(z_size, -1, D) for x in (x0_one, x0_two, x0_three)]
    all_x0 = jnp.concatenate(all_x0, axis=1).reshape(-1, D)
    onehot = (
        jnp.where(inside, at, -1)[None, :]
        == lax.broadcasted_iota(jnp.int32, (word_plane.shape[0], flat_ids.shape[0]), 0)
    ).astype(low)
    word_grad = jnp.einsum("rv,rd->vd", grad_logits, head_b, preferred_element_type=jnp.float32)
    word_grad = word_grad + jnp.dot(onehot, all_x0, preferred_element_type=jnp.float32)
    word_grad, attn_grad, side_grad = lax.optimization_barrier(
        (word_grad.astype(low), attn_grad, side_grad)
    )
    word_red = comm_scatter_sum(word_grad, plane).astype(jnp.float32)
    from_a, from_s = links.exchange(
        "grad_spread_z", ("spread", ("z",), 0, BIG, attn_grad), ("spread", ("z",), 0, BIG, side_grad)
    )

    def total(value, received):
        kept = lax.dynamic_index_in_dim(value, z_at, 0, False).astype(jnp.float32)
        return kept + jnp.sum(received.astype(jnp.float32), axis=0)

    attn_red, side_quarter = total(attn_grad, from_a), total(side_grad, from_s)
    type_zero = jnp.sum(jnp.where(own_types[:, None] == 0, grad_x0, 0.0), axis=0)
    type_one = jnp.sum(jnp.where(own_types[:, None] == 1, grad_x0, 0.0), axis=0)
    vec_grad = jnp.stack(
        [
            grad_g0, grad_s0, out_bias_one, grad_g1, grad_s1, out_bias_two, grad_g2, grad_s2,
            dense_bias_grad, grad_g9, grad_s9, pooler_bias_grad, type_zero, type_one,
            class_grad[0], class_grad[1],
        ],
        axis=0,
    )
    split_grad = jnp.concatenate(
        [
            packed_sums,
            ff_bias_grad.reshape(mp_size, attn_cols, 4).transpose(0, 2, 1),
        ],
        axis=1,
    )
    late = lanes(jnp.concatenate([vec_grad.reshape(-1), split_grad.reshape(-1), decoder_part]))
    late, side_quarter = lax.optimization_barrier((late, side_quarter))
    small = links.combine(
        "small_sum",
        late,
    ).reshape(z_size, -1)
    (side_red,) = links.exchange(
        "side_gather", ("gather", ("y", "c"), 0, FAST, side_quarter.astype(low))
    )
    side_red = side_red.reshape(side_weight.shape).astype(jnp.float32)
    narrow = vec_grad.size + split_grad.size
    summed = jnp.sum(small[:, :narrow], axis=0)
    vec_all = summed[: vec_grad.size].reshape(vec_grad.shape)
    split_all = summed[vec_grad.size :].reshape(split_grad.shape)
    vec_red = lax.dynamic_slice_in_dim(vec_all, dp_rank * vec_cols, vec_cols, 1)
    split_red = lax.dynamic_index_in_dim(split_all, mp_rank, 0, False)
    decoder_red = lax.dynamic_index_in_dim(
        small[:, narrow : narrow + decoder_part.size].reshape(z_size, x_size, mp_size, vocab_own),
        mp_rank,
        2,
        False,
    ).reshape(-1)
    word_f, attn_f, ff_f = (
        word_red,
        attn_red.reshape(attn_weight.shape),
        row_major(
            ff_red.astype(jnp.float32).reshape(2, rows_own, ff_cols).transpose(1, 0, 2)
        ),
    )
    own_square = (
        jnp.sum(word_f * word_f)
        + jnp.sum(attn_f * attn_f)
        + jnp.sum(ff_f * ff_f)
        + jnp.sum(side_red * side_red) / mp_size
        + jnp.sum(vec_red * vec_red) / mp_size
        + (jnp.sum(split_red * split_red) + jnp.sum(decoder_red * decoder_red)) / dp_size
    )
    loss_part = mlm_sum / total_count / z_size + nsp_sum / total_seqs
    ends = jnp.where(
        lax.broadcasted_iota(jnp.int32, (8, 128), 0) == 0, own_square, loss_part
    )
    ends = jnp.sum(links.combine("norm_sum", ends), axis=0)
    grad_square, total_loss = ends[0, 0], ends[1, 0]
    grad_norm = jnp.sqrt(grad_square)
    clip_scale = max_norm / jnp.maximum(grad_norm, max_norm)
    return (
        total_loss,
        grad_norm,
        *adam_step(word_table, word_m, word_v, word_f, clip_scale, True),
        *adam_step(attn_weight, attn_m, attn_v, attn_f, clip_scale, True),
        *adam_step(ff_weight, ff_m, ff_v, ff_f, clip_scale, True),
        *adam_step(side_weight, side_m, side_v, side_red, clip_scale, True),
        *adam_step(vectors, vec_m, vec_v, vec_red, clip_scale, False),
        *adam_step(split_bias, split_m, split_v, split_red, clip_scale, False),
        *adam_step(decoder_bias, decoder_m, decoder_v, decoder_red, clip_scale, False),
    )


def solution(mesh):
    dp_size, mp_size = mesh.shape["dp"], mesh.shape["mp"]
    x_size = 2 if dp_size % 2 == 0 else 1
    c_size = 2 if mp_size % 2 == 0 else 1
    sizes = (dp_size // x_size, x_size, mp_size // c_size, c_size)
    fine = Mesh(mesh.devices.reshape(sizes), ("z", "x", "y", "c"))
    dp, mp = ("z", "x"), ("y", "c")
    word = P(("y", "c", "z", "x"), None)
    cube = P(dp, None, mp)
    kinds = (
        [P(dp, None)] * 5
        + [P(dp)]
        + [word] * 3
        + [cube] * 6
        + [P(dp, None)] * 3
        + [P(None, dp)] * 3
        + [P(None, mp)] * 3
        + [P(mp)] * 3
    )
    return jax.shard_map(
        functools.partial(step, sizes),
        mesh=fine,
        in_specs=tuple(kinds),
        out_specs=(P(), P(), *kinds[6:]),
        check_vma=False,
    )
```

```python
import functools
import math

import jax
import jax.numpy as jnp
from jax import lax
from jax.experimental.layout import Layout, with_layout_constraint
from jax.experimental import pallas as pl
from jax.experimental.pallas import tpu as pltpu
from jax.sharding import Mesh, PartitionSpec as P

D = 768
HEAD_DIM = 64


beta_one = 0.9
beta_two = 0.999
adam_eps = 1e-06
learn_rate = 0.2
decay_rate = 0.01
step_count = 10
max_norm = 0.05
norm_eps = 1e-12
highest = lax.Precision.HIGHEST


def layer_norm(inputs, norm_gain, norm_shift):
    center = inputs - jnp.mean(inputs, axis=-1, keepdims=True)
    spread = jnp.mean(center * center, axis=-1, keepdims=True)
    return center * lax.rsqrt(spread + norm_eps) * norm_gain + norm_shift


def normal_cdf(inputs):
    return 0.5 + 0.5 * lax.erf(inputs * math.sqrt(0.5))


def gelu_exact(inputs):
    return inputs * normal_cdf(inputs)


def gelu_slope(inputs):
    density = jnp.exp(-0.5 * inputs * inputs) * (1.0 / math.sqrt(2.0 * math.pi))
    return normal_cdf(inputs) + inputs * density


def norm_backward(inputs, norm_gain, norm_shift, upstream):
    _, pullback = jax.vjp(layer_norm, inputs, norm_gain, norm_shift)
    return pullback(upstream)


def adam_step(weight, moment, square, gradient, clip_scale, decays):
    gradient = gradient * clip_scale
    moment = beta_one * moment + (1 - beta_one) * gradient
    square = beta_two * square + (1 - beta_two) * gradient * gradient
    mean_hat = moment / (1 - beta_one**step_count)
    var_hat = square / (1 - beta_two**step_count)
    change = mean_hat / (jnp.sqrt(var_hat) + adam_eps)
    if decays:
        change = change + decay_rate * weight
    return (weight - learn_rate * change, moment, square)


def comm_all_gather(value, axes):
    return lax.all_gather(value, axes, axis=0, tiled=True)


def comm_scatter_sum(value, axes):
    return lax.psum_scatter(value, axes, scatter_dimension=0, tiled=True)


MESH = pl.DeviceIdType.MESH
BIG, FAST = pl.ANY, pltpu.VMEM


class Links:
    def __init__(self, sizes):
        self.sizes = dict(zip(("z", "x", "y", "c"), sizes))
        self.used = 0

    def next_id(self):
        self.used += 1
        return self.used - 1

    def count(self, axes):
        return math.prod(self.sizes[a] for a in axes)

    def place(self, axes):
        at = 0
        for a in axes:
            at = at * self.sizes[a] + lax.axis_index(a)
        return at

    def target(self, axes, flat):
        where = {}
        for a in reversed(axes):
            where[a] = lax.rem(flat, self.sizes[a])
            flat = lax.div(flat, self.sizes[a])
        return where

    def greet(self, groups):
        barrier = pltpu.get_barrier_semaphore()
        total = 0
        for axes in groups:
            size, me = self.count(axes), self.place(axes)
            for r in range(1, size):
                pl.semaphore_signal(
                    barrier,
                    inc=1,
                    device_id=self.target(axes, lax.rem(me + r, size)),
                    device_id_type=MESH,
                )
            total += size - 1
        pl.semaphore_wait(barrier, total)

    def call(self, kernel, outs, spaces, out_spaces, scratch, values, wire, name):
        result = pl.pallas_call(
            kernel,
            out_shape=outs,
            in_specs=[pl.BlockSpec(memory_space=m) for m in spaces],
            out_specs=[pl.BlockSpec(memory_space=m) for m in out_spaces],
            scratch_shapes=scratch,
            compiler_params=pltpu.CompilerParams(
                collective_id=self.next_id(),
                has_side_effects=True,
                vmem_limit_bytes=40 * 2**20,
            ),
            cost_estimate=pl.CostEstimate(flops=0, bytes_accessed=wire, transcendentals=0),
            name=name,
        )(*values)
        return result

    def exchange(self, name, *moves):
        outs, scratch = [], []
        for kind, axes, dim, _, value in moves:
            size = self.count(axes)
            shape, sends, lands = value.shape, (size - 1,), (size - 1,)
            if kind == "gather":
                shape = (size, *shape)
            elif kind == "swap":
                shape = shape[:dim] + shape[dim + 1 :]
            elif kind == "spread":
                shape = (size - 1, *shape[1:])
            elif kind == "relay":
                shape, sends = (size, *shape), (2, size - 1, shape[0])
                lands = sends
            elif kind == "plane":
                shape, sends, lands = (2, 2, 2, *shape), (7 * shape[0],), (7, shape[0])
            outs.append(jax.ShapeDtypeStruct(shape, value.dtype))
            scratch += [
                pltpu.SemaphoreType.DMA(sends),
                pltpu.SemaphoreType.DMA(lands),
                pltpu.SemaphoreType.DMA((1,)),
            ]
        spaces = [m[3] for m in moves]
        groups = []
        for kind, axes, *_ in moves:
            groups += [(a,) for a in axes] if kind == "plane" else [axes]
        groups = list(dict.fromkeys(groups))

        def kernel(*refs):
            ins, dests = refs[: len(moves)], refs[len(moves) : 2 * len(moves)]
            sems = refs[2 * len(moves) :]
            self.greet(groups)
            started, later = [], []
            for i, ((kind, axes, dim, _, _), source, dest) in enumerate(zip(moves, ins, dests)):
                sends, lands, own_sem = sems[3 * i : 3 * i + 3]
                size, me = self.count(axes), self.place(axes)
                if kind in ("relay", "plane"):
                    act = self.relay if kind == "relay" else self.plane
                    later.append(functools.partial(act, axes, source, dest, sends, lands))
                for r in range(1, size):
                    peer = lax.rem(me + r, size)
                    if kind == "gather":
                        src, dst = source, dest.at[me]
                    elif kind == "swap":
                        src, dst = source.at[(slice(None),) * dim + (peer,)], dest
                    elif kind == "spread":
                        src, dst = source.at[peer], dest.at[r - 1]
                    elif kind == "trade":
                        src, dst = source, dest
                    else:
                        continue
                    copy = pltpu.make_async_remote_copy(
                        src_ref=src,
                        dst_ref=dst,
                        send_sem=sends.at[r - 1],
                        recv_sem=lands.at[r - 1],
                        device_id=self.target(axes, peer),
                        device_id_type=MESH,
                    )
                    copy.start()
                    started.append(copy)
            runs = [act() for act in later]
            for run in runs:
                next(run)
            for i, ((kind, axes, *_), source, dest) in enumerate(zip(moves, ins, dests)):
                if kind in ("gather", "relay", "plane"):
                    at = self.place(axes)
                    if kind == "plane":
                        at = tuple(lax.axis_index(a) for a in axes)
                    copy = pltpu.make_async_copy(source, dest.at[at], sems[3 * i + 2].at[0])
                    copy.start()
                    started.append(copy)
            for run in runs:
                next(run, None)
            for copy in started:
                copy.wait()

        return self.call(
            kernel,
            outs,
            spaces,
            spaces,
            scratch,
            [m[4] for m in moves],
            sum(2 * math.prod(o.shape) * o.dtype.itemsize for o in outs),
            name,
        )

    def relay(self, axes, source, dest, sends, lands):
        (axis,) = axes
        size, parts = self.sizes[axis], source.shape[0]
        me = lax.axis_index(axis)

        def copy_of(way, hop, part):
            step = 1 if way == 0 else -1
            place = (me - step * hop, part)
            return pltpu.make_async_remote_copy(
                src_ref=source.at[part] if hop == 0 else dest.at[place],
                dst_ref=dest.at[place],
                send_sem=sends.at[way, hop, part],
                recv_sem=lands.at[way, hop, part],
                device_id={axis: me + step},
                device_id_type=MESH,
            )

        def landing(way, hop, part):
            step = 1 if way == 0 else -1
            landed = dest.at[me - step * hop, part]
            return pltpu.make_async_remote_copy(
                src_ref=landed,
                dst_ref=landed,
                send_sem=sends.at[way, hop - 1, part],
                recv_sem=lands.at[way, hop - 1, part],
                device_id={axis: me - step},
                device_id_type=MESH,
            )

        def held(way, hop):
            return me - hop >= 0 if way == 0 else me + hop <= size - 1

        def sending(way, hop):
            return held(way, hop) & (me < size - 1 if way == 0 else me > 0)

        for hop in range(size):
            for part in range(parts):
                for way in range(2):
                    if hop > 0:

                        @pl.when(held(way, hop))
                        def _():
                            landing(way, hop, part).wait_recv()

                    if hop < size - 1:

                        @pl.when(sending(way, hop))
                        def _():
                            copy_of(way, hop, part).start()

            if hop == 0:
                yield
        for hop in range(size - 1):
            for part in range(parts):
                for way in range(2):

                    @pl.when(sending(way, hop))
                    def _():
                        copy_of(way, hop, part).wait_send()

    def plane(self, axes, own, out, sends, lands):
        parts = own.shape[0]
        head = (parts + 1) // 2
        x, y, c = (lax.axis_index(a) for a in axes)
        by_x, by_y, by_c = {"x": 1 - x}, {"y": 1 - y}, {"c": 1 - c}
        started = []

        def send(src, place, part, slot, peer):
            copy = pltpu.make_async_remote_copy(
                src_ref=src,
                dst_ref=out.at[(*place, part)],
                send_sem=sends.at[len(started)],
                recv_sem=lands.at[slot, part],
                device_id=peer,
                device_id_type=MESH,
            )
            copy.start()
            started.append(copy)

        def arrived(place, part, slot):
            landed = out.at[(*place, part)]
            pltpu.make_async_remote_copy(
                src_ref=landed,
                dst_ref=landed,
                send_sem=sends.at[0],
                recv_sem=lands.at[slot, part],
                device_id=by_c,
                device_id_type=MESH,
            ).wait_recv()
            return landed

        me, at_x, at_y, at_xy = (x, y, c), (1 - x, y, c), (x, 1 - y, c), (1 - x, 1 - y, c)
        for part in range(parts):
            send(own.at[part], me, part, 0, by_x)
            send(own.at[part], me, part, 1, by_y)
        for part in range(parts):
            send(own.at[part], me, part, 3, by_c)
        yield
        for part in range(parts):
            landed = arrived(at_x, part, 0)
            if part < head:
                send(landed, at_x, part, 2, by_y)
            send(landed, at_x, part, 4, by_c)
            landed = arrived(at_y, part, 1)
            if part >= head:
                send(landed, at_y, part, 2, by_x)
            send(landed, at_y, part, 5, by_c)
        for part in range(parts):
            landed = arrived(at_xy, part, 2)
            send(landed, at_xy, part, 6, by_c)
        for slot, place in ((3, me), (4, at_x), (5, at_y), (6, at_xy)):
            for part in range(parts):
                arrived((place[0], place[1], 1 - c), part, slot)
        for copy in started:
            copy.wait_send()

    def fold(self, name, value):
        size, parts = value.shape[:2]
        block = value.shape[1:]

        def kernel(source, out, land, sends, lands):
            self.greet([("z",)])
            me = lax.axis_index("z")

            def beyond(way, hop):
                return me + hop <= size - 1 if way == 0 else me - hop >= 0

            def behind(way):
                return me > 0 if way == 0 else me < size - 1

            def copy_of(way, hop, part, src):
                return pltpu.make_async_remote_copy(
                    src_ref=src,
                    dst_ref=land.at[way, hop - 1, part],
                    send_sem=sends.at[way, hop - 1, part],
                    recv_sem=lands.at[way, hop - 1, part],
                    device_id={"z": me + (1 if way == 0 else -1)},
                    device_id_type=MESH,
                )

            def landing(way, hop, part):
                landed = land.at[way, hop, part]
                return pltpu.make_async_remote_copy(
                    src_ref=landed,
                    dst_ref=landed,
                    send_sem=sends.at[way, hop, part],
                    recv_sem=lands.at[way, hop, part],
                    device_id={"z": me - (1 if way == 0 else -1)},
                    device_id_type=MESH,
                )

            for hop in range(size - 1, 0, -1):
                for part in range(parts):
                    for way in range(2):
                        goal = me + hop if way == 0 else me - hop

                        @pl.when(beyond(way, hop) & jnp.logical_not(behind(way)))
                        def _():
                            copy_of(way, hop, part, source.at[goal, part]).start()

                        if hop < size - 1:

                            @pl.when(beyond(way, hop) & behind(way))
                            def _():
                                landing(way, hop, part).wait_recv()
                                land[way, hop, part] += source[goal, part]
                                copy_of(way, hop, part, land.at[way, hop, part]).start()

            for part in range(parts):
                out[part] = source[me, part]
                for way in range(2):

                    @pl.when(behind(way))
                    def _():
                        landing(way, 0, part).wait_recv()
                        out[part] += land[way, 0, part]

            for hop in range(size - 1, 0, -1):
                for part in range(parts):
                    for way in range(2):

                        @pl.when(beyond(way, hop))
                        def _():
                            copy_of(way, hop, part, source.at[0, part]).wait_send()

        return self.call(
            kernel,
            [jax.ShapeDtypeStruct(block, value.dtype)],
            [FAST],
            [FAST],
            [
                pltpu.VMEM((2, size - 1, *block), value.dtype),
                pltpu.SemaphoreType.DMA((2, size - 1, parts)),
                pltpu.SemaphoreType.DMA((2, size - 1, parts)),
            ],
            [value],
            4 * value.size,
            name,
        )[0]

    def line_move(self, value, part_rows, memory):
        parts = value.shape[0] // part_rows if value.shape[0] % part_rows == 0 else 1
        kind = "relay" if self.sizes["z"] <= 8 else "gather"
        return (kind, ("z",), 0, memory, value.reshape(parts, -1, value.shape[1]))

    def combine(self, name, value):
        pairs = [a for a in ("c", "x", "y") if self.sizes[a] > 1]
        depth = self.sizes["z"]
        steps = len(pairs)

        def kernel(x_ref, out_ref, sums, land, sends, lands):
            self.greet([(a,) for a in pairs] + [("z",)])
            me = lax.axis_index("z")
            for i, a in enumerate(pairs):
                source = x_ref if i == 0 else sums.at[i - 1]
                copy = pltpu.make_async_remote_copy(
                    src_ref=source,
                    dst_ref=land.at[i],
                    send_sem=sends.at[i],
                    recv_sem=lands.at[i],
                    device_id={a: 1 - lax.axis_index(a)},
                    device_id_type=MESH,
                )
                copy.start()
                copy.wait()
                sums[i] = source[...] + land[i]
            out_ref[me] = sums[steps - 1]
            started = []
            for r in range(1, depth):
                copy = pltpu.make_async_remote_copy(
                    src_ref=sums.at[steps - 1],
                    dst_ref=out_ref.at[me],
                    send_sem=sends.at[steps + r - 1],
                    recv_sem=lands.at[steps + r - 1],
                    device_id={"z": lax.rem(me + r, depth)},
                    device_id_type=MESH,
                )
                copy.start()
                started.append(copy)
            for copy in started:
                copy.wait()

        return self.call(
            kernel,
            [jax.ShapeDtypeStruct((depth, *value.shape), value.dtype)],
            [FAST],
            [FAST],
            [
                pltpu.VMEM((steps, *value.shape), value.dtype),
                pltpu.VMEM((steps, *value.shape), value.dtype),
                pltpu.SemaphoreType.DMA((steps + depth - 1,)),
                pltpu.SemaphoreType.DMA((steps + depth - 1,)),
            ],
            [value],
            16 * value.size * 4,
            name,
        )[0]


def row_major(value):
    return with_layout_constraint(value, Layout(major_to_minor=tuple(range(value.ndim))))


def lanes(flat):
    padded = jnp.pad(flat, (0, -flat.size % 1024))
    return padded.reshape(-1, 128)


HEAD_SCALE = math.log2(math.e) / math.sqrt(HEAD_DIM)
PAIR = 2 * HEAD_DIM
ROWS = 256


def dots(left, right, left_dim, right_dim):
    return lax.dot_general(
        left, right, (((left_dim,), (right_dim,)), ((), ())), preferred_element_type=jnp.float32
    )


def half_lanes(value, half):
    lane = lax.broadcasted_iota(jnp.int32, value.shape, 1)
    return jnp.where((lane >= HEAD_DIM) == (half == 1), value, jnp.zeros((), value.dtype))


def forward_kernel(q_ref, k0_ref, k1_ref, v0_ref, v1_ref, out_ref, norm_ref):
    keys = jnp.concatenate([k0_ref[...], k1_ref[...]], axis=0)
    values = jnp.concatenate([v0_ref[...], v1_ref[...]], axis=0)
    for start in range(0, q_ref.shape[0], ROWS):
        rows = pl.ds(start, ROWS)
        queries = q_ref[rows, :]
        halves = []
        for half in range(2):
            scores = dots(keys, half_lanes(queries, half), 1, 1)
            top = jnp.max(scores, axis=0, keepdims=True)
            powers = jnp.exp2((scores - top) * HEAD_SCALE)
            total = jnp.sum(powers, axis=0, keepdims=True)
            probs = (powers * (1.0 / total)).astype(jnp.bfloat16)
            norm_ref[0, half : half + 1, rows] = top * HEAD_SCALE + jnp.log2(total)
            mixed = dots(values, probs, 0, 0)
            halves.append(mixed[half * HEAD_DIM : (half + 1) * HEAD_DIM])
        out_ref[rows, :] = jnp.concatenate(halves, axis=0).T.astype(out_ref.dtype)


def attention_forward(queries, keys, values):
    length, width = queries.shape
    pairs = width // PAIR
    block = pl.BlockSpec((length, PAIR), lambda i: (0, i))
    flops = 8 * length * length * width
    return pl.pallas_call(
        forward_kernel,
        grid=(pairs,),
        out_shape=[
            jax.ShapeDtypeStruct((length, width), queries.dtype),
            jax.ShapeDtypeStruct((pairs, 2, length), jnp.float32),
        ],
        in_specs=[block] * 5,
        out_specs=[block, pl.BlockSpec((1, 2, length), lambda i: (i, 0, 0))],
        cost_estimate=pl.CostEstimate(
            flops=2 * flops, bytes_accessed=16 * length * width, transcendentals=flops // 256
        ),
        name="attention_forward",
    )(queries, *keys, *values)


def backward_kernel(
    q_ref, k0_ref, k1_ref, v0_ref, v1_ref, norm_ref, g_ref, dq_ref, dk0_ref, dk1_ref, dv0_ref, dv1_ref
):
    own = k0_ref.shape[0]
    keys = jnp.concatenate([k0_ref[...], k1_ref[...]], axis=0)
    values = jnp.concatenate([v0_ref[...], v1_ref[...]], axis=0)
    grad_keys = grad_values = 0.0
    for start in range(0, q_ref.shape[0], ROWS):
        rows = pl.ds(start, ROWS)
        halves = []
        for half in range(2):
            queries = half_lanes(q_ref[rows, :], half)
            upstream = half_lanes(g_ref[rows, :], half)
            scores = dots(keys, queries, 1, 1)
            probs = jnp.exp2(scores * HEAD_SCALE - norm_ref[0, half : half + 1, rows])
            grad_probs = dots(values, upstream, 1, 1)
            row_dot = jnp.sum(grad_probs * probs, axis=0, keepdims=True)
            grad_scores = (probs * (grad_probs - row_dot)).astype(jnp.bfloat16)
            grad_values = grad_values + dots(probs.astype(jnp.bfloat16), upstream, 1, 0)
            grad_keys = grad_keys + dots(grad_scores, queries, 1, 0)
            grad_queries = dots(keys, grad_scores, 0, 0)
            halves.append(grad_queries[half * HEAD_DIM : (half + 1) * HEAD_DIM])
        grad_queries = jnp.concatenate(halves, axis=0) * (1.0 / math.sqrt(HEAD_DIM))
        dq_ref[rows, :] = grad_queries.T.astype(dq_ref.dtype)
    grad_keys = grad_keys * (1.0 / math.sqrt(HEAD_DIM))
    dk0_ref[...] = grad_keys[:own]
    dk1_ref[...] = grad_keys[own:]
    dv0_ref[...] = grad_values[:own]
    dv1_ref[...] = grad_values[own:]


def attention_backward(queries, keys, values, log_norm, grad_mixed):
    length, width = queries.shape
    pairs = width // PAIR
    block = pl.BlockSpec((length, PAIR), lambda i: (0, i))
    flops = 20 * length * length * width
    wide = jax.ShapeDtypeStruct((length, width), jnp.float32)
    return pl.pallas_call(
        backward_kernel,
        grid=(pairs,),
        out_shape=[jax.ShapeDtypeStruct((length, width), queries.dtype)] + [wide] * 4,
        in_specs=[block] * 5 + [pl.BlockSpec((1, 2, length), lambda i: (i, 0, 0)), block],
        out_specs=[block] * 5,
        cost_estimate=pl.CostEstimate(
            flops=2 * flops, bytes_accessed=32 * length * width, transcendentals=flops // 640
        ),
        name="attention_backward",
    )(queries, *keys, *values, log_norm, grad_mixed)


def project_kernel(hidden_ref, weight_ref, bias_ref, q_ref, k_ref, v_ref):
    blocks, width = weight_ref.shape[0], weight_ref.shape[2] // 4
    packed = [dots(hidden_ref[...], weight_ref[m], 1, 0) for m in range(blocks)]

    def slot(at):
        return jnp.concatenate([p[:, at * width : (at + 1) * width] for p in packed], axis=1)

    q_ref[...] = (slot(0) + bias_ref[0:1]).astype(q_ref.dtype)
    k_ref[...] = slot(1).astype(k_ref.dtype)
    v_ref[...] = (slot(2) + bias_ref[1:2]).astype(v_ref.dtype)


def project(hidden, blocks, biases):
    rows = hidden.shape[0]
    return pl.pallas_call(
        project_kernel,
        out_shape=[jax.ShapeDtypeStruct((rows, D), hidden.dtype)] * 3,
        cost_estimate=pl.CostEstimate(
            flops=8 * rows * D * D, bytes_accessed=8 * D * D, transcendentals=0
        ),
        name="project_heads",
    )(hidden, blocks, biases)


def mixed_grad_kernel(dy_ref, weight_ref, out_ref):
    blocks, width = weight_ref.shape[0], weight_ref.shape[2] // 4
    dy = dy_ref[...]
    packed = [dots(dy, weight_ref[m][:, 3 * width :], 1, 0) for m in range(blocks)]
    out_ref[...] = jnp.concatenate(packed, axis=1).astype(out_ref.dtype)


def hidden_grad_kernel(dq_ref, dk_ref, dv_ref, weight_ref, out_ref):
    blocks, width = weight_ref.shape[0], weight_ref.shape[2] // 4
    grads = [r[...].astype(jnp.float32) for r in (dq_ref, dk_ref, dv_ref)]
    empty = jnp.zeros((grads[0].shape[0], width), jnp.float32)
    total = 0.0
    for m in range(blocks):
        block = [g[:, m * width : (m + 1) * width] for g in grads] + [empty]
        block = jnp.concatenate(block, axis=1).astype(weight_ref.dtype)
        total = total + dots(block, weight_ref[m], 1, 1)
    out_ref[...] = total


def projected(kernel, name, kind, *values):
    rows = values[0].shape[0]
    return pl.pallas_call(
        kernel,
        out_shape=jax.ShapeDtypeStruct((rows, D), kind),
        cost_estimate=pl.CostEstimate(
            flops=8 * rows * D * D, bytes_accessed=8 * D * D, transcendentals=0
        ),
        name=name,
    )(*values)


def attn_grad_kernel(hidden_ref, dq_ref, dk_ref, dv_ref, dy_ref, mixed_ref, out_ref):
    blocks, width = out_ref.shape[0], out_ref.shape[2] // 4
    hidden, dy = hidden_ref[...], dy_ref[...]
    grads = [dots(hidden, r[...], 0, 0) for r in (dq_ref, dk_ref, dv_ref)]
    grads.append(dots(dy, mixed_ref[...], 0, 0))
    for m in range(blocks):
        block = [g[:, m * width : (m + 1) * width] for g in grads]
        out_ref[m] = jnp.concatenate(block, axis=1).astype(out_ref.dtype)


def attn_weight_grad(blocks, *values):
    rows = values[0].shape[0]
    return pl.pallas_call(
        attn_grad_kernel,
        out_shape=jax.ShapeDtypeStruct((blocks, D, 4 * D // blocks), values[0].dtype),
        cost_estimate=pl.CostEstimate(
            flops=8 * rows * D * D, bytes_accessed=8 * D * D, transcendentals=0
        ),
        name="attn_weight_grad",
    )(*values)


def ff_grad_kernel(hidden_ref, dz_ref, up_ref, active_ref, out_ref):
    def put(left, right):
        grad = dots(left[...], right[0], 0, 0).astype(out_ref.dtype)
        out_ref[0, :, 0] = grad.reshape(out_ref.shape[1], *out_ref.shape[3:])

    @pl.when(pl.program_id(1) == 0)
    def _():
        put(hidden_ref, up_ref)

    @pl.when(pl.program_id(1) == 1)
    def _():
        put(dz_ref, active_ref)


def ff_weight_grad(shards, hidden, dz, grad_up, active):
    blocks, rows, width = active.shape
    whole = pl.BlockSpec((rows, D), lambda m, s: (0, 0))
    block = pl.BlockSpec((1, rows, width), lambda m, s: (m, 0, 0))
    return pl.pallas_call(
        ff_grad_kernel,
        grid=(blocks, 2),
        out_shape=jax.ShapeDtypeStruct((blocks, shards, 2, D // shards, width), hidden.dtype),
        in_specs=[whole, whole, block, block],
        out_specs=pl.BlockSpec((1, shards, 1, D // shards, width), lambda m, s: (m, 0, s, 0, 0)),
        cost_estimate=pl.CostEstimate(
            flops=4 * rows * D * blocks * width,
            bytes_accessed=4 * D * blocks * width,
            transcendentals=0,
        ),
        name="ff_weight_grad",
    )(hidden, dz, grad_up, active)


def score_kernel(head_ref, word_ref, bias_ref, label_ref, stat_ref, top, total, target):
    at, last = pl.program_id(1), pl.num_programs(1) - 1
    logits = dots(head_ref[...], word_ref[...], 1, 1) + bias_ref[...]
    column = at * logits.shape[1] + lax.broadcasted_iota(jnp.int32, logits.shape, 1)

    @pl.when(at == 0)
    def _():
        top[...] = jnp.full(top.shape, -jnp.inf, jnp.float32)
        total[...] = jnp.zeros(total.shape, jnp.float32)
        target[...] = jnp.zeros(target.shape, jnp.float32)

    old = top[...]
    new = jnp.maximum(old, jnp.max(logits, axis=1, keepdims=True))
    added = jnp.sum(jnp.exp(logits - new), axis=1, keepdims=True)
    total[...] = total[...] * jnp.exp(old - new) + added
    top[...] = new
    hits = jnp.where(column == label_ref[...], logits, 0.0)
    target[...] += jnp.sum(hits, axis=1, keepdims=True)

    @pl.when(at == last)
    def _():
        lane = lax.broadcasted_iota(jnp.int32, stat_ref.shape, 1)
        stat_ref[...] = jnp.where(
            lane == 0, top[...], jnp.where(lane == 1, total[...], target[...])
        )


def slope_kernel(
    head_ref, word_ref, bias_ref, label_ref, norm_ref, weight_ref, slope_ref, sum_ref, grad_ref
):
    at = pl.program_id(1)
    logits = dots(head_ref[...], word_ref[...], 1, 1) + bias_ref[...]
    column = at * logits.shape[1] + lax.broadcasted_iota(jnp.int32, logits.shape, 1)
    hits = jnp.where(column == label_ref[...], 1.0, 0.0)
    slope = ((jnp.exp(logits - norm_ref[...]) - hits) * weight_ref[...]).astype(jnp.bfloat16)
    slope_ref[...] = slope
    sum_ref[0] = jnp.sum(slope.astype(jnp.float32), axis=0, keepdims=True)
    part = dots(slope, word_ref[...], 1, 0)

    @pl.when(at == 0)
    def _():
        grad_ref[...] = part

    @pl.when(at > 0)
    def _():
        grad_ref[...] += part


def head_blocks(head, word, bias):
    rows, vocab = head.shape[0], word.shape[0]
    row_block = 512 if rows % 512 == 0 else rows
    block = 768 if vocab % 768 == 0 else vocab
    grid = (rows // row_block, vocab // block)
    column = pl.BlockSpec((row_block, 1), lambda i, j: (i, 0))
    specs = [
        pl.BlockSpec((row_block, D), lambda i, j: (i, 0)),
        pl.BlockSpec((block, D), lambda i, j: (j, 0)),
        pl.BlockSpec((1, block), lambda i, j: (0, j)),
        column,
    ]
    cost = pl.CostEstimate(
        flops=2 * rows * vocab * D, bytes_accessed=2 * vocab * D, transcendentals=rows * vocab
    )
    return row_block, block, grid, column, specs, cost


def word_grad_kernel(slope_ref, head_ref, at_ref, x0_ref, out_ref, total):
    chunk, last = pl.program_id(1), pl.num_programs(1) - 1
    first_row = pl.program_id(0) * total.shape[0]
    rows = first_row + lax.broadcasted_iota(jnp.int32, (total.shape[0], at_ref.shape[1]), 0)
    onehot = jnp.where(rows == at_ref[...], 1.0, 0.0).astype(jnp.bfloat16)
    part = dots(onehot, x0_ref[...], 1, 0)

    @pl.when(chunk == 0)
    def _():
        total[...] = part + dots(slope_ref[...], head_ref[...], 0, 0)

    @pl.when(chunk > 0)
    def _():
        total[...] += part

    @pl.when(chunk == last)
    def _():
        out_ref[...] = total[...].astype(out_ref.dtype)


def word_weight_grad(slopes, head, at, x0):
    (rows, vocab), tokens = slopes.shape, at.shape[0]
    block = 768 if vocab % 768 == 0 else vocab
    chunk = 2048 if tokens % 2048 == 0 else tokens
    return pl.pallas_call(
        word_grad_kernel,
        grid=(vocab // block, tokens // chunk),
        out_shape=jax.ShapeDtypeStruct((vocab, D), head.dtype),
        in_specs=[
            pl.BlockSpec((rows, block), lambda i, j: (0, i)),
            pl.BlockSpec((rows, D), lambda i, j: (0, 0)),
            pl.BlockSpec((1, chunk), lambda i, j: (0, j)),
            pl.BlockSpec((chunk, D), lambda i, j: (j, 0)),
        ],
        out_specs=pl.BlockSpec((block, D), lambda i, j: (i, 0)),
        scratch_shapes=[pltpu.VMEM((block, D), jnp.float32)],
        cost_estimate=pl.CostEstimate(
            flops=2 * (rows + tokens) * vocab * D,
            bytes_accessed=2 * vocab * (rows + D),
            transcendentals=0,
        ),
        name="word_weight_grad",
    )(slopes, head, at[None], x0)


def head_scores(head, word, bias, labels):
    row_block, _, grid, _, specs, cost = head_blocks(head, word, bias)
    stats = pl.pallas_call(
        score_kernel,
        grid=grid,
        out_shape=jax.ShapeDtypeStruct((head.shape[0], 128), jnp.float32),
        in_specs=specs,
        out_specs=pl.BlockSpec((row_block, 128), lambda i, j: (i, 0)),
        scratch_shapes=[pltpu.VMEM((row_block, 1), jnp.float32)] * 3,
        cost_estimate=cost,
        name="head_scores",
    )(head, word, bias[None], labels[:, None])
    return stats[:, :3].T


def head_slopes(head, word, bias, labels, norms, weights):
    row_block, block, grid, column, specs, cost = head_blocks(head, word, bias)
    rows, vocab = head.shape[0], word.shape[0]
    slopes, sums, grad = pl.pallas_call(
        slope_kernel,
        grid=grid,
        out_shape=[
            jax.ShapeDtypeStruct((rows, vocab), head.dtype),
            jax.ShapeDtypeStruct((grid[0], 1, vocab), jnp.float32),
            jax.ShapeDtypeStruct((rows, D), jnp.float32),
        ],
        in_specs=specs + [column] * 2,
        out_specs=[
            pl.BlockSpec((row_block, block), lambda i, j: (i, j)),
            pl.BlockSpec((1, 1, block), lambda i, j: (i, 0, j)),
            pl.BlockSpec((row_block, D), lambda i, j: (i, 0)),
        ],
        cost_estimate=cost,
        name="head_slopes",
    )(head, word, bias[None], labels[:, None], norms[:, None], weights[:, None])
    return slopes, jnp.sum(sums[:, 0], axis=0), grad


def step(sizes, *args):
    (
        token_ids, type_ids, mask_pos, mask_valid, mlm_labels, nsp_labels,
        word_table, word_m, word_v, attn_weight, attn_m, attn_v,
        ff_weight, ff_m, ff_v, side_weight, side_m, side_v,
        vectors, vec_m, vec_v, split_bias, split_m, split_v,
        decoder_bias, decoder_m, decoder_v,
    ) = args
    z_size, x_size, y_size, c_size = sizes
    dp_size, mp_size = z_size * x_size, y_size * c_size
    z_at, x_at, y_at, c_at = (lax.axis_index(a) for a in ("z", "x", "y", "c"))
    dp_rank, mp_rank = z_at * x_size + x_at, y_at * c_size + c_at
    every = ("z", "x", "y", "c")
    mp_first = ("y", "c", "z", "x")
    plane = ("x", "y", "c")
    batch_size, length = token_ids.shape
    slots = mask_pos.shape[1]
    own_len, own_slots = length // c_size, slots // c_size
    vocab_own = word_table.shape[0]
    attn_cols, ff_cols = attn_weight.shape[2], ff_weight.shape[2]
    rows_own = attn_weight.shape[0]
    low = jnp.bfloat16
    links = Links(sizes)

    def mine(rows, size):
        row = lax.dynamic_index_in_dim(rows, y_at, 0, False)
        return lax.dynamic_slice_in_dim(row, c_at * size, size, 0)

    own_ids = mine(token_ids, own_len)
    own_types = mine(type_ids, own_len)
    seq_pos = lax.dynamic_index_in_dim(mask_pos, y_at, 0, False)
    own_pos = mine(mask_pos, own_slots)
    own_valid = mine(mask_valid, own_slots)
    own_labels = mine(mlm_labels, own_slots)
    first_core = (c_at == 0).astype(jnp.float32)

    side_rows = side_weight.shape[0] // mp_size
    vec_cols = vectors.shape[1]
    stripe = vocab_own * x_size
    bias_mine = lax.dynamic_slice_in_dim(decoder_bias, z_at * stripe, stripe, 0)
    int_count = own_len + 2 * own_slots
    side_own = lax.dynamic_slice_in_dim(side_weight, mp_rank * side_rows, side_rows, 0)
    both = jnp.concatenate([attn_weight.reshape(rows_own, 4 * attn_cols), side_own]).astype(low)
    word_parts = 4 if vocab_own % 64 == 0 else 1
    word_plane, both, ints, vec_parts, counts, mp_small = links.exchange(
        "word_gather",
        ("plane", plane, 0, BIG, word_table.astype(low).reshape(word_parts, -1, D)),
        links.line_move(both, 88, BIG),
        ("gather", ("z",), 0, FAST, lanes(jnp.concatenate([own_ids, own_labels, own_valid]))),
        ("gather", ("z", "x"), 0, FAST, jnp.pad(vectors.astype(low), ((0, 0), (0, 128 - vec_cols)))),
        (
            "gather",
            ("z", "x"),
            0,
            FAST,
            jnp.full((8, 128), jnp.sum(mask_valid.astype(jnp.float32))),
        ),
        ("gather", ("y", "c"), 0, FAST, lanes(jnp.concatenate([bias_mine, split_bias.reshape(-1)]))),
    )
    ints = ints.reshape(z_size, -1)[:, :int_count]
    z_ids, z_labels, z_valid = (
        ints[:, :own_len],
        ints[:, own_len : own_len + own_slots],
        ints[:, own_len + own_slots :],
    )
    total_count = jnp.sum(counts[:, 0, 0])
    total_seqs = jnp.float32(batch_size * dp_size)
    vec_rows = (
        vec_parts[:, :, :vec_cols]
        .transpose(1, 0, 2)
        .reshape(vectors.shape[0], D)
        .astype(jnp.float32)
    )
    mp_small = mp_small.reshape(mp_size, -1)
    word_plane = word_plane.reshape(-1, D)
    ff_own = ff_weight.astype(low).reshape(rows_own, 2 * ff_cols)
    word_plane, both, ff_own = lax.optimization_barrier((word_plane, both, ff_own))
    both = comm_all_gather(both.reshape(-1, D), ("y", "c", "x"))
    both = both.reshape(mp_size, x_size, z_size, -1, D)
    attn_blocks = both[:, :, :, :rows_own].transpose(0, 2, 1, 3, 4).reshape(mp_size, D, 4 * attn_cols)
    side_full = both[:, :, :, rows_own:].transpose(2, 1, 0, 3, 4).reshape(-1, D)
    ff_blocks = comm_all_gather(ff_own, mp_first).reshape(mp_size, D, 2 * ff_cols)
    bias_plane = (
        mp_small[:, :stripe].reshape(mp_size, x_size, vocab_own).transpose(1, 0, 2).reshape(-1)
    )
    split_full = mp_small[:, stripe : stripe + 6 * attn_cols].reshape(mp_size, 6, attn_cols)

    def plane_index(ids):
        block = ids // stripe
        offset = ids % stripe
        inside = block % z_size == z_at
        at = ((offset // vocab_own) * mp_size + block // z_size) * vocab_own + offset % vocab_own
        return inside, at

    flat_ids = z_ids.reshape(-1)
    inside, at = plane_index(flat_ids)
    looked = jnp.where(inside[:, None], word_plane[jnp.where(inside, at, 0)], jnp.zeros((), low))
    if z_size <= 8:
        looked = looked.reshape(z_size, 8, own_len // 8, D)
        embedded = links.fold("token_fold", looked).reshape(own_len, D).astype(jnp.float32)
    else:
        looked = looked.reshape(z_size, own_len, D)
        (found,) = links.exchange("token_spread", ("spread", ("z",), 0, BIG, looked))
        embedded = lax.dynamic_index_in_dim(looked, z_at, 0, False).astype(jnp.float32)
        embedded = embedded + jnp.sum(found.astype(jnp.float32), axis=0)
    position_rows = lax.dynamic_slice_in_dim(side_full, 2 * D + c_at * own_len, own_len, 0)
    embedded = (
        embedded
        + position_rows.astype(jnp.float32)
        + jnp.where(own_types[:, None] == 0, vec_rows[12], vec_rows[13])
    )
    hidden0 = layer_norm(embedded, vec_rows[0], vec_rows[1])
    hidden0_b = hidden0.astype(low)

    out_blocks = attn_blocks[:, :, 3 * attn_cols :]
    head_bias = split_full[:, :2].transpose(1, 0, 2).reshape(2, D)
    queries, own_keys, own_values = project(hidden0_b, attn_blocks, head_bias)
    other_keys, other_values = links.exchange(
        "key_trade", ("trade", ("c",), 0, FAST, own_keys), ("trade", ("c",), 0, FAST, own_values)
    )
    keys, values = (own_keys, other_keys), (own_values, other_values)
    mixed, log_norm = attention_forward(queries, keys, values)
    attn_out = jnp.einsum(
        "tme,mde->td",
        mixed.reshape(own_len, mp_size, attn_cols),
        out_blocks,
        preferred_element_type=jnp.float32,
    )
    resid1 = hidden0 + (attn_out + vec_rows[2])
    hidden1 = layer_norm(resid1, vec_rows[3], vec_rows[4])
    hidden1_b = hidden1.astype(low)
    ff_bias = split_full[:, 2:6].transpose(0, 2, 1).reshape(mp_size, ff_cols)
    ff_in, ff_out = ff_blocks[:, :, :ff_cols], ff_blocks[:, :, ff_cols:]
    upward = jnp.einsum("td,mdf->mtf", hidden1_b, ff_in, preferred_element_type=jnp.float32)
    upward = upward + ff_bias[:, None]
    active = gelu_exact(upward).astype(low)
    ffn_out = jnp.einsum("mtf,mdf->td", active, ff_out, preferred_element_type=jnp.float32)
    resid2 = hidden1 + (ffn_out + vec_rows[5])
    hidden2 = layer_norm(resid2, vec_rows[6], vec_rows[7])

    hidden2_b = hidden2.astype(low)
    (other_h2,) = links.exchange("hidden_trade", ("trade", ("c",), 0, FAST, hidden2_b))
    picked_b = jnp.concatenate([hidden2_b, other_h2])[
        own_pos % own_len + jnp.where(own_pos // own_len == c_at, 0, own_len)
    ]
    dense_w = side_full[D : 2 * D]
    dense_out = jnp.dot(picked_b, dense_w, preferred_element_type=jnp.float32) + vec_rows[8]
    act_dense = gelu_exact(dense_out)
    head_rows = layer_norm(act_dense, vec_rows[9], vec_rows[10])
    (head_b,) = links.exchange("head_gather", links.line_move(head_rows.astype(low), 32, FAST))
    head_b = head_b.reshape(-1, D)
    label_in, label_at = plane_index(z_labels.reshape(-1))
    label_at = jnp.where(label_in, label_at, -1)
    stats = jnp.pad(head_scores(head_b, word_plane, bias_plane, label_at), ((0, 5), (0, 0)))
    (stats,) = links.exchange("stat_gather", ("gather", ("z",), 0, FAST, stats))
    top_all = jnp.max(stats[:, 0], axis=0)
    total_all = jnp.sum(stats[:, 1] * jnp.exp(stats[:, 0] - top_all), axis=0)
    target_all = jnp.sum(stats[:, 2], axis=0)
    log_total = top_all + jnp.log(total_all)
    valid_rows = z_valid.reshape(-1).astype(jnp.float32)
    mlm_sum = -jnp.sum(valid_rows * (target_all - log_total))
    weight_rows = valid_rows / total_count
    grad_logits, decoder_part, head_part = head_slopes(
        head_b, word_plane, bias_plane, label_at, log_total, weight_rows
    )
    head_part = head_part.reshape(z_size, own_slots, D)
    (head_others,) = links.exchange("head_spread", ("spread", ("z",), 0, FAST, head_part.astype(low)))
    grad_head = lax.dynamic_index_in_dim(head_part, z_at, 0, False) + jnp.sum(
        head_others.astype(jnp.float32), axis=0
    )
    grad_act, grad_g9, grad_s9 = norm_backward(act_dense, vec_rows[9], vec_rows[10], grad_head)
    grad_dense = (grad_act * gelu_slope(dense_out)).astype(low)
    dense_bias_grad = jnp.sum(grad_dense.astype(jnp.float32), axis=0)
    dense_grad = jnp.einsum("rd,re->de", picked_b, grad_dense, preferred_element_type=jnp.float32)
    grad_picked = jnp.einsum("re,de->rd", grad_dense, dense_w, preferred_element_type=jnp.float32)
    (other_picked,) = links.exchange("picked_trade", ("trade", ("c",), 0, FAST, grad_picked))
    seq_picked = jnp.concatenate([grad_picked, other_picked])
    other_pos = lax.dynamic_slice_in_dim(seq_pos, (1 - c_at) * own_slots, own_slots, 0)
    place = (
        jnp.concatenate([own_pos, other_pos])[None, :]
        == c_at * own_len + lax.broadcasted_iota(jnp.int32, (own_len, slots), 0)
    ).astype(jnp.float32)
    grad_top = jnp.dot(place, seq_picked, precision=highest)

    cls_row = hidden2_b[0:1]
    pooler_w = side_full[:D]
    pooled = jnp.tanh(jnp.dot(cls_row, pooler_w, preferred_element_type=jnp.float32) + vec_rows[11])
    classes = vec_rows[14:16]
    nsp_logp = jax.nn.log_softmax(jnp.dot(pooled, classes.T, precision=highest), axis=-1)
    own_nsp = lax.dynamic_slice_in_dim(nsp_labels, y_at, 1, 0)
    pick_nsp = own_nsp[:, None] == lax.broadcasted_iota(jnp.int32, (1, 2), 1)
    nsp_sum = -jnp.sum(jnp.where(pick_nsp, nsp_logp, 0.0)) * first_core
    grad_nsp = (jnp.exp(nsp_logp) - pick_nsp.astype(jnp.float32)) / total_seqs * first_core
    class_grad = grad_nsp[0][:, None] * pooled
    grad_pre = jnp.dot(grad_nsp, classes, precision=highest) * (1.0 - pooled * pooled)
    pooler_bias_grad = grad_pre[0]
    pooler_grad = cls_row.astype(jnp.float32).T * grad_pre
    grad_cls = jnp.dot(grad_pre, pooler_w.astype(jnp.float32).T, precision=highest)
    first_row = lax.broadcasted_iota(jnp.int32, (own_len, 1), 0) == 0
    grad_top = grad_top + jnp.where(first_row, grad_cls, 0.0)

    grad_r2, grad_g2, grad_s2 = norm_backward(resid2, vec_rows[6], vec_rows[7], grad_top)
    ffn_grad_b = grad_r2.astype(low)
    out_bias_two = jnp.sum(ffn_grad_b.astype(jnp.float32), axis=0)
    grad_active = jnp.einsum("td,mdf->mtf", ffn_grad_b, ff_out, preferred_element_type=jnp.float32)
    grad_up = (grad_active * gelu_slope(upward)).astype(low)
    ff_bias_grad = jnp.sum(grad_up.astype(jnp.float32), axis=1)
    hidden1_part = jnp.einsum("mtf,mdf->td", grad_up, ff_in, preferred_element_type=jnp.float32)
    if rows_own % 16 == 0:
        ff_grad = ff_weight_grad(dp_size, hidden1_b, ffn_grad_b, grad_up, active)
    else:
        ff_grad = jnp.stack(
            [
                jnp.einsum("td,mtf->mdf", left, right, preferred_element_type=jnp.float32)
                .astype(low)
                .reshape(mp_size * dp_size, rows_own, ff_cols)
                for left, right in ((hidden1_b, grad_up), (ffn_grad_b, active))
            ],
            axis=1,
        )
    ff_grad, hidden1_part = lax.optimization_barrier((ff_grad, hidden1_part))
    ff_red = comm_scatter_sum(ff_grad.reshape(-1, ff_cols), mp_first)
    grad_h1 = grad_r2 + hidden1_part
    grad_r1, grad_g1, grad_s1 = norm_backward(resid1, vec_rows[3], vec_rows[4], grad_h1)
    attn_grad_b = grad_r1.astype(low)
    out_bias_one = jnp.sum(attn_grad_b.astype(jnp.float32), axis=0)
    grad_mixed = projected(mixed_grad_kernel, "mixed_grad", low, attn_grad_b, attn_blocks)
    grad_q, own_k, part_k, own_v, part_v = attention_backward(
        queries, keys, values, log_norm, grad_mixed
    )
    from_k, from_v = links.exchange(
        "key_grad_trade",
        ("trade", ("c",), 0, FAST, part_k),
        ("trade", ("c",), 0, FAST, part_v),
    )
    grad_k = (own_k + from_k).astype(low)
    grad_v = (own_v + from_v).astype(low)
    packed_sums = jnp.stack(
        [
            jnp.sum(g.astype(jnp.float32), axis=0).reshape(mp_size, attn_cols)
            for g in (grad_q, grad_v)
        ],
        axis=1,
    )
    hidden0_part = projected(
        hidden_grad_kernel, "hidden_grad", jnp.float32, grad_q, grad_k, grad_v, attn_blocks
    )
    attn_grad = attn_weight_grad(mp_size, hidden0_b, grad_q, grad_k, grad_v, attn_grad_b, mixed)
    attn_grad = attn_grad.reshape(y_size, c_size, z_size, x_size, rows_own, 4 * attn_cols)
    grad_h0 = grad_r1 + hidden0_part
    grad_x0, grad_g0, grad_s0 = norm_backward(embedded, vec_rows[0], vec_rows[1], grad_h0)

    position_grad = lax.dynamic_update_slice_in_dim(
        jnp.zeros((length, D), low), grad_x0.astype(low), c_at * own_len, 0
    )
    side_grad = jnp.concatenate([pooler_grad.astype(low), dense_grad.astype(low), position_grad], axis=0)
    side_grad = side_grad.reshape(z_size, x_size, y_size, c_size, side_rows, D)

    def joined(value, at, dim, received):
        kept = lax.dynamic_index_in_dim(value, at, dim, False)
        return (kept.astype(jnp.float32) + received.astype(jnp.float32)).astype(low)

    x0_b = grad_x0.astype(low)
    cut_one, cut_two = own_len // 8, 5 * own_len // 8
    from_a, from_s, x0_one = links.exchange(
        "grad_swap_c",
        ("swap", ("c",), 1, BIG, attn_grad),
        ("swap", ("c",), 3, BIG, side_grad),
        links.line_move(x0_b[:cut_one], 64, BIG),
    )
    attn_grad, side_grad = joined(attn_grad, c_at, 1, from_a), joined(side_grad, c_at, 3, from_s)
    from_a, from_s, x0_two = links.exchange(
        "grad_swap_xy",
        ("swap", ("x",), 2, BIG, attn_grad),
        ("swap", ("y",), 2, BIG, side_grad),
        links.line_move(x0_b[cut_one:cut_two], 64, BIG),
    )
    attn_grad, side_grad = joined(attn_grad, x_at, 2, from_a), joined(side_grad, y_at, 2, from_s)
    from_a, from_s, x0_three = links.exchange(
        "grad_swap_yx",
        ("swap", ("y",), 0, BIG, attn_grad),
        ("swap", ("x",), 1, BIG, side_grad),
        links.line_move(x0_b[cut_two:], 64, BIG),
    )
    attn_grad, side_grad = joined(attn_grad, y_at, 0, from_a), joined(side_grad, x_at, 1, from_s)

    ff_red, x0_three = lax.optimization_barrier((ff_red, x0_three))
    all_x0 = [x.reshape(z_size, -1, D) for x in (x0_one, x0_two, x0_three)]
    all_x0 = jnp.concatenate(all_x0, axis=1).reshape(-1, D)
    word_grad = word_weight_grad(grad_logits, head_b, jnp.where(inside, at, -1), all_x0)
    word_grad, attn_grad, side_grad = lax.optimization_barrier(
        (word_grad, attn_grad, side_grad)
    )
    word_red = comm_scatter_sum(word_grad, plane).astype(jnp.float32)
    from_a, from_s = links.exchange(
        "grad_spread_z", ("spread", ("z",), 0, BIG, attn_grad), ("spread", ("z",), 0, BIG, side_grad)
    )

    def total(value, received):
        kept = lax.dynamic_index_in_dim(value, z_at, 0, False).astype(jnp.float32)
        return kept + jnp.sum(received.astype(jnp.float32), axis=0)

    attn_red, side_quarter = total(attn_grad, from_a), total(side_grad, from_s)
    type_zero = jnp.sum(jnp.where(own_types[:, None] == 0, grad_x0, 0.0), axis=0)
    type_one = jnp.sum(jnp.where(own_types[:, None] == 1, grad_x0, 0.0), axis=0)
    vec_grad = jnp.stack(
        [
            grad_g0, grad_s0, out_bias_one, grad_g1, grad_s1, out_bias_two, grad_g2, grad_s2,
            dense_bias_grad, grad_g9, grad_s9, pooler_bias_grad, type_zero, type_one,
            class_grad[0], class_grad[1],
        ],
        axis=0,
    )
    split_grad = jnp.concatenate(
        [
            packed_sums,
            ff_bias_grad.reshape(mp_size, attn_cols, 4).transpose(0, 2, 1),
        ],
        axis=1,
    )
    late = lanes(jnp.concatenate([vec_grad.reshape(-1), split_grad.reshape(-1), decoder_part]))
    late, side_quarter = lax.optimization_barrier((late, side_quarter))
    small = links.combine(
        "small_sum",
        late,
    ).reshape(z_size, -1)
    (side_red,) = links.exchange(
        "side_gather", ("gather", ("y", "c"), 0, FAST, side_quarter.astype(low))
    )
    side_red = side_red.reshape(side_weight.shape).astype(jnp.float32)
    narrow = vec_grad.size + split_grad.size
    summed = jnp.sum(small[:, :narrow], axis=0)
    vec_all = summed[: vec_grad.size].reshape(vec_grad.shape)
    split_all = summed[vec_grad.size :].reshape(split_grad.shape)
    vec_red = lax.dynamic_slice_in_dim(vec_all, dp_rank * vec_cols, vec_cols, 1)
    split_red = lax.dynamic_index_in_dim(split_all, mp_rank, 0, False)
    decoder_red = lax.dynamic_index_in_dim(
        small[:, narrow : narrow + decoder_part.size].reshape(z_size, x_size, mp_size, vocab_own),
        mp_rank,
        2,
        False,
    ).reshape(-1)
    word_f, attn_f, ff_f = (
        word_red,
        attn_red.reshape(attn_weight.shape),
        row_major(
            ff_red.astype(jnp.float32).reshape(2, rows_own, ff_cols).transpose(1, 0, 2)
        ),
    )
    own_square = (
        jnp.sum(word_f * word_f)
        + jnp.sum(attn_f * attn_f)
        + jnp.sum(ff_f * ff_f)
        + jnp.sum(side_red * side_red) / mp_size
        + jnp.sum(vec_red * vec_red) / mp_size
        + (jnp.sum(split_red * split_red) + jnp.sum(decoder_red * decoder_red)) / dp_size
    )
    loss_part = mlm_sum / total_count / z_size + nsp_sum / total_seqs
    ends = jnp.where(
        lax.broadcasted_iota(jnp.int32, (8, 128), 0) == 0, own_square, loss_part
    )
    ends = jnp.sum(links.combine("norm_sum", ends), axis=0)
    grad_square, total_loss = ends[0, 0], ends[1, 0]
    grad_norm = jnp.sqrt(grad_square)
    clip_scale = max_norm / jnp.maximum(grad_norm, max_norm)
    return (
        total_loss,
        grad_norm,
        *adam_step(word_table, word_m, word_v, word_f, clip_scale, True),
        *adam_step(attn_weight, attn_m, attn_v, attn_f, clip_scale, True),
        *adam_step(ff_weight, ff_m, ff_v, ff_f, clip_scale, True),
        *adam_step(side_weight, side_m, side_v, side_red, clip_scale, True),
        *adam_step(vectors, vec_m, vec_v, vec_red, clip_scale, False),
        *adam_step(split_bias, split_m, split_v, split_red, clip_scale, False),
        *adam_step(decoder_bias, decoder_m, decoder_v, decoder_red, clip_scale, False),
    )


def solution(mesh):
    dp_size, mp_size = mesh.shape["dp"], mesh.shape["mp"]
    x_size = 2 if dp_size % 2 == 0 else 1
    c_size = 2 if mp_size % 2 == 0 else 1
    sizes = (dp_size // x_size, x_size, mp_size // c_size, c_size)
    fine = Mesh(mesh.devices.reshape(sizes), ("z", "x", "y", "c"))
    dp, mp = ("z", "x"), ("y", "c")
    word = P(("y", "c", "z", "x"), None)
    cube = P(dp, None, mp)
    kinds = (
        [P(dp, None)] * 5
        + [P(dp)]
        + [word] * 3
        + [cube] * 6
        + [P(dp, None)] * 3
        + [P(None, dp)] * 3
        + [P(None, mp)] * 3
        + [P(mp)] * 3
    )
    return jax.shard_map(
        functools.partial(step, sizes),
        mesh=fine,
        in_specs=tuple(kinds),
        out_specs=(P(), P(), *kinds[6:]),
        check_vma=False,
    )
```

```python
import functools
import math

import jax
import jax.numpy as jnp
from jax import lax
from jax.experimental.layout import Layout, with_layout_constraint
from jax.experimental import pallas as pl
from jax.experimental.pallas import tpu as pltpu
from jax.sharding import Mesh, PartitionSpec as P

D = 768
HEAD_DIM = 64


beta_one = 0.9
beta_two = 0.999
adam_eps = 1e-06
learn_rate = 0.2
decay_rate = 0.01
step_count = 10
max_norm = 0.05
norm_eps = 1e-12
highest = lax.Precision.HIGHEST


def layer_norm(inputs, norm_gain, norm_shift):
    center = inputs - jnp.mean(inputs, axis=-1, keepdims=True)
    spread = jnp.mean(center * center, axis=-1, keepdims=True)
    return center * lax.rsqrt(spread + norm_eps) * norm_gain + norm_shift


def normal_cdf(inputs):
    return 0.5 + 0.5 * lax.erf(inputs * math.sqrt(0.5))


def gelu_exact(inputs):
    return inputs * normal_cdf(inputs)


def gelu_slope(inputs):
    density = jnp.exp(-0.5 * inputs * inputs) * (1.0 / math.sqrt(2.0 * math.pi))
    return normal_cdf(inputs) + inputs * density


def norm_backward(inputs, norm_gain, norm_shift, upstream):
    _, pullback = jax.vjp(layer_norm, inputs, norm_gain, norm_shift)
    return pullback(upstream)


def adam_step(weight, moment, square, gradient, clip_scale, decays):
    gradient = gradient * clip_scale
    moment = beta_one * moment + (1 - beta_one) * gradient
    square = beta_two * square + (1 - beta_two) * gradient * gradient
    mean_hat = moment / (1 - beta_one**step_count)
    var_hat = square / (1 - beta_two**step_count)
    change = mean_hat / (jnp.sqrt(var_hat) + adam_eps)
    if decays:
        change = change + decay_rate * weight
    return (weight - learn_rate * change, moment, square)


def comm_all_gather(value, axes):
    return lax.all_gather(value, axes, axis=0, tiled=True)


def comm_scatter_sum(value, axes):
    return lax.psum_scatter(value, axes, scatter_dimension=0, tiled=True)


MESH = pl.DeviceIdType.MESH
BIG, FAST = pl.ANY, pltpu.VMEM


class Links:
    def __init__(self, sizes):
        self.sizes = dict(zip(("z", "x", "y", "c"), sizes))
        self.used = 0

    def next_id(self):
        self.used += 1
        return self.used - 1

    def count(self, axes):
        return math.prod(self.sizes[a] for a in axes)

    def place(self, axes):
        at = 0
        for a in axes:
            at = at * self.sizes[a] + lax.axis_index(a)
        return at

    def target(self, axes, flat):
        where = {}
        for a in reversed(axes):
            where[a] = lax.rem(flat, self.sizes[a])
            flat = lax.div(flat, self.sizes[a])
        return where

    def greet(self, groups):
        barrier = pltpu.get_barrier_semaphore()
        total = 0
        for axes in groups:
            size, me = self.count(axes), self.place(axes)
            for r in range(1, size):
                pl.semaphore_signal(
                    barrier,
                    inc=1,
                    device_id=self.target(axes, lax.rem(me + r, size)),
                    device_id_type=MESH,
                )
            total += size - 1
        pl.semaphore_wait(barrier, total)

    def call(self, kernel, outs, spaces, out_spaces, scratch, values, wire, name):
        result = pl.pallas_call(
            kernel,
            out_shape=outs,
            in_specs=[pl.BlockSpec(memory_space=m) for m in spaces],
            out_specs=[pl.BlockSpec(memory_space=m) for m in out_spaces],
            scratch_shapes=scratch,
            compiler_params=pltpu.CompilerParams(
                collective_id=self.next_id(),
                has_side_effects=True,
                vmem_limit_bytes=40 * 2**20,
            ),
            cost_estimate=pl.CostEstimate(flops=0, bytes_accessed=wire, transcendentals=0),
            name=name,
        )(*values)
        return result

    def exchange(self, name, *moves):
        outs, scratch = [], []
        for kind, axes, dim, _, value in moves:
            size = self.count(axes)
            shape, sends, lands = value.shape, (size - 1,), (size - 1,)
            if kind == "gather":
                shape = (size, *shape)
            elif kind == "swap":
                shape = shape[:dim] + shape[dim + 1 :]
            elif kind == "spread":
                shape = (size - 1, *shape[1:])
            elif kind == "relay":
                shape, sends = (size, *shape), (2, size - 1, shape[0])
                lands = sends
            elif kind == "plane":
                shape, sends, lands = (2, 2, 2, *shape), (7 * shape[0],), (7, shape[0])
            outs.append(jax.ShapeDtypeStruct(shape, value.dtype))
            scratch += [
                pltpu.SemaphoreType.DMA(sends),
                pltpu.SemaphoreType.DMA(lands),
                pltpu.SemaphoreType.DMA((1,)),
            ]
        spaces = [m[3] for m in moves]
        groups = []
        for kind, axes, *_ in moves:
            groups += [(a,) for a in axes] if kind == "plane" else [axes]
        groups = list(dict.fromkeys(groups))

        def kernel(*refs):
            ins, dests = refs[: len(moves)], refs[len(moves) : 2 * len(moves)]
            sems = refs[2 * len(moves) :]
            self.greet(groups)
            started, later = [], []
            for i, ((kind, axes, dim, _, _), source, dest) in enumerate(zip(moves, ins, dests)):
                sends, lands, own_sem = sems[3 * i : 3 * i + 3]
                size, me = self.count(axes), self.place(axes)
                if kind in ("relay", "plane"):
                    act = self.relay if kind == "relay" else self.plane
                    later.append(functools.partial(act, axes, source, dest, sends, lands))
                for r in range(1, size):
                    peer = lax.rem(me + r, size)
                    if kind == "gather":
                        src, dst = source, dest.at[me]
                    elif kind == "swap":
                        src, dst = source.at[(slice(None),) * dim + (peer,)], dest
                    elif kind == "spread":
                        src, dst = source.at[peer], dest.at[r - 1]
                    elif kind == "trade":
                        src, dst = source, dest
                    else:
                        continue
                    copy = pltpu.make_async_remote_copy(
                        src_ref=src,
                        dst_ref=dst,
                        send_sem=sends.at[r - 1],
                        recv_sem=lands.at[r - 1],
                        device_id=self.target(axes, peer),
                        device_id_type=MESH,
                    )
                    copy.start()
                    started.append(copy)
            runs = [act() for act in later]
            for run in runs:
                next(run)
            for i, ((kind, axes, *_), source, dest) in enumerate(zip(moves, ins, dests)):
                if kind in ("gather", "relay", "plane"):
                    at = self.place(axes)
                    if kind == "plane":
                        at = tuple(lax.axis_index(a) for a in axes)
                    copy = pltpu.make_async_copy(source, dest.at[at], sems[3 * i + 2].at[0])
                    copy.start()
                    started.append(copy)
            while runs:
                runs = [run for run in runs if next(run, run) is None]
            for copy in started:
                copy.wait()

        return self.call(
            kernel,
            outs,
            spaces,
            spaces,
            scratch,
            [m[4] for m in moves],
            sum(2 * math.prod(o.shape) * o.dtype.itemsize for o in outs),
            name,
        )

    def relay(self, axes, source, dest, sends, lands):
        (axis,) = axes
        size, parts = self.sizes[axis], source.shape[0]
        me = lax.axis_index(axis)

        def copy_of(way, hop, part):
            step = 1 if way == 0 else -1
            place = (me - step * hop, part)
            return pltpu.make_async_remote_copy(
                src_ref=source.at[part] if hop == 0 else dest.at[place],
                dst_ref=dest.at[place],
                send_sem=sends.at[way, hop, part],
                recv_sem=lands.at[way, hop, part],
                device_id={axis: me + step},
                device_id_type=MESH,
            )

        def landing(way, hop, part):
            step = 1 if way == 0 else -1
            landed = dest.at[me - step * hop, part]
            return pltpu.make_async_remote_copy(
                src_ref=landed,
                dst_ref=landed,
                send_sem=sends.at[way, hop - 1, part],
                recv_sem=lands.at[way, hop - 1, part],
                device_id={axis: me - step},
                device_id_type=MESH,
            )

        def held(way, hop):
            return me - hop >= 0 if way == 0 else me + hop <= size - 1

        def sending(way, hop):
            return held(way, hop) & (me < size - 1 if way == 0 else me > 0)

        for hop in range(size):
            for part in range(parts):
                for way in range(2):
                    if hop > 0:

                        @pl.when(held(way, hop))
                        def _():
                            landing(way, hop, part).wait_recv()

                    if hop < size - 1:

                        @pl.when(sending(way, hop))
                        def _():
                            copy_of(way, hop, part).start()

            yield
        for hop in range(size - 1):
            for part in range(parts):
                for way in range(2):

                    @pl.when(sending(way, hop))
                    def _():
                        copy_of(way, hop, part).wait_send()

    def plane(self, axes, own, out, sends, lands):
        parts = own.shape[0]
        head = (parts + 1) // 2
        x, y, c = (lax.axis_index(a) for a in axes)
        by_x, by_y, by_c = {"x": 1 - x}, {"y": 1 - y}, {"c": 1 - c}
        started = []

        def send(src, place, part, slot, peer):
            copy = pltpu.make_async_remote_copy(
                src_ref=src,
                dst_ref=out.at[(*place, part)],
                send_sem=sends.at[len(started)],
                recv_sem=lands.at[slot, part],
                device_id=peer,
                device_id_type=MESH,
            )
            copy.start()
            started.append(copy)

        def arrived(place, part, slot):
            landed = out.at[(*place, part)]
            pltpu.make_async_remote_copy(
                src_ref=landed,
                dst_ref=landed,
                send_sem=sends.at[0],
                recv_sem=lands.at[slot, part],
                device_id=by_c,
                device_id_type=MESH,
            ).wait_recv()
            return landed

        me, at_x, at_y, at_xy = (x, y, c), (1 - x, y, c), (x, 1 - y, c), (1 - x, 1 - y, c)
        for part in range(parts):
            send(own.at[part], me, part, 0, by_x)
            send(own.at[part], me, part, 1, by_y)
        for part in range(parts):
            send(own.at[part], me, part, 3, by_c)
        yield
        for part in range(parts):
            landed = arrived(at_x, part, 0)
            if part < head:
                send(landed, at_x, part, 2, by_y)
            send(landed, at_x, part, 4, by_c)
            landed = arrived(at_y, part, 1)
            if part >= head:
                send(landed, at_y, part, 2, by_x)
            send(landed, at_y, part, 5, by_c)
            yield
        for part in range(parts):
            landed = arrived(at_xy, part, 2)
            send(landed, at_xy, part, 6, by_c)
        yield
        for slot, place in ((3, me), (4, at_x), (5, at_y), (6, at_xy)):
            for part in range(parts):
                arrived((place[0], place[1], 1 - c), part, slot)
        for copy in started:
            copy.wait_send()

    def fold(self, name, value):
        size, parts = value.shape[:2]
        block = value.shape[1:]

        def kernel(source, out, land, sends, lands):
            self.greet([("z",)])
            me = lax.axis_index("z")

            def beyond(way, hop):
                return me + hop <= size - 1 if way == 0 else me - hop >= 0

            def behind(way):
                return me > 0 if way == 0 else me < size - 1

            def copy_of(way, hop, part, src):
                return pltpu.make_async_remote_copy(
                    src_ref=src,
                    dst_ref=land.at[way, hop - 1, part],
                    send_sem=sends.at[way, hop - 1, part],
                    recv_sem=lands.at[way, hop - 1, part],
                    device_id={"z": me + (1 if way == 0 else -1)},
                    device_id_type=MESH,
                )

            def landing(way, hop, part):
                landed = land.at[way, hop, part]
                return pltpu.make_async_remote_copy(
                    src_ref=landed,
                    dst_ref=landed,
                    send_sem=sends.at[way, hop, part],
                    recv_sem=lands.at[way, hop, part],
                    device_id={"z": me - (1 if way == 0 else -1)},
                    device_id_type=MESH,
                )

            for hop in range(size - 1, 0, -1):
                for part in range(parts):
                    for way in range(2):
                        goal = me + hop if way == 0 else me - hop

                        @pl.when(beyond(way, hop) & jnp.logical_not(behind(way)))
                        def _():
                            copy_of(way, hop, part, source.at[goal, part]).start()

                        if hop < size - 1:

                            @pl.when(beyond(way, hop) & behind(way))
                            def _():
                                landing(way, hop, part).wait_recv()
                                land[way, hop, part] += source[goal, part]
                                copy_of(way, hop, part, land.at[way, hop, part]).start()

            for part in range(parts):
                out[part] = source[me, part]
                for way in range(2):

                    @pl.when(behind(way))
                    def _():
                        landing(way, 0, part).wait_recv()
                        out[part] += land[way, 0, part]

            for hop in range(size - 1, 0, -1):
                for part in range(parts):
                    for way in range(2):

                        @pl.when(beyond(way, hop))
                        def _():
                            copy_of(way, hop, part, source.at[0, part]).wait_send()

        return self.call(
            kernel,
            [jax.ShapeDtypeStruct(block, value.dtype)],
            [FAST],
            [FAST],
            [
                pltpu.VMEM((2, size - 1, *block), value.dtype),
                pltpu.SemaphoreType.DMA((2, size - 1, parts)),
                pltpu.SemaphoreType.DMA((2, size - 1, parts)),
            ],
            [value],
            4 * value.size,
            name,
        )[0]

    def line_move(self, value, part_rows, memory):
        parts = value.shape[0] // part_rows if value.shape[0] % part_rows == 0 else 1
        kind = "relay" if self.sizes["z"] <= 8 else "gather"
        return (kind, ("z",), 0, memory, value.reshape(parts, -1, value.shape[1]))

    def combine(self, name, value):
        pairs = [a for a in ("c", "x", "y") if self.sizes[a] > 1]
        depth = self.sizes["z"]
        steps = len(pairs)

        def kernel(x_ref, out_ref, sums, land, sends, lands):
            self.greet([(a,) for a in pairs] + [("z",)])
            me = lax.axis_index("z")
            for i, a in enumerate(pairs):
                source = x_ref if i == 0 else sums.at[i - 1]
                copy = pltpu.make_async_remote_copy(
                    src_ref=source,
                    dst_ref=land.at[i],
                    send_sem=sends.at[i],
                    recv_sem=lands.at[i],
                    device_id={a: 1 - lax.axis_index(a)},
                    device_id_type=MESH,
                )
                copy.start()
                copy.wait()
                sums[i] = source[...] + land[i]
            out_ref[me] = sums[steps - 1]
            started = []
            for r in range(1, depth):
                copy = pltpu.make_async_remote_copy(
                    src_ref=sums.at[steps - 1],
                    dst_ref=out_ref.at[me],
                    send_sem=sends.at[steps + r - 1],
                    recv_sem=lands.at[steps + r - 1],
                    device_id={"z": lax.rem(me + r, depth)},
                    device_id_type=MESH,
                )
                copy.start()
                started.append(copy)
            for copy in started:
                copy.wait()

        return self.call(
            kernel,
            [jax.ShapeDtypeStruct((depth, *value.shape), value.dtype)],
            [FAST],
            [FAST],
            [
                pltpu.VMEM((steps, *value.shape), value.dtype),
                pltpu.VMEM((steps, *value.shape), value.dtype),
                pltpu.SemaphoreType.DMA((steps + depth - 1,)),
                pltpu.SemaphoreType.DMA((steps + depth - 1,)),
            ],
            [value],
            16 * value.size * 4,
            name,
        )[0]


def row_major(value):
    return with_layout_constraint(value, Layout(major_to_minor=tuple(range(value.ndim))))


def lanes(flat):
    padded = jnp.pad(flat, (0, -flat.size % 1024))
    return padded.reshape(-1, 128)


HEAD_SCALE = math.log2(math.e) / math.sqrt(HEAD_DIM)
PAIR = 2 * HEAD_DIM
ROWS = 256


def dots(left, right, left_dim, right_dim):
    return lax.dot_general(
        left, right, (((left_dim,), (right_dim,)), ((), ())), preferred_element_type=jnp.float32
    )


def half_lanes(value, half):
    lane = lax.broadcasted_iota(jnp.int32, value.shape, 1)
    return jnp.where((lane >= HEAD_DIM) == (half == 1), value, jnp.zeros((), value.dtype))


def forward_kernel(q_ref, k0_ref, k1_ref, v0_ref, v1_ref, out_ref, norm_ref):
    keys = jnp.concatenate([k0_ref[...], k1_ref[...]], axis=0)
    values = jnp.concatenate([v0_ref[...], v1_ref[...]], axis=0)
    for start in range(0, q_ref.shape[0], ROWS):
        rows = pl.ds(start, ROWS)
        queries = q_ref[rows, :]
        halves = []
        for half in range(2):
            scores = dots(keys, half_lanes(queries, half), 1, 1)
            top = jnp.max(scores, axis=0, keepdims=True)
            powers = jnp.exp2((scores - top) * HEAD_SCALE)
            total = jnp.sum(powers, axis=0, keepdims=True)
            probs = (powers * (1.0 / total)).astype(jnp.bfloat16)
            norm_ref[0, half : half + 1, rows] = top * HEAD_SCALE + jnp.log2(total)
            mixed = dots(values, probs, 0, 0)
            halves.append(mixed[half * HEAD_DIM : (half + 1) * HEAD_DIM])
        out_ref[rows, :] = jnp.concatenate(halves, axis=0).T.astype(out_ref.dtype)


def attention_forward(queries, keys, values):
    length, width = queries.shape
    pairs = width // PAIR
    block = pl.BlockSpec((length, PAIR), lambda i: (0, i))
    flops = 8 * length * length * width
    return pl.pallas_call(
        forward_kernel,
        grid=(pairs,),
        out_shape=[
            jax.ShapeDtypeStruct((length, width), queries.dtype),
            jax.ShapeDtypeStruct((pairs, 2, length), jnp.float32),
        ],
        in_specs=[block] * 5,
        out_specs=[block, pl.BlockSpec((1, 2, length), lambda i: (i, 0, 0))],
        cost_estimate=pl.CostEstimate(
            flops=2 * flops, bytes_accessed=16 * length * width, transcendentals=flops // 256
        ),
        name="attention_forward",
    )(queries, *keys, *values)


def backward_kernel(
    q_ref, k0_ref, k1_ref, v0_ref, v1_ref, norm_ref, g_ref, dq_ref, dk0_ref, dk1_ref, dv0_ref, dv1_ref
):
    own = k0_ref.shape[0]
    keys = jnp.concatenate([k0_ref[...], k1_ref[...]], axis=0)
    values = jnp.concatenate([v0_ref[...], v1_ref[...]], axis=0)
    grad_keys = grad_values = 0.0
    for start in range(0, q_ref.shape[0], ROWS):
        rows = pl.ds(start, ROWS)
        halves = []
        for half in range(2):
            queries = half_lanes(q_ref[rows, :], half)
            upstream = half_lanes(g_ref[rows, :], half)
            scores = dots(keys, queries, 1, 1)
            probs = jnp.exp2(scores * HEAD_SCALE - norm_ref[0, half : half + 1, rows])
            grad_probs = dots(values, upstream, 1, 1)
            row_dot = jnp.sum(grad_probs * probs, axis=0, keepdims=True)
            grad_scores = (probs * (grad_probs - row_dot)).astype(jnp.bfloat16)
            grad_values = grad_values + dots(probs.astype(jnp.bfloat16), upstream, 1, 0)
            grad_keys = grad_keys + dots(grad_scores, queries, 1, 0)
            grad_queries = dots(keys, grad_scores, 0, 0)
            halves.append(grad_queries[half * HEAD_DIM : (half + 1) * HEAD_DIM])
        grad_queries = jnp.concatenate(halves, axis=0) * (1.0 / math.sqrt(HEAD_DIM))
        dq_ref[rows, :] = grad_queries.T.astype(dq_ref.dtype)
    grad_keys = grad_keys * (1.0 / math.sqrt(HEAD_DIM))
    dk0_ref[...] = grad_keys[:own]
    dk1_ref[...] = grad_keys[own:]
    dv0_ref[...] = grad_values[:own]
    dv1_ref[...] = grad_values[own:]


def attention_backward(queries, keys, values, log_norm, grad_mixed):
    length, width = queries.shape
    pairs = width // PAIR
    block = pl.BlockSpec((length, PAIR), lambda i: (0, i))
    flops = 20 * length * length * width
    wide = jax.ShapeDtypeStruct((length, width), jnp.float32)
    return pl.pallas_call(
        backward_kernel,
        grid=(pairs,),
        out_shape=[jax.ShapeDtypeStruct((length, width), queries.dtype)] + [wide] * 4,
        in_specs=[block] * 5 + [pl.BlockSpec((1, 2, length), lambda i: (i, 0, 0)), block],
        out_specs=[block] * 5,
        cost_estimate=pl.CostEstimate(
            flops=2 * flops, bytes_accessed=32 * length * width, transcendentals=flops // 640
        ),
        name="attention_backward",
    )(queries, *keys, *values, log_norm, grad_mixed)


def project_kernel(hidden_ref, weight_ref, bias_ref, q_ref, k_ref, v_ref):
    blocks, width = weight_ref.shape[0], weight_ref.shape[2] // 4
    packed = [dots(hidden_ref[...], weight_ref[m], 1, 0) for m in range(blocks)]

    def slot(at):
        return jnp.concatenate([p[:, at * width : (at + 1) * width] for p in packed], axis=1)

    q_ref[...] = (slot(0) + bias_ref[0:1]).astype(q_ref.dtype)
    k_ref[...] = slot(1).astype(k_ref.dtype)
    v_ref[...] = (slot(2) + bias_ref[1:2]).astype(v_ref.dtype)


def project(hidden, blocks, biases):
    rows = hidden.shape[0]
    return pl.pallas_call(
        project_kernel,
        out_shape=[jax.ShapeDtypeStruct((rows, D), hidden.dtype)] * 3,
        cost_estimate=pl.CostEstimate(
            flops=8 * rows * D * D, bytes_accessed=8 * D * D, transcendentals=0
        ),
        name="project_heads",
    )(hidden, blocks, biases)


def mixed_grad_kernel(dy_ref, weight_ref, out_ref):
    blocks, width = weight_ref.shape[0], weight_ref.shape[2] // 4
    dy = dy_ref[...]
    packed = [dots(dy, weight_ref[m][:, 3 * width :], 1, 0) for m in range(blocks)]
    out_ref[...] = jnp.concatenate(packed, axis=1).astype(out_ref.dtype)


def hidden_grad_kernel(dq_ref, dk_ref, dv_ref, weight_ref, out_ref):
    blocks, width = weight_ref.shape[0], weight_ref.shape[2] // 4
    grads = [r[...].astype(jnp.float32) for r in (dq_ref, dk_ref, dv_ref)]
    empty = jnp.zeros((grads[0].shape[0], width), jnp.float32)
    total = 0.0
    for m in range(blocks):
        block = [g[:, m * width : (m + 1) * width] for g in grads] + [empty]
        block = jnp.concatenate(block, axis=1).astype(weight_ref.dtype)
        total = total + dots(block, weight_ref[m], 1, 1)
    out_ref[...] = total


def projected(kernel, name, kind, *values):
    rows = values[0].shape[0]
    return pl.pallas_call(
        kernel,
        out_shape=jax.ShapeDtypeStruct((rows, D), kind),
        cost_estimate=pl.CostEstimate(
            flops=8 * rows * D * D, bytes_accessed=8 * D * D, transcendentals=0
        ),
        name=name,
    )(*values)


def attn_grad_kernel(hidden_ref, dq_ref, dk_ref, dv_ref, dy_ref, mixed_ref, out_ref):
    blocks, width = out_ref.shape[0], out_ref.shape[2] // 4
    hidden, dy = hidden_ref[...], dy_ref[...]
    grads = [dots(hidden, r[...], 0, 0) for r in (dq_ref, dk_ref, dv_ref)]
    grads.append(dots(dy, mixed_ref[...], 0, 0))
    for m in range(blocks):
        block = [g[:, m * width : (m + 1) * width] for g in grads]
        out_ref[m] = jnp.concatenate(block, axis=1).astype(out_ref.dtype)


def attn_weight_grad(blocks, *values):
    rows = values[0].shape[0]
    return pl.pallas_call(
        attn_grad_kernel,
        out_shape=jax.ShapeDtypeStruct((blocks, D, 4 * D // blocks), values[0].dtype),
        cost_estimate=pl.CostEstimate(
            flops=8 * rows * D * D, bytes_accessed=8 * D * D, transcendentals=0
        ),
        name="attn_weight_grad",
    )(*values)


def ff_grad_kernel(hidden_ref, dz_ref, up_ref, active_ref, out_ref):
    def put(left, right):
        grad = dots(left[...], right[0], 0, 0).astype(out_ref.dtype)
        _, wide, deep, _, rows, width = out_ref.shape
        grad = grad.reshape(deep, wide, rows, width)
        for x in range(wide):
            out_ref[0, x, :, 0] = grad[:, x]

    @pl.when(pl.program_id(1) == 0)
    def _():
        put(hidden_ref, up_ref)

    @pl.when(pl.program_id(1) == 1)
    def _():
        put(dz_ref, active_ref)


def ff_weight_grad(deep, wide, hidden, dz, grad_up, active):
    blocks, rows, width = active.shape
    piece = (wide, deep, 2, D // (deep * wide), width)
    whole = pl.BlockSpec((rows, D), lambda m, s: (0, 0))
    block = pl.BlockSpec((1, rows, width), lambda m, s: (m, 0, 0))
    return pl.pallas_call(
        ff_grad_kernel,
        grid=(blocks, 2),
        out_shape=jax.ShapeDtypeStruct((blocks, *piece), hidden.dtype),
        in_specs=[whole, whole, block, block],
        out_specs=pl.BlockSpec((1, wide, deep, 1, *piece[3:]), lambda m, s: (m, 0, 0, s, 0, 0)),
        cost_estimate=pl.CostEstimate(
            flops=4 * rows * D * blocks * width,
            bytes_accessed=4 * D * blocks * width,
            transcendentals=0,
        ),
        name="ff_weight_grad",
    )(hidden, dz, grad_up, active)


def score_kernel(head_ref, word_ref, bias_ref, label_ref, stat_ref, top, total, target):
    at, last = pl.program_id(1), pl.num_programs(1) - 1
    logits = dots(head_ref[...], word_ref[...], 1, 1) + bias_ref[...]
    column = at * logits.shape[1] + lax.broadcasted_iota(jnp.int32, logits.shape, 1)

    @pl.when(at == 0)
    def _():
        top[...] = jnp.full(top.shape, -jnp.inf, jnp.float32)
        total[...] = jnp.zeros(total.shape, jnp.float32)
        target[...] = jnp.zeros(target.shape, jnp.float32)

    old = top[...]
    new = jnp.maximum(old, jnp.max(logits, axis=1, keepdims=True))
    added = jnp.sum(jnp.exp(logits - new), axis=1, keepdims=True)
    total[...] = total[...] * jnp.exp(old - new) + added
    top[...] = new
    hits = jnp.where(column == label_ref[...], logits, 0.0)
    target[...] += jnp.sum(hits, axis=1, keepdims=True)

    @pl.when(at == last)
    def _():
        lane = lax.broadcasted_iota(jnp.int32, stat_ref.shape, 1)
        stat_ref[...] = jnp.where(
            lane == 0, top[...], jnp.where(lane == 1, total[...], target[...])
        )


def slope_kernel(
    head_ref, word_ref, bias_ref, label_ref, norm_ref, weight_ref, slope_ref, sum_ref, grad_ref
):
    at = pl.program_id(1)
    logits = dots(head_ref[...], word_ref[...], 1, 1) + bias_ref[...]
    column = at * logits.shape[1] + lax.broadcasted_iota(jnp.int32, logits.shape, 1)
    hits = jnp.where(column == label_ref[...], 1.0, 0.0)
    slope = ((jnp.exp(logits - norm_ref[...]) - hits) * weight_ref[...]).astype(jnp.bfloat16)
    slope_ref[...] = slope
    sum_ref[0] = jnp.sum(slope.astype(jnp.float32), axis=0, keepdims=True)
    part = dots(slope, word_ref[...], 1, 0)

    @pl.when(at == 0)
    def _():
        grad_ref[...] = part

    @pl.when(at > 0)
    def _():
        grad_ref[...] += part


def head_blocks(head, word, bias):
    rows, vocab = head.shape[0], word.shape[0]
    row_block = 512 if rows % 512 == 0 else rows
    block = 768 if vocab % 768 == 0 else vocab
    grid = (rows // row_block, vocab // block)
    column = pl.BlockSpec((row_block, 1), lambda i, j: (i, 0))
    specs = [
        pl.BlockSpec((row_block, D), lambda i, j: (i, 0)),
        pl.BlockSpec((block, D), lambda i, j: (j, 0)),
        pl.BlockSpec((1, block), lambda i, j: (0, j)),
        column,
    ]
    cost = pl.CostEstimate(
        flops=2 * rows * vocab * D, bytes_accessed=2 * vocab * D, transcendentals=rows * vocab
    )
    return row_block, block, grid, column, specs, cost


def word_grad_kernel(slope_ref, head_ref, at_ref, x0_ref, out_ref, total):
    chunk, last = pl.program_id(1), pl.num_programs(1) - 1
    first_row = pl.program_id(0) * total.shape[0]
    rows = first_row + lax.broadcasted_iota(jnp.int32, (total.shape[0], at_ref.shape[1]), 0)
    onehot = jnp.where(rows == at_ref[...], 1.0, 0.0).astype(jnp.bfloat16)
    part = dots(onehot, x0_ref[...], 1, 0)

    @pl.when(chunk == 0)
    def _():
        total[...] = part + dots(slope_ref[...], head_ref[...], 0, 0)

    @pl.when(chunk > 0)
    def _():
        total[...] += part

    @pl.when(chunk == last)
    def _():
        out_ref[...] = total[...].astype(out_ref.dtype)


def word_weight_grad(slopes, head, at, x0):
    (rows, vocab), tokens = slopes.shape, at.shape[0]
    block = 768 if vocab % 768 == 0 else vocab
    chunk = 2048 if tokens % 2048 == 0 else tokens
    return pl.pallas_call(
        word_grad_kernel,
        grid=(vocab // block, tokens // chunk),
        out_shape=jax.ShapeDtypeStruct((vocab, D), head.dtype),
        in_specs=[
            pl.BlockSpec((rows, block), lambda i, j: (0, i)),
            pl.BlockSpec((rows, D), lambda i, j: (0, 0)),
            pl.BlockSpec((1, chunk), lambda i, j: (0, j)),
            pl.BlockSpec((chunk, D), lambda i, j: (j, 0)),
        ],
        out_specs=pl.BlockSpec((block, D), lambda i, j: (i, 0)),
        scratch_shapes=[pltpu.VMEM((block, D), jnp.float32)],
        cost_estimate=pl.CostEstimate(
            flops=2 * (rows + tokens) * vocab * D,
            bytes_accessed=2 * vocab * (rows + D),
            transcendentals=0,
        ),
        name="word_weight_grad",
    )(slopes, head, at[None], x0)


def head_scores(head, word, bias, labels):
    row_block, _, grid, _, specs, cost = head_blocks(head, word, bias)
    stats = pl.pallas_call(
        score_kernel,
        grid=grid,
        out_shape=jax.ShapeDtypeStruct((head.shape[0], 128), jnp.float32),
        in_specs=specs,
        out_specs=pl.BlockSpec((row_block, 128), lambda i, j: (i, 0)),
        scratch_shapes=[pltpu.VMEM((row_block, 1), jnp.float32)] * 3,
        cost_estimate=cost,
        name="head_scores",
    )(head, word, bias[None], labels[:, None])
    return stats[:, :3].T


def head_slopes(head, word, bias, labels, norms, weights):
    row_block, block, grid, column, specs, cost = head_blocks(head, word, bias)
    rows, vocab = head.shape[0], word.shape[0]
    slopes, sums, grad = pl.pallas_call(
        slope_kernel,
        grid=grid,
        out_shape=[
            jax.ShapeDtypeStruct((rows, vocab), head.dtype),
            jax.ShapeDtypeStruct((grid[0], 1, vocab), jnp.float32),
            jax.ShapeDtypeStruct((rows, D), jnp.float32),
        ],
        in_specs=specs + [column] * 2,
        out_specs=[
            pl.BlockSpec((row_block, block), lambda i, j: (i, j)),
            pl.BlockSpec((1, 1, block), lambda i, j: (i, 0, j)),
            pl.BlockSpec((row_block, D), lambda i, j: (i, 0)),
        ],
        cost_estimate=cost,
        name="head_slopes",
    )(head, word, bias[None], labels[:, None], norms[:, None], weights[:, None])
    return slopes, jnp.sum(sums[:, 0], axis=0), grad


def step(sizes, *args):
    (
        token_ids, type_ids, mask_pos, mask_valid, mlm_labels, nsp_labels,
        word_table, word_m, word_v, attn_weight, attn_m, attn_v,
        ff_weight, ff_m, ff_v, side_weight, side_m, side_v,
        vectors, vec_m, vec_v, split_bias, split_m, split_v,
        decoder_bias, decoder_m, decoder_v,
    ) = args
    z_size, x_size, y_size, c_size = sizes
    dp_size, mp_size = z_size * x_size, y_size * c_size
    z_at, x_at, y_at, c_at = (lax.axis_index(a) for a in ("z", "x", "y", "c"))
    dp_rank, mp_rank = z_at * x_size + x_at, y_at * c_size + c_at
    every = ("z", "x", "y", "c")
    mp_first = ("y", "c", "z", "x")
    plane = ("x", "y", "c")
    batch_size, length = token_ids.shape
    slots = mask_pos.shape[1]
    own_len, own_slots = length // c_size, slots // c_size
    vocab_own = word_table.shape[0]
    attn_cols, ff_cols = attn_weight.shape[2], ff_weight.shape[2]
    rows_own = attn_weight.shape[0]
    low = jnp.bfloat16
    links = Links(sizes)

    def mine(rows, size):
        row = lax.dynamic_index_in_dim(rows, y_at, 0, False)
        return lax.dynamic_slice_in_dim(row, c_at * size, size, 0)

    own_ids = mine(token_ids, own_len)
    own_types = mine(type_ids, own_len)
    seq_pos = lax.dynamic_index_in_dim(mask_pos, y_at, 0, False)
    own_pos = mine(mask_pos, own_slots)
    own_valid = mine(mask_valid, own_slots)
    own_labels = mine(mlm_labels, own_slots)
    first_core = (c_at == 0).astype(jnp.float32)

    side_rows = side_weight.shape[0] // mp_size
    vec_cols = vectors.shape[1]
    stripe = vocab_own * x_size
    bias_mine = lax.dynamic_slice_in_dim(decoder_bias, z_at * stripe, stripe, 0)
    int_count = own_len + 2 * own_slots
    side_own = lax.dynamic_slice_in_dim(side_weight, mp_rank * side_rows, side_rows, 0)
    both = jnp.concatenate([attn_weight.reshape(rows_own, 4 * attn_cols), side_own]).astype(low)
    word_parts = 4 if vocab_own % 64 == 0 else 1
    word_plane, both, ints, vec_parts, counts, mp_small = links.exchange(
        "word_gather",
        ("plane", plane, 0, BIG, word_table.astype(low).reshape(word_parts, -1, D)),
        links.line_move(both, 88, BIG),
        ("gather", ("z",), 0, FAST, lanes(jnp.concatenate([own_ids, own_labels, own_valid]))),
        ("gather", ("z", "x"), 0, FAST, jnp.pad(vectors.astype(low), ((0, 0), (0, 128 - vec_cols)))),
        (
            "gather",
            ("z", "x"),
            0,
            FAST,
            jnp.full((8, 128), jnp.sum(mask_valid.astype(jnp.float32))),
        ),
        ("gather", ("y", "c"), 0, FAST, lanes(jnp.concatenate([bias_mine, split_bias.reshape(-1)]))),
    )
    ints = ints.reshape(z_size, -1)[:, :int_count]
    z_ids, z_labels, z_valid = (
        ints[:, :own_len],
        ints[:, own_len : own_len + own_slots],
        ints[:, own_len + own_slots :],
    )
    total_count = jnp.sum(counts[:, 0, 0])
    total_seqs = jnp.float32(batch_size * dp_size)
    vec_rows = (
        vec_parts[:, :, :vec_cols]
        .transpose(1, 0, 2)
        .reshape(vectors.shape[0], D)
        .astype(jnp.float32)
    )
    mp_small = mp_small.reshape(mp_size, -1)
    word_plane = word_plane.reshape(-1, D)
    ff_own = ff_weight.astype(low).reshape(rows_own, 2 * ff_cols)
    word_plane, both, ff_own = lax.optimization_barrier((word_plane, both, ff_own))
    both = comm_all_gather(both.reshape(-1, D), ("y", "c", "x"))
    both = both.reshape(mp_size, x_size, z_size, -1, D)
    attn_blocks = both[:, :, :, :rows_own].transpose(0, 2, 1, 3, 4).reshape(mp_size, D, 4 * attn_cols)
    side_full = both[:, :, :, rows_own:].transpose(2, 1, 0, 3, 4).reshape(-1, D)
    ff_blocks = comm_all_gather(ff_own, mp_first).reshape(mp_size, D, 2 * ff_cols)
    bias_plane = (
        mp_small[:, :stripe].reshape(mp_size, x_size, vocab_own).transpose(1, 0, 2).reshape(-1)
    )
    split_full = mp_small[:, stripe : stripe + 6 * attn_cols].reshape(mp_size, 6, attn_cols)

    def plane_index(ids):
        block = ids // stripe
        offset = ids % stripe
        inside = block % z_size == z_at
        at = ((offset // vocab_own) * mp_size + block // z_size) * vocab_own + offset % vocab_own
        return inside, at

    flat_ids = z_ids.reshape(-1)
    inside, at = plane_index(flat_ids)
    looked = jnp.where(inside[:, None], word_plane[jnp.where(inside, at, 0)], jnp.zeros((), low))
    if z_size <= 8:
        looked = looked.reshape(z_size, 8, own_len // 8, D)
        embedded = links.fold("token_fold", looked).reshape(own_len, D).astype(jnp.float32)
    else:
        looked = looked.reshape(z_size, own_len, D)
        (found,) = links.exchange("token_spread", ("spread", ("z",), 0, BIG, looked))
        embedded = lax.dynamic_index_in_dim(looked, z_at, 0, False).astype(jnp.float32)
        embedded = embedded + jnp.sum(found.astype(jnp.float32), axis=0)
    position_rows = lax.dynamic_slice_in_dim(side_full, 2 * D + c_at * own_len, own_len, 0)
    embedded = (
        embedded
        + position_rows.astype(jnp.float32)
        + jnp.where(own_types[:, None] == 0, vec_rows[12], vec_rows[13])
    )
    hidden0 = layer_norm(embedded, vec_rows[0], vec_rows[1])
    hidden0_b = hidden0.astype(low)

    out_blocks = attn_blocks[:, :, 3 * attn_cols :]
    head_bias = split_full[:, :2].transpose(1, 0, 2).reshape(2, D)
    queries, own_keys, own_values = project(hidden0_b, attn_blocks, head_bias)
    other_keys, other_values = links.exchange(
        "key_trade", ("trade", ("c",), 0, FAST, own_keys), ("trade", ("c",), 0, FAST, own_values)
    )
    keys, values = (own_keys, other_keys), (own_values, other_values)
    mixed, log_norm = attention_forward(queries, keys, values)
    attn_out = jnp.einsum(
        "tme,mde->td",
        mixed.reshape(own_len, mp_size, attn_cols),
        out_blocks,
        preferred_element_type=jnp.float32,
    )
    resid1 = hidden0 + (attn_out + vec_rows[2])
    hidden1 = layer_norm(resid1, vec_rows[3], vec_rows[4])
    hidden1_b = hidden1.astype(low)
    ff_bias = split_full[:, 2:6].transpose(0, 2, 1).reshape(mp_size, ff_cols)
    ff_in, ff_out = ff_blocks[:, :, :ff_cols], ff_blocks[:, :, ff_cols:]
    upward = jnp.einsum("td,mdf->mtf", hidden1_b, ff_in, preferred_element_type=jnp.float32)
    upward = upward + ff_bias[:, None]
    active = gelu_exact(upward).astype(low)
    ffn_out = jnp.einsum("mtf,mdf->td", active, ff_out, preferred_element_type=jnp.float32)
    resid2 = hidden1 + (ffn_out + vec_rows[5])
    hidden2 = layer_norm(resid2, vec_rows[6], vec_rows[7])

    hidden2_b = hidden2.astype(low)
    (other_h2,) = links.exchange("hidden_trade", ("trade", ("c",), 0, FAST, hidden2_b))
    picked_b = jnp.concatenate([hidden2_b, other_h2])[
        own_pos % own_len + jnp.where(own_pos // own_len == c_at, 0, own_len)
    ]
    dense_w = side_full[D : 2 * D]
    dense_out = jnp.dot(picked_b, dense_w, preferred_element_type=jnp.float32) + vec_rows[8]
    act_dense = gelu_exact(dense_out)
    head_rows = layer_norm(act_dense, vec_rows[9], vec_rows[10])
    (head_b,) = links.exchange("head_gather", links.line_move(head_rows.astype(low), 32, FAST))
    head_b = head_b.reshape(-1, D)
    label_in, label_at = plane_index(z_labels.reshape(-1))
    label_at = jnp.where(label_in, label_at, -1)
    stats = jnp.pad(head_scores(head_b, word_plane, bias_plane, label_at), ((0, 5), (0, 0)))
    (stats,) = links.exchange("stat_gather", ("gather", ("z",), 0, FAST, stats))
    top_all = jnp.max(stats[:, 0], axis=0)
    total_all = jnp.sum(stats[:, 1] * jnp.exp(stats[:, 0] - top_all), axis=0)
    target_all = jnp.sum(stats[:, 2], axis=0)
    log_total = top_all + jnp.log(total_all)
    valid_rows = z_valid.reshape(-1).astype(jnp.float32)
    mlm_sum = -jnp.sum(valid_rows * (target_all - log_total))
    weight_rows = valid_rows / total_count
    grad_logits, decoder_part, head_part = head_slopes(
        head_b, word_plane, bias_plane, label_at, log_total, weight_rows
    )
    head_part = head_part.reshape(z_size, own_slots, D)
    (head_others,) = links.exchange("head_spread", ("spread", ("z",), 0, FAST, head_part.astype(low)))
    grad_head = lax.dynamic_index_in_dim(head_part, z_at, 0, False) + jnp.sum(
        head_others.astype(jnp.float32), axis=0
    )
    grad_act, grad_g9, grad_s9 = norm_backward(act_dense, vec_rows[9], vec_rows[10], grad_head)
    grad_dense = (grad_act * gelu_slope(dense_out)).astype(low)
    dense_bias_grad = jnp.sum(grad_dense.astype(jnp.float32), axis=0)
    dense_grad = jnp.einsum("rd,re->de", picked_b, grad_dense, preferred_element_type=jnp.float32)
    grad_picked = jnp.einsum("re,de->rd", grad_dense, dense_w, preferred_element_type=jnp.float32)
    (other_picked,) = links.exchange("picked_trade", ("trade", ("c",), 0, FAST, grad_picked))
    seq_picked = jnp.concatenate([grad_picked, other_picked])
    other_pos = lax.dynamic_slice_in_dim(seq_pos, (1 - c_at) * own_slots, own_slots, 0)
    place = (
        jnp.concatenate([own_pos, other_pos])[None, :]
        == c_at * own_len + lax.broadcasted_iota(jnp.int32, (own_len, slots), 0)
    ).astype(jnp.float32)
    grad_top = jnp.dot(place, seq_picked, precision=highest)

    cls_row = hidden2_b[0:1]
    pooler_w = side_full[:D]
    pooled = jnp.tanh(jnp.dot(cls_row, pooler_w, preferred_element_type=jnp.float32) + vec_rows[11])
    classes = vec_rows[14:16]
    nsp_logp = jax.nn.log_softmax(jnp.dot(pooled, classes.T, precision=highest), axis=-1)
    own_nsp = lax.dynamic_slice_in_dim(nsp_labels, y_at, 1, 0)
    pick_nsp = own_nsp[:, None] == lax.broadcasted_iota(jnp.int32, (1, 2), 1)
    nsp_sum = -jnp.sum(jnp.where(pick_nsp, nsp_logp, 0.0)) * first_core
    grad_nsp = (jnp.exp(nsp_logp) - pick_nsp.astype(jnp.float32)) / total_seqs * first_core
    class_grad = grad_nsp[0][:, None] * pooled
    grad_pre = jnp.dot(grad_nsp, classes, precision=highest) * (1.0 - pooled * pooled)
    pooler_bias_grad = grad_pre[0]
    pooler_grad = cls_row.astype(jnp.float32).T * grad_pre
    grad_cls = jnp.dot(grad_pre, pooler_w.astype(jnp.float32).T, precision=highest)
    first_row = lax.broadcasted_iota(jnp.int32, (own_len, 1), 0) == 0
    grad_top = grad_top + jnp.where(first_row, grad_cls, 0.0)

    grad_r2, grad_g2, grad_s2 = norm_backward(resid2, vec_rows[6], vec_rows[7], grad_top)
    ffn_grad_b = grad_r2.astype(low)
    out_bias_two = jnp.sum(ffn_grad_b.astype(jnp.float32), axis=0)
    grad_active = jnp.einsum("td,mdf->mtf", ffn_grad_b, ff_out, preferred_element_type=jnp.float32)
    grad_up = (grad_active * gelu_slope(upward)).astype(low)
    ff_bias_grad = jnp.sum(grad_up.astype(jnp.float32), axis=1)
    hidden1_part = jnp.einsum("mtf,mdf->td", grad_up, ff_in, preferred_element_type=jnp.float32)
    if rows_own % 16 == 0:
        ff_grad = ff_weight_grad(z_size, x_size, hidden1_b, ffn_grad_b, grad_up, active)
    else:
        ff_grad = jnp.stack(
            [
                jnp.einsum("td,mtf->mdf", left, right, preferred_element_type=jnp.float32)
                .astype(low)
                .reshape(mp_size, z_size, x_size, rows_own, ff_cols)
                .transpose(0, 2, 1, 3, 4)
                for left, right in ((hidden1_b, grad_up), (ffn_grad_b, active))
            ],
            axis=3,
        )
    ff_grad, hidden1_part = lax.optimization_barrier((ff_grad, hidden1_part))
    ff_red = comm_scatter_sum(ff_grad.reshape(-1, ff_cols), ("y", "c", "x"))
    ff_red = ff_red.reshape(z_size, 2 * rows_own, ff_cols)
    grad_h1 = grad_r2 + hidden1_part
    grad_r1, grad_g1, grad_s1 = norm_backward(resid1, vec_rows[3], vec_rows[4], grad_h1)
    attn_grad_b = grad_r1.astype(low)
    out_bias_one = jnp.sum(attn_grad_b.astype(jnp.float32), axis=0)
    grad_mixed = projected(mixed_grad_kernel, "mixed_grad", low, attn_grad_b, attn_blocks)
    grad_q, own_k, part_k, own_v, part_v = attention_backward(
        queries, keys, values, log_norm, grad_mixed
    )
    from_k, from_v = links.exchange(
        "key_grad_trade",
        ("trade", ("c",), 0, FAST, part_k),
        ("trade", ("c",), 0, FAST, part_v),
    )
    grad_k = (own_k + from_k).astype(low)
    grad_v = (own_v + from_v).astype(low)
    packed_sums = jnp.stack(
        [
            jnp.sum(g.astype(jnp.float32), axis=0).reshape(mp_size, attn_cols)
            for g in (grad_q, grad_v)
        ],
        axis=1,
    )
    hidden0_part = projected(
        hidden_grad_kernel, "hidden_grad", jnp.float32, grad_q, grad_k, grad_v, attn_blocks
    )
    attn_grad = attn_weight_grad(mp_size, hidden0_b, grad_q, grad_k, grad_v, attn_grad_b, mixed)
    attn_grad = attn_grad.reshape(y_size, c_size, z_size, x_size, rows_own, 4 * attn_cols)
    grad_h0 = grad_r1 + hidden0_part
    grad_x0, grad_g0, grad_s0 = norm_backward(embedded, vec_rows[0], vec_rows[1], grad_h0)

    position_grad = lax.dynamic_update_slice_in_dim(
        jnp.zeros((length, D), low), grad_x0.astype(low), c_at * own_len, 0
    )
    side_grad = jnp.concatenate([pooler_grad.astype(low), dense_grad.astype(low), position_grad], axis=0)
    side_grad = side_grad.reshape(z_size, x_size, y_size, c_size, side_rows, D)

    def joined(value, at, dim, received):
        kept = lax.dynamic_index_in_dim(value, at, dim, False)
        return (kept.astype(jnp.float32) + received.astype(jnp.float32)).astype(low)

    x0_b = grad_x0.astype(low)
    cut_one, cut_two = own_len // 8, 5 * own_len // 8
    from_a, from_s, x0_one = links.exchange(
        "grad_swap_c",
        ("swap", ("c",), 1, BIG, attn_grad),
        ("swap", ("c",), 3, BIG, side_grad),
        links.line_move(x0_b[:cut_one], 64, BIG),
    )
    attn_grad, side_grad = joined(attn_grad, c_at, 1, from_a), joined(side_grad, c_at, 3, from_s)
    from_a, from_s, x0_two = links.exchange(
        "grad_swap_xy",
        ("swap", ("x",), 2, BIG, attn_grad),
        ("swap", ("y",), 2, BIG, side_grad),
        links.line_move(x0_b[cut_one:cut_two], 64, BIG),
    )
    attn_grad, side_grad = joined(attn_grad, x_at, 2, from_a), joined(side_grad, y_at, 2, from_s)
    from_a, from_s, x0_three = links.exchange(
        "grad_swap_yx",
        ("swap", ("y",), 0, BIG, attn_grad),
        ("swap", ("x",), 1, BIG, side_grad),
        links.line_move(x0_b[cut_two:], 64, BIG),
    )
    attn_grad, side_grad = joined(attn_grad, y_at, 0, from_a), joined(side_grad, x_at, 1, from_s)

    ff_red, x0_three = lax.optimization_barrier((ff_red, x0_three))
    all_x0 = [x.reshape(z_size, -1, D) for x in (x0_one, x0_two, x0_three)]
    all_x0 = jnp.concatenate(all_x0, axis=1).reshape(-1, D)
    word_grad = word_weight_grad(grad_logits, head_b, jnp.where(inside, at, -1), all_x0)
    word_grad, attn_grad, side_grad = lax.optimization_barrier(
        (word_grad, attn_grad, side_grad)
    )
    word_red = comm_scatter_sum(word_grad, plane).astype(jnp.float32)
    from_a, from_s, from_f = links.exchange(
        "grad_spread_z",
        ("spread", ("z",), 0, BIG, attn_grad),
        ("spread", ("z",), 0, BIG, side_grad),
        ("spread", ("z",), 0, BIG, ff_red),
    )

    def total(value, received):
        kept = lax.dynamic_index_in_dim(value, z_at, 0, False).astype(jnp.float32)
        return kept + jnp.sum(received.astype(jnp.float32), axis=0)

    attn_red, side_quarter = total(attn_grad, from_a), total(side_grad, from_s)
    ff_red = total(ff_red, from_f)
    type_zero = jnp.sum(jnp.where(own_types[:, None] == 0, grad_x0, 0.0), axis=0)
    type_one = jnp.sum(jnp.where(own_types[:, None] == 1, grad_x0, 0.0), axis=0)
    vec_grad = jnp.stack(
        [
            grad_g0, grad_s0, out_bias_one, grad_g1, grad_s1, out_bias_two, grad_g2, grad_s2,
            dense_bias_grad, grad_g9, grad_s9, pooler_bias_grad, type_zero, type_one,
            class_grad[0], class_grad[1],
        ],
        axis=0,
    )
    split_grad = jnp.concatenate(
        [
            packed_sums,
            ff_bias_grad.reshape(mp_size, attn_cols, 4).transpose(0, 2, 1),
        ],
        axis=1,
    )
    late = lanes(jnp.concatenate([vec_grad.reshape(-1), split_grad.reshape(-1), decoder_part]))
    late, side_quarter = lax.optimization_barrier((late, side_quarter))
    small = links.combine(
        "small_sum",
        late,
    ).reshape(z_size, -1)
    (side_red,) = links.exchange(
        "side_gather", ("gather", ("y", "c"), 0, FAST, side_quarter.astype(low))
    )
    side_red = side_red.reshape(side_weight.shape).astype(jnp.float32)
    narrow = vec_grad.size + split_grad.size
    summed = jnp.sum(small[:, :narrow], axis=0)
    vec_all = summed[: vec_grad.size].reshape(vec_grad.shape)
    split_all = summed[vec_grad.size :].reshape(split_grad.shape)
    vec_red = lax.dynamic_slice_in_dim(vec_all, dp_rank * vec_cols, vec_cols, 1)
    split_red = lax.dynamic_index_in_dim(split_all, mp_rank, 0, False)
    decoder_red = lax.dynamic_index_in_dim(
        small[:, narrow : narrow + decoder_part.size].reshape(z_size, x_size, mp_size, vocab_own),
        mp_rank,
        2,
        False,
    ).reshape(-1)
    word_f, attn_f, ff_f = (
        word_red,
        attn_red.reshape(attn_weight.shape),
        row_major(
            ff_red.reshape(2, rows_own, ff_cols).transpose(1, 0, 2)
        ),
    )
    own_square = (
        jnp.sum(word_f * word_f)
        + jnp.sum(attn_f * attn_f)
        + jnp.sum(ff_f * ff_f)
        + jnp.sum(side_red * side_red) / mp_size
        + jnp.sum(vec_red * vec_red) / mp_size
        + (jnp.sum(split_red * split_red) + jnp.sum(decoder_red * decoder_red)) / dp_size
    )
    loss_part = mlm_sum / total_count / z_size + nsp_sum / total_seqs
    ends = jnp.where(
        lax.broadcasted_iota(jnp.int32, (8, 128), 0) == 0, own_square, loss_part
    )
    ends = jnp.sum(links.combine("norm_sum", ends), axis=0)
    grad_square, total_loss = ends[0, 0], ends[1, 0]
    grad_norm = jnp.sqrt(grad_square)
    clip_scale = max_norm / jnp.maximum(grad_norm, max_norm)
    return (
        total_loss,
        grad_norm,
        *adam_step(word_table, word_m, word_v, word_f, clip_scale, True),
        *adam_step(attn_weight, attn_m, attn_v, attn_f, clip_scale, True),
        *adam_step(ff_weight, ff_m, ff_v, ff_f, clip_scale, True),
        *adam_step(side_weight, side_m, side_v, side_red, clip_scale, True),
        *adam_step(vectors, vec_m, vec_v, vec_red, clip_scale, False),
        *adam_step(split_bias, split_m, split_v, split_red, clip_scale, False),
        *adam_step(decoder_bias, decoder_m, decoder_v, decoder_red, clip_scale, False),
    )


def solution(mesh):
    dp_size, mp_size = mesh.shape["dp"], mesh.shape["mp"]
    x_size = 2 if dp_size % 2 == 0 else 1
    c_size = 2 if mp_size % 2 == 0 else 1
    sizes = (dp_size // x_size, x_size, mp_size // c_size, c_size)
    fine = Mesh(mesh.devices.reshape(sizes), ("z", "x", "y", "c"))
    dp, mp = ("z", "x"), ("y", "c")
    word = P(("y", "c", "z", "x"), None)
    cube = P(dp, None, mp)
    kinds = (
        [P(dp, None)] * 5
        + [P(dp)]
        + [word] * 3
        + [cube] * 6
        + [P(dp, None)] * 3
        + [P(None, dp)] * 3
        + [P(None, mp)] * 3
        + [P(mp)] * 3
    )
    return jax.shard_map(
        functools.partial(step, sizes),
        mesh=fine,
        in_specs=tuple(kinds),
        out_specs=(P(), P(), *kinds[6:]),
        check_vma=False,
    )
```

```python
import functools
import math

import jax
import jax.numpy as jnp
from jax import lax
from jax.experimental.layout import Layout, with_layout_constraint
from jax.experimental import pallas as pl
from jax.experimental.pallas import tpu as pltpu
from jax.sharding import Mesh, PartitionSpec as P

D = 768
HEAD_DIM = 64


beta_one = 0.9
beta_two = 0.999
adam_eps = 1e-06
learn_rate = 0.2
decay_rate = 0.01
step_count = 10
max_norm = 0.05
norm_eps = 1e-12
highest = lax.Precision.HIGHEST


def layer_norm(inputs, norm_gain, norm_shift):
    center = inputs - jnp.mean(inputs, axis=-1, keepdims=True)
    spread = jnp.mean(center * center, axis=-1, keepdims=True)
    return center * lax.rsqrt(spread + norm_eps) * norm_gain + norm_shift


def normal_cdf(inputs):
    return 0.5 + 0.5 * lax.erf(inputs * math.sqrt(0.5))


def gelu_exact(inputs):
    return inputs * normal_cdf(inputs)


def gelu_slope(inputs):
    density = jnp.exp(-0.5 * inputs * inputs) * (1.0 / math.sqrt(2.0 * math.pi))
    return normal_cdf(inputs) + inputs * density


def norm_backward(inputs, norm_gain, norm_shift, upstream):
    _, pullback = jax.vjp(layer_norm, inputs, norm_gain, norm_shift)
    return pullback(upstream)


def adam_step(weight, moment, square, gradient, clip_scale, decays):
    gradient = gradient * clip_scale
    moment = beta_one * moment + (1 - beta_one) * gradient
    square = beta_two * square + (1 - beta_two) * gradient * gradient
    mean_hat = moment / (1 - beta_one**step_count)
    var_hat = square / (1 - beta_two**step_count)
    change = mean_hat / (jnp.sqrt(var_hat) + adam_eps)
    if decays:
        change = change + decay_rate * weight
    return (weight - learn_rate * change, moment, square)


def comm_all_gather(value, axes):
    return lax.all_gather(value, axes, axis=0, tiled=True)


def comm_scatter_sum(value, axes):
    return lax.psum_scatter(value, axes, scatter_dimension=0, tiled=True)


MESH = pl.DeviceIdType.MESH
BIG, FAST = pl.ANY, pltpu.VMEM


class Links:
    def __init__(self, sizes):
        self.sizes = dict(zip(("z", "x", "y", "c"), sizes))
        self.used = 0

    def next_id(self):
        self.used += 1
        return self.used - 1

    def count(self, axes):
        return math.prod(self.sizes[a] for a in axes)

    def place(self, axes):
        at = 0
        for a in axes:
            at = at * self.sizes[a] + lax.axis_index(a)
        return at

    def target(self, axes, flat):
        where = {}
        for a in reversed(axes):
            where[a] = lax.rem(flat, self.sizes[a])
            flat = lax.div(flat, self.sizes[a])
        return where

    def greet(self, groups):
        barrier = pltpu.get_barrier_semaphore()
        total = 0
        for axes in groups:
            size, me = self.count(axes), self.place(axes)
            for r in range(1, size):
                pl.semaphore_signal(
                    barrier,
                    inc=1,
                    device_id=self.target(axes, lax.rem(me + r, size)),
                    device_id_type=MESH,
                )
            total += size - 1
        pl.semaphore_wait(barrier, total)

    def call(self, kernel, outs, spaces, out_spaces, scratch, values, wire, name):
        result = pl.pallas_call(
            kernel,
            out_shape=outs,
            in_specs=[pl.BlockSpec(memory_space=m) for m in spaces],
            out_specs=[pl.BlockSpec(memory_space=m) for m in out_spaces],
            scratch_shapes=scratch,
            compiler_params=pltpu.CompilerParams(
                collective_id=self.next_id(),
                has_side_effects=True,
                vmem_limit_bytes=40 * 2**20,
            ),
            cost_estimate=pl.CostEstimate(flops=0, bytes_accessed=wire, transcendentals=0),
            name=name,
        )(*values)
        return result

    def exchange(self, name, *moves):
        outs, scratch = [], []
        for kind, axes, dim, _, value in moves:
            size = self.count(axes)
            shape, sends, lands = value.shape, (size - 1,), (size - 1,)
            if kind == "gather":
                shape = (size, *shape)
            elif kind == "swap":
                shape = shape[:dim] + shape[dim + 1 :]
            elif kind == "spread":
                shape = (size - 1, *shape[1:])
            elif kind == "relay":
                shape, sends = (size, *shape), (2, size - 1, shape[0])
                lands = sends
            elif kind == "plane":
                shape, sends, lands = (2, 2, 2, *shape), (7 * shape[0],), (7, shape[0])
            outs.append(jax.ShapeDtypeStruct(shape, value.dtype))
            scratch += [
                pltpu.SemaphoreType.DMA(sends),
                pltpu.SemaphoreType.DMA(lands),
                pltpu.SemaphoreType.DMA((1,)),
            ]
        spaces = [m[3] for m in moves]
        groups = []
        for kind, axes, *_ in moves:
            groups += [(a,) for a in axes] if kind == "plane" else [axes]
        groups = list(dict.fromkeys(groups))

        def kernel(*refs):
            ins, dests = refs[: len(moves)], refs[len(moves) : 2 * len(moves)]
            sems = refs[2 * len(moves) :]
            self.greet(groups)
            started, later = [], []
            for i, ((kind, axes, dim, _, _), source, dest) in enumerate(zip(moves, ins, dests)):
                sends, lands, own_sem = sems[3 * i : 3 * i + 3]
                size, me = self.count(axes), self.place(axes)
                if kind in ("relay", "plane"):
                    act = self.relay if kind == "relay" else self.plane
                    later.append(functools.partial(act, axes, source, dest, sends, lands))
                for r in range(1, size):
                    peer = lax.rem(me + r, size)
                    if kind == "gather":
                        src, dst = source, dest.at[me]
                    elif kind == "swap":
                        src, dst = source.at[(slice(None),) * dim + (peer,)], dest
                    elif kind == "spread":
                        src, dst = source.at[peer], dest.at[r - 1]
                    elif kind == "trade":
                        src, dst = source, dest
                    else:
                        continue
                    copy = pltpu.make_async_remote_copy(
                        src_ref=src,
                        dst_ref=dst,
                        send_sem=sends.at[r - 1],
                        recv_sem=lands.at[r - 1],
                        device_id=self.target(axes, peer),
                        device_id_type=MESH,
                    )
                    copy.start()
                    started.append(copy)
            runs = [act() for act in later]
            for run in runs:
                next(run)
            for i, ((kind, axes, *_), source, dest) in enumerate(zip(moves, ins, dests)):
                if kind in ("gather", "relay", "plane"):
                    at = self.place(axes)
                    if kind == "plane":
                        at = tuple(lax.axis_index(a) for a in axes)
                    copy = pltpu.make_async_copy(source, dest.at[at], sems[3 * i + 2].at[0])
                    copy.start()
                    started.append(copy)
            while runs:
                runs = [run for run in runs if next(run, run) is None]
            for copy in started:
                copy.wait()

        return self.call(
            kernel,
            outs,
            spaces,
            spaces,
            scratch,
            [m[4] for m in moves],
            sum(2 * math.prod(o.shape) * o.dtype.itemsize for o in outs),
            name,
        )

    def relay(self, axes, source, dest, sends, lands):
        (axis,) = axes
        size, parts = self.sizes[axis], source.shape[0]
        me = lax.axis_index(axis)

        def copy_of(way, hop, part):
            step = 1 if way == 0 else -1
            place = (me - step * hop, part)
            return pltpu.make_async_remote_copy(
                src_ref=source.at[part] if hop == 0 else dest.at[place],
                dst_ref=dest.at[place],
                send_sem=sends.at[way, hop, part],
                recv_sem=lands.at[way, hop, part],
                device_id={axis: me + step},
                device_id_type=MESH,
            )

        def landing(way, hop, part):
            step = 1 if way == 0 else -1
            landed = dest.at[me - step * hop, part]
            return pltpu.make_async_remote_copy(
                src_ref=landed,
                dst_ref=landed,
                send_sem=sends.at[way, hop - 1, part],
                recv_sem=lands.at[way, hop - 1, part],
                device_id={axis: me - step},
                device_id_type=MESH,
            )

        def held(way, hop):
            return me - hop >= 0 if way == 0 else me + hop <= size - 1

        def sending(way, hop):
            return held(way, hop) & (me < size - 1 if way == 0 else me > 0)

        for hop in range(size):
            for part in range(parts):
                for way in range(2):
                    if hop > 0:

                        @pl.when(held(way, hop))
                        def _():
                            landing(way, hop, part).wait_recv()

                    if hop < size - 1:

                        @pl.when(sending(way, hop))
                        def _():
                            copy_of(way, hop, part).start()

            yield
        for hop in range(size - 1):
            for part in range(parts):
                for way in range(2):

                    @pl.when(sending(way, hop))
                    def _():
                        copy_of(way, hop, part).wait_send()

    def plane(self, axes, own, out, sends, lands):
        parts = own.shape[0]
        head = (parts + 1) // 2
        x, y, c = (lax.axis_index(a) for a in axes)
        by_x, by_y, by_c = {"x": 1 - x}, {"y": 1 - y}, {"c": 1 - c}
        started = []

        def send(src, place, part, slot, peer):
            copy = pltpu.make_async_remote_copy(
                src_ref=src,
                dst_ref=out.at[(*place, part)],
                send_sem=sends.at[len(started)],
                recv_sem=lands.at[slot, part],
                device_id=peer,
                device_id_type=MESH,
            )
            copy.start()
            started.append(copy)

        def arrived(place, part, slot):
            landed = out.at[(*place, part)]
            pltpu.make_async_remote_copy(
                src_ref=landed,
                dst_ref=landed,
                send_sem=sends.at[0],
                recv_sem=lands.at[slot, part],
                device_id=by_c,
                device_id_type=MESH,
            ).wait_recv()
            return landed

        me, at_x, at_y, at_xy = (x, y, c), (1 - x, y, c), (x, 1 - y, c), (1 - x, 1 - y, c)
        for part in range(parts):
            send(own.at[part], me, part, 0, by_x)
            send(own.at[part], me, part, 1, by_y)
        for part in range(parts):
            send(own.at[part], me, part, 3, by_c)
        yield
        for part in range(parts):
            landed = arrived(at_x, part, 0)
            if part < head:
                send(landed, at_x, part, 2, by_y)
            send(landed, at_x, part, 4, by_c)
            landed = arrived(at_y, part, 1)
            if part >= head:
                send(landed, at_y, part, 2, by_x)
            send(landed, at_y, part, 5, by_c)
            yield
        for part in range(parts):
            landed = arrived(at_xy, part, 2)
            send(landed, at_xy, part, 6, by_c)
        yield
        for slot, place in ((3, me), (4, at_x), (5, at_y), (6, at_xy)):
            for part in range(parts):
                arrived((place[0], place[1], 1 - c), part, slot)
        for copy in started:
            copy.wait_send()

    def fold(self, name, value):
        size, parts = value.shape[:2]
        block = value.shape[1:]

        def kernel(source, out, land, sends, lands):
            self.greet([("z",)])
            me = lax.axis_index("z")

            def beyond(way, hop):
                return me + hop <= size - 1 if way == 0 else me - hop >= 0

            def behind(way):
                return me > 0 if way == 0 else me < size - 1

            def copy_of(way, hop, part, src):
                return pltpu.make_async_remote_copy(
                    src_ref=src,
                    dst_ref=land.at[way, hop - 1, part],
                    send_sem=sends.at[way, hop - 1, part],
                    recv_sem=lands.at[way, hop - 1, part],
                    device_id={"z": me + (1 if way == 0 else -1)},
                    device_id_type=MESH,
                )

            def landing(way, hop, part):
                landed = land.at[way, hop, part]
                return pltpu.make_async_remote_copy(
                    src_ref=landed,
                    dst_ref=landed,
                    send_sem=sends.at[way, hop, part],
                    recv_sem=lands.at[way, hop, part],
                    device_id={"z": me - (1 if way == 0 else -1)},
                    device_id_type=MESH,
                )

            for hop in range(size - 1, 0, -1):
                for part in range(parts):
                    for way in range(2):
                        goal = me + hop if way == 0 else me - hop

                        @pl.when(beyond(way, hop) & jnp.logical_not(behind(way)))
                        def _():
                            copy_of(way, hop, part, source.at[goal, part]).start()

                        if hop < size - 1:

                            @pl.when(beyond(way, hop) & behind(way))
                            def _():
                                landing(way, hop, part).wait_recv()
                                land[way, hop, part] += source[goal, part]
                                copy_of(way, hop, part, land.at[way, hop, part]).start()

            for part in range(parts):
                out[part] = source[me, part]
                for way in range(2):

                    @pl.when(behind(way))
                    def _():
                        landing(way, 0, part).wait_recv()
                        out[part] += land[way, 0, part]

            for hop in range(size - 1, 0, -1):
                for part in range(parts):
                    for way in range(2):

                        @pl.when(beyond(way, hop))
                        def _():
                            copy_of(way, hop, part, source.at[0, part]).wait_send()

        return self.call(
            kernel,
            [jax.ShapeDtypeStruct(block, value.dtype)],
            [FAST],
            [FAST],
            [
                pltpu.VMEM((2, size - 1, *block), value.dtype),
                pltpu.SemaphoreType.DMA((2, size - 1, parts)),
                pltpu.SemaphoreType.DMA((2, size - 1, parts)),
            ],
            [value],
            4 * value.size,
            name,
        )[0]

    def line_move(self, value, part_rows, memory):
        parts = value.shape[0] // part_rows if value.shape[0] % part_rows == 0 else 1
        kind = "relay" if self.sizes["z"] <= 8 else "gather"
        return (kind, ("z",), 0, memory, value.reshape(parts, -1, value.shape[1]))

    def combine(self, name, value, extra=None, axes=()):
        pairs = [a for a in ("c", "x", "y") if self.sizes[a] > 1]
        depth = self.sizes["z"]
        steps = len(pairs)

        more = [] if extra is None else [extra]
        peers = self.count(axes) - 1

        def kernel(x_ref, *refs):
            if more:
                e_ref, out_ref, all_ref, sums, land, sends, lands, e_sends, e_lands, e_own = refs
            else:
                out_ref, sums, land, sends, lands = refs
            self.greet([(a,) for a in pairs] + [("z",)] + ([axes] if more else []))
            me = lax.axis_index("z")
            beside = []
            for r in range(1, peers + 1) if more else ():
                at = self.place(axes)
                copy = pltpu.make_async_remote_copy(
                    src_ref=e_ref,
                    dst_ref=all_ref.at[at],
                    send_sem=e_sends.at[r - 1],
                    recv_sem=e_lands.at[r - 1],
                    device_id=self.target(axes, lax.rem(at + r, peers + 1)),
                    device_id_type=MESH,
                )
                copy.start()
                beside.append(copy)
            if more:
                copy = pltpu.make_async_copy(e_ref, all_ref.at[self.place(axes)], e_own.at[0])
                copy.start()
                beside.append(copy)
            for i, a in enumerate(pairs):
                source = x_ref if i == 0 else sums.at[i - 1]
                copy = pltpu.make_async_remote_copy(
                    src_ref=source,
                    dst_ref=land.at[i],
                    send_sem=sends.at[i],
                    recv_sem=lands.at[i],
                    device_id={a: 1 - lax.axis_index(a)},
                    device_id_type=MESH,
                )
                copy.start()
                copy.wait()
                sums[i] = source[...] + land[i]
            out_ref[me] = sums[steps - 1]
            started = []
            for r in range(1, depth):
                copy = pltpu.make_async_remote_copy(
                    src_ref=sums.at[steps - 1],
                    dst_ref=out_ref.at[me],
                    send_sem=sends.at[steps + r - 1],
                    recv_sem=lands.at[steps + r - 1],
                    device_id={"z": lax.rem(me + r, depth)},
                    device_id_type=MESH,
                )
                copy.start()
                started.append(copy)
            for copy in started + beside:
                copy.wait()

        outs = [jax.ShapeDtypeStruct((depth, *value.shape), value.dtype)]
        outs += [jax.ShapeDtypeStruct((peers + 1, *v.shape), v.dtype) for v in more]
        more_sems = [
            pltpu.SemaphoreType.DMA((peers,)),
            pltpu.SemaphoreType.DMA((peers,)),
            pltpu.SemaphoreType.DMA((1,)),
        ]
        return self.call(
            kernel,
            outs,
            [FAST] * len(outs),
            [FAST] * len(outs),
            [
                pltpu.VMEM((steps, *value.shape), value.dtype),
                pltpu.VMEM((steps, *value.shape), value.dtype),
                pltpu.SemaphoreType.DMA((steps + depth - 1,)),
                pltpu.SemaphoreType.DMA((steps + depth - 1,)),
                *(more_sems if more else []),
            ],
            [value, *more],
            16 * value.size * 4,
            name,
        )


def row_major(value):
    return with_layout_constraint(value, Layout(major_to_minor=tuple(range(value.ndim))))


def lanes(flat):
    padded = jnp.pad(flat, (0, -flat.size % 1024))
    return padded.reshape(-1, 128)


HEAD_SCALE = math.log2(math.e) / math.sqrt(HEAD_DIM)
PAIR = 2 * HEAD_DIM
ROWS = 256


def dots(left, right, left_dim, right_dim):
    return lax.dot_general(
        left, right, (((left_dim,), (right_dim,)), ((), ())), preferred_element_type=jnp.float32
    )


def half_lanes(value, half):
    lane = lax.broadcasted_iota(jnp.int32, value.shape, 1)
    return jnp.where((lane >= HEAD_DIM) == (half == 1), value, jnp.zeros((), value.dtype))


def forward_kernel(q_ref, k0_ref, k1_ref, v0_ref, v1_ref, out_ref, norm_ref):
    keys = jnp.concatenate([k0_ref[...], k1_ref[...]], axis=0)
    values = jnp.concatenate([v0_ref[...], v1_ref[...]], axis=0)
    for start in range(0, q_ref.shape[0], ROWS):
        rows = pl.ds(start, ROWS)
        queries = q_ref[rows, :]
        halves = []
        for half in range(2):
            scores = dots(keys, half_lanes(queries, half), 1, 1)
            top = jnp.max(scores, axis=0, keepdims=True)
            powers = jnp.exp2((scores - top) * HEAD_SCALE)
            total = jnp.sum(powers, axis=0, keepdims=True)
            probs = (powers * (1.0 / total)).astype(jnp.bfloat16)
            norm_ref[0, half : half + 1, rows] = top * HEAD_SCALE + jnp.log2(total)
            mixed = dots(values, probs, 0, 0)
            halves.append(mixed[half * HEAD_DIM : (half + 1) * HEAD_DIM])
        out_ref[rows, :] = jnp.concatenate(halves, axis=0).T.astype(out_ref.dtype)


def attention_forward(queries, keys, values):
    length, width = queries.shape
    pairs = width // PAIR
    block = pl.BlockSpec((length, PAIR), lambda i: (0, i))
    flops = 8 * length * length * width
    return pl.pallas_call(
        forward_kernel,
        grid=(pairs,),
        out_shape=[
            jax.ShapeDtypeStruct((length, width), queries.dtype),
            jax.ShapeDtypeStruct((pairs, 2, length), jnp.float32),
        ],
        in_specs=[block] * 5,
        out_specs=[block, pl.BlockSpec((1, 2, length), lambda i: (i, 0, 0))],
        cost_estimate=pl.CostEstimate(
            flops=2 * flops, bytes_accessed=16 * length * width, transcendentals=flops // 256
        ),
        name="attention_forward",
    )(queries, *keys, *values)


def backward_kernel(
    q_ref, k0_ref, k1_ref, v0_ref, v1_ref, norm_ref, g_ref, dq_ref, dk0_ref, dk1_ref, dv0_ref, dv1_ref
):
    own = k0_ref.shape[0]
    keys = jnp.concatenate([k0_ref[...], k1_ref[...]], axis=0)
    values = jnp.concatenate([v0_ref[...], v1_ref[...]], axis=0)
    grad_keys = grad_values = 0.0
    for start in range(0, q_ref.shape[0], ROWS):
        rows = pl.ds(start, ROWS)
        halves = []
        for half in range(2):
            queries = half_lanes(q_ref[rows, :], half)
            upstream = half_lanes(g_ref[rows, :], half)
            scores = dots(keys, queries, 1, 1)
            probs = jnp.exp2(scores * HEAD_SCALE - norm_ref[0, half : half + 1, rows])
            grad_probs = dots(values, upstream, 1, 1)
            row_dot = jnp.sum(grad_probs * probs, axis=0, keepdims=True)
            grad_scores = (probs * (grad_probs - row_dot)).astype(jnp.bfloat16)
            grad_values = grad_values + dots(probs.astype(jnp.bfloat16), upstream, 1, 0)
            grad_keys = grad_keys + dots(grad_scores, queries, 1, 0)
            grad_queries = dots(keys, grad_scores, 0, 0)
            halves.append(grad_queries[half * HEAD_DIM : (half + 1) * HEAD_DIM])
        grad_queries = jnp.concatenate(halves, axis=0) * (1.0 / math.sqrt(HEAD_DIM))
        dq_ref[rows, :] = grad_queries.T.astype(dq_ref.dtype)
    grad_keys = grad_keys * (1.0 / math.sqrt(HEAD_DIM))
    dk0_ref[...] = grad_keys[:own]
    dk1_ref[...] = grad_keys[own:]
    dv0_ref[...] = grad_values[:own]
    dv1_ref[...] = grad_values[own:]


def attention_backward(queries, keys, values, log_norm, grad_mixed):
    length, width = queries.shape
    pairs = width // PAIR
    block = pl.BlockSpec((length, PAIR), lambda i: (0, i))
    flops = 20 * length * length * width
    wide = jax.ShapeDtypeStruct((length, width), jnp.float32)
    return pl.pallas_call(
        backward_kernel,
        grid=(pairs,),
        out_shape=[jax.ShapeDtypeStruct((length, width), queries.dtype)] + [wide] * 4,
        in_specs=[block] * 5 + [pl.BlockSpec((1, 2, length), lambda i: (i, 0, 0)), block],
        out_specs=[block] * 5,
        cost_estimate=pl.CostEstimate(
            flops=2 * flops, bytes_accessed=32 * length * width, transcendentals=flops // 640
        ),
        name="attention_backward",
    )(queries, *keys, *values, log_norm, grad_mixed)


def project_kernel(hidden_ref, weight_ref, bias_ref, q_ref, k_ref, v_ref):
    blocks, width = weight_ref.shape[0], weight_ref.shape[2] // 4
    packed = [dots(hidden_ref[...], weight_ref[m], 1, 0) for m in range(blocks)]

    def slot(at):
        return jnp.concatenate([p[:, at * width : (at + 1) * width] for p in packed], axis=1)

    q_ref[...] = (slot(0) + bias_ref[0:1]).astype(q_ref.dtype)
    k_ref[...] = slot(1).astype(k_ref.dtype)
    v_ref[...] = (slot(2) + bias_ref[1:2]).astype(v_ref.dtype)


def project(hidden, blocks, biases):
    rows = hidden.shape[0]
    return pl.pallas_call(
        project_kernel,
        out_shape=[jax.ShapeDtypeStruct((rows, D), hidden.dtype)] * 3,
        cost_estimate=pl.CostEstimate(
            flops=8 * rows * D * D, bytes_accessed=8 * D * D, transcendentals=0
        ),
        name="project_heads",
    )(hidden, blocks, biases)


def mixed_grad_kernel(dy_ref, weight_ref, out_ref):
    blocks, width = weight_ref.shape[0], weight_ref.shape[2] // 4
    dy = dy_ref[...]
    packed = [dots(dy, weight_ref[m][:, 3 * width :], 1, 0) for m in range(blocks)]
    out_ref[...] = jnp.concatenate(packed, axis=1).astype(out_ref.dtype)


def hidden_grad_kernel(dq_ref, dk_ref, dv_ref, weight_ref, out_ref):
    blocks, width = weight_ref.shape[0], weight_ref.shape[2] // 4
    grads = [r[...].astype(jnp.float32) for r in (dq_ref, dk_ref, dv_ref)]
    empty = jnp.zeros((grads[0].shape[0], width), jnp.float32)
    total = 0.0
    for m in range(blocks):
        block = [g[:, m * width : (m + 1) * width] for g in grads] + [empty]
        block = jnp.concatenate(block, axis=1).astype(weight_ref.dtype)
        total = total + dots(block, weight_ref[m], 1, 1)
    out_ref[...] = total


def projected(kernel, name, kind, *values):
    rows = values[0].shape[0]
    return pl.pallas_call(
        kernel,
        out_shape=jax.ShapeDtypeStruct((rows, D), kind),
        cost_estimate=pl.CostEstimate(
            flops=8 * rows * D * D, bytes_accessed=8 * D * D, transcendentals=0
        ),
        name=name,
    )(*values)


def attn_grad_kernel(hidden_ref, dq_ref, dk_ref, dv_ref, dy_ref, mixed_ref, out_ref):
    blocks, width = out_ref.shape[0], out_ref.shape[2] // 4
    hidden, dy = hidden_ref[...], dy_ref[...]
    grads = [dots(hidden, r[...], 0, 0) for r in (dq_ref, dk_ref, dv_ref)]
    grads.append(dots(dy, mixed_ref[...], 0, 0))
    for m in range(blocks):
        block = [g[:, m * width : (m + 1) * width] for g in grads]
        out_ref[m] = jnp.concatenate(block, axis=1).astype(out_ref.dtype)


def attn_weight_grad(blocks, *values):
    rows = values[0].shape[0]
    return pl.pallas_call(
        attn_grad_kernel,
        out_shape=jax.ShapeDtypeStruct((blocks, D, 4 * D // blocks), values[0].dtype),
        cost_estimate=pl.CostEstimate(
            flops=8 * rows * D * D, bytes_accessed=8 * D * D, transcendentals=0
        ),
        name="attn_weight_grad",
    )(*values)


def ff_grad_kernel(hidden_ref, dz_ref, up_ref, active_ref, out_ref):
    def put(left, right):
        grad = dots(left[...], right[0], 0, 0).astype(out_ref.dtype)
        _, wide, deep, _, rows, width = out_ref.shape
        grad = grad.reshape(deep, wide, rows, width)
        for x in range(wide):
            out_ref[0, x, :, 0] = grad[:, x]

    @pl.when(pl.program_id(1) == 0)
    def _():
        put(hidden_ref, up_ref)

    @pl.when(pl.program_id(1) == 1)
    def _():
        put(dz_ref, active_ref)


def ff_weight_grad(deep, wide, hidden, dz, grad_up, active):
    blocks, rows, width = active.shape
    piece = (wide, deep, 2, D // (deep * wide), width)
    whole = pl.BlockSpec((rows, D), lambda m, s: (0, 0))
    block = pl.BlockSpec((1, rows, width), lambda m, s: (m, 0, 0))
    return pl.pallas_call(
        ff_grad_kernel,
        grid=(blocks, 2),
        out_shape=jax.ShapeDtypeStruct((blocks, *piece), hidden.dtype),
        in_specs=[whole, whole, block, block],
        out_specs=pl.BlockSpec((1, wide, deep, 1, *piece[3:]), lambda m, s: (m, 0, 0, s, 0, 0)),
        cost_estimate=pl.CostEstimate(
            flops=4 * rows * D * blocks * width,
            bytes_accessed=4 * D * blocks * width,
            transcendentals=0,
        ),
        name="ff_weight_grad",
    )(hidden, dz, grad_up, active)


def score_kernel(head_ref, word_ref, bias_ref, label_ref, stat_ref, top, total, target):
    at, last = pl.program_id(1), pl.num_programs(1) - 1
    logits = dots(head_ref[...], word_ref[...], 1, 1) + bias_ref[...]
    column = at * logits.shape[1] + lax.broadcasted_iota(jnp.int32, logits.shape, 1)

    @pl.when(at == 0)
    def _():
        top[...] = jnp.full(top.shape, -jnp.inf, jnp.float32)
        total[...] = jnp.zeros(total.shape, jnp.float32)
        target[...] = jnp.zeros(target.shape, jnp.float32)

    old = top[...]
    new = jnp.maximum(old, jnp.max(logits, axis=1, keepdims=True))
    added = jnp.sum(jnp.exp(logits - new), axis=1, keepdims=True)
    total[...] = total[...] * jnp.exp(old - new) + added
    top[...] = new
    hits = jnp.where(column == label_ref[...], logits, 0.0)
    target[...] += jnp.sum(hits, axis=1, keepdims=True)

    @pl.when(at == last)
    def _():
        lane = lax.broadcasted_iota(jnp.int32, stat_ref.shape, 1)
        stat_ref[...] = jnp.where(
            lane == 0, top[...], jnp.where(lane == 1, total[...], target[...])
        )


def slope_kernel(
    head_ref, word_ref, bias_ref, label_ref, norm_ref, weight_ref, slope_ref, sum_ref, grad_ref
):
    at = pl.program_id(1)
    logits = dots(head_ref[...], word_ref[...], 1, 1) + bias_ref[...]
    column = at * logits.shape[1] + lax.broadcasted_iota(jnp.int32, logits.shape, 1)
    hits = jnp.where(column == label_ref[...], 1.0, 0.0)
    slope = ((jnp.exp(logits - norm_ref[...]) - hits) * weight_ref[...]).astype(jnp.bfloat16)
    slope_ref[...] = slope
    sum_ref[0] = jnp.sum(slope.astype(jnp.float32), axis=0, keepdims=True)
    part = dots(slope, word_ref[...], 1, 0)

    @pl.when(at == 0)
    def _():
        grad_ref[...] = part

    @pl.when(at > 0)
    def _():
        grad_ref[...] += part


def head_blocks(head, word, bias):
    rows, vocab = head.shape[0], word.shape[0]
    row_block = 512 if rows % 512 == 0 else rows
    block = 768 if vocab % 768 == 0 else vocab
    grid = (rows // row_block, vocab // block)
    column = pl.BlockSpec((row_block, 1), lambda i, j: (i, 0))
    specs = [
        pl.BlockSpec((row_block, D), lambda i, j: (i, 0)),
        pl.BlockSpec((block, D), lambda i, j: (j, 0)),
        pl.BlockSpec((1, block), lambda i, j: (0, j)),
        column,
    ]
    cost = pl.CostEstimate(
        flops=2 * rows * vocab * D, bytes_accessed=2 * vocab * D, transcendentals=rows * vocab
    )
    return row_block, block, grid, column, specs, cost


def word_grad_kernel(slope_ref, head_ref, at_ref, x0_ref, out_ref, total):
    chunk, last = pl.program_id(1), pl.num_programs(1) - 1
    first_row = pl.program_id(0) * total.shape[0]
    rows = first_row + lax.broadcasted_iota(jnp.int32, (total.shape[0], at_ref.shape[1]), 0)
    onehot = jnp.where(rows == at_ref[...], 1.0, 0.0).astype(jnp.bfloat16)
    part = dots(onehot, x0_ref[...], 1, 0)

    @pl.when(chunk == 0)
    def _():
        total[...] = part + dots(slope_ref[...], head_ref[...], 0, 0)

    @pl.when(chunk > 0)
    def _():
        total[...] += part

    @pl.when(chunk == last)
    def _():
        out_ref[...] = total[...].astype(out_ref.dtype)


def word_weight_grad(slopes, head, at, x0):
    (rows, vocab), tokens = slopes.shape, at.shape[0]
    block = 768 if vocab % 768 == 0 else vocab
    chunk = 2048 if tokens % 2048 == 0 else tokens
    return pl.pallas_call(
        word_grad_kernel,
        grid=(vocab // block, tokens // chunk),
        out_shape=jax.ShapeDtypeStruct((vocab, D), head.dtype),
        in_specs=[
            pl.BlockSpec((rows, block), lambda i, j: (0, i)),
            pl.BlockSpec((rows, D), lambda i, j: (0, 0)),
            pl.BlockSpec((1, chunk), lambda i, j: (0, j)),
            pl.BlockSpec((chunk, D), lambda i, j: (j, 0)),
        ],
        out_specs=pl.BlockSpec((block, D), lambda i, j: (i, 0)),
        scratch_shapes=[pltpu.VMEM((block, D), jnp.float32)],
        cost_estimate=pl.CostEstimate(
            flops=2 * (rows + tokens) * vocab * D,
            bytes_accessed=2 * vocab * (rows + D),
            transcendentals=0,
        ),
        name="word_weight_grad",
    )(slopes, head, at[None], x0)


def head_scores(head, word, bias, labels):
    row_block, _, grid, _, specs, cost = head_blocks(head, word, bias)
    stats = pl.pallas_call(
        score_kernel,
        grid=grid,
        out_shape=jax.ShapeDtypeStruct((head.shape[0], 128), jnp.float32),
        in_specs=specs,
        out_specs=pl.BlockSpec((row_block, 128), lambda i, j: (i, 0)),
        scratch_shapes=[pltpu.VMEM((row_block, 1), jnp.float32)] * 3,
        cost_estimate=cost,
        name="head_scores",
    )(head, word, bias[None], labels[:, None])
    return stats[:, :3].T


def head_slopes(head, word, bias, labels, norms, weights):
    row_block, block, grid, column, specs, cost = head_blocks(head, word, bias)
    rows, vocab = head.shape[0], word.shape[0]
    slopes, sums, grad = pl.pallas_call(
        slope_kernel,
        grid=grid,
        out_shape=[
            jax.ShapeDtypeStruct((rows, vocab), head.dtype),
            jax.ShapeDtypeStruct((grid[0], 1, vocab), jnp.float32),
            jax.ShapeDtypeStruct((rows, D), jnp.float32),
        ],
        in_specs=specs + [column] * 2,
        out_specs=[
            pl.BlockSpec((row_block, block), lambda i, j: (i, j)),
            pl.BlockSpec((1, 1, block), lambda i, j: (i, 0, j)),
            pl.BlockSpec((row_block, D), lambda i, j: (i, 0)),
        ],
        cost_estimate=cost,
        name="head_slopes",
    )(head, word, bias[None], labels[:, None], norms[:, None], weights[:, None])
    return slopes, jnp.sum(sums[:, 0], axis=0), grad


def step(sizes, *args):
    (
        token_ids, type_ids, mask_pos, mask_valid, mlm_labels, nsp_labels,
        word_table, word_m, word_v, attn_weight, attn_m, attn_v,
        ff_weight, ff_m, ff_v, side_weight, side_m, side_v,
        vectors, vec_m, vec_v, split_bias, split_m, split_v,
        decoder_bias, decoder_m, decoder_v,
    ) = args
    z_size, x_size, y_size, c_size = sizes
    dp_size, mp_size = z_size * x_size, y_size * c_size
    z_at, x_at, y_at, c_at = (lax.axis_index(a) for a in ("z", "x", "y", "c"))
    dp_rank, mp_rank = z_at * x_size + x_at, y_at * c_size + c_at
    every = ("z", "x", "y", "c")
    mp_first = ("y", "c", "z", "x")
    plane = ("x", "y", "c")
    batch_size, length = token_ids.shape
    slots = mask_pos.shape[1]
    own_len, own_slots = length // c_size, slots // c_size
    vocab_own = word_table.shape[0]
    attn_cols, ff_cols = attn_weight.shape[2], ff_weight.shape[2]
    rows_own = attn_weight.shape[0]
    low = jnp.bfloat16
    links = Links(sizes)

    def mine(rows, size):
        row = lax.dynamic_index_in_dim(rows, y_at, 0, False)
        return lax.dynamic_slice_in_dim(row, c_at * size, size, 0)

    own_ids = mine(token_ids, own_len)
    own_types = mine(type_ids, own_len)
    seq_pos = lax.dynamic_index_in_dim(mask_pos, y_at, 0, False)
    own_pos = mine(mask_pos, own_slots)
    own_valid = mine(mask_valid, own_slots)
    own_labels = mine(mlm_labels, own_slots)
    first_core = (c_at == 0).astype(jnp.float32)

    side_rows = side_weight.shape[0] // mp_size
    vec_cols = vectors.shape[1]
    stripe = vocab_own * x_size
    bias_mine = lax.dynamic_slice_in_dim(decoder_bias, z_at * stripe, stripe, 0)
    int_count = own_len + 2 * own_slots
    side_own = lax.dynamic_slice_in_dim(side_weight, mp_rank * side_rows, side_rows, 0)
    both = jnp.concatenate([attn_weight.reshape(rows_own, 4 * attn_cols), side_own]).astype(low)
    word_parts = 4 if vocab_own % 64 == 0 else 1
    word_plane, both, ints, vec_parts, counts, mp_small = links.exchange(
        "word_gather",
        ("plane", plane, 0, BIG, word_table.astype(low).reshape(word_parts, -1, D)),
        links.line_move(both, 88, BIG),
        ("gather", ("z",), 0, FAST, lanes(jnp.concatenate([own_ids, own_labels, own_valid]))),
        ("gather", ("z", "x"), 0, FAST, jnp.pad(vectors.astype(low), ((0, 0), (0, 128 - vec_cols)))),
        (
            "gather",
            ("z", "x"),
            0,
            FAST,
            jnp.full((8, 128), jnp.sum(mask_valid.astype(jnp.float32))),
        ),
        ("gather", ("y", "c"), 0, FAST, lanes(jnp.concatenate([bias_mine, split_bias.reshape(-1)]))),
    )
    ints = ints.reshape(z_size, -1)[:, :int_count]
    z_ids, z_labels, z_valid = (
        ints[:, :own_len],
        ints[:, own_len : own_len + own_slots],
        ints[:, own_len + own_slots :],
    )
    total_count = jnp.sum(counts[:, 0, 0])
    total_seqs = jnp.float32(batch_size * dp_size)
    vec_rows = (
        vec_parts[:, :, :vec_cols]
        .transpose(1, 0, 2)
        .reshape(vectors.shape[0], D)
        .astype(jnp.float32)
    )
    mp_small = mp_small.reshape(mp_size, -1)
    word_plane = word_plane.reshape(-1, D)
    ff_own = ff_weight.astype(low).reshape(rows_own, 2 * ff_cols)
    word_plane, both, ff_own = lax.optimization_barrier((word_plane, both, ff_own))
    both = comm_all_gather(both.reshape(-1, D), ("y", "c", "x"))
    both = both.reshape(mp_size, x_size, z_size, -1, D)
    attn_blocks = both[:, :, :, :rows_own].transpose(0, 2, 1, 3, 4).reshape(mp_size, D, 4 * attn_cols)
    side_full = both[:, :, :, rows_own:].transpose(2, 1, 0, 3, 4).reshape(-1, D)
    ff_blocks = comm_all_gather(ff_own, mp_first).reshape(mp_size, D, 2 * ff_cols)
    bias_plane = (
        mp_small[:, :stripe].reshape(mp_size, x_size, vocab_own).transpose(1, 0, 2).reshape(-1)
    )
    split_full = mp_small[:, stripe : stripe + 6 * attn_cols].reshape(mp_size, 6, attn_cols)

    def plane_index(ids):
        block = ids // stripe
        offset = ids % stripe
        inside = block % z_size == z_at
        at = ((offset // vocab_own) * mp_size + block // z_size) * vocab_own + offset % vocab_own
        return inside, at

    flat_ids = z_ids.reshape(-1)
    inside, at = plane_index(flat_ids)
    looked = jnp.where(inside[:, None], word_plane[jnp.where(inside, at, 0)], jnp.zeros((), low))
    if z_size <= 8:
        looked = looked.reshape(z_size, 8, own_len // 8, D)
        embedded = links.fold("token_fold", looked).reshape(own_len, D).astype(jnp.float32)
    else:
        looked = looked.reshape(z_size, own_len, D)
        (found,) = links.exchange("token_spread", ("spread", ("z",), 0, BIG, looked))
        embedded = lax.dynamic_index_in_dim(looked, z_at, 0, False).astype(jnp.float32)
        embedded = embedded + jnp.sum(found.astype(jnp.float32), axis=0)
    position_rows = lax.dynamic_slice_in_dim(side_full, 2 * D + c_at * own_len, own_len, 0)
    embedded = (
        embedded
        + position_rows.astype(jnp.float32)
        + jnp.where(own_types[:, None] == 0, vec_rows[12], vec_rows[13])
    )
    hidden0 = layer_norm(embedded, vec_rows[0], vec_rows[1])
    hidden0_b = hidden0.astype(low)

    out_blocks = attn_blocks[:, :, 3 * attn_cols :]
    head_bias = split_full[:, :2].transpose(1, 0, 2).reshape(2, D)
    queries, own_keys, own_values = project(hidden0_b, attn_blocks, head_bias)
    other_keys, other_values = links.exchange(
        "key_trade", ("trade", ("c",), 0, FAST, own_keys), ("trade", ("c",), 0, FAST, own_values)
    )
    keys, values = (own_keys, other_keys), (own_values, other_values)
    mixed, log_norm = attention_forward(queries, keys, values)
    attn_out = jnp.einsum(
        "tme,mde->td",
        mixed.reshape(own_len, mp_size, attn_cols),
        out_blocks,
        preferred_element_type=jnp.float32,
    )
    resid1 = hidden0 + (attn_out + vec_rows[2])
    hidden1 = layer_norm(resid1, vec_rows[3], vec_rows[4])
    hidden1_b = hidden1.astype(low)
    ff_bias = split_full[:, 2:6].transpose(0, 2, 1).reshape(mp_size, ff_cols)
    ff_in, ff_out = ff_blocks[:, :, :ff_cols], ff_blocks[:, :, ff_cols:]
    upward = jnp.einsum("td,mdf->mtf", hidden1_b, ff_in, preferred_element_type=jnp.float32)
    upward = upward + ff_bias[:, None]
    active = gelu_exact(upward).astype(low)
    ffn_out = jnp.einsum("mtf,mdf->td", active, ff_out, preferred_element_type=jnp.float32)
    resid2 = hidden1 + (ffn_out + vec_rows[5])
    hidden2 = layer_norm(resid2, vec_rows[6], vec_rows[7])

    hidden2_b = hidden2.astype(low)
    (other_h2,) = links.exchange("hidden_trade", ("trade", ("c",), 0, FAST, hidden2_b))
    picked_b = jnp.concatenate([hidden2_b, other_h2])[
        own_pos % own_len + jnp.where(own_pos // own_len == c_at, 0, own_len)
    ]
    dense_w = side_full[D : 2 * D]
    dense_out = jnp.dot(picked_b, dense_w, preferred_element_type=jnp.float32) + vec_rows[8]
    act_dense = gelu_exact(dense_out)
    head_rows = layer_norm(act_dense, vec_rows[9], vec_rows[10])
    (head_b,) = links.exchange("head_gather", links.line_move(head_rows.astype(low), 32, FAST))
    head_b = head_b.reshape(-1, D)
    label_in, label_at = plane_index(z_labels.reshape(-1))
    label_at = jnp.where(label_in, label_at, -1)
    stats = jnp.pad(head_scores(head_b, word_plane, bias_plane, label_at), ((0, 5), (0, 0)))
    (stats,) = links.exchange("stat_gather", ("gather", ("z",), 0, FAST, stats))
    top_all = jnp.max(stats[:, 0], axis=0)
    total_all = jnp.sum(stats[:, 1] * jnp.exp(stats[:, 0] - top_all), axis=0)
    target_all = jnp.sum(stats[:, 2], axis=0)
    log_total = top_all + jnp.log(total_all)
    valid_rows = z_valid.reshape(-1).astype(jnp.float32)
    mlm_sum = -jnp.sum(valid_rows * (target_all - log_total))
    weight_rows = valid_rows / total_count
    grad_logits, decoder_part, head_part = head_slopes(
        head_b, word_plane, bias_plane, label_at, log_total, weight_rows
    )
    head_part = head_part.reshape(z_size, own_slots, D)
    (head_others,) = links.exchange("head_spread", ("spread", ("z",), 0, FAST, head_part.astype(low)))
    grad_head = lax.dynamic_index_in_dim(head_part, z_at, 0, False) + jnp.sum(
        head_others.astype(jnp.float32), axis=0
    )
    grad_act, grad_g9, grad_s9 = norm_backward(act_dense, vec_rows[9], vec_rows[10], grad_head)
    grad_dense = (grad_act * gelu_slope(dense_out)).astype(low)
    dense_bias_grad = jnp.sum(grad_dense.astype(jnp.float32), axis=0)
    dense_grad = jnp.einsum("rd,re->de", picked_b, grad_dense, preferred_element_type=jnp.float32)
    grad_picked = jnp.einsum("re,de->rd", grad_dense, dense_w, preferred_element_type=jnp.float32)
    (other_picked,) = links.exchange("picked_trade", ("trade", ("c",), 0, FAST, grad_picked))
    seq_picked = jnp.concatenate([grad_picked, other_picked])
    other_pos = lax.dynamic_slice_in_dim(seq_pos, (1 - c_at) * own_slots, own_slots, 0)
    place = (
        jnp.concatenate([own_pos, other_pos])[None, :]
        == c_at * own_len + lax.broadcasted_iota(jnp.int32, (own_len, slots), 0)
    ).astype(jnp.float32)
    grad_top = jnp.dot(place, seq_picked, precision=highest)

    cls_row = hidden2_b[0:1]
    pooler_w = side_full[:D]
    pooled = jnp.tanh(jnp.dot(cls_row, pooler_w, preferred_element_type=jnp.float32) + vec_rows[11])
    classes = vec_rows[14:16]
    nsp_logp = jax.nn.log_softmax(jnp.dot(pooled, classes.T, precision=highest), axis=-1)
    own_nsp = lax.dynamic_slice_in_dim(nsp_labels, y_at, 1, 0)
    pick_nsp = own_nsp[:, None] == lax.broadcasted_iota(jnp.int32, (1, 2), 1)
    nsp_sum = -jnp.sum(jnp.where(pick_nsp, nsp_logp, 0.0)) * first_core
    grad_nsp = (jnp.exp(nsp_logp) - pick_nsp.astype(jnp.float32)) / total_seqs * first_core
    class_grad = grad_nsp[0][:, None] * pooled
    grad_pre = jnp.dot(grad_nsp, classes, precision=highest) * (1.0 - pooled * pooled)
    pooler_bias_grad = grad_pre[0]
    pooler_grad = cls_row.astype(jnp.float32).T * grad_pre
    grad_cls = jnp.dot(grad_pre, pooler_w.astype(jnp.float32).T, precision=highest)
    first_row = lax.broadcasted_iota(jnp.int32, (own_len, 1), 0) == 0
    grad_top = grad_top + jnp.where(first_row, grad_cls, 0.0)

    grad_r2, grad_g2, grad_s2 = norm_backward(resid2, vec_rows[6], vec_rows[7], grad_top)
    ffn_grad_b = grad_r2.astype(low)
    out_bias_two = jnp.sum(ffn_grad_b.astype(jnp.float32), axis=0)
    grad_active = jnp.einsum("td,mdf->mtf", ffn_grad_b, ff_out, preferred_element_type=jnp.float32)
    grad_up = (grad_active * gelu_slope(upward)).astype(low)
    ff_bias_grad = jnp.sum(grad_up.astype(jnp.float32), axis=1)
    hidden1_part = jnp.einsum("mtf,mdf->td", grad_up, ff_in, preferred_element_type=jnp.float32)
    if rows_own % 16 == 0:
        ff_grad = ff_weight_grad(z_size, x_size, hidden1_b, ffn_grad_b, grad_up, active)
    else:
        ff_grad = jnp.stack(
            [
                jnp.einsum("td,mtf->mdf", left, right, preferred_element_type=jnp.float32)
                .astype(low)
                .reshape(mp_size, z_size, x_size, rows_own, ff_cols)
                .transpose(0, 2, 1, 3, 4)
                for left, right in ((hidden1_b, grad_up), (ffn_grad_b, active))
            ],
            axis=3,
        )
    ff_grad, hidden1_part = lax.optimization_barrier((ff_grad, hidden1_part))
    ff_red = comm_scatter_sum(ff_grad.reshape(-1, ff_cols), ("y", "c", "x"))
    ff_red = ff_red.reshape(z_size, 2 * rows_own, ff_cols)
    grad_h1 = grad_r2 + hidden1_part
    grad_r1, grad_g1, grad_s1 = norm_backward(resid1, vec_rows[3], vec_rows[4], grad_h1)
    attn_grad_b = grad_r1.astype(low)
    out_bias_one = jnp.sum(attn_grad_b.astype(jnp.float32), axis=0)
    grad_mixed = projected(mixed_grad_kernel, "mixed_grad", low, attn_grad_b, attn_blocks)
    grad_q, own_k, part_k, own_v, part_v = attention_backward(
        queries, keys, values, log_norm, grad_mixed
    )
    from_k, from_v = links.exchange(
        "key_grad_trade",
        ("trade", ("c",), 0, FAST, part_k),
        ("trade", ("c",), 0, FAST, part_v),
    )
    grad_k = (own_k + from_k).astype(low)
    grad_v = (own_v + from_v).astype(low)
    packed_sums = jnp.stack(
        [
            jnp.sum(g.astype(jnp.float32), axis=0).reshape(mp_size, attn_cols)
            for g in (grad_q, grad_v)
        ],
        axis=1,
    )
    hidden0_part = projected(
        hidden_grad_kernel, "hidden_grad", jnp.float32, grad_q, grad_k, grad_v, attn_blocks
    )
    attn_grad = attn_weight_grad(mp_size, hidden0_b, grad_q, grad_k, grad_v, attn_grad_b, mixed)
    attn_grad = attn_grad.reshape(y_size, c_size, z_size, x_size, rows_own, 4 * attn_cols)
    grad_h0 = grad_r1 + hidden0_part
    grad_x0, grad_g0, grad_s0 = norm_backward(embedded, vec_rows[0], vec_rows[1], grad_h0)

    position_grad = lax.dynamic_update_slice_in_dim(
        jnp.zeros((length, D), low), grad_x0.astype(low), c_at * own_len, 0
    )
    side_grad = jnp.concatenate([pooler_grad.astype(low), dense_grad.astype(low), position_grad], axis=0)
    side_grad = side_grad.reshape(z_size, x_size, y_size, c_size, side_rows, D)

    def joined(value, at, dim, received):
        kept = lax.dynamic_index_in_dim(value, at, dim, False)
        return (kept.astype(jnp.float32) + received.astype(jnp.float32)).astype(low)

    x0_b = grad_x0.astype(low)
    cut_one, cut_two = own_len // 8, 5 * own_len // 8
    from_a, from_s, x0_one = links.exchange(
        "grad_swap_c",
        ("swap", ("c",), 1, BIG, attn_grad),
        ("swap", ("c",), 3, BIG, side_grad),
        links.line_move(x0_b[:cut_one], 64, BIG),
    )
    attn_grad, side_grad = joined(attn_grad, c_at, 1, from_a), joined(side_grad, c_at, 3, from_s)
    from_a, from_s, x0_two = links.exchange(
        "grad_swap_xy",
        ("swap", ("x",), 2, BIG, attn_grad),
        ("swap", ("y",), 2, BIG, side_grad),
        links.line_move(x0_b[cut_one:cut_two], 64, BIG),
    )
    attn_grad, side_grad = joined(attn_grad, x_at, 2, from_a), joined(side_grad, y_at, 2, from_s)
    from_a, from_s, x0_three = links.exchange(
        "grad_swap_yx",
        ("swap", ("y",), 0, BIG, attn_grad),
        ("swap", ("x",), 1, BIG, side_grad),
        links.line_move(x0_b[cut_two:], 64, BIG),
    )
    attn_grad, side_grad = joined(attn_grad, y_at, 0, from_a), joined(side_grad, x_at, 1, from_s)

    ff_red, x0_three = lax.optimization_barrier((ff_red, x0_three))
    all_x0 = [x.reshape(z_size, -1, D) for x in (x0_one, x0_two, x0_three)]
    all_x0 = jnp.concatenate(all_x0, axis=1).reshape(-1, D)
    word_grad = word_weight_grad(grad_logits, head_b, jnp.where(inside, at, -1), all_x0)
    word_grad, attn_grad, side_grad = lax.optimization_barrier(
        (word_grad, attn_grad, side_grad)
    )
    word_red = comm_scatter_sum(word_grad, plane).astype(jnp.float32)
    from_a, from_s, from_f = links.exchange(
        "grad_spread_z",
        ("spread", ("z",), 0, BIG, attn_grad),
        ("spread", ("z",), 0, BIG, side_grad),
        ("spread", ("z",), 0, BIG, ff_red),
    )

    def total(value, received):
        kept = lax.dynamic_index_in_dim(value, z_at, 0, False).astype(jnp.float32)
        return kept + jnp.sum(received.astype(jnp.float32), axis=0)

    attn_red, side_quarter = total(attn_grad, from_a), total(side_grad, from_s)
    ff_red = total(ff_red, from_f)
    type_zero = jnp.sum(jnp.where(own_types[:, None] == 0, grad_x0, 0.0), axis=0)
    type_one = jnp.sum(jnp.where(own_types[:, None] == 1, grad_x0, 0.0), axis=0)
    vec_grad = jnp.stack(
        [
            grad_g0, grad_s0, out_bias_one, grad_g1, grad_s1, out_bias_two, grad_g2, grad_s2,
            dense_bias_grad, grad_g9, grad_s9, pooler_bias_grad, type_zero, type_one,
            class_grad[0], class_grad[1],
        ],
        axis=0,
    )
    split_grad = jnp.concatenate(
        [
            packed_sums,
            ff_bias_grad.reshape(mp_size, attn_cols, 4).transpose(0, 2, 1),
        ],
        axis=1,
    )
    late = lanes(jnp.concatenate([vec_grad.reshape(-1), split_grad.reshape(-1), decoder_part]))
    late, side_quarter = lax.optimization_barrier((late, side_quarter))
    small, side_red = links.combine("small_sum", late, side_quarter.astype(low), ("y", "c"))
    small = small.reshape(z_size, -1)
    side_red = side_red.reshape(side_weight.shape).astype(jnp.float32)
    narrow = vec_grad.size + split_grad.size
    summed = jnp.sum(small[:, :narrow], axis=0)
    vec_all = summed[: vec_grad.size].reshape(vec_grad.shape)
    split_all = summed[vec_grad.size :].reshape(split_grad.shape)
    vec_red = lax.dynamic_slice_in_dim(vec_all, dp_rank * vec_cols, vec_cols, 1)
    split_red = lax.dynamic_index_in_dim(split_all, mp_rank, 0, False)
    decoder_red = lax.dynamic_index_in_dim(
        small[:, narrow : narrow + decoder_part.size].reshape(z_size, x_size, mp_size, vocab_own),
        mp_rank,
        2,
        False,
    ).reshape(-1)
    word_f, attn_f, ff_f = (
        word_red,
        attn_red.reshape(attn_weight.shape),
        row_major(
            ff_red.reshape(2, rows_own, ff_cols).transpose(1, 0, 2)
        ),
    )
    own_square = (
        jnp.sum(word_f * word_f)
        + jnp.sum(attn_f * attn_f)
        + jnp.sum(ff_f * ff_f)
        + jnp.sum(side_red * side_red) / mp_size
        + jnp.sum(vec_red * vec_red) / mp_size
        + (jnp.sum(split_red * split_red) + jnp.sum(decoder_red * decoder_red)) / dp_size
    )
    loss_part = mlm_sum / total_count / z_size + nsp_sum / total_seqs
    ends = jnp.where(
        lax.broadcasted_iota(jnp.int32, (8, 128), 0) == 0, own_square, loss_part
    )
    ends = jnp.sum(links.combine("norm_sum", ends)[0], axis=0)
    grad_square, total_loss = ends[0, 0], ends[1, 0]
    grad_norm = jnp.sqrt(grad_square)
    clip_scale = max_norm / jnp.maximum(grad_norm, max_norm)
    return (
        total_loss,
        grad_norm,
        *adam_step(word_table, word_m, word_v, word_f, clip_scale, True),
        *adam_step(attn_weight, attn_m, attn_v, attn_f, clip_scale, True),
        *adam_step(ff_weight, ff_m, ff_v, ff_f, clip_scale, True),
        *adam_step(side_weight, side_m, side_v, side_red, clip_scale, True),
        *adam_step(vectors, vec_m, vec_v, vec_red, clip_scale, False),
        *adam_step(split_bias, split_m, split_v, split_red, clip_scale, False),
        *adam_step(decoder_bias, decoder_m, decoder_v, decoder_red, clip_scale, False),
    )


def solution(mesh):
    dp_size, mp_size = mesh.shape["dp"], mesh.shape["mp"]
    x_size = 2 if dp_size % 2 == 0 else 1
    c_size = 2 if mp_size % 2 == 0 else 1
    sizes = (dp_size // x_size, x_size, mp_size // c_size, c_size)
    fine = Mesh(mesh.devices.reshape(sizes), ("z", "x", "y", "c"))
    dp, mp = ("z", "x"), ("y", "c")
    word = P(("y", "c", "z", "x"), None)
    cube = P(dp, None, mp)
    kinds = (
        [P(dp, None)] * 5
        + [P(dp)]
        + [word] * 3
        + [cube] * 6
        + [P(dp, None)] * 3
        + [P(None, dp)] * 3
        + [P(None, mp)] * 3
        + [P(mp)] * 3
    )
    return jax.shard_map(
        functools.partial(step, sizes),
        mesh=fine,
        in_specs=tuple(kinds),
        out_specs=(P(), P(), *kinds[6:]),
        check_vma=False,
    )
```
